32 devices in a mesh: dp: 4 (over z), ctx: 4 (over y, core), tensor: 2 (over x).
Axes of the slice: x: 2, y: 2, z: 4, core: 2. Of those that a mesh axis runs over, the one named last changes fastest.
Arguments:
- layer_input: bfloat16 [8, 1024, 2048], P('dp', 'ctx'), may hold values from -6 to 6
- attn_gain: bfloat16 [2048], P(('dp', 'ctx')), may hold values from 0.099609375 to 1.8984375
- w_query: bfloat16 [2048, 2048], P(('dp', 'ctx'), 'tensor'), may hold values from -0.25 to 0.25
- w_key: bfloat16 [2048, 512], P(('dp', 'ctx'), 'tensor'), may hold values from -0.125 to 0.125
- w_value: bfloat16 [2048, 512], P(('dp', 'ctx'), 'tensor'), may hold values from -0.125 to 0.125
- w_out: bfloat16 [2048, 2048], P('tensor', ('dp', 'ctx')), may hold values from -0.75 to 0.75
- ffn_gain: bfloat16 [2048], P(('dp', 'ctx')), may hold values from 0.099609375 to 1.8984375
- w_gate: bfloat16 [2048, 8192], P(('dp', 'ctx'), 'tensor'), may hold values from -0.125 to 0.125
- w_up: bfloat16 [2048, 8192], P(('dp', 'ctx'), 'tensor'), may hold values from -0.125 to 0.125
- w_down: bfloat16 [8192, 2048], P('tensor', ('dp', 'ctx')), may hold values from -0.0625 to 0.0625
- cotangent: bfloat16 [8, 1024, 2048], P('dp', 'ctx'), may hold values from -6 to 6
Outputs:
- layer_output: bfloat16 [8, 1024, 2048], P('dp', 'ctx')
- input_grad: float32 [8, 1024, 2048], P('dp', 'ctx')
- attn_gain_grad: float32 [2048], P(('dp', 'ctx'))
- w_query_grad: float32 [2048, 2048], P(('dp', 'ctx'), 'tensor')
- w_key_grad: float32 [2048, 512], P(('dp', 'ctx'), 'tensor')
- w_value_grad: float32 [2048, 512], P(('dp', 'ctx'), 'tensor')
- w_out_grad: float32 [2048, 2048], P('tensor', ('dp', 'ctx'))
- ffn_gain_grad: float32 [2048], P(('dp', 'ctx'))
- w_gate_grad: float32 [2048, 8192], P(('dp', 'ctx'), 'tensor')
- w_up_grad: float32 [2048, 8192], P(('dp', 'ctx'), 'tensor')
- w_down_grad: float32 [8192, 2048], P('tensor', ('dp', 'ctx'))
The draws below stay inside these ranges and needn't reach their ends.
All inputs are finite; a program needn't handle non-finite values.
Results may differ from the reference program's by a relative error of at most 0.017.
Values may be sent and summed in bfloat16 or wider, within the bound.
A program may use at most 256 MiB of HBM per device.

```python
import math
import jax
import jax.numpy as jnp
from jax import lax

D = 2048
HEADS = 32
KV_HEADS = 8
HEAD_DIM = 64
FF = 8192
SEQS = 8
LENGTH = 1024


def with_spikes(values, key, source, target, blocks, factor):
    owner, partner = [(jnp.arange(values.shape[position]) // (values.shape[position] // blocks)).reshape([-1 if axis == position else 1 for axis in range(values.ndim)]) for position in (source, target)]
    chosen = jax.random.permutation(key, blocks)[partner]
    strong = (owner == chosen) | (owner == (partner + blocks // 2) % blocks)
    return jnp.where(strong, factor * values, values)


def block_scale(key, shape, pieces, least, largest):
    level = 1.0
    for position, blocks in pieces:
        heights = jax.random.uniform(jax.random.fold_in(jax.random.fold_in(key, 6), position), (blocks,), jnp.float32, least / len(pieces), largest / len(pieces))
        level = level * jnp.repeat(jnp.exp(heights), shape[position] // blocks).reshape((-1,) + (1,) * (len(shape) - 1 - position))
    return level


def scatter_about(own_key, shape, deviation, most, shards=(), held_as=jnp.bfloat16):
    loudness = block_scale(own_key, shape, shards, -0.22, 0.18) if shards else 1.0
    drawn = jax.random.normal(own_key, shape, jnp.float32) * deviation * loudness
    return jnp.minimum(jnp.maximum(drawn, -most), most).astype(held_as)


def bell_draw_with(rng, dims, deviation, limit, cuts, heavy, held_as=jnp.bfloat16):
    result = deviation * jax.random.normal(rng, dims, jnp.float32)
    if cuts:
        result = result * block_scale(rng, dims, cuts, -0.22, 0.18)
    return jnp.clip(with_spikes(result, jax.random.fold_in(rng, 3), *heavy), -limit, limit).astype(held_as)


def setup_inputs(seed: int = 0) -> dict:
    streams_of = jax.random.split(jax.random.key(seed), 12)
    layer_input = bell_draw_with(streams_of[0], (SEQS, LENGTH, D), 1.0, 6.0, ((0, 4), (1, 4)), (1, 2, 4, 2.0))
    attn_gain = jnp.clip(1.0 + 0.18 * jax.random.normal(streams_of[1], (D,), jnp.float32), 0.099609375, 1.8984375).astype(jnp.bfloat16)
    w_query = scatter_about(streams_of[2], (D, HEADS * HEAD_DIM), (D // 4) ** -0.5, 0.25, ((0, 16), (1, 2)))
    w_key = scatter_about(streams_of[3], (D, KV_HEADS * HEAD_DIM), D ** -0.5, 0.125, ((0, 16), (1, 2)))
    w_value = scatter_about(streams_of[4], (D, KV_HEADS * HEAD_DIM), D ** -0.5, 0.125, ((0, 16), (1, 2)))
    w_out = scatter_about(streams_of[5], (HEADS * HEAD_DIM, D), HEAD_DIM ** -0.5, 0.75, ((0, 2), (1, 16)))
    ffn_gain = jnp.clip(1.0 + 0.18 * jax.random.normal(streams_of[6], (D,), jnp.float32), 0.099609375, 1.8984375).astype(jnp.bfloat16)
    w_gate = scatter_about(streams_of[7], (D, FF), D ** -0.5, 0.125, ((0, 16), (1, 2)))
    w_up = scatter_about(streams_of[8], (D, FF), D ** -0.5, 0.125, ((0, 16), (1, 2)))
    w_down = scatter_about(streams_of[9], (FF, D), FF ** -0.5, 0.0625, ((0, 2), (1, 16)))
    cotangent = bell_draw_with(streams_of[10], (SEQS, LENGTH, D), 1.0, 6.0, ((0, 4), (1, 4)), (1, 2, 4, 2.0))
    return dict(layer_input=layer_input, attn_gain=attn_gain, w_query=w_query, w_key=w_key, w_value=w_value, w_out=w_out, ffn_gain=ffn_gain, w_gate=w_gate, w_up=w_up, w_down=w_down, cotangent=cotangent)


EPSILON = 1e-05
ROPE_BASE = 500000.0
HIGHEST = lax.Precision.HIGHEST

@jax.custom_vjp
def low(v):
    return lax.optimization_barrier(v.astype(jnp.bfloat16)).astype(jnp.float32)

@jax.custom_vjp
def low_back(v):
    return v

def low_keep(v):
    return (low(v), None)

def low_pass(kept, grad):
    return (grad,)

def back_keep(v):
    return (v, None)

def back_low(kept, grad):
    return (low(grad),)
low.defvjp(low_keep, low_pass)
low_back.defvjp(back_keep, back_low)

def rotate(values, cosine, sine_val):
    middle = values.shape[-1] // 2
    leading = values[..., :middle]
    trailing = values[..., middle:]
    return jnp.concatenate([leading * cosine - trailing * sine_val, trailing * cosine + leading * sine_val], axis=-1)

def angles(positions, head_dim):
    exponent = jnp.arange(head_dim // 2).astype(jnp.float32) * (-2.0 * math.log(ROPE_BASE) / head_dim)
    return positions.astype(jnp.float32)[:, None] * jnp.exp(exponent)[None, :]

def layer(inputs, attn_gain, w_query, w_key, w_value, w_out, ffn_gain, w_gate, w_up, w_down):
    seq_len = inputs.shape[1]
    group_size = HEADS // KV_HEADS
    scale = HEAD_DIM ** (-0.5)
    theta = angles(jnp.arange(seq_len), HEAD_DIM)
    cosine = jnp.cos(theta)
    sine_val = jnp.sin(theta)
    causal = jnp.arange(seq_len)[:, None] >= jnp.arange(seq_len)[None, :]

    def single(tokens):
        factor_one = lax.rsqrt(lax.optimization_barrier(jnp.mean(tokens * tokens, axis=-1, keepdims=True)) + EPSILON)
        normed_one = low(tokens * factor_one * attn_gain)
        query_pre = low_back(jnp.dot(normed_one, w_query, precision=HIGHEST)).reshape(seq_len, KV_HEADS, group_size, HEAD_DIM)
        queries = low(rotate(query_pre, cosine[:, None, None, :], sine_val[:, None, None, :]))
        key_pre = low_back(jnp.dot(normed_one, w_key, precision=HIGHEST)).reshape(seq_len, KV_HEADS, HEAD_DIM)
        keys = low(rotate(key_pre, cosine[:, None, :], sine_val[:, None, :]))
        values = low(low_back(jnp.dot(normed_one, w_value, precision=HIGHEST))).reshape(seq_len, KV_HEADS, HEAD_DIM)
        raw_scores = jnp.einsum('qhgd,khd->hgqk', queries, keys, precision=HIGHEST)
        scores = jnp.where(causal, low_back(raw_scores * scale), -1e+30)
        peak_row = lax.optimization_barrier(jnp.max(scores, axis=-1, keepdims=True))
        powers = jnp.exp(scores - peak_row)
        probability = low(powers / lax.optimization_barrier(jnp.sum(powers, axis=-1, keepdims=True)))
        mixed = jnp.einsum('hgqk,khd->qhgd', probability, values, precision=HIGHEST)
        attended = low(low_back(mixed.reshape(seq_len, HEADS * HEAD_DIM)))
        hidden = tokens + low_back(jnp.dot(attended, w_out, precision=HIGHEST))
        factor_two = lax.rsqrt(lax.optimization_barrier(jnp.mean(hidden * hidden, axis=-1, keepdims=True)) + EPSILON)
        normed_two = low(hidden * factor_two * ffn_gain)
        gate_pre = low_back(jnp.dot(normed_two, w_gate, precision=HIGHEST))
        up_pre = low_back(jnp.dot(normed_two, w_up, precision=HIGHEST))
        product = low(jax.nn.silu(gate_pre) * up_pre)
        return hidden + low_back(jnp.dot(product, w_down, precision=HIGHEST))
    return lax.map(jax.checkpoint(single), inputs)

def reference(layer_input, attn_gain, w_query, w_key, w_value, w_out, ffn_gain, w_gate, w_up, w_down, cotangent):
    params = tuple((member.astype(jnp.float32) for member in (layer_input, attn_gain, w_query, w_key, w_value, w_out, ffn_gain, w_gate, w_up, w_down)))
    output, pullback = jax.vjp(layer, *params)
    gradients = pullback(cotangent.astype(jnp.float32))
    return (output.astype(jnp.bfloat16), gradients[0], gradients[1], gradients[2], gradients[3], gradients[4], gradients[5], gradients[6], gradients[7], gradients[8], gradients[9])
```

```python
import functools
import math

import jax
import jax.numpy as jnp
from jax import lax
from jax.experimental import pallas as pl
from jax.experimental.pallas import tpu as pltpu
from jax.sharding import PartitionSpec as P

HEAD_DIM = 64


EPSILON = 1e-05
ROPE_BASE = 500000.0


def rotate(values, cosine, sine_val):
    middle = values.shape[-1] // 2
    leading = values[..., :middle]
    trailing = values[..., middle:]
    return jnp.concatenate(
        [leading * cosine - trailing * sine_val, trailing * cosine + leading * sine_val], axis=-1
    )


def unrotate(gradient, cosine, sine_val):
    middle = gradient.shape[-1] // 2
    leading = gradient[..., :middle]
    trailing = gradient[..., middle:]
    return jnp.concatenate(
        [leading * cosine + trailing * sine_val, trailing * cosine - leading * sine_val], axis=-1
    )


def angles(positions, head_dim):
    exponent = jnp.arange(head_dim // 2).astype(jnp.float32) * (
        -2.0 * math.log(ROPE_BASE) / head_dim
    )
    return positions.astype(jnp.float32)[:, None] * jnp.exp(exponent)[None, :]


def rms_factor(row_values):
    return lax.rsqrt(jnp.mean(row_values * row_values, axis=-1, keepdims=True) + EPSILON)


def rms_back(upstream, row_values, factor, gain_row):
    scaled = upstream * gain_row
    gain_term = jnp.sum(upstream * row_values * factor, axis=0)
    inner_mean = jnp.mean(scaled * row_values, axis=-1, keepdims=True)
    return (factor * scaled - row_values * (factor * factor * factor) * inner_mean, gain_term)


def matmul_t(left_op, right_op):
    return lax.dot_general(
        left_op, right_op, (((0,), (0,)), ((), ())), preferred_element_type=jnp.float32
    )


def matmul_nt(left_op, right_op):
    return lax.dot_general(
        left_op, right_op, (((1,), (1,)), ((), ())), preferred_element_type=jnp.float32
    )


def on_device(
    layer_input,
    attn_gain,
    w_query,
    w_key,
    w_value,
    w_out,
    ffn_gain,
    w_gate,
    w_up,
    w_down,
    cotangent,
):
    seq_dev, span_len, model_width = layer_input.shape
    row_count = seq_dev * span_len
    length_all = span_len * lax.axis_size("ctx")
    full_q, full_k, full_v, full_o, full_gate, full_up, full_down, gain_attn, gain_ffn = (
        lax.all_gather(w_query, ("dp", "ctx"), axis=0, tiled=True),
        lax.all_gather(w_key, ("dp", "ctx"), axis=0, tiled=True),
        lax.all_gather(w_value, ("dp", "ctx"), axis=0, tiled=True),
        lax.all_gather(w_out, ("dp", "ctx"), axis=1, tiled=True),
        lax.all_gather(w_gate, ("dp", "ctx"), axis=0, tiled=True),
        lax.all_gather(w_up, ("dp", "ctx"), axis=0, tiled=True),
        lax.all_gather(w_down, ("dp", "ctx"), axis=1, tiled=True),
        lax.all_gather(attn_gain, ("dp", "ctx"), axis=0, tiled=True),
        lax.all_gather(ffn_gain, ("dp", "ctx"), axis=0, tiled=True),
    )
    kv_local = full_k.shape[1] // HEAD_DIM
    group_size = full_q.shape[1] // HEAD_DIM // kv_local
    block_count = seq_dev * kv_local
    scale = HEAD_DIM ** (-0.5)
    query_pos = lax.axis_index("ctx") * span_len + jnp.arange(span_len)
    theta = angles(query_pos, HEAD_DIM)
    cosine = jnp.cos(theta)
    sine_val = jnp.sin(theta)
    causal = query_pos[:, None] >= jnp.arange(length_all)[None, :]
    inputs_f = layer_input.reshape(row_count, model_width).astype(jnp.float32)
    gain_one = gain_attn.astype(jnp.float32)
    gain_two = gain_ffn.astype(jnp.float32)
    factor_one = rms_factor(inputs_f)
    normed_one = (inputs_f * factor_one * gain_one).astype(jnp.bfloat16)
    query_pre = jnp.dot(normed_one, full_q, preferred_element_type=jnp.float32).reshape(
        seq_dev, span_len, kv_local, group_size, HEAD_DIM
    )
    queries = rotate(
        query_pre, cosine[None, :, None, None, :], sine_val[None, :, None, None, :]
    ).astype(jnp.bfloat16)
    key_pre = jnp.dot(normed_one, full_k, preferred_element_type=jnp.float32).reshape(
        seq_dev, span_len, kv_local, HEAD_DIM
    )
    keys_own = (
        rotate(key_pre, cosine[None, :, None, :], sine_val[None, :, None, :])
        .astype(jnp.bfloat16)
        .reshape(seq_dev, span_len, kv_local * HEAD_DIM)
    )
    values_own = (
        jnp.dot(normed_one, full_v, preferred_element_type=jnp.float32)
        .astype(jnp.bfloat16)
        .reshape(seq_dev, span_len, kv_local * HEAD_DIM)
    )
    keys_all, values_all = (
        lax.all_gather(keys_own, "ctx", axis=1, tiled=True),
        lax.all_gather(values_own, "ctx", axis=1, tiled=True),
    )
    query_blocks = jnp.transpose(queries, (0, 2, 1, 3, 4)).reshape(
        block_count, span_len, group_size, HEAD_DIM
    )
    key_blocks = jnp.transpose(
        keys_all.reshape(seq_dev, length_all, kv_local, HEAD_DIM), (0, 2, 1, 3)
    ).reshape(block_count, length_all, HEAD_DIM)
    value_blocks = jnp.transpose(
        values_all.reshape(seq_dev, length_all, kv_local, HEAD_DIM), (0, 2, 1, 3)
    ).reshape(block_count, length_all, HEAD_DIM)

    def scores_of(query_b, key_b):
        raw_scores = jnp.einsum("qgd,kd->gqk", query_b, key_b, preferred_element_type=jnp.float32)
        return jnp.where(causal[None], raw_scores * scale, -1e30)

    def attend(block_in):
        query_b, key_b, value_b = block_in
        scores = scores_of(query_b, key_b)
        peak_row = jnp.max(scores, axis=-1, keepdims=True)
        powers = jnp.exp(scores - peak_row)
        total_sum = jnp.sum(powers, axis=-1, keepdims=True)
        probability = (powers / total_sum).astype(jnp.bfloat16)
        mixed = jnp.einsum("gqk,kd->qgd", probability, value_b, preferred_element_type=jnp.float32)
        return (mixed.astype(jnp.bfloat16), peak_row + jnp.log(total_sum))

    mixed_blocks, logsum = lax.map(attend, (query_blocks, key_blocks, value_blocks))
    attended = jnp.transpose(
        mixed_blocks.reshape(seq_dev, kv_local, span_len, group_size, HEAD_DIM), (0, 2, 1, 3, 4)
    ).reshape(row_count, kv_local * group_size * HEAD_DIM)
    attn_part = jnp.dot(attended, full_o, preferred_element_type=jnp.float32)
    hidden = inputs_f + lax.psum(attn_part, "tensor")
    factor_two = rms_factor(hidden)
    normed_two = (hidden * factor_two * gain_two).astype(jnp.bfloat16)
    gate_pre = jnp.dot(normed_two, full_gate, preferred_element_type=jnp.float32)
    up_pre = jnp.dot(normed_two, full_up, preferred_element_type=jnp.float32)
    sigma = jax.nn.sigmoid(gate_pre)
    product = (gate_pre * sigma * up_pre).astype(jnp.bfloat16)
    ffn_part = jnp.dot(product, full_down, preferred_element_type=jnp.float32)
    out_f = hidden + lax.psum(ffn_part.astype(jnp.bfloat16), "tensor").astype(jnp.float32)
    layer_output = out_f.astype(jnp.bfloat16).reshape(seq_dev, span_len, model_width)
    grad_out = cotangent.reshape(row_count, model_width).astype(jnp.float32)
    grad_low = cotangent.reshape(row_count, model_width)
    down_grad = matmul_t(product, grad_low)
    prod_grad = matmul_nt(grad_low, full_down)
    gate_grad = (prod_grad * up_pre * sigma * (1.0 + gate_pre * (1.0 - sigma))).astype(jnp.bfloat16)
    up_grad = (prod_grad * gate_pre * sigma).astype(jnp.bfloat16)
    gate_w_grad = matmul_t(normed_two, gate_grad)
    up_w_grad = matmul_t(normed_two, up_grad)
    normed_two_part = matmul_nt(gate_grad, full_gate) + matmul_nt(up_grad, full_up)
    normed_two_grad = lax.psum(normed_two_part, "tensor")
    hidden_back, ffn_gain_term = rms_back(normed_two_grad, hidden, factor_two, gain_two)
    hidden_grad = grad_out + hidden_back
    hidden_low = hidden_grad.astype(jnp.bfloat16)
    out_w_grad = matmul_t(attended, hidden_low)
    attended_grad = matmul_nt(hidden_low, full_o).astype(jnp.bfloat16)
    upstream_blocks = jnp.transpose(
        attended_grad.reshape(seq_dev, span_len, kv_local, group_size, HEAD_DIM), (0, 2, 1, 3, 4)
    ).reshape(block_count, span_len, group_size, HEAD_DIM)

    def attend_back(block_in):
        query_b, key_b, value_b, logsum_b, upstream_b = block_in
        scores = scores_of(query_b, key_b)
        probability = jnp.exp(scores - logsum_b)
        rounded = probability.astype(jnp.bfloat16)
        value_grad = jnp.einsum(
            "gqk,qgd->kd", rounded, upstream_b, preferred_element_type=jnp.float32
        )
        prob_grad = jnp.einsum(
            "qgd,kd->gqk", upstream_b, value_b, preferred_element_type=jnp.float32
        )
        inner_sum = jnp.sum(probability * prob_grad, axis=-1, keepdims=True)
        score_grad = (probability * (prob_grad - inner_sum)).astype(jnp.bfloat16)
        query_grad = (
            jnp.einsum("gqk,kd->qgd", score_grad, key_b, preferred_element_type=jnp.float32) * scale
        )
        key_grad = (
            jnp.einsum("gqk,qgd->kd", score_grad, query_b, preferred_element_type=jnp.float32)
            * scale
        )
        return (query_grad, key_grad, value_grad)

    query_grads, key_grads, value_grads = lax.map(
        attend_back, (query_blocks, key_blocks, value_blocks, logsum, upstream_blocks)
    )
    key_rows = jnp.transpose(
        key_grads.reshape(seq_dev, kv_local, length_all, HEAD_DIM), (0, 2, 1, 3)
    ).reshape(seq_dev, length_all, kv_local * HEAD_DIM)
    value_rows = jnp.transpose(
        value_grads.reshape(seq_dev, kv_local, length_all, HEAD_DIM), (0, 2, 1, 3)
    ).reshape(seq_dev, length_all, kv_local * HEAD_DIM)
    key_mine, value_mine = (
        lax.psum_scatter(key_rows, "ctx", scatter_dimension=1, tiled=True),
        lax.psum_scatter(value_rows, "ctx", scatter_dimension=1, tiled=True),
    )
    key_low = (
        unrotate(
            key_mine.reshape(seq_dev, span_len, kv_local, HEAD_DIM),
            cosine[None, :, None, :],
            sine_val[None, :, None, :],
        )
        .astype(jnp.bfloat16)
        .reshape(row_count, kv_local * HEAD_DIM)
    )
    value_low = value_mine.astype(jnp.bfloat16).reshape(row_count, kv_local * HEAD_DIM)
    query_rot = jnp.transpose(
        query_grads.reshape(seq_dev, kv_local, span_len, group_size, HEAD_DIM), (0, 2, 1, 3, 4)
    )
    query_low = (
        unrotate(query_rot, cosine[None, :, None, None, :], sine_val[None, :, None, None, :])
        .astype(jnp.bfloat16)
        .reshape(row_count, kv_local * group_size * HEAD_DIM)
    )
    query_w_grad = matmul_t(normed_one, query_low)
    key_w_grad = matmul_t(normed_one, key_low)
    value_w_grad = matmul_t(normed_one, value_low)
    normed_one_part = (
        matmul_nt(query_low, full_q) + matmul_nt(key_low, full_k) + matmul_nt(value_low, full_v)
    )
    normed_one_grad = lax.psum(normed_one_part.astype(jnp.bfloat16), "tensor").astype(jnp.float32)
    input_back, attn_gain_term = rms_back(normed_one_grad, inputs_f, factor_one, gain_one)
    input_grad = (hidden_grad + input_back).reshape(seq_dev, span_len, model_width)
    (
        query_sum,
        key_sum,
        value_sum,
        out_sum,
        gate_sum,
        up_sum,
        down_sum,
        attn_gain_sum,
        ffn_gain_sum,
    ) = (
        lax.psum_scatter(query_w_grad, ("dp", "ctx"), scatter_dimension=0, tiled=True),
        lax.psum_scatter(key_w_grad, ("dp", "ctx"), scatter_dimension=0, tiled=True),
        lax.psum_scatter(value_w_grad, ("dp", "ctx"), scatter_dimension=0, tiled=True),
        lax.psum_scatter(out_w_grad, ("dp", "ctx"), scatter_dimension=1, tiled=True),
        lax.psum_scatter(gate_w_grad, ("dp", "ctx"), scatter_dimension=0, tiled=True),
        lax.psum_scatter(up_w_grad, ("dp", "ctx"), scatter_dimension=0, tiled=True),
        lax.psum_scatter(down_grad, ("dp", "ctx"), scatter_dimension=1, tiled=True),
        lax.psum_scatter(attn_gain_term, ("dp", "ctx"), scatter_dimension=0, tiled=True),
        lax.psum_scatter(ffn_gain_term, ("dp", "ctx"), scatter_dimension=0, tiled=True),
    )
    return (
        layer_output,
        input_grad,
        attn_gain_sum,
        query_sum,
        key_sum,
        value_sum,
        out_sum,
        ffn_gain_sum,
        gate_sum,
        up_sum,
        down_sum,
    )


MESH_ID = pl.DeviceIdType.MESH
BF16 = jnp.bfloat16
F32 = jnp.float32
QB = 256


def place():
    side = lax.axis_index("tensor")
    ctx = lax.axis_index("ctx")
    row = ctx // 2
    core = ctx % 2
    near_core = {"ctx": row * 2 + (1 - core)}
    near_side = {"tensor": 1 - side}
    near_row = {"ctx": (1 - row) * 2 + core}
    return side, row, core, near_core, near_side, near_row


def greet(neighbours):
    barrier = pltpu.get_barrier_semaphore()
    for target in neighbours:
        pl.semaphore_signal(barrier, inc=1, device_id=target, device_id_type=MESH_ID)
    pl.semaphore_wait(barrier, len(neighbours))


def remote(source, target, send_sem, recv_sem, device):
    return pltpu.make_async_remote_copy(
        src_ref=source,
        dst_ref=target,
        send_sem=send_sem,
        recv_sem=recv_sem,
        device_id=device,
        device_id_type=MESH_ID,
    )


def gather_kernel(rows, block_ref, all_ref, send_sems, recv_sems, local_sem):
    side, row, core, near_core, near_side, near_row = place()
    half = rows // 2

    def spot(a, b, c, part=None):
        start = (a * 4 + b * 2 + c) * rows
        if part is None:
            return all_ref.at[pl.ds(pl.multiple_of(start, rows), rows)]
        return all_ref.at[pl.ds(pl.multiple_of(start + part * half, half), half)]

    greet((near_core, near_side, near_row))
    copies = []

    def send(number, source, target, device):
        copy = remote(source, target, send_sems.at[number], recv_sems.at[number], device)
        copy.start()
        copies.append(copy)
        return copy

    first = block_ref.at[pl.ds(0, half)]
    second = block_ref.at[pl.ds(half, half)]
    side_b = send(0, second, spot(side, row, core, 1), near_side)
    row_a = send(1, first, spot(side, row, core, 0), near_row)
    side_a = send(2, first, spot(side, row, core, 0), near_side)
    row_b = send(3, second, spot(side, row, core, 1), near_row)
    core_own = send(4, block_ref, spot(side, row, core), near_core)
    local = pltpu.make_async_copy(block_ref, spot(side, row, core), local_sem)
    local.start()
    side_b.wait_recv()
    away_b = send(5, spot(1 - side, row, core, 1), spot(1 - side, row, core, 1), near_row)
    row_a.wait_recv()
    away_a = send(6, spot(side, 1 - row, core, 0), spot(side, 1 - row, core, 0), near_side)
    side_a.wait_recv()
    core_side = send(7, spot(1 - side, row, core), spot(1 - side, row, core), near_core)
    row_b.wait_recv()
    core_row = send(8, spot(side, 1 - row, core), spot(side, 1 - row, core), near_core)
    away_a.wait_recv()
    core_away_a = send(
        9, spot(1 - side, 1 - row, core, 0), spot(1 - side, 1 - row, core, 0), near_core
    )
    away_b.wait_recv()
    core_away_b = send(
        10, spot(1 - side, 1 - row, core, 1), spot(1 - side, 1 - row, core, 1), near_core
    )
    for copy in (core_own, core_side, core_row, core_away_a, core_away_b):
        copy.wait_recv()
    for copy in copies:
        copy.wait_send()
    local.wait()


def plane_gather(block):
    rows, width = block.shape
    return pl.pallas_call(
        functools.partial(gather_kernel, rows),
        out_shape=jax.ShapeDtypeStruct((8 * rows, width), block.dtype),
        in_specs=[pl.BlockSpec(memory_space=pl.ANY)],
        out_specs=pl.BlockSpec(memory_space=pl.ANY),
        scratch_shapes=[
            pltpu.SemaphoreType.DMA((11,)),
            pltpu.SemaphoreType.DMA((11,)),
            pltpu.SemaphoreType.DMA,
        ],
        compiler_params=pltpu.CompilerParams(collective_id=0, has_side_effects=True),
        cost_estimate=pl.CostEstimate(
            flops=0, bytes_accessed=64 * rows * width * 2, transcendentals=0
        ),
        name="plane_gather",
    )(block)


def scatter_kernel(
    rows,
    part_ref,
    out_ref,
    mine,
    other,
    to_side,
    to_row,
    from_side,
    from_row,
    on_side,
    on_row,
    got_side,
    got_row,
    send_sems,
    recv_sems,
    local_sems,
):
    side, row, core, near_core, near_side, near_row = place()
    half = rows // 2
    tile = 32

    def spot(a, b, c):
        return part_ref.at[pl.ds(pl.multiple_of((a * 4 + b * 2 + c) * rows, rows), rows)]

    chips = ((side, row), (1 - side, row), (side, 1 - row), (1 - side, 1 - row))
    locals_, pairs = {}, {}
    for number in (3, 1, 2, 0):
        locals_[number] = pltpu.make_async_copy(
            spot(*chips[number], core), mine.at[number], local_sems.at[number]
        )
        locals_[number].start()
    greet((near_core, near_side, near_row))
    copies = []

    def send(number, source, target, device):
        copy = remote(source, target, send_sems.at[number], recv_sems.at[number], device)
        copy.start()
        copies.append(copy)
        return copy

    for number in (3, 1, 2, 0):
        pairs[number] = send(number, spot(*chips[number], 1 - core), other.at[number], near_core)

    def ready(number):
        locals_[number].wait()
        pairs[number].wait_recv()

    def both(number, part, at):
        at = part * half + at
        here = mine[number, pl.ds(at, tile), :].astype(F32)
        return here + other[number, pl.ds(at, tile), :].astype(F32)

    def each(body):
        def step(index, carry):
            body(pl.multiple_of(index * tile, tile))
            return carry

        lax.fori_loop(0, half // tile, step, 0)

    def put(target, number, part, extra=None):
        def body(at):
            value = both(number, part, at)
            if extra is not None:
                value = value + extra[pl.ds(at, tile), :].astype(F32)
            target[pl.ds(at, tile), :] = value.astype(BF16)

        each(body)

    ready(3)
    put(to_side.at[0], 3, 0)
    side_0 = send(4, to_side.at[0], from_side.at[0], near_side)
    put(to_row.at[0], 3, 1)
    row_0 = send(5, to_row.at[0], from_row.at[0], near_row)
    ready(1)
    put(to_side.at[1], 1, 0)
    side_1 = send(6, to_side.at[1], from_side.at[1], near_side)
    ready(2)
    put(to_row.at[1], 2, 1)
    row_1 = send(7, to_row.at[1], from_row.at[1], near_row)
    side_0.wait_recv()
    put(on_row, 2, 0, from_side.at[0])
    fin_row = send(8, on_row, got_row, near_row)
    row_0.wait_recv()
    put(on_side, 1, 1, from_row.at[0])
    fin_side = send(9, on_side, got_side, near_side)
    ready(0)
    side_1.wait_recv()
    row_1.wait_recv()

    def first_sum(at):
        out_ref[pl.ds(at, tile), :] = both(0, 0, at) + from_side[1, pl.ds(at, tile), :].astype(F32)
        out_ref[pl.ds(half + at, tile), :] = both(0, 1, at) + from_row[
            1, pl.ds(at, tile), :
        ].astype(F32)

    each(first_sum)
    fin_row.wait_recv()
    fin_side.wait_recv()

    def last_sum(at):
        out_ref[pl.ds(at, tile), :] += got_row[pl.ds(at, tile), :].astype(F32)
        out_ref[pl.ds(half + at, tile), :] += got_side[pl.ds(at, tile), :].astype(F32)

    each(last_sum)
    for copy in copies:
        copy.wait_send()


def plane_scatter(partial):
    total, width = partial.shape
    rows = total // 8
    half = rows // 2
    return pl.pallas_call(
        functools.partial(scatter_kernel, rows),
        out_shape=jax.ShapeDtypeStruct((rows, width), F32),
        in_specs=[pl.BlockSpec(memory_space=pl.ANY)],
        out_specs=pl.BlockSpec(memory_space=pltpu.VMEM),
        scratch_shapes=[
            pltpu.VMEM((4, rows, width), BF16),
            pltpu.VMEM((4, rows, width), BF16),
            pltpu.VMEM((2, half, width), BF16),
            pltpu.VMEM((2, half, width), BF16),
            pltpu.VMEM((2, half, width), BF16),
            pltpu.VMEM((2, half, width), BF16),
            pltpu.VMEM((half, width), BF16),
            pltpu.VMEM((half, width), BF16),
            pltpu.VMEM((half, width), BF16),
            pltpu.VMEM((half, width), BF16),
            pltpu.SemaphoreType.DMA((10,)),
            pltpu.SemaphoreType.DMA((10,)),
            pltpu.SemaphoreType.DMA((4,)),
        ],
        compiler_params=pltpu.CompilerParams(
            collective_id=1, has_side_effects=True, vmem_limit_bytes=32 * 1024 * 1024
        ),
        cost_estimate=pl.CostEstimate(
            flops=0, bytes_accessed=8 * total * width * 2, transcendentals=0
        ),
        name="plane_scatter",
    )(partial)


def swap_halves(values):
    width = values.shape[-1]
    lane = lax.broadcasted_iota(jnp.int32, values.shape, 1)
    ahead = pltpu.roll(values, width - HEAD_DIM // 2, 1)
    behind = pltpu.roll(values, HEAD_DIM // 2, 1)
    return jnp.where(lane % HEAD_DIM < HEAD_DIM // 2, ahead, behind)


def pieces_of(block):
    return ((0, block * QB, False), (block * QB, QB, True)) if block else ((0, QB, True),)


def masked_scores(query, keys, diagonal):
    scores = matmul_nt(query, keys)
    if diagonal:
        here = lax.broadcasted_iota(jnp.int32, scores.shape, 0)
        there = lax.broadcasted_iota(jnp.int32, scores.shape, 1)
        scores = jnp.where(here >= there, scores, -1e30)
    return scores


def attend_kernel(length, q_ref, kv_ref, cos_ref, sin_ref, att_ref, qrot_ref, kvrot_ref, log_ref):
    cosine = cos_ref[...]
    signed = sin_ref[...]
    scale = HEAD_DIM ** (-0.5)
    pre = q_ref[...]
    qrot_ref[...] = (pre * cosine + swap_halves(pre) * signed).astype(BF16)
    pre = kv_ref[...]
    lane = lax.broadcasted_iota(jnp.int32, pre.shape, 1)
    turned = jnp.where(lane < HEAD_DIM, pre * cosine + swap_halves(pre) * signed, pre)
    kvrot_ref[...] = turned.astype(BF16)
    for block in range(length // QB):
        here = pl.ds(block * QB, QB)
        logs = []
        mixed = []
        for head in range(2):
            query = qrot_ref[here, head * HEAD_DIM : (head + 1) * HEAD_DIM] * jnp.asarray(
                scale, BF16
            )
            scores = []
            for start, size, diagonal in pieces_of(block):
                keys = kvrot_ref[pl.ds(start, size), :HEAD_DIM]
                scores.append(masked_scores(query, keys, diagonal))
            peak = functools.reduce(
                jnp.maximum, [jnp.max(s, axis=1, keepdims=True) for s in scores]
            )
            powers = [jnp.exp(s - peak) for s in scores]
            total = sum(jnp.sum(p, axis=1, keepdims=True) for p in powers)
            inverse = 1.0 / total
            out = None
            for (start, size, _), power in zip(pieces_of(block), powers):
                values = kvrot_ref[pl.ds(start, size), HEAD_DIM:]
                term = jnp.dot(
                    (power * inverse).astype(BF16), values, preferred_element_type=F32
                )
                out = term if out is None else out + term
            mixed.append(out)
            logs.append(peak + jnp.log(total))
        att_ref[here, :] = jnp.concatenate(mixed, axis=1).astype(BF16)
        lane = lax.broadcasted_iota(jnp.int32, (QB, 128), 1)
        log_ref[here, :] = jnp.where(lane < HEAD_DIM, logs[0], logs[1])


def attend(pre, cosine, signed, seqs):
    rows = pre.shape[0]
    length = rows // seqs
    pairs = pre.shape[1] // 128 - 1
    block = (length, 128)
    return pl.pallas_call(
        functools.partial(attend_kernel, length),
        grid=(seqs, pairs),
        out_shape=(
            jax.ShapeDtypeStruct((rows, pairs * 128), BF16),
            jax.ShapeDtypeStruct((rows, pairs * 128), BF16),
            jax.ShapeDtypeStruct((rows, 128), BF16),
            jax.ShapeDtypeStruct((rows, pairs * 128), F32),
        ),
        in_specs=[
            pl.BlockSpec(block, lambda s, h: (s, h)),
            pl.BlockSpec(block, lambda s, h: (s, pairs)),
            pl.BlockSpec(block, lambda s, h: (0, 0)),
            pl.BlockSpec(block, lambda s, h: (0, 0)),
        ],
        out_specs=(
            pl.BlockSpec(block, lambda s, h: (s, h)),
            pl.BlockSpec(block, lambda s, h: (s, h)),
            pl.BlockSpec(block, lambda s, h: (s, 0)),
            pl.BlockSpec(block, lambda s, h: (s, h)),
        ),
        compiler_params=pltpu.CompilerParams(vmem_limit_bytes=48 * 1024 * 1024),
        cost_estimate=pl.CostEstimate(
            flops=8 * rows * length * 128 * pairs,
            bytes_accessed=rows * pairs * 128 * 12,
            transcendentals=rows * length * 2 * pairs,
        ),
        name="attend",
    )(pre, pre, cosine, signed)


def attend_back_kernel(
    length, q_ref, kv_ref, up_ref, log_ref, cos_ref, sin_ref, dq_ref, dkv_ref, sum_ref
):
    pair = pl.program_id(1)
    scale = HEAD_DIM ** (-0.5)

    @pl.when(pair == 0)
    def _():
        sum_ref[...] = jnp.zeros_like(sum_ref)

    for block in range(length // QB):
        here = pl.ds(block * QB, QB)
        turned = []
        for head in range(2):
            lanes = slice(head * HEAD_DIM, (head + 1) * HEAD_DIM)
            query = q_ref[here, lanes] * jnp.asarray(scale, BF16)
            upstream = up_ref[here, lanes]
            logs = log_ref[here, head * HEAD_DIM : head * HEAD_DIM + 1]
            saved = []
            inner = None
            for start, size, diagonal in pieces_of(block):
                keys = kv_ref[pl.ds(start, size), :HEAD_DIM]
                values = kv_ref[pl.ds(start, size), HEAD_DIM:]
                probability = jnp.exp(masked_scores(query, keys, diagonal) - logs)
                prob_grad = matmul_nt(upstream, values)
                term = jnp.sum(probability * prob_grad, axis=1, keepdims=True)
                inner = term if inner is None else inner + term
                saved.append((start, size, probability, prob_grad))
            out = None
            for start, size, probability, prob_grad in saved:
                keys = kv_ref[pl.ds(start, size), :HEAD_DIM]
                score_grad = (probability * (prob_grad - inner)).astype(BF16)
                rounded = probability.astype(BF16)
                term = jnp.dot(score_grad, keys, preferred_element_type=F32)
                out = term if out is None else out + term
                sum_ref[pl.ds(start, size), :] += jnp.concatenate(
                    [matmul_t(score_grad, query), matmul_t(rounded, upstream)], axis=1
                )
            turned.append(out * scale)
        grad = jnp.concatenate(turned, axis=1)
        dq_ref[here, :] = (grad * cos_ref[here, :] - swap_halves(grad) * sin_ref[here, :]).astype(
            BF16
        )

    @pl.when(pair == pl.num_programs(1) - 1)
    def _():
        grad = sum_ref[...]
        lane = lax.broadcasted_iota(jnp.int32, grad.shape, 1)
        back = grad * cos_ref[...] - swap_halves(grad) * sin_ref[...]
        dkv_ref[...] = jnp.where(lane < HEAD_DIM, back, grad).astype(BF16)


def attend_back(queries, keyvals, upstream, logs, cosine, signed, seqs):
    rows, width = queries.shape
    length = rows // seqs
    pairs = width // 128
    block = (length, 128)
    by_pair = pl.BlockSpec(block, lambda s, h: (s, h))
    by_seq = pl.BlockSpec(block, lambda s, h: (s, 0))
    same = pl.BlockSpec(block, lambda s, h: (0, 0))
    return pl.pallas_call(
        functools.partial(attend_back_kernel, length),
        grid=(seqs, pairs),
        out_shape=(
            jax.ShapeDtypeStruct((rows, width), BF16),
            jax.ShapeDtypeStruct((rows, 128), BF16),
        ),
        in_specs=[by_pair, by_seq, by_pair, by_pair, same, same],
        out_specs=(by_pair, by_seq),
        scratch_shapes=[pltpu.VMEM(block, F32)],
        compiler_params=pltpu.CompilerParams(vmem_limit_bytes=48 * 1024 * 1024),
        cost_estimate=pl.CostEstimate(
            flops=20 * rows * length * 128 * pairs,
            bytes_accessed=rows * pairs * 128 * 12,
            transcendentals=rows * length * 2 * pairs,
        ),
        name="attend_back",
    )(queries, keyvals, upstream, logs, cosine, signed)


def to_units(weight):
    return lax.all_to_all(weight, "ctx", split_axis=1, concat_axis=0, tiled=True)


def from_units(grad):
    return lax.all_to_all(grad, "ctx", split_axis=0, concat_axis=1, tiled=True)


def on_plane(
    layer_input,
    attn_gain,
    w_query,
    w_key,
    w_value,
    w_out,
    ffn_gain,
    w_gate,
    w_up,
    w_down,
    cotangent,
):
    seqs, span, width = layer_input.shape
    planes = lax.axis_size("dp")
    parts = lax.axis_size("ctx")
    side = lax.axis_index("tensor")
    length = span * parts
    rows_w = w_query.shape[0]
    q_cols = w_query.shape[1] // parts
    kv_cols = w_key.shape[1] // parts

    theta = angles(jnp.arange(length), HEAD_DIM)
    cosine = jnp.tile(jnp.cos(theta), (1, 4))
    sine = jnp.sin(theta)
    signed = jnp.tile(jnp.concatenate([-sine, sine], axis=1), (1, 2))

    gain_row = jnp.concatenate(
        [attn_gain, ffn_gain, jnp.zeros((2 * q_cols + 2 * kv_cols - 2 * rows_w,), BF16)]
    )
    gain_rows = jnp.broadcast_to(gain_row[None, None, :], (parts, 8, gain_row.shape[0]))
    mixed = jnp.concatenate(
        [
            w_query.reshape(rows_w, parts, q_cols),
            w_key.reshape(rows_w, parts, kv_cols),
            w_value.reshape(rows_w, parts, kv_cols),
            w_out.T.reshape(rows_w, parts, q_cols),
        ],
        axis=2,
    ).transpose(1, 0, 2)
    mixed = jnp.concatenate([mixed, gain_rows], axis=1)
    mixed = lax.all_to_all(mixed, "ctx", split_axis=0, concat_axis=0, tiled=True)
    mixed = lax.all_gather(mixed, "dp", axis=0, tiled=True)
    attn_w = mixed[:, :rows_w].reshape(width, -1)
    gain_one = mixed[:, rows_w, :rows_w].reshape(width).astype(F32)
    gain_two = mixed[:, rows_w, rows_w : 2 * rows_w].reshape(width).astype(F32)
    qkv_cols = q_cols + 2 * kv_cols
    w_qkv = attn_w[:, :qkv_cols]
    w_out_t = attn_w[:, qkv_cols:]

    gate_w, up_w, down_w = (
        lax.all_gather(to_units(w), "dp", axis=0, tiled=True) for w in (w_gate, w_up, w_down.T)
    )

    own_in = lax.dynamic_index_in_dim(layer_input, side, 0, keepdims=False)
    own_cot = lax.dynamic_index_in_dim(cotangent, side, 0, keepdims=False)
    all_in = plane_gather(own_in)
    all_cot = plane_gather(own_cot)

    all_f = all_in.astype(F32)
    normed_one = (all_f * rms_factor(all_f) * gain_one).astype(BF16)
    pre = jnp.dot(normed_one, w_qkv, preferred_element_type=F32)
    attended, queries, keyvals, logs = attend(pre, cosine, signed, seqs)
    attn_part = matmul_nt(attended, w_out_t).astype(BF16)
    inputs_f = own_in.astype(F32)
    factor_one = rms_factor(inputs_f)
    hidden = inputs_f + plane_scatter(attn_part)
    factor_two = rms_factor(hidden)
    normed_own = (hidden * factor_two * gain_two).astype(BF16)
    normed_two = plane_gather(normed_own)

    gate_pre = jnp.dot(normed_two, gate_w, preferred_element_type=F32)
    up_pre = jnp.dot(normed_two, up_w, preferred_element_type=F32)
    sigma = jax.nn.sigmoid(gate_pre)
    product = (gate_pre * sigma * up_pre).astype(BF16)
    down_grad = matmul_t(all_cot, product).astype(BF16)
    prod_grad = jnp.dot(all_cot, down_w, preferred_element_type=F32)
    gate_grad = (prod_grad * up_pre * sigma * (1.0 + gate_pre * (1.0 - sigma))).astype(BF16)
    up_grad = (prod_grad * gate_pre * sigma).astype(BF16)
    gate_w_grad = matmul_t(normed_two, gate_grad).astype(BF16)
    up_w_grad = matmul_t(normed_two, up_grad).astype(BF16)
    back_part = (matmul_nt(gate_grad, gate_w) + matmul_nt(up_grad, up_w)).astype(BF16)
    ffn_part = matmul_nt(product, down_w).astype(BF16)
    down_sum, gate_sum, up_sum = (
        lax.psum_scatter(g, "dp", scatter_dimension=0, tiled=True)
        for g in (down_grad, gate_w_grad, up_w_grad)
    )

    normed_two_grad = plane_scatter(back_part)
    hidden_back, ffn_gain_term = rms_back(normed_two_grad, hidden, factor_two, gain_two)
    hidden_grad = own_cot.astype(F32) + hidden_back
    hidden_low = plane_gather(hidden_grad.astype(BF16))
    attended_grad = jnp.dot(hidden_low, w_out_t, preferred_element_type=F32).astype(BF16)
    out_w_grad = matmul_t(hidden_low, attended).astype(BF16)
    query_low, keyval_low = attend_back(
        queries, keyvals, attended_grad, logs, cosine, signed, seqs
    )
    back = jnp.concatenate([query_low, keyval_low], axis=1)
    qkv_grad = matmul_t(normed_one, back).astype(BF16)
    attn_grad = jnp.concatenate([qkv_grad, out_w_grad], axis=1)
    attn_sum = lax.psum_scatter(attn_grad, "dp", scatter_dimension=0, tiled=True)
    one_part = matmul_nt(back, w_qkv).astype(BF16)
    normed_one_grad = plane_scatter(one_part)
    input_back, attn_gain_term = rms_back(normed_one_grad, inputs_f, factor_one, gain_one)
    input_own = hidden_grad + input_back
    out_own = (hidden + plane_scatter(ffn_part)).astype(BF16)

    def both_sides(own):
        other = lax.ppermute(own, "tensor", [(0, 1), (1, 0)])
        return jnp.where(side == 0, jnp.stack([own, other]), jnp.stack([other, own]))

    layer_output = both_sides(out_own)
    input_grad = both_sides(input_own.astype(BF16)).astype(F32)
    gain_terms = lax.psum(jnp.stack([attn_gain_term, ffn_gain_term]), ("dp", "ctx", "tensor"))
    own_start = (lax.axis_index("dp") * parts + lax.axis_index("ctx")) * rows_w
    gain_own = lax.dynamic_slice_in_dim(gain_terms, own_start, rows_w, axis=1)

    down_out, gate_out, up_out = (from_units(g) for g in (down_sum, gate_sum, up_sum))
    attn_out = lax.all_to_all(
        attn_sum.reshape(parts, rows_w, -1), "ctx", split_axis=0, concat_axis=0, tiled=True
    )

    def columns(start, size):
        return attn_out[:, :, start : start + size].transpose(1, 0, 2).reshape(rows_w, -1)

    return (
        layer_output,
        input_grad,
        gain_own[0],
        columns(0, q_cols).astype(F32),
        columns(q_cols, kv_cols).astype(F32),
        columns(q_cols + kv_cols, kv_cols).astype(F32),
        columns(qkv_cols, q_cols).T.astype(F32),
        gain_own[1],
        gate_out.astype(F32),
        up_out.astype(F32),
        down_out.T.astype(F32),
    )


def fits_plane(mesh, shapes):
    sizes = mesh.shape
    seqs, length, width = shapes[0].shape
    kv_heads = shapes[3].shape[1] // HEAD_DIM
    return (
        sizes["tensor"] == 2
        and sizes["ctx"] == 4
        and seqs == 2 * sizes["dp"]
        and kv_heads == 8
        and shapes[2].shape[1] == 4 * shapes[3].shape[1]
        and length % (4 * QB) == 0
        and width % (128 * 4 * sizes["dp"]) == 0
    )


def placed(mesh, function):
    return jax.shard_map(
        function,
        mesh=mesh,
        in_specs=(
            P("dp", "ctx", None),
            P(("dp", "ctx")),
            P(("dp", "ctx"), "tensor"),
            P(("dp", "ctx"), "tensor"),
            P(("dp", "ctx"), "tensor"),
            P("tensor", ("dp", "ctx")),
            P(("dp", "ctx")),
            P(("dp", "ctx"), "tensor"),
            P(("dp", "ctx"), "tensor"),
            P("tensor", ("dp", "ctx")),
            P("dp", "ctx", None),
        ),
        out_specs=(
            P("dp", "ctx", None),
            P("dp", "ctx", None),
            P(("dp", "ctx")),
            P(("dp", "ctx"), "tensor"),
            P(("dp", "ctx"), "tensor"),
            P(("dp", "ctx"), "tensor"),
            P("tensor", ("dp", "ctx")),
            P(("dp", "ctx")),
            P(("dp", "ctx"), "tensor"),
            P(("dp", "ctx"), "tensor"),
            P("tensor", ("dp", "ctx")),
        ),
        check_vma=False,
    )


def solution(mesh):
    def whole(*arrays):
        return placed(mesh, on_plane if fits_plane(mesh, arrays) else on_device)(*arrays)

    return whole
```

```python
import functools
import math

import jax
import jax.numpy as jnp
from jax import lax
from jax.experimental import pallas as pl
from jax.experimental.pallas import tpu as pltpu
from jax.sharding import PartitionSpec as P

HEAD_DIM = 64


EPSILON = 1e-05
ROPE_BASE = 500000.0


def rotate(values, cosine, sine_val):
    middle = values.shape[-1] // 2
    leading = values[..., :middle]
    trailing = values[..., middle:]
    return jnp.concatenate(
        [leading * cosine - trailing * sine_val, trailing * cosine + leading * sine_val], axis=-1
    )


def unrotate(gradient, cosine, sine_val):
    middle = gradient.shape[-1] // 2
    leading = gradient[..., :middle]
    trailing = gradient[..., middle:]
    return jnp.concatenate(
        [leading * cosine + trailing * sine_val, trailing * cosine - leading * sine_val], axis=-1
    )


def angles(positions, head_dim):
    exponent = jnp.arange(head_dim // 2).astype(jnp.float32) * (
        -2.0 * math.log(ROPE_BASE) / head_dim
    )
    return positions.astype(jnp.float32)[:, None] * jnp.exp(exponent)[None, :]


def rms_factor(row_values):
    return lax.rsqrt(jnp.mean(row_values * row_values, axis=-1, keepdims=True) + EPSILON)


def rms_back(upstream, row_values, factor, gain_row):
    scaled = upstream * gain_row
    gain_term = jnp.sum(upstream * row_values * factor, axis=0)
    inner_mean = jnp.mean(scaled * row_values, axis=-1, keepdims=True)
    return (factor * scaled - row_values * (factor * factor * factor) * inner_mean, gain_term)


def matmul_t(left_op, right_op):
    return lax.dot_general(
        left_op, right_op, (((0,), (0,)), ((), ())), preferred_element_type=jnp.float32
    )


def matmul_nt(left_op, right_op):
    return lax.dot_general(
        left_op, right_op, (((1,), (1,)), ((), ())), preferred_element_type=jnp.float32
    )


def on_device(
    layer_input,
    attn_gain,
    w_query,
    w_key,
    w_value,
    w_out,
    ffn_gain,
    w_gate,
    w_up,
    w_down,
    cotangent,
):
    seq_dev, span_len, model_width = layer_input.shape
    row_count = seq_dev * span_len
    length_all = span_len * lax.axis_size("ctx")
    full_q, full_k, full_v, full_o, full_gate, full_up, full_down, gain_attn, gain_ffn = (
        lax.all_gather(w_query, ("dp", "ctx"), axis=0, tiled=True),
        lax.all_gather(w_key, ("dp", "ctx"), axis=0, tiled=True),
        lax.all_gather(w_value, ("dp", "ctx"), axis=0, tiled=True),
        lax.all_gather(w_out, ("dp", "ctx"), axis=1, tiled=True),
        lax.all_gather(w_gate, ("dp", "ctx"), axis=0, tiled=True),
        lax.all_gather(w_up, ("dp", "ctx"), axis=0, tiled=True),
        lax.all_gather(w_down, ("dp", "ctx"), axis=1, tiled=True),
        lax.all_gather(attn_gain, ("dp", "ctx"), axis=0, tiled=True),
        lax.all_gather(ffn_gain, ("dp", "ctx"), axis=0, tiled=True),
    )
    kv_local = full_k.shape[1] // HEAD_DIM
    group_size = full_q.shape[1] // HEAD_DIM // kv_local
    block_count = seq_dev * kv_local
    scale = HEAD_DIM ** (-0.5)
    query_pos = lax.axis_index("ctx") * span_len + jnp.arange(span_len)
    theta = angles(query_pos, HEAD_DIM)
    cosine = jnp.cos(theta)
    sine_val = jnp.sin(theta)
    causal = query_pos[:, None] >= jnp.arange(length_all)[None, :]
    inputs_f = layer_input.reshape(row_count, model_width).astype(jnp.float32)
    gain_one = gain_attn.astype(jnp.float32)
    gain_two = gain_ffn.astype(jnp.float32)
    factor_one = rms_factor(inputs_f)
    normed_one = (inputs_f * factor_one * gain_one).astype(jnp.bfloat16)
    query_pre = jnp.dot(normed_one, full_q, preferred_element_type=jnp.float32).reshape(
        seq_dev, span_len, kv_local, group_size, HEAD_DIM
    )
    queries = rotate(
        query_pre, cosine[None, :, None, None, :], sine_val[None, :, None, None, :]
    ).astype(jnp.bfloat16)
    key_pre = jnp.dot(normed_one, full_k, preferred_element_type=jnp.float32).reshape(
        seq_dev, span_len, kv_local, HEAD_DIM
    )
    keys_own = (
        rotate(key_pre, cosine[None, :, None, :], sine_val[None, :, None, :])
        .astype(jnp.bfloat16)
        .reshape(seq_dev, span_len, kv_local * HEAD_DIM)
    )
    values_own = (
        jnp.dot(normed_one, full_v, preferred_element_type=jnp.float32)
        .astype(jnp.bfloat16)
        .reshape(seq_dev, span_len, kv_local * HEAD_DIM)
    )
    keys_all, values_all = (
        lax.all_gather(keys_own, "ctx", axis=1, tiled=True),
        lax.all_gather(values_own, "ctx", axis=1, tiled=True),
    )
    query_blocks = jnp.transpose(queries, (0, 2, 1, 3, 4)).reshape(
        block_count, span_len, group_size, HEAD_DIM
    )
    key_blocks = jnp.transpose(
        keys_all.reshape(seq_dev, length_all, kv_local, HEAD_DIM), (0, 2, 1, 3)
    ).reshape(block_count, length_all, HEAD_DIM)
    value_blocks = jnp.transpose(
        values_all.reshape(seq_dev, length_all, kv_local, HEAD_DIM), (0, 2, 1, 3)
    ).reshape(block_count, length_all, HEAD_DIM)

    def scores_of(query_b, key_b):
        raw_scores = jnp.einsum("qgd,kd->gqk", query_b, key_b, preferred_element_type=jnp.float32)
        return jnp.where(causal[None], raw_scores * scale, -1e30)

    def attend(block_in):
        query_b, key_b, value_b = block_in
        scores = scores_of(query_b, key_b)
        peak_row = jnp.max(scores, axis=-1, keepdims=True)
        powers = jnp.exp(scores - peak_row)
        total_sum = jnp.sum(powers, axis=-1, keepdims=True)
        probability = (powers / total_sum).astype(jnp.bfloat16)
        mixed = jnp.einsum("gqk,kd->qgd", probability, value_b, preferred_element_type=jnp.float32)
        return (mixed.astype(jnp.bfloat16), peak_row + jnp.log(total_sum))

    mixed_blocks, logsum = lax.map(attend, (query_blocks, key_blocks, value_blocks))
    attended = jnp.transpose(
        mixed_blocks.reshape(seq_dev, kv_local, span_len, group_size, HEAD_DIM), (0, 2, 1, 3, 4)
    ).reshape(row_count, kv_local * group_size * HEAD_DIM)
    attn_part = jnp.dot(attended, full_o, preferred_element_type=jnp.float32)
    hidden = inputs_f + lax.psum(attn_part, "tensor")
    factor_two = rms_factor(hidden)
    normed_two = (hidden * factor_two * gain_two).astype(jnp.bfloat16)
    gate_pre = jnp.dot(normed_two, full_gate, preferred_element_type=jnp.float32)
    up_pre = jnp.dot(normed_two, full_up, preferred_element_type=jnp.float32)
    sigma = jax.nn.sigmoid(gate_pre)
    product = (gate_pre * sigma * up_pre).astype(jnp.bfloat16)
    ffn_part = jnp.dot(product, full_down, preferred_element_type=jnp.float32)
    out_f = hidden + lax.psum(ffn_part.astype(jnp.bfloat16), "tensor").astype(jnp.float32)
    layer_output = out_f.astype(jnp.bfloat16).reshape(seq_dev, span_len, model_width)
    grad_out = cotangent.reshape(row_count, model_width).astype(jnp.float32)
    grad_low = cotangent.reshape(row_count, model_width)
    down_grad = matmul_t(product, grad_low)
    prod_grad = matmul_nt(grad_low, full_down)
    gate_grad = (prod_grad * up_pre * sigma * (1.0 + gate_pre * (1.0 - sigma))).astype(jnp.bfloat16)
    up_grad = (prod_grad * gate_pre * sigma).astype(jnp.bfloat16)
    gate_w_grad = matmul_t(normed_two, gate_grad)
    up_w_grad = matmul_t(normed_two, up_grad)
    normed_two_part = matmul_nt(gate_grad, full_gate) + matmul_nt(up_grad, full_up)
    normed_two_grad = lax.psum(normed_two_part, "tensor")
    hidden_back, ffn_gain_term = rms_back(normed_two_grad, hidden, factor_two, gain_two)
    hidden_grad = grad_out + hidden_back
    hidden_low = hidden_grad.astype(jnp.bfloat16)
    out_w_grad = matmul_t(attended, hidden_low)
    attended_grad = matmul_nt(hidden_low, full_o).astype(jnp.bfloat16)
    upstream_blocks = jnp.transpose(
        attended_grad.reshape(seq_dev, span_len, kv_local, group_size, HEAD_DIM), (0, 2, 1, 3, 4)
    ).reshape(block_count, span_len, group_size, HEAD_DIM)

    def attend_back(block_in):
        query_b, key_b, value_b, logsum_b, upstream_b = block_in
        scores = scores_of(query_b, key_b)
        probability = jnp.exp(scores - logsum_b)
        rounded = probability.astype(jnp.bfloat16)
        value_grad = jnp.einsum(
            "gqk,qgd->kd", rounded, upstream_b, preferred_element_type=jnp.float32
        )
        prob_grad = jnp.einsum(
            "qgd,kd->gqk", upstream_b, value_b, preferred_element_type=jnp.float32
        )
        inner_sum = jnp.sum(probability * prob_grad, axis=-1, keepdims=True)
        score_grad = (probability * (prob_grad - inner_sum)).astype(jnp.bfloat16)
        query_grad = (
            jnp.einsum("gqk,kd->qgd", score_grad, key_b, preferred_element_type=jnp.float32) * scale
        )
        key_grad = (
            jnp.einsum("gqk,qgd->kd", score_grad, query_b, preferred_element_type=jnp.float32)
            * scale
        )
        return (query_grad, key_grad, value_grad)

    query_grads, key_grads, value_grads = lax.map(
        attend_back, (query_blocks, key_blocks, value_blocks, logsum, upstream_blocks)
    )
    key_rows = jnp.transpose(
        key_grads.reshape(seq_dev, kv_local, length_all, HEAD_DIM), (0, 2, 1, 3)
    ).reshape(seq_dev, length_all, kv_local * HEAD_DIM)
    value_rows = jnp.transpose(
        value_grads.reshape(seq_dev, kv_local, length_all, HEAD_DIM), (0, 2, 1, 3)
    ).reshape(seq_dev, length_all, kv_local * HEAD_DIM)
    key_mine, value_mine = (
        lax.psum_scatter(key_rows, "ctx", scatter_dimension=1, tiled=True),
        lax.psum_scatter(value_rows, "ctx", scatter_dimension=1, tiled=True),
    )
    key_low = (
        unrotate(
            key_mine.reshape(seq_dev, span_len, kv_local, HEAD_DIM),
            cosine[None, :, None, :],
            sine_val[None, :, None, :],
        )
        .astype(jnp.bfloat16)
        .reshape(row_count, kv_local * HEAD_DIM)
    )
    value_low = value_mine.astype(jnp.bfloat16).reshape(row_count, kv_local * HEAD_DIM)
    query_rot = jnp.transpose(
        query_grads.reshape(seq_dev, kv_local, span_len, group_size, HEAD_DIM), (0, 2, 1, 3, 4)
    )
    query_low = (
        unrotate(query_rot, cosine[None, :, None, None, :], sine_val[None, :, None, None, :])
        .astype(jnp.bfloat16)
        .reshape(row_count, kv_local * group_size * HEAD_DIM)
    )
    query_w_grad = matmul_t(normed_one, query_low)
    key_w_grad = matmul_t(normed_one, key_low)
    value_w_grad = matmul_t(normed_one, value_low)
    normed_one_part = (
        matmul_nt(query_low, full_q) + matmul_nt(key_low, full_k) + matmul_nt(value_low, full_v)
    )
    normed_one_grad = lax.psum(normed_one_part.astype(jnp.bfloat16), "tensor").astype(jnp.float32)
    input_back, attn_gain_term = rms_back(normed_one_grad, inputs_f, factor_one, gain_one)
    input_grad = (hidden_grad + input_back).reshape(seq_dev, span_len, model_width)
    (
        query_sum,
        key_sum,
        value_sum,
        out_sum,
        gate_sum,
        up_sum,
        down_sum,
        attn_gain_sum,
        ffn_gain_sum,
    ) = (
        lax.psum_scatter(query_w_grad, ("dp", "ctx"), scatter_dimension=0, tiled=True),
        lax.psum_scatter(key_w_grad, ("dp", "ctx"), scatter_dimension=0, tiled=True),
        lax.psum_scatter(value_w_grad, ("dp", "ctx"), scatter_dimension=0, tiled=True),
        lax.psum_scatter(out_w_grad, ("dp", "ctx"), scatter_dimension=1, tiled=True),
        lax.psum_scatter(gate_w_grad, ("dp", "ctx"), scatter_dimension=0, tiled=True),
        lax.psum_scatter(up_w_grad, ("dp", "ctx"), scatter_dimension=0, tiled=True),
        lax.psum_scatter(down_grad, ("dp", "ctx"), scatter_dimension=1, tiled=True),
        lax.psum_scatter(attn_gain_term, ("dp", "ctx"), scatter_dimension=0, tiled=True),
        lax.psum_scatter(ffn_gain_term, ("dp", "ctx"), scatter_dimension=0, tiled=True),
    )
    return (
        layer_output,
        input_grad,
        attn_gain_sum,
        query_sum,
        key_sum,
        value_sum,
        out_sum,
        ffn_gain_sum,
        gate_sum,
        up_sum,
        down_sum,
    )


MESH_ID = pl.DeviceIdType.MESH
BF16 = jnp.bfloat16
F32 = jnp.float32
QB = 256


def place():
    side = lax.axis_index("tensor")
    ctx = lax.axis_index("ctx")
    row = ctx // 2
    core = ctx % 2
    near_core = {"ctx": row * 2 + (1 - core)}
    near_side = {"tensor": 1 - side}
    near_row = {"ctx": (1 - row) * 2 + core}
    return side, row, core, near_core, near_side, near_row


def greet(neighbours):
    barrier = pltpu.get_barrier_semaphore()
    for target in neighbours:
        pl.semaphore_signal(barrier, inc=1, device_id=target, device_id_type=MESH_ID)
    pl.semaphore_wait(barrier, len(neighbours))


def remote(source, target, send_sem, recv_sem, device):
    return pltpu.make_async_remote_copy(
        src_ref=source,
        dst_ref=target,
        send_sem=send_sem,
        recv_sem=recv_sem,
        device_id=device,
        device_id_type=MESH_ID,
    )


def gather_kernel(rows, block_ref, all_ref, send_sems, recv_sems, local_sem):
    side, row, core, near_core, near_side, near_row = place()
    half = rows // 2

    def spot(a, b, c, part=None):
        start = (a * 4 + b * 2 + c) * rows
        if part is None:
            return all_ref.at[pl.ds(pl.multiple_of(start, rows), rows)]
        return all_ref.at[pl.ds(pl.multiple_of(start + part * half, half), half)]

    greet((near_core, near_side, near_row))
    copies = []

    def send(number, source, target, device):
        copy = remote(source, target, send_sems.at[number], recv_sems.at[number], device)
        copy.start()
        copies.append(copy)
        return copy

    first = block_ref.at[pl.ds(0, half)]
    second = block_ref.at[pl.ds(half, half)]
    side_b = send(0, second, spot(side, row, core, 1), near_side)
    row_a = send(1, first, spot(side, row, core, 0), near_row)
    side_a = send(2, first, spot(side, row, core, 0), near_side)
    row_b = send(3, second, spot(side, row, core, 1), near_row)
    core_own = send(4, block_ref, spot(side, row, core), near_core)
    local = pltpu.make_async_copy(block_ref, spot(side, row, core), local_sem)
    local.start()
    side_b.wait_recv()
    away_b = send(5, spot(1 - side, row, core, 1), spot(1 - side, row, core, 1), near_row)
    row_a.wait_recv()
    away_a = send(6, spot(side, 1 - row, core, 0), spot(side, 1 - row, core, 0), near_side)
    side_a.wait_recv()
    core_side = send(7, spot(1 - side, row, core), spot(1 - side, row, core), near_core)
    row_b.wait_recv()
    core_row = send(8, spot(side, 1 - row, core), spot(side, 1 - row, core), near_core)
    away_a.wait_recv()
    core_away_a = send(
        9, spot(1 - side, 1 - row, core, 0), spot(1 - side, 1 - row, core, 0), near_core
    )
    away_b.wait_recv()
    core_away_b = send(
        10, spot(1 - side, 1 - row, core, 1), spot(1 - side, 1 - row, core, 1), near_core
    )
    for copy in (core_own, core_side, core_row, core_away_a, core_away_b):
        copy.wait_recv()
    for copy in copies:
        copy.wait_send()
    local.wait()


def plane_gather(block):
    rows, width = block.shape
    return pl.pallas_call(
        functools.partial(gather_kernel, rows),
        out_shape=jax.ShapeDtypeStruct((8 * rows, width), block.dtype),
        in_specs=[pl.BlockSpec(memory_space=pl.ANY)],
        out_specs=pl.BlockSpec(memory_space=pl.ANY),
        scratch_shapes=[
            pltpu.SemaphoreType.DMA((11,)),
            pltpu.SemaphoreType.DMA((11,)),
            pltpu.SemaphoreType.DMA,
        ],
        compiler_params=pltpu.CompilerParams(collective_id=0, has_side_effects=True),
        cost_estimate=pl.CostEstimate(
            flops=0, bytes_accessed=64 * rows * width * 2, transcendentals=0
        ),
        name="plane_gather",
    )(block)


def swap_scratch():
    return [pltpu.SemaphoreType.DMA((3,))] * 2 + [pltpu.SemaphoreType.DMA]


def swap_copies(in_ref, out_ref, send_sems, recv_sems, local_sem):
    _, row, core, *_ = place()
    rows = out_ref.shape[1]
    here = row * 2 + core

    def block(index):
        return in_ref.at[pl.ds(pl.multiple_of(index * rows, rows), rows)]

    peers = (row * 2 + 1 - core, (1 - row) * 2 + core, (1 - row) * 2 + 1 - core)
    away = [
        remote(block(peer), out_ref.at[here], send_sems.at[at], recv_sems.at[at], {"ctx": peer})
        for at, peer in enumerate(peers)
    ]
    return away, pltpu.make_async_copy(block(here), out_ref.at[here], local_sem)


def scatter_steps(rows, lefts, right, out_ref, scratch, prepare=None, swap=None):
    mine, theirs, other, to_side, to_row, from_side, from_row = scratch[:7]
    on_side, on_row, got_side, got_row, send_sems, recv_sems = scratch[7:]
    side, row, core, near_core, near_side, near_row = place()
    half = rows // 2
    tile = 32
    width = out_ref.shape[1]
    wide = 512

    chips = ((side, row), (1 - side, row), (side, 1 - row), (1 - side, 1 - row))
    routes = [(theirs.at[chip], other.at[chip], near_core) for chip in range(4)] + [
        (to_side.at[0], from_side.at[0], near_side),
        (to_row.at[0], from_row.at[0], near_row),
        (to_side.at[1], from_side.at[1], near_side),
        (to_row.at[1], from_row.at[1], near_row),
        (on_row, got_row, near_row),
        (on_side, got_side, near_side),
    ]
    copies = [
        remote(source, target, send_sems.at[at], recv_sems.at[at], device)
        for at, (source, target, device) in enumerate(routes)
    ]

    order = [(chip, owner) for chip in (3, 1, 2, 0) for owner in (1 - core, core)]
    starts = [
        pl.multiple_of((chips[chip][0] * 4 + chips[chip][1] * 2 + owner) * rows, rows)
        for chip, owner in order
    ]

    swapped = None if swap is None else swap_copies(*swap)

    def product(target, number, twin):
        turn = 2 * (3, 1, 2, 0).index(number) + twin
        start = starts[turn]
        if prepare is not None:
            prepare(turn, starts)

        def step(index, carry):
            at = pl.multiple_of(index * wide, wide)
            value = None
            for which, left in enumerate(lefts):
                term = matmul_nt(left[pl.ds(start, rows), :], right[which, pl.ds(at, wide), :])
                value = term if value is None else value + term
            target[number, :, pl.ds(at, wide)] = value.astype(BF16)
            return carry

        lax.fori_loop(0, width // wide, step, 0)

    def give(number):
        product(theirs, number, 0)
        if number == 3:
            partners = (near_core, near_side, near_row)
            if swap is not None:
                partners += ({"ctx": (1 - row) * 2 + 1 - core},)
            greet(partners)
        copies[number].start()

    def take(number):
        product(mine, number, 1)
        copies[number].wait_recv()

    def both(number, part, at):
        at = part * half + at
        here = mine[number, pl.ds(at, tile), :].astype(F32)
        return here + other[number, pl.ds(at, tile), :].astype(F32)

    def each(body):
        def step(index, carry):
            body(pl.multiple_of(index * tile, tile))
            return carry

        lax.fori_loop(0, half // tile, step, 0)

    def put(target, number, part, extra=None):
        def body(at):
            value = both(number, part, at)
            if extra is not None:
                value = value + extra[pl.ds(at, tile), :].astype(F32)
            target[pl.ds(at, tile), :] = value.astype(BF16)

        each(body)

    def across():
        give(3)
        take(3)
        put(to_side.at[0], 3, 0)
        copies[4].start()
        put(to_row.at[0], 3, 1)
        copies[5].start()
        if swap is not None:
            for copy in swapped[0] + [swapped[1]]:
                copy.start()

    def along():
        give(1)
        take(1)
        put(to_side.at[1], 1, 0)
        copies[6].start()
        give(2)
        take(2)
        put(to_row.at[1], 2, 1)
        copies[7].start()

    def forward():
        copies[4].wait_recv()
        put(on_row, 2, 0, from_side.at[0])
        copies[8].start()
        copies[5].wait_recv()
        put(on_side, 1, 1, from_row.at[0])
        copies[9].start()

    def own():
        give(0)
        take(0)

    def finish():
        copies[6].wait_recv()
        copies[7].wait_recv()

        def first_sum(at):
            out_ref[pl.ds(at, tile), :] = both(0, 0, at) + from_side[
                1, pl.ds(at, tile), :
            ].astype(F32)
            out_ref[pl.ds(half + at, tile), :] = both(0, 1, at) + from_row[
                1, pl.ds(at, tile), :
            ].astype(F32)

        each(first_sum)
        copies[8].wait_recv()
        copies[9].wait_recv()

        def last_sum(at):
            out_ref[pl.ds(at, tile), :] += got_row[pl.ds(at, tile), :].astype(F32)
            out_ref[pl.ds(half + at, tile), :] += got_side[pl.ds(at, tile), :].astype(F32)

        each(last_sum)
        for copy in copies:
            copy.wait_send()
        if swap is not None:
            for copy in swapped[0]:
                copy.wait()
            swapped[1].wait()

    return across, along, forward, own, finish


def scatter_scratch(rows, width):
    half = rows // 2
    return (
        [pltpu.VMEM((4, rows, width), BF16)] * 3
        + [pltpu.VMEM((2, half, width), BF16)] * 4
        + [pltpu.VMEM((half, width), BF16)] * 4
        + [pltpu.SemaphoreType.DMA((10,))] * 2
    )


def scatter_kernel(rows, terms, swaps, *refs):
    lefts, right, refs = refs[:terms], refs[terms], refs[terms + 1 :]
    swap = None
    if swaps:
        in_ref, out_ref, swapped_ref, *scratch = refs
        swap = (in_ref, swapped_ref, *scratch[-3:])
        scratch = scratch[:-3]
    else:
        out_ref, *scratch = refs
    for step in scatter_steps(rows, lefts, right, out_ref, scratch, swap=swap):
        step()


def product_scatter(number, lefts, right, swap=None):
    total = lefts[0].shape[0]
    width = right.shape[1]
    rows = total // 8
    vmem = pl.BlockSpec(memory_space=pltpu.VMEM)
    shapes, ins, scratch = [jax.ShapeDtypeStruct((rows, width), F32)], [vmem] * (len(lefts) + 1), []
    operands = [*lefts, right]
    if swap is not None:
        shapes.append(jax.ShapeDtypeStruct((4, swap.shape[0] // 4, swap.shape[1]), swap.dtype))
        ins.append(pl.BlockSpec(memory_space=pl.ANY))
        operands.append(swap)
        scratch = swap_scratch()
    return pl.pallas_call(
        functools.partial(scatter_kernel, rows, len(lefts), swap is not None),
        out_shape=tuple(shapes),
        in_specs=ins,
        out_specs=tuple([vmem] * len(shapes)),
        scratch_shapes=scatter_scratch(rows, width) + scratch,
        compiler_params=pltpu.CompilerParams(
            collective_id=number, has_side_effects=True, vmem_limit_bytes=56 * 1024 * 1024
        ),
        cost_estimate=pl.CostEstimate(flops=0, bytes_accessed=1024, transcendentals=0),
        name="product_scatter",
    )(*operands)


def ffn_back_kernel(
    rows,
    cot_ref,
    gate_slope_ref,
    up_slope_ref,
    down_ref,
    right_ref,
    out_ref,
    gate_ref,
    up_ref,
    cots,
    gate_slopes,
    up_slopes,
    sems,
    *scratch,
):
    wide = 512
    sources = ((cot_ref, cots), (gate_slope_ref, gate_slopes), (up_slope_ref, up_slopes))

    def fetch(turn, starts):
        return [
            pltpu.make_async_copy(
                source.at[pl.ds(starts[turn], rows)], target.at[turn % 2], sems.at[which, turn % 2]
            )
            for which, (source, target) in enumerate(sources)
        ]

    def prepare(turn, starts):
        if turn == 0:
            for copy in fetch(0, starts):
                copy.start()
        if turn < 7:
            for copy in fetch(turn + 1, starts):
                copy.start()
        for copy in fetch(turn, starts):
            copy.wait()
        slot = turn % 2
        here = pl.ds(starts[turn], rows)

        def step(index, carry):
            at = pl.ds(pl.multiple_of(index * wide, wide), wide)
            grad = jnp.dot(cots[slot], down_ref[:, at], preferred_element_type=F32)
            gate_ref[here, at] = (grad * gate_slopes[slot, :, at].astype(F32)).astype(BF16)
            up_ref[here, at] = (grad * up_slopes[slot, :, at].astype(F32)).astype(BF16)
            return carry

        lax.fori_loop(0, down_ref.shape[1] // wide, step, 0)

    for step in scatter_steps(rows, [gate_ref, up_ref], right_ref, out_ref, scratch, prepare):
        step()


def ffn_back(number, cot, gate_slope, up_slope, down_w, gate_up):
    total, width = cot.shape
    units = down_w.shape[1]
    rows = total // 8
    vmem = pl.BlockSpec(memory_space=pltpu.VMEM)
    left = pl.BlockSpec(memory_space=pl.ANY)
    return pl.pallas_call(
        functools.partial(ffn_back_kernel, rows),
        out_shape=(
            jax.ShapeDtypeStruct((rows, width), F32),
            jax.ShapeDtypeStruct((total, units), BF16),
            jax.ShapeDtypeStruct((total, units), BF16),
        ),
        in_specs=[left, left, left, vmem, vmem],
        out_specs=(vmem, vmem, vmem),
        scratch_shapes=[
            pltpu.VMEM((2, rows, width), BF16),
            pltpu.VMEM((2, rows, units), BF16),
            pltpu.VMEM((2, rows, units), BF16),
            pltpu.SemaphoreType.DMA((3, 2)),
        ]
        + scatter_scratch(rows, width),
        compiler_params=pltpu.CompilerParams(
            collective_id=number, has_side_effects=True, vmem_limit_bytes=56 * 1024 * 1024
        ),
        cost_estimate=pl.CostEstimate(flops=0, bytes_accessed=1024, transcendentals=0),
        name="ffn_back",
    )(cot, gate_slope, up_slope, down_w, gate_up)


def ffn_kernel(in_ref, w_ref, product_ref, gate_slope_ref, up_slope_ref):
    wide = 256
    rows_in = in_ref[...]

    def step(index, carry):
        at = pl.ds(pl.multiple_of(index * wide, wide), wide)
        gate = jnp.dot(rows_in, w_ref[0, :, at], preferred_element_type=F32)
        up = jnp.dot(rows_in, w_ref[1, :, at], preferred_element_type=F32)
        sigma = jax.nn.sigmoid(gate)
        active = gate * sigma
        product_ref[:, at] = (active * up).astype(BF16)
        gate_slope_ref[:, at] = (up * sigma * (1.0 + gate * (1.0 - sigma))).astype(BF16)
        up_slope_ref[:, at] = active.astype(BF16)
        return carry

    lax.fori_loop(0, w_ref.shape[2] // wide, step, 0)


def ffn(rows_in, gate_up):
    total, width = rows_in.shape
    units = gate_up.shape[2]
    rows = 256
    out = pl.BlockSpec((rows, units), lambda i: (i, 0))
    return pl.pallas_call(
        ffn_kernel,
        grid=(total // rows,),
        out_shape=(jax.ShapeDtypeStruct((total, units), BF16),) * 3,
        in_specs=[
            pl.BlockSpec((rows, width), lambda i: (i, 0)),
            pl.BlockSpec(
                (2, width, units), lambda i: (0, 0, 0), pipeline_mode=pl.Buffered(1)
            ),
        ],
        out_specs=(out, out, out),
        compiler_params=pltpu.CompilerParams(vmem_limit_bytes=40 * 1024 * 1024),
        cost_estimate=pl.CostEstimate(flops=0, bytes_accessed=1024, transcendentals=0),
        name="ffn",
    )(rows_in, gate_up)


def swap_halves(values):
    width = values.shape[-1]
    lane = lax.broadcasted_iota(jnp.int32, values.shape, 1)
    ahead = pltpu.roll(values, width - HEAD_DIM // 2, 1)
    behind = pltpu.roll(values, HEAD_DIM // 2, 1)
    return jnp.where(lane % HEAD_DIM < HEAD_DIM // 2, ahead, behind)


def pieces_of(block):
    return ((0, block * QB, False), (block * QB, QB, True)) if block else ((0, QB, True),)


def masked_scores(query, keys, diagonal):
    scores = matmul_nt(query, keys)
    if diagonal:
        here = lax.broadcasted_iota(jnp.int32, scores.shape, 0)
        there = lax.broadcasted_iota(jnp.int32, scores.shape, 1)
        scores = jnp.where(here >= there, scores, -1e30)
    return scores


def attend_kernel(length, q_ref, kv_ref, cos_ref, sin_ref, att_ref, qrot_ref, kvrot_ref, log_ref):
    cosine = cos_ref[...]
    signed = sin_ref[...]
    scale = HEAD_DIM ** (-0.5)
    pre = q_ref[...]
    qrot_ref[...] = (pre * cosine + swap_halves(pre) * signed).astype(BF16)
    pre = kv_ref[...]
    lane = lax.broadcasted_iota(jnp.int32, pre.shape, 1)
    turned = jnp.where(lane < HEAD_DIM, pre * cosine + swap_halves(pre) * signed, pre)
    kvrot_ref[...] = turned.astype(BF16)
    for block in range(length // QB):
        here = pl.ds(block * QB, QB)
        logs = []
        mixed = []
        for head in range(2):
            query = qrot_ref[here, head * HEAD_DIM : (head + 1) * HEAD_DIM] * jnp.asarray(
                scale, BF16
            )
            scores = []
            for start, size, diagonal in pieces_of(block):
                keys = kvrot_ref[pl.ds(start, size), :HEAD_DIM]
                scores.append(masked_scores(query, keys, diagonal))
            peak = functools.reduce(
                jnp.maximum, [jnp.max(s, axis=1, keepdims=True) for s in scores]
            )
            powers = [jnp.exp(s - peak) for s in scores]
            total = sum(jnp.sum(p, axis=1, keepdims=True) for p in powers)
            inverse = 1.0 / total
            out = None
            for (start, size, _), power in zip(pieces_of(block), powers):
                values = kvrot_ref[pl.ds(start, size), HEAD_DIM:]
                term = jnp.dot(
                    (power * inverse).astype(BF16), values, preferred_element_type=F32
                )
                out = term if out is None else out + term
            mixed.append(out)
            logs.append(peak + jnp.log(total))
        att_ref[here, :] = jnp.concatenate(mixed, axis=1).astype(BF16)
        lane = lax.broadcasted_iota(jnp.int32, (QB, 128), 1)
        log_ref[here, :] = jnp.where(lane < HEAD_DIM, logs[0], logs[1])


def attend(pre, cosine, signed, seqs):
    rows = pre.shape[0]
    length = rows // seqs
    pairs = pre.shape[1] // 128 - 1
    block = (length, 128)
    return pl.pallas_call(
        functools.partial(attend_kernel, length),
        grid=(seqs, pairs),
        out_shape=(
            jax.ShapeDtypeStruct((rows, pairs * 128), BF16),
            jax.ShapeDtypeStruct((rows, pairs * 128), BF16),
            jax.ShapeDtypeStruct((rows, 128), BF16),
            jax.ShapeDtypeStruct((rows, pairs * 128), F32),
        ),
        in_specs=[
            pl.BlockSpec(block, lambda s, h: (s, h)),
            pl.BlockSpec(block, lambda s, h: (s, pairs)),
            pl.BlockSpec(block, lambda s, h: (0, 0)),
            pl.BlockSpec(block, lambda s, h: (0, 0)),
        ],
        out_specs=(
            pl.BlockSpec(block, lambda s, h: (s, h)),
            pl.BlockSpec(block, lambda s, h: (s, h)),
            pl.BlockSpec(block, lambda s, h: (s, 0)),
            pl.BlockSpec(block, lambda s, h: (s, h)),
        ),
        compiler_params=pltpu.CompilerParams(vmem_limit_bytes=48 * 1024 * 1024),
        cost_estimate=pl.CostEstimate(
            flops=8 * rows * length * 128 * pairs,
            bytes_accessed=rows * pairs * 128 * 12,
            transcendentals=rows * length * 2 * pairs,
        ),
        name="attend",
    )(pre, pre, cosine, signed)


def attend_back_kernel(
    seqs,
    rows,
    q_ref,
    kv_ref,
    up_ref,
    log_ref,
    cos_ref,
    sin_ref,
    left_ref,
    right_ref,
    in_ref,
    dq_ref,
    dkv_ref,
    out_ref,
    swapped_ref,
    sum_ref,
    *scratch,
):
    across, along, forward, own, finish = scatter_steps(
        rows,
        [left_ref],
        right_ref,
        out_ref,
        scratch[:-3],
        swap=(in_ref, swapped_ref, *scratch[-3:]),
    )
    scale = HEAD_DIM ** (-0.5)
    length = q_ref.shape[0] // seqs
    pairs = q_ref.shape[1] // 128
    across()
    along()

    def one_pair(index, carry):
        seq = index // pairs
        pair = index % pairs
        lanes_at = pl.ds(pl.multiple_of(pair * 128, 128), 128)
        base = pl.multiple_of(seq * length, length)

        @pl.when(index == 1)
        def _():
            forward()

        @pl.when(index == 2)
        def _():
            own()

        @pl.when(pair == 0)
        def _():
            sum_ref[...] = jnp.zeros_like(sum_ref)

        for block in range(length // QB):
            here = pl.ds(base + block * QB, QB)
            turned = []
            q_pair = q_ref[here, lanes_at]
            up_pair = up_ref[here, lanes_at]
            log_pair = log_ref[here, lanes_at]
            for head in range(2):
                lanes = slice(head * HEAD_DIM, (head + 1) * HEAD_DIM)
                query = q_pair[:, lanes] * jnp.asarray(scale, BF16)
                upstream = up_pair[:, lanes]
                logs = log_pair[:, head * HEAD_DIM : head * HEAD_DIM + 1]
                saved = []
                inner = None
                for start, size, diagonal in pieces_of(block):
                    keys = kv_ref[pl.ds(base + start, size), :HEAD_DIM]
                    values = kv_ref[pl.ds(base + start, size), HEAD_DIM:]
                    probability = jnp.exp(masked_scores(query, keys, diagonal) - logs)
                    prob_grad = matmul_nt(upstream, values)
                    term = jnp.sum(probability * prob_grad, axis=1, keepdims=True)
                    inner = term if inner is None else inner + term
                    saved.append((start, size, probability, prob_grad))
                out = None
                for start, size, probability, prob_grad in saved:
                    keys = kv_ref[pl.ds(base + start, size), :HEAD_DIM]
                    score_grad = (probability * (prob_grad - inner)).astype(BF16)
                    rounded = probability.astype(BF16)
                    term = jnp.dot(score_grad, keys, preferred_element_type=F32)
                    out = term if out is None else out + term
                    sum_ref[pl.ds(start, size), :] += jnp.concatenate(
                        [matmul_t(score_grad, query), matmul_t(rounded, upstream)], axis=1
                    )
                turned.append(out * scale)
            grad = jnp.concatenate(turned, axis=1)
            angle = pl.ds(block * QB, QB)
            dq_ref[here, lanes_at] = (
                grad * cos_ref[angle, :] - swap_halves(grad) * sin_ref[angle, :]
            ).astype(BF16)

        @pl.when(pair == pairs - 1)
        def _():
            grad = sum_ref[...]
            lane = lax.broadcasted_iota(jnp.int32, grad.shape, 1)
            back = grad * cos_ref[...] - swap_halves(grad) * sin_ref[...]
            dkv_ref[pl.ds(base, length), :] = jnp.where(lane < HEAD_DIM, back, grad).astype(BF16)

        return carry

    lax.fori_loop(0, seqs * pairs, one_pair, 0)
    finish()


def attend_back(number, queries, keyvals, upstream, logs, cosine, signed, seqs, left, right, swap):
    total, width = queries.shape
    length = total // seqs
    rows = total // 8
    vmem = pl.BlockSpec(memory_space=pltpu.VMEM)
    return pl.pallas_call(
        functools.partial(attend_back_kernel, seqs, rows),
        out_shape=(
            jax.ShapeDtypeStruct((total, width), BF16),
            jax.ShapeDtypeStruct((total, 128), BF16),
            jax.ShapeDtypeStruct((rows, right.shape[1]), F32),
            jax.ShapeDtypeStruct((4, swap.shape[0] // 4, swap.shape[1]), swap.dtype),
        ),
        in_specs=[vmem] * 8 + [pl.BlockSpec(memory_space=pl.ANY)],
        out_specs=(vmem, vmem, vmem, vmem),
        scratch_shapes=[pltpu.VMEM((length, 128), F32)]
        + scatter_scratch(rows, right.shape[1])
        + swap_scratch(),
        compiler_params=pltpu.CompilerParams(
            collective_id=number, has_side_effects=True, vmem_limit_bytes=56 * 1024 * 1024
        ),
        cost_estimate=pl.CostEstimate(flops=0, bytes_accessed=1024, transcendentals=0),
        name="attend_back",
    )(queries, keyvals, upstream, logs, cosine, signed, left, right, swap)


def gain_kernel(
    planes, parts, cols, terms_ref, out_ref, total, seen, far, mine, across, send_sems, recv_sems
):
    side, row, core, near_core, near_side, near_row = place()
    plane = lax.axis_index("dp")
    ctx = row * 2 + core
    others = [{"dp": (plane + step) % planes} for step in range(1, planes)]
    greet((near_core, near_side, near_row) + tuple(others))
    total[...] = terms_ref[...]
    copies = []
    for number, target in enumerate((near_core, near_row)):
        copy = remote(
            total, seen.at[number], send_sems.at[number], recv_sems.at[number], target
        )
        copy.start()
        copy.wait()
        total[...] += seen[number]
    for step, target in enumerate(others, 1):
        start = (((plane + step) % planes) * parts + ctx) * cols
        copy = remote(
            total.at[:, pl.ds(pl.multiple_of(start, cols), cols)],
            far.at[step - 1],
            send_sems.at[2 + step],
            recv_sems.at[2 + step],
            target,
        )
        copy.start()
        copies.append(copy)
    start = (plane * parts + ctx) * cols
    value = total[:, pl.ds(pl.multiple_of(start, cols), cols)]
    for number, copy in enumerate(copies):
        copy.wait_recv()
        value += far[number]
    mine[...] = value
    last = remote(mine, across, send_sems.at[2], recv_sems.at[2], near_side)
    last.start()
    copies.append(last)
    last.wait_recv()
    out_ref[...] = value + across[...]
    for copy in copies:
        copy.wait_send()


def gain_sum(terms):
    planes = lax.axis_size("dp")
    parts = lax.axis_size("ctx")
    rows, width = terms.shape
    cols = width // (planes * parts)
    return pl.pallas_call(
        functools.partial(gain_kernel, planes, parts, cols),
        out_shape=jax.ShapeDtypeStruct((rows, cols), F32),
        in_specs=[pl.BlockSpec(memory_space=pltpu.VMEM)],
        out_specs=pl.BlockSpec(memory_space=pltpu.VMEM),
        scratch_shapes=[
            pltpu.VMEM((rows, width), F32),
            pltpu.VMEM((2, rows, width), F32),
            pltpu.VMEM((planes - 1, rows, cols), F32),
            pltpu.VMEM((rows, cols), F32),
            pltpu.VMEM((rows, cols), F32),
            pltpu.SemaphoreType.DMA((planes + 2,)),
            pltpu.SemaphoreType.DMA((planes + 2,)),
        ],
        compiler_params=pltpu.CompilerParams(collective_id=2, has_side_effects=True),
        name="gain_sum",
    )(terms)


def lay_kernel(own_ref, far_ref, twin_ref, twin_far_ref, all_ref, sems):
    ctx = lax.axis_index("ctx")
    row, core = ctx // 2, ctx % 2
    span = own_ref.shape[1]
    copies = []
    for number, (part, a, b) in enumerate(
        (
            (own_ref, row, core),
            (twin_ref, row, 1 - core),
            (far_ref, 1 - row, core),
            (twin_far_ref, 1 - row, 1 - core),
        )
    ):
        start = pl.multiple_of((a * 2 + b) * span, span)
        copies.append(
            pltpu.make_async_copy(part, all_ref.at[:, pl.ds(start, span)], sems.at[number])
        )
        copies[-1].start()
    for copy in copies:
        copy.wait()


def along_ctx(block, earlier, later):
    seqs, span, width = block.shape
    cores = [(0, 1), (1, 0), (2, 3), (3, 2)]
    far = lax.ppermute(after(block, earlier), "ctx", [(0, 2), (1, 3), (2, 0), (3, 1)])
    far = after(far, later)
    twin, twin_far = lax.ppermute(block, "ctx", cores), lax.ppermute(far, "ctx", cores)
    whole = pl.pallas_call(
        lay_kernel,
        out_shape=jax.ShapeDtypeStruct((seqs, 4 * span, width), block.dtype),
        in_specs=[pl.BlockSpec(memory_space=pl.ANY)] * 4,
        out_specs=pl.BlockSpec(memory_space=pltpu.VMEM),
        scratch_shapes=[pltpu.SemaphoreType.DMA((4,))],
        compiler_params=pltpu.CompilerParams(vmem_limit_bytes=24 * 1024 * 1024),
        name="lay",
    )(block, far, twin, twin_far)
    return whole.reshape(seqs * 4 * span, width)


def after(value, *earlier):
    return lax.optimization_barrier((value,) + earlier)[0]


def to_units(weight):
    return lax.all_to_all(weight, "ctx", split_axis=1, concat_axis=0, tiled=True)


def from_units(grad):
    return lax.all_to_all(grad, "ctx", split_axis=0, concat_axis=1, tiled=True)


def on_plane(
    layer_input,
    attn_gain,
    w_query,
    w_key,
    w_value,
    w_out,
    ffn_gain,
    w_gate,
    w_up,
    w_down,
    cotangent,
):
    seqs, span, width = layer_input.shape
    planes = lax.axis_size("dp")
    parts = lax.axis_size("ctx")
    side = lax.axis_index("tensor")
    length = span * parts
    rows_w = w_query.shape[0]
    q_cols = w_query.shape[1] // parts
    kv_cols = w_key.shape[1] // parts

    theta = angles(jnp.arange(length), HEAD_DIM)
    cosine = jnp.tile(jnp.cos(theta), (1, 4))
    sine = jnp.sin(theta)
    signed = jnp.tile(jnp.concatenate([-sine, sine], axis=1), (1, 2))

    gain_row = jnp.concatenate(
        [attn_gain, ffn_gain, jnp.zeros((2 * q_cols + 2 * kv_cols - 2 * rows_w,), BF16)]
    )
    gain_rows = jnp.broadcast_to(gain_row[None, None, :], (parts, 8, gain_row.shape[0]))
    mixed = jnp.concatenate(
        [
            w_query.reshape(rows_w, parts, q_cols),
            w_key.reshape(rows_w, parts, kv_cols),
            w_value.reshape(rows_w, parts, kv_cols),
            w_out.T.reshape(rows_w, parts, q_cols),
        ],
        axis=2,
    ).transpose(1, 0, 2)
    mixed = jnp.concatenate([mixed, gain_rows], axis=1)
    mixed = lax.all_to_all(mixed, "ctx", split_axis=0, concat_axis=0, tiled=True)
    ready_w = mixed
    mixed = lax.all_gather(mixed, "dp", axis=0, tiled=True)
    attn_w = mixed[:, :rows_w].reshape(width, -1)
    gain_one = mixed[:, rows_w, :rows_w].reshape(width).astype(F32)
    gain_two = mixed[:, rows_w, rows_w : 2 * rows_w].reshape(width).astype(F32)
    qkv_cols = q_cols + 2 * kv_cols
    w_qkv = attn_w[:, :qkv_cols]
    w_out_t = attn_w[:, qkv_cols:]

    half_units = w_gate.shape[1] // parts
    gate_up = jnp.stack(
        [w_gate.reshape(rows_w, parts, half_units), w_up.reshape(rows_w, parts, half_units)]
    )
    gate_up = after(gate_up, ready_w).transpose(2, 0, 1, 3)
    gate_up = lax.all_to_all(gate_up, "ctx", split_axis=0, concat_axis=0, tiled=True)
    own_in = lax.dynamic_index_in_dim(layer_input, side, 0, keepdims=False)
    own_cot = lax.dynamic_index_in_dim(cotangent, side, 0, keepdims=False)
    all_in = plane_gather(after(own_in, ready_w))
    gate_up = gate_up.transpose(1, 0, 2, 3).reshape(2, parts * rows_w, half_units)
    gate_up = lax.all_gather(gate_up, "dp", axis=1, tiled=True)
    down_own = to_units(after(w_down, all_in).T)
    down_w = lax.all_gather(down_own, "dp", axis=0, tiled=True)

    all_f = all_in.astype(F32)
    normed_one = (all_f * rms_factor(all_f) * gain_one).astype(BF16)
    pre = after(jnp.dot(normed_one, w_qkv, preferred_element_type=F32), down_own)
    attended, queries, keyvals, logs = attend(pre, cosine, signed, seqs)
    inputs_f = own_in.astype(F32)
    factor_one = rms_factor(inputs_f)
    hidden = inputs_f + product_scatter(1, [attended], w_out_t[None])[0]
    factor_two = rms_factor(hidden)
    normed_own = (hidden * factor_two * gain_two).astype(BF16)
    normed_two = plane_gather(normed_own)
    all_cot = along_ctx(cotangent, down_own, attended)

    product, gate_slope, up_slope = ffn(normed_two, gate_up)
    down_grad = matmul_t(all_cot, product).astype(BF16)
    down_sum = lax.psum_scatter(down_grad, "dp", scatter_dimension=0, tiled=True)
    normed_two_grad, gate_grad, up_grad = ffn_back(
        3, after(all_cot, down_grad), gate_slope, up_slope, down_w, gate_up
    )
    gate_w_grad = matmul_t(normed_two, gate_grad).astype(BF16)
    gate_sum = lax.psum_scatter(gate_w_grad, "dp", scatter_dimension=0, tiled=True)
    hidden_back, ffn_gain_term = rms_back(normed_two_grad, hidden, factor_two, gain_two)
    hidden_grad = own_cot.astype(F32) + hidden_back
    hidden_low = plane_gather(after(hidden_grad.astype(BF16), gate_w_grad))
    up_w_grad = matmul_t(normed_two, after(up_grad, hidden_low)).astype(BF16)
    up_sum = lax.psum_scatter(up_w_grad, "dp", scatter_dimension=0, tiled=True)
    attended_grad = jnp.dot(after(hidden_low, up_w_grad), w_out_t, preferred_element_type=F32).astype(BF16)
    out_w_grad = matmul_t(hidden_low, attended).astype(BF16)
    query_low, keyval_low, ffn_own, down_out = attend_back(
        5,
        queries,
        keyvals,
        attended_grad,
        logs,
        cosine,
        signed,
        seqs,
        product,
        down_w[None],
        down_sum,
    )
    back = jnp.concatenate([query_low, keyval_low], axis=1)
    qkv_grad = matmul_t(normed_one, back).astype(BF16)
    attn_grad = jnp.concatenate([qkv_grad, out_w_grad], axis=1)
    attn_sum = lax.psum_scatter(attn_grad, "dp", scatter_dimension=0, tiled=True)
    normed_one_grad, gate_out = product_scatter(
        4, [after(back, attn_grad)], w_qkv[None], gate_sum
    )
    input_back, attn_gain_term = rms_back(normed_one_grad, inputs_f, factor_one, gain_one)
    input_own = (hidden_grad + input_back).astype(BF16)
    gain_own = gain_sum(after(jnp.stack([attn_gain_term, ffn_gain_term]), input_own))
    out_own = (hidden + ffn_own).astype(BF16)

    def both_sides(own):
        other = lax.ppermute(own, "tensor", [(0, 1), (1, 0)])
        return jnp.where(side == 0, jnp.stack([own, other]), jnp.stack([other, own]))

    layer_output = both_sides(out_own)
    input_grad = both_sides(input_own).astype(F32)
    down_out, gate_out = (
        swapped.transpose(1, 0, 2).reshape(rows_w, -1) for swapped in (down_out, gate_out)
    )
    up_out = from_units(after(up_sum, gain_own))
    attn_out = lax.all_to_all(
        after(attn_sum, up_out).reshape(parts, rows_w, -1), "ctx", split_axis=0, concat_axis=0, tiled=True
    )

    def columns(start, size):
        return attn_out[:, :, start : start + size].transpose(1, 0, 2).reshape(rows_w, -1)

    return (
        layer_output,
        input_grad,
        gain_own[0],
        columns(0, q_cols).astype(F32),
        columns(q_cols, kv_cols).astype(F32),
        columns(q_cols + kv_cols, kv_cols).astype(F32),
        columns(qkv_cols, q_cols).T.astype(F32),
        gain_own[1],
        gate_out.astype(F32),
        up_out.astype(F32),
        down_out.T.astype(F32),
    )


def fits_plane(mesh, shapes):
    sizes = mesh.shape
    seqs, length, width = shapes[0].shape
    kv_heads = shapes[3].shape[1] // HEAD_DIM
    return (
        sizes["tensor"] == 2
        and sizes["ctx"] == 4
        and seqs == 2 * sizes["dp"]
        and kv_heads == 8
        and shapes[2].shape[1] == 4 * shapes[3].shape[1]
        and length % (4 * QB) == 0
        and width % (128 * 4 * sizes["dp"]) == 0
    )


def placed(mesh, function):
    return jax.shard_map(
        function,
        mesh=mesh,
        in_specs=(
            P("dp", "ctx", None),
            P(("dp", "ctx")),
            P(("dp", "ctx"), "tensor"),
            P(("dp", "ctx"), "tensor"),
            P(("dp", "ctx"), "tensor"),
            P("tensor", ("dp", "ctx")),
            P(("dp", "ctx")),
            P(("dp", "ctx"), "tensor"),
            P(("dp", "ctx"), "tensor"),
            P("tensor", ("dp", "ctx")),
            P("dp", "ctx", None),
        ),
        out_specs=(
            P("dp", "ctx", None),
            P("dp", "ctx", None),
            P(("dp", "ctx")),
            P(("dp", "ctx"), "tensor"),
            P(("dp", "ctx"), "tensor"),
            P(("dp", "ctx"), "tensor"),
            P("tensor", ("dp", "ctx")),
            P(("dp", "ctx")),
            P(("dp", "ctx"), "tensor"),
            P(("dp", "ctx"), "tensor"),
            P("tensor", ("dp", "ctx")),
        ),
        check_vma=False,
    )


def solution(mesh):
    def whole(*arrays):
        return placed(mesh, on_plane if fits_plane(mesh, arrays) else on_device)(*arrays)

    return whole
```

```python
import functools
import math

import jax
import jax.numpy as jnp
from jax import lax
from jax.experimental import pallas as pl
from jax.experimental.pallas import tpu as pltpu
from jax.sharding import PartitionSpec as P

HEAD_DIM = 64


EPSILON = 1e-05
ROPE_BASE = 500000.0


def rotate(values, cosine, sine_val):
    middle = values.shape[-1] // 2
    leading = values[..., :middle]
    trailing = values[..., middle:]
    return jnp.concatenate(
        [leading * cosine - trailing * sine_val, trailing * cosine + leading * sine_val], axis=-1
    )


def unrotate(gradient, cosine, sine_val):
    middle = gradient.shape[-1] // 2
    leading = gradient[..., :middle]
    trailing = gradient[..., middle:]
    return jnp.concatenate(
        [leading * cosine + trailing * sine_val, trailing * cosine - leading * sine_val], axis=-1
    )


def angles(positions, head_dim):
    exponent = jnp.arange(head_dim // 2).astype(jnp.float32) * (
        -2.0 * math.log(ROPE_BASE) / head_dim
    )
    return positions.astype(jnp.float32)[:, None] * jnp.exp(exponent)[None, :]


def rms_factor(row_values):
    return lax.rsqrt(jnp.mean(row_values * row_values, axis=-1, keepdims=True) + EPSILON)


def rms_back(upstream, row_values, factor, gain_row):
    scaled = upstream * gain_row
    gain_term = jnp.sum(upstream * row_values * factor, axis=0)
    inner_mean = jnp.mean(scaled * row_values, axis=-1, keepdims=True)
    return (factor * scaled - row_values * (factor * factor * factor) * inner_mean, gain_term)


def matmul_t(left_op, right_op):
    return lax.dot_general(
        left_op, right_op, (((0,), (0,)), ((), ())), preferred_element_type=jnp.float32
    )


def matmul_nt(left_op, right_op):
    return lax.dot_general(
        left_op, right_op, (((1,), (1,)), ((), ())), preferred_element_type=jnp.float32
    )


def on_device(
    layer_input,
    attn_gain,
    w_query,
    w_key,
    w_value,
    w_out,
    ffn_gain,
    w_gate,
    w_up,
    w_down,
    cotangent,
):
    seq_dev, span_len, model_width = layer_input.shape
    row_count = seq_dev * span_len
    length_all = span_len * lax.axis_size("ctx")
    full_q, full_k, full_v, full_o, full_gate, full_up, full_down, gain_attn, gain_ffn = (
        lax.all_gather(w_query, ("dp", "ctx"), axis=0, tiled=True),
        lax.all_gather(w_key, ("dp", "ctx"), axis=0, tiled=True),
        lax.all_gather(w_value, ("dp", "ctx"), axis=0, tiled=True),
        lax.all_gather(w_out, ("dp", "ctx"), axis=1, tiled=True),
        lax.all_gather(w_gate, ("dp", "ctx"), axis=0, tiled=True),
        lax.all_gather(w_up, ("dp", "ctx"), axis=0, tiled=True),
        lax.all_gather(w_down, ("dp", "ctx"), axis=1, tiled=True),
        lax.all_gather(attn_gain, ("dp", "ctx"), axis=0, tiled=True),
        lax.all_gather(ffn_gain, ("dp", "ctx"), axis=0, tiled=True),
    )
    kv_local = full_k.shape[1] // HEAD_DIM
    group_size = full_q.shape[1] // HEAD_DIM // kv_local
    block_count = seq_dev * kv_local
    scale = HEAD_DIM ** (-0.5)
    query_pos = lax.axis_index("ctx") * span_len + jnp.arange(span_len)
    theta = angles(query_pos, HEAD_DIM)
    cosine = jnp.cos(theta)
    sine_val = jnp.sin(theta)
    causal = query_pos[:, None] >= jnp.arange(length_all)[None, :]
    inputs_f = layer_input.reshape(row_count, model_width).astype(jnp.float32)
    gain_one = gain_attn.astype(jnp.float32)
    gain_two = gain_ffn.astype(jnp.float32)
    factor_one = rms_factor(inputs_f)
    normed_one = (inputs_f * factor_one * gain_one).astype(jnp.bfloat16)
    query_pre = jnp.dot(normed_one, full_q, preferred_element_type=jnp.float32).reshape(
        seq_dev, span_len, kv_local, group_size, HEAD_DIM
    )
    queries = rotate(
        query_pre, cosine[None, :, None, None, :], sine_val[None, :, None, None, :]
    ).astype(jnp.bfloat16)
    key_pre = jnp.dot(normed_one, full_k, preferred_element_type=jnp.float32).reshape(
        seq_dev, span_len, kv_local, HEAD_DIM
    )
    keys_own = (
        rotate(key_pre, cosine[None, :, None, :], sine_val[None, :, None, :])
        .astype(jnp.bfloat16)
        .reshape(seq_dev, span_len, kv_local * HEAD_DIM)
    )
    values_own = (
        jnp.dot(normed_one, full_v, preferred_element_type=jnp.float32)
        .astype(jnp.bfloat16)
        .reshape(seq_dev, span_len, kv_local * HEAD_DIM)
    )
    keys_all, values_all = (
        lax.all_gather(keys_own, "ctx", axis=1, tiled=True),
        lax.all_gather(values_own, "ctx", axis=1, tiled=True),
    )
    query_blocks = jnp.transpose(queries, (0, 2, 1, 3, 4)).reshape(
        block_count, span_len, group_size, HEAD_DIM
    )
    key_blocks = jnp.transpose(
        keys_all.reshape(seq_dev, length_all, kv_local, HEAD_DIM), (0, 2, 1, 3)
    ).reshape(block_count, length_all, HEAD_DIM)
    value_blocks = jnp.transpose(
        values_all.reshape(seq_dev, length_all, kv_local, HEAD_DIM), (0, 2, 1, 3)
    ).reshape(block_count, length_all, HEAD_DIM)

    def scores_of(query_b, key_b):
        raw_scores = jnp.einsum("qgd,kd->gqk", query_b, key_b, preferred_element_type=jnp.float32)
        return jnp.where(causal[None], raw_scores * scale, -1e30)

    def attend(block_in):
        query_b, key_b, value_b = block_in
        scores = scores_of(query_b, key_b)
        peak_row = jnp.max(scores, axis=-1, keepdims=True)
        powers = jnp.exp(scores - peak_row)
        total_sum = jnp.sum(powers, axis=-1, keepdims=True)
        probability = (powers / total_sum).astype(jnp.bfloat16)
        mixed = jnp.einsum("gqk,kd->qgd", probability, value_b, preferred_element_type=jnp.float32)
        return (mixed.astype(jnp.bfloat16), peak_row + jnp.log(total_sum))

    mixed_blocks, logsum = lax.map(attend, (query_blocks, key_blocks, value_blocks))
    attended = jnp.transpose(
        mixed_blocks.reshape(seq_dev, kv_local, span_len, group_size, HEAD_DIM), (0, 2, 1, 3, 4)
    ).reshape(row_count, kv_local * group_size * HEAD_DIM)
    attn_part = jnp.dot(attended, full_o, preferred_element_type=jnp.float32)
    hidden = inputs_f + lax.psum(attn_part, "tensor")
    factor_two = rms_factor(hidden)
    normed_two = (hidden * factor_two * gain_two).astype(jnp.bfloat16)
    gate_pre = jnp.dot(normed_two, full_gate, preferred_element_type=jnp.float32)
    up_pre = jnp.dot(normed_two, full_up, preferred_element_type=jnp.float32)
    sigma = jax.nn.sigmoid(gate_pre)
    product = (gate_pre * sigma * up_pre).astype(jnp.bfloat16)
    ffn_part = jnp.dot(product, full_down, preferred_element_type=jnp.float32)
    out_f = hidden + lax.psum(ffn_part.astype(jnp.bfloat16), "tensor").astype(jnp.float32)
    layer_output = out_f.astype(jnp.bfloat16).reshape(seq_dev, span_len, model_width)
    grad_out = cotangent.reshape(row_count, model_width).astype(jnp.float32)
    grad_low = cotangent.reshape(row_count, model_width)
    down_grad = matmul_t(product, grad_low)
    prod_grad = matmul_nt(grad_low, full_down)
    gate_grad = (prod_grad * up_pre * sigma * (1.0 + gate_pre * (1.0 - sigma))).astype(jnp.bfloat16)
    up_grad = (prod_grad * gate_pre * sigma).astype(jnp.bfloat16)
    gate_w_grad = matmul_t(normed_two, gate_grad)
    up_w_grad = matmul_t(normed_two, up_grad)
    normed_two_part = matmul_nt(gate_grad, full_gate) + matmul_nt(up_grad, full_up)
    normed_two_grad = lax.psum(normed_two_part, "tensor")
    hidden_back, ffn_gain_term = rms_back(normed_two_grad, hidden, factor_two, gain_two)
    hidden_grad = grad_out + hidden_back
    hidden_low = hidden_grad.astype(jnp.bfloat16)
    out_w_grad = matmul_t(attended, hidden_low)
    attended_grad = matmul_nt(hidden_low, full_o).astype(jnp.bfloat16)
    upstream_blocks = jnp.transpose(
        attended_grad.reshape(seq_dev, span_len, kv_local, group_size, HEAD_DIM), (0, 2, 1, 3, 4)
    ).reshape(block_count, span_len, group_size, HEAD_DIM)

    def attend_back(block_in):
        query_b, key_b, value_b, logsum_b, upstream_b = block_in
        scores = scores_of(query_b, key_b)
        probability = jnp.exp(scores - logsum_b)
        rounded = probability.astype(jnp.bfloat16)
        value_grad = jnp.einsum(
            "gqk,qgd->kd", rounded, upstream_b, preferred_element_type=jnp.float32
        )
        prob_grad = jnp.einsum(
            "qgd,kd->gqk", upstream_b, value_b, preferred_element_type=jnp.float32
        )
        inner_sum = jnp.sum(probability * prob_grad, axis=-1, keepdims=True)
        score_grad = (probability * (prob_grad - inner_sum)).astype(jnp.bfloat16)
        query_grad = (
            jnp.einsum("gqk,kd->qgd", score_grad, key_b, preferred_element_type=jnp.float32) * scale
        )
        key_grad = (
            jnp.einsum("gqk,qgd->kd", score_grad, query_b, preferred_element_type=jnp.float32)
            * scale
        )
        return (query_grad, key_grad, value_grad)

    query_grads, key_grads, value_grads = lax.map(
        attend_back, (query_blocks, key_blocks, value_blocks, logsum, upstream_blocks)
    )
    key_rows = jnp.transpose(
        key_grads.reshape(seq_dev, kv_local, length_all, HEAD_DIM), (0, 2, 1, 3)
    ).reshape(seq_dev, length_all, kv_local * HEAD_DIM)
    value_rows = jnp.transpose(
        value_grads.reshape(seq_dev, kv_local, length_all, HEAD_DIM), (0, 2, 1, 3)
    ).reshape(seq_dev, length_all, kv_local * HEAD_DIM)
    key_mine, value_mine = (
        lax.psum_scatter(key_rows, "ctx", scatter_dimension=1, tiled=True),
        lax.psum_scatter(value_rows, "ctx", scatter_dimension=1, tiled=True),
    )
    key_low = (
        unrotate(
            key_mine.reshape(seq_dev, span_len, kv_local, HEAD_DIM),
            cosine[None, :, None, :],
            sine_val[None, :, None, :],
        )
        .astype(jnp.bfloat16)
        .reshape(row_count, kv_local * HEAD_DIM)
    )
    value_low = value_mine.astype(jnp.bfloat16).reshape(row_count, kv_local * HEAD_DIM)
    query_rot = jnp.transpose(
        query_grads.reshape(seq_dev, kv_local, span_len, group_size, HEAD_DIM), (0, 2, 1, 3, 4)
    )
    query_low = (
        unrotate(query_rot, cosine[None, :, None, None, :], sine_val[None, :, None, None, :])
        .astype(jnp.bfloat16)
        .reshape(row_count, kv_local * group_size * HEAD_DIM)
    )
    query_w_grad = matmul_t(normed_one, query_low)
    key_w_grad = matmul_t(normed_one, key_low)
    value_w_grad = matmul_t(normed_one, value_low)
    normed_one_part = (
        matmul_nt(query_low, full_q) + matmul_nt(key_low, full_k) + matmul_nt(value_low, full_v)
    )
    normed_one_grad = lax.psum(normed_one_part.astype(jnp.bfloat16), "tensor").astype(jnp.float32)
    input_back, attn_gain_term = rms_back(normed_one_grad, inputs_f, factor_one, gain_one)
    input_grad = (hidden_grad + input_back).reshape(seq_dev, span_len, model_width)
    (
        query_sum,
        key_sum,
        value_sum,
        out_sum,
        gate_sum,
        up_sum,
        down_sum,
        attn_gain_sum,
        ffn_gain_sum,
    ) = (
        lax.psum_scatter(query_w_grad, ("dp", "ctx"), scatter_dimension=0, tiled=True),
        lax.psum_scatter(key_w_grad, ("dp", "ctx"), scatter_dimension=0, tiled=True),
        lax.psum_scatter(value_w_grad, ("dp", "ctx"), scatter_dimension=0, tiled=True),
        lax.psum_scatter(out_w_grad, ("dp", "ctx"), scatter_dimension=1, tiled=True),
        lax.psum_scatter(gate_w_grad, ("dp", "ctx"), scatter_dimension=0, tiled=True),
        lax.psum_scatter(up_w_grad, ("dp", "ctx"), scatter_dimension=0, tiled=True),
        lax.psum_scatter(down_grad, ("dp", "ctx"), scatter_dimension=1, tiled=True),
        lax.psum_scatter(attn_gain_term, ("dp", "ctx"), scatter_dimension=0, tiled=True),
        lax.psum_scatter(ffn_gain_term, ("dp", "ctx"), scatter_dimension=0, tiled=True),
    )
    return (
        layer_output,
        input_grad,
        attn_gain_sum,
        query_sum,
        key_sum,
        value_sum,
        out_sum,
        ffn_gain_sum,
        gate_sum,
        up_sum,
        down_sum,
    )


MESH_ID = pl.DeviceIdType.MESH
BF16 = jnp.bfloat16
F32 = jnp.float32
QB = 256


def place():
    side = lax.axis_index("tensor")
    ctx = lax.axis_index("ctx")
    row = ctx // 2
    core = ctx % 2
    near_core = {"ctx": row * 2 + (1 - core)}
    near_side = {"tensor": 1 - side}
    near_row = {"ctx": (1 - row) * 2 + core}
    return side, row, core, near_core, near_side, near_row


def greet(neighbours):
    barrier = pltpu.get_barrier_semaphore()
    for target in neighbours:
        pl.semaphore_signal(barrier, inc=1, device_id=target, device_id_type=MESH_ID)
    pl.semaphore_wait(barrier, len(neighbours))


def remote(source, target, send_sem, recv_sem, device):
    return pltpu.make_async_remote_copy(
        src_ref=source,
        dst_ref=target,
        send_sem=send_sem,
        recv_sem=recv_sem,
        device_id=device,
        device_id_type=MESH_ID,
    )


def gather_kernel(rows, works, planes, block_ref, *refs):
    if works:
        left_ref, right_ref, all_ref, grad_ref, send_sems, recv_sems, local_sem = refs
    elif planes:
        gains_ref, all_ref, all_gains_ref, send_sems, recv_sems, local_sem, *gain_sems = refs
    else:
        all_ref, send_sems, recv_sems, local_sem = refs
    side, row, core, near_core, near_side, near_row = place()
    half = rows // 2

    def work(first, last):
        if not works:
            return
        size = left_ref.shape[1] // works

        def step(index, carry):
            at = pl.ds(pl.multiple_of(index * size, size), size)
            grad_ref[at, :] = matmul_t(left_ref[:, at], right_ref[...]).astype(BF16)
            return carry

        lax.fori_loop(first * works // 8, last * works // 8, step, 0)

    def spot(a, b, c, part=None):
        start = (a * 4 + b * 2 + c) * rows
        if part is None:
            return all_ref.at[pl.ds(pl.multiple_of(start, rows), rows)]
        return all_ref.at[pl.ds(pl.multiple_of(start + part * half, half), half)]

    targets = []
    if planes:
        plane = lax.axis_index("dp")
        here = row * 2 + core
        targets = [
            {"dp": (plane + step) % planes, "ctx": (here + turn) % 4}
            for step in range(planes)
            for turn in range(4)
            if step or turn
        ]
    greet([near_side] + (targets if planes else [near_core, near_row]))
    copies = []

    def send(number, source, target, device):
        copy = remote(source, target, send_sems.at[number], recv_sems.at[number], device)
        copy.start()
        copies.append(copy)
        return copy

    gain_copies = []
    if planes:
        mine = all_gains_ref.at[plane * 4 + here]
        gain_copies = [
            remote(gains_ref, mine, gain_sems[0].at[at], gain_sems[1].at[at], target)
            for at, target in enumerate(targets)
        ] + [pltpu.make_async_copy(gains_ref, mine, gain_sems[2])]
        for copy in gain_copies:
            copy.start()
    first = block_ref.at[pl.ds(0, half)]
    second = block_ref.at[pl.ds(half, half)]
    side_b = send(0, second, spot(side, row, core, 1), near_side)
    row_a = send(1, first, spot(side, row, core, 0), near_row)
    side_a = send(2, first, spot(side, row, core, 0), near_side)
    row_b = send(3, second, spot(side, row, core, 1), near_row)
    core_own = send(4, block_ref, spot(side, row, core), near_core)
    local = pltpu.make_async_copy(block_ref, spot(side, row, core), local_sem)
    local.start()
    work(0, 6)
    side_b.wait_recv()
    away_b = send(5, spot(1 - side, row, core, 1), spot(1 - side, row, core, 1), near_row)
    row_a.wait_recv()
    away_a = send(6, spot(side, 1 - row, core, 0), spot(side, 1 - row, core, 0), near_side)
    work(6, 8)
    side_a.wait_recv()
    core_side = send(7, spot(1 - side, row, core), spot(1 - side, row, core), near_core)
    row_b.wait_recv()
    core_row = send(8, spot(side, 1 - row, core), spot(side, 1 - row, core), near_core)
    away_a.wait_recv()
    core_away_a = send(
        9, spot(1 - side, 1 - row, core, 0), spot(1 - side, 1 - row, core, 0), near_core
    )
    away_b.wait_recv()
    core_away_b = send(
        10, spot(1 - side, 1 - row, core, 1), spot(1 - side, 1 - row, core, 1), near_core
    )
    for copy in (core_own, core_side, core_row, core_away_a, core_away_b):
        copy.wait_recv()
    for copy in copies:
        copy.wait_send()
    for copy in gain_copies:
        copy.wait()
    local.wait()


def plane_gather(block, number=0, pair=None, gains=None):
    rows, width = block.shape
    anywhere, vmem = pl.BlockSpec(memory_space=pl.ANY), pl.BlockSpec(memory_space=pltpu.VMEM)
    shapes, ins, outs = [jax.ShapeDtypeStruct((8 * rows, width), block.dtype)], [anywhere], [anywhere]
    operands = [block]
    if pair is not None:
        shapes.append(jax.ShapeDtypeStruct((pair[0].shape[1], pair[1].shape[1]), BF16))
        ins += [vmem, vmem]
        outs += [vmem]
        operands += pair
    planes, scratch = 0, []
    if gains is not None:
        planes = lax.axis_size("dp")
        shapes.append(jax.ShapeDtypeStruct((4 * planes,) + gains.shape, gains.dtype))
        ins += [vmem]
        outs += [vmem]
        operands += [gains]
        scratch = [pltpu.SemaphoreType.DMA((4 * planes - 1,))] * 2 + [pltpu.SemaphoreType.DMA]
    return pl.pallas_call(
        functools.partial(gather_kernel, rows, 8 if pair is not None else 0, planes),
        out_shape=tuple(shapes),
        in_specs=ins,
        out_specs=tuple(outs),
        scratch_shapes=[
            pltpu.SemaphoreType.DMA((11,)),
            pltpu.SemaphoreType.DMA((11,)),
            pltpu.SemaphoreType.DMA,
        ]
        + scratch,
        compiler_params=pltpu.CompilerParams(
            collective_id=number, has_side_effects=True, vmem_limit_bytes=60 * 1024 * 1024
        ),
        cost_estimate=pl.CostEstimate(flops=0, bytes_accessed=1024, transcendentals=0),
        name="plane_gather",
    )(*operands)


def swap_scratch():
    return [pltpu.SemaphoreType.DMA((3,))] * 2 + [pltpu.SemaphoreType.DMA]


def swap_copies(in_ref, out_ref, send_sems, recv_sems, local_sem):
    _, row, core, *_ = place()
    rows = out_ref.shape[1]
    here = row * 2 + core

    def block(index):
        return in_ref.at[pl.ds(pl.multiple_of(index * rows, rows), rows)]

    peers = (row * 2 + 1 - core, (1 - row) * 2 + core, (1 - row) * 2 + 1 - core)
    away = [
        remote(block(peer), out_ref.at[here], send_sems.at[at], recv_sems.at[at], {"ctx": peer})
        for at, peer in enumerate(peers)
    ]
    return away, pltpu.make_async_copy(block(here), out_ref.at[here], local_sem)


def scatter_steps(rows, left_of, right_of, out_ref, scratch, swap=None, late=None):
    made, other, to_side, to_row, from_side, from_row = scratch[:6]
    on_side, on_row, got_side, got_row, send_sems, recv_sems = scratch[6:]
    side, row, core, near_core, near_side, near_row = place()
    tile = 32
    wide = out_ref.shape[1] // 2

    chips = ((side, row), (1 - side, row), (side, 1 - row), (1 - side, 1 - row))
    routes = [
        (made.at[chip, part, 1 - core], other.at[chip, part], near_core)
        for chip in range(4)
        for part in range(2)
    ] + [
        (to_side.at[0], from_side.at[0], near_side),
        (to_row.at[0], from_row.at[0], near_row),
        (to_side.at[1], from_side.at[1], near_side),
        (to_row.at[1], from_row.at[1], near_row),
        (on_row, got_row, near_row),
        (on_side, got_side, near_side),
    ]
    copies = [
        remote(source, target, send_sems.at[at], recv_sems.at[at], device)
        for at, (source, target, device) in enumerate(routes)
    ]
    side_0, row_0, side_1, row_1, last_row, last_side = copies[8:]
    swapped = None if swap is None else swap_copies(*swap)

    def make(chip, part, first=False):
        a, b = chips[chip]
        start = pl.multiple_of((a * 4 + b * 2) * rows, 2 * rows)
        value = matmul_nt(left_of(chip, start), right_of(pl.ds(part * wide, wide)))
        made[chip, part, 0] = value[:rows].astype(BF16)
        made[chip, part, 1] = value[rows:].astype(BF16)
        if first:
            partners = (near_core, near_side, near_row)
            if swap is not None:
                partners += ({"ctx": (1 - row) * 2 + 1 - core},)
            greet(partners)
        copies[2 * chip + part].start()

    def both(chip, part, at):
        here = made[chip, part, core, pl.ds(at, tile), :].astype(F32)
        return here + other[chip, part, pl.ds(at, tile), :].astype(F32)

    def each(body):
        def step(index, carry):
            body(pl.multiple_of(index * tile, tile))
            return carry

        lax.fori_loop(0, rows // tile, step, 0)

    def put(target, chip, part, copy, extra=None):
        copies[2 * chip + part].wait_recv()

        def body(at):
            value = both(chip, part, at)
            if extra is not None:
                value = value + extra[pl.ds(at, tile), :].astype(F32)
            target[pl.ds(at, tile), :] = value.astype(BF16)

        each(body)
        copy.start()

    def across():
        make(3, 0, True)
        make(3, 1)
        put(to_side.at[0], 3, 0, side_0)
        put(to_row.at[0], 3, 1, row_0)
        if swap is not None:
            for copy in swapped[0] + [swapped[1]]:
                copy.start()

    def along():
        make(1, 0)
        make(2, 1)
        put(to_side.at[1], 1, 0, side_1)
        put(to_row.at[1], 2, 1, row_1)

    def forward():
        make(1, 1)
        make(2, 0)
        row_0.wait_recv()
        put(on_side, 1, 1, last_side, from_row.at[0])
        side_0.wait_recv()
        put(on_row, 2, 0, last_row, from_side.at[0])

    def own():
        make(0, 0)
        make(0, 1)

    def finish():
        copies[0].wait_recv()
        copies[1].wait_recv()
        side_1.wait_recv()
        row_1.wait_recv()

        def first_sum(at):
            here = pl.ds(at, tile)
            out_ref[here, :wide] = both(0, 0, at) + from_side[1, here, :].astype(F32)
            out_ref[here, wide:] = both(0, 1, at) + from_row[1, here, :].astype(F32)

        each(first_sum)
        if swap is not None:
            for copy in swapped[0]:
                copy.wait()
            swapped[1].wait()
            late()
        last_side.wait_recv()
        last_row.wait_recv()

        def last_sum(at):
            here = pl.ds(at, tile)
            out_ref[here, :wide] += got_row[here, :].astype(F32)
            out_ref[here, wide:] += got_side[here, :].astype(F32)

        each(last_sum)
        for copy in copies:
            copy.wait_send()

    return across, along, forward, own, finish


def scatter_scratch(rows, width):
    half = width // 2
    return (
        [pltpu.VMEM((4, 2, 2, rows, half), BF16), pltpu.VMEM((4, 2, rows, half), BF16)]
        + [pltpu.VMEM((2, rows, half), BF16)] * 4
        + [pltpu.VMEM((rows, half), BF16)] * 4
        + [pltpu.SemaphoreType.DMA((14,))] * 2
    )


def scatter_kernel(rows, swaps, columns, left, right, *refs):
    swap, late = None, None
    if swaps:
        in_ref, out_ref, laid_ref, *scratch = refs
        swapped = scratch[-4]
        swap = (in_ref, swapped, *scratch[-3:])
        scratch = scratch[:-4]

        def late():
            size = swapped.shape[2]
            for part in range(4):
                laid_ref[:, part * size : (part + 1) * size] = swapped[part]

    else:
        out_ref, *scratch = refs

    def left_of(chip, start):
        return left[pl.ds(start, 2 * rows), :]

    def right_of(at):
        return right[at, columns]

    for step in scatter_steps(rows, left_of, right_of, out_ref, scratch, swap=swap, late=late):
        step()


def product_scatter(number, left, right, start, size, swap=None):
    total = left.shape[0]
    width = right.shape[0]
    rows = total // 8
    vmem = pl.BlockSpec(memory_space=pltpu.VMEM)
    shapes, ins, scratch = [jax.ShapeDtypeStruct((rows, width), F32)], [vmem, vmem], []
    operands = [left, right]
    if swap is not None:
        deep = swap.shape[0] // 4
        shapes.append(jax.ShapeDtypeStruct((deep, 4 * swap.shape[1]), swap.dtype))
        ins.append(pl.BlockSpec(memory_space=pl.ANY))
        operands.append(swap)
        scratch = [pltpu.VMEM((4, deep, swap.shape[1]), swap.dtype)] + swap_scratch()
    return pl.pallas_call(
        functools.partial(scatter_kernel, rows, swap is not None, slice(start, start + size)),
        out_shape=tuple(shapes),
        in_specs=ins,
        out_specs=tuple([vmem] * len(shapes)),
        scratch_shapes=scatter_scratch(rows, width) + scratch,
        compiler_params=pltpu.CompilerParams(
            collective_id=number, has_side_effects=True, vmem_limit_bytes=56 * 1024 * 1024
        ),
        cost_estimate=pl.CostEstimate(flops=0, bytes_accessed=1024, transcendentals=0),
        name="product_scatter",
    )(*operands)


def ffn_back_kernel(
    rows,
    own_ref,
    far_ref,
    twin_ref,
    twin_far_ref,
    gate_slope_ref,
    up_slope_ref,
    down_ref,
    right_ref,
    out_ref,
    gate_ref,
    up_ref,
    cots,
    gate_slopes,
    up_slopes,
    lefts,
    sems,
    out_sems,
    *scratch,
):
    side, row, core, *_ = place()
    units = down_ref.shape[1]
    turns = (3, 1, 2, 0)
    chips = ((side, row), (1 - side, row), (side, 1 - row), (1 - side, 1 - row))
    starts = [pl.multiple_of((a * 4 + b * 2) * rows, 2 * rows) for a, b in chips]
    stored = []

    def fetch(turn):
        chip = turns[turn]
        near, away = (own_ref, twin_ref) if chip < 2 else (far_ref, twin_far_ref)
        there = pl.ds(starts[chip], 2 * rows)
        slot = turn % 2
        return [
            pltpu.make_async_copy(source, target, sems.at[which, slot])
            for which, (source, target) in enumerate(
                (
                    (near.at[chips[chip][0]], cots.at[slot, core]),
                    (away.at[chips[chip][0]], cots.at[slot, 1 - core]),
                    (gate_slope_ref.at[there], gate_slopes.at[slot]),
                    (up_slope_ref.at[there], up_slopes.at[slot]),
                )
            )
        ]

    def store(turn):
        there = pl.ds(starts[turns[turn]], 2 * rows)
        slot = turn % 2
        return [
            pltpu.make_async_copy(
                lefts.at[slot, :, pl.ds(which * units, units)],
                target.at[there],
                out_sems.at[which, slot],
            )
            for which, target in enumerate((gate_ref, up_ref))
        ]

    def start(copies):
        for copy in copies:
            copy.start()

    def wait(copies):
        for copy in copies:
            copy.wait()

    def left_of(chip, _):
        turn = turns.index(chip)
        slot = turn % 2
        if chip in stored:
            return lefts[slot]
        stored.append(chip)
        if turn == 0:
            start(fetch(0))
        if turn == 1:
            start(fetch(2))
        if turn == 2:
            start(fetch(3))
        if turn == 0:
            start(fetch(1))
        wait(fetch(turn))
        if turn > 1:
            wait(store(turn - 2))
        cot = cots[slot].reshape(2 * rows, cots.shape[3])
        grad = jnp.dot(cot, down_ref[...], preferred_element_type=F32)
        lefts[slot, :, :units] = (grad * gate_slopes[slot].astype(F32)).astype(BF16)
        lefts[slot, :, units:] = (grad * up_slopes[slot].astype(F32)).astype(BF16)
        start(store(turn))
        return lefts[slot]

    def right_of(at):
        return right_ref[at, :]

    for step in scatter_steps(rows, left_of, right_of, out_ref, scratch):
        step()
    wait(store(2))
    wait(store(3))


def ffn_back(number, cots, gate_slope, up_slope, down_w, gate_up):
    total, units = gate_slope.shape
    width = down_w.shape[0]
    rows = total // 8
    vmem = pl.BlockSpec(memory_space=pltpu.VMEM)
    anywhere = pl.BlockSpec(memory_space=pl.ANY)
    return pl.pallas_call(
        functools.partial(ffn_back_kernel, rows),
        out_shape=(
            jax.ShapeDtypeStruct((rows, width), F32),
            jax.ShapeDtypeStruct((total, units), BF16),
            jax.ShapeDtypeStruct((total, units), BF16),
        ),
        in_specs=[anywhere] * 6 + [vmem, vmem],
        out_specs=(vmem, anywhere, anywhere),
        scratch_shapes=[
            pltpu.VMEM((2, 2, rows, width), BF16),
            pltpu.VMEM((2, 2 * rows, units), BF16),
            pltpu.VMEM((2, 2 * rows, units), BF16),
            pltpu.VMEM((2, 2 * rows, 2 * units), BF16),
            pltpu.SemaphoreType.DMA((4, 2)),
            pltpu.SemaphoreType.DMA((2, 2)),
        ]
        + scatter_scratch(rows, width),
        compiler_params=pltpu.CompilerParams(
            collective_id=number, has_side_effects=True, vmem_limit_bytes=60 * 1024 * 1024
        ),
        cost_estimate=pl.CostEstimate(flops=0, bytes_accessed=1024, transcendentals=0),
        name="ffn_back",
    )(*cots, gate_slope, up_slope, down_w, gate_up)


def ffn_kernel(in_ref, w_ref, product_ref, gate_slope_ref, up_slope_ref):
    units = product_ref.shape[1]
    wide = 512
    rows_in = in_ref[...]
    for start in range(0, units, wide):
        at = pl.ds(start, wide)
        gate = jnp.dot(rows_in, w_ref[:, at], preferred_element_type=F32)
        up = jnp.dot(rows_in, w_ref[:, pl.ds(units + start, wide)], preferred_element_type=F32)
        sigma = jax.nn.sigmoid(gate)
        active = gate * sigma
        product_ref[:, at] = (active * up).astype(BF16)
        gate_slope_ref[:, at] = (up * sigma * (1.0 + gate * (1.0 - sigma))).astype(BF16)
        up_slope_ref[:, at] = active.astype(BF16)


def ffn(rows_in, gate_up):
    total, width = rows_in.shape
    units = gate_up.shape[1] // 2
    rows = 512
    out = pl.BlockSpec((rows, units), lambda i: (i, 0))
    return pl.pallas_call(
        ffn_kernel,
        grid=(total // rows,),
        out_shape=(jax.ShapeDtypeStruct((total, units), BF16),) * 3,
        in_specs=[
            pl.BlockSpec((rows, width), lambda i: (i, 0)),
            pl.BlockSpec(
                (width, 2 * units), lambda i: (0, 0), pipeline_mode=pl.Buffered(1)
            ),
        ],
        out_specs=(out, out, out),
        compiler_params=pltpu.CompilerParams(vmem_limit_bytes=60 * 1024 * 1024),
        cost_estimate=pl.CostEstimate(flops=0, bytes_accessed=1024, transcendentals=0),
        name="ffn",
    )(rows_in, gate_up)


def swap_halves(values):
    width = values.shape[-1]
    lane = lax.broadcasted_iota(jnp.int32, values.shape, 1)
    ahead = pltpu.roll(values, width - HEAD_DIM // 2, 1)
    behind = pltpu.roll(values, HEAD_DIM // 2, 1)
    return jnp.where(lane % HEAD_DIM < HEAD_DIM // 2, ahead, behind)


def pieces_of(block):
    return ((0, block * QB, False), (block * QB, QB, True)) if block else ((0, QB, True),)


def masked_scores(query, keys, diagonal):
    scores = matmul_nt(query, keys)
    if diagonal:
        here = lax.broadcasted_iota(jnp.int32, scores.shape, 0)
        there = lax.broadcasted_iota(jnp.int32, scores.shape, 1)
        scores = jnp.where(here >= there, scores, -1e30)
    return scores


def attend_kernel(length, q_ref, kv_ref, cos_ref, sin_ref, att_ref, qrot_ref, kvrot_ref, log_ref):
    cosine = cos_ref[...]
    signed = sin_ref[...]
    scale = HEAD_DIM ** (-0.5)
    pre = q_ref[...]
    qrot_ref[...] = (pre * cosine + swap_halves(pre) * signed).astype(BF16)
    pre = kv_ref[...]
    lane = lax.broadcasted_iota(jnp.int32, pre.shape, 1)
    turned = jnp.where(lane < HEAD_DIM, pre * cosine + swap_halves(pre) * signed, pre)
    kvrot_ref[...] = turned.astype(BF16)
    for block in range(length // QB):
        here = pl.ds(block * QB, QB)
        logs = []
        mixed = []
        for head in range(2):
            query = qrot_ref[here, head * HEAD_DIM : (head + 1) * HEAD_DIM] * jnp.asarray(
                scale, BF16
            )
            scores = []
            for start, size, diagonal in pieces_of(block):
                keys = kvrot_ref[pl.ds(start, size), :HEAD_DIM]
                scores.append(masked_scores(query, keys, diagonal))
            peak = functools.reduce(
                jnp.maximum, [jnp.max(s, axis=1, keepdims=True) for s in scores]
            )
            powers = [jnp.exp(s - peak) for s in scores]
            total = sum(jnp.sum(p, axis=1, keepdims=True) for p in powers)
            inverse = 1.0 / total
            out = None
            for (start, size, _), power in zip(pieces_of(block), powers):
                values = kvrot_ref[pl.ds(start, size), HEAD_DIM:]
                term = jnp.dot(
                    (power * inverse).astype(BF16), values, preferred_element_type=F32
                )
                out = term if out is None else out + term
            mixed.append(out)
            logs.append(peak + jnp.log(total))
        att_ref[here, :] = jnp.concatenate(mixed, axis=1).astype(BF16)
        lane = lax.broadcasted_iota(jnp.int32, (QB, 128), 1)
        log_ref[here, :] = jnp.where(lane < HEAD_DIM, logs[0], logs[1])


def attend(pre, cosine, signed, seqs):
    rows = pre.shape[0]
    length = rows // seqs
    pairs = pre.shape[1] // 128 - 1
    block = (length, 128)
    return pl.pallas_call(
        functools.partial(attend_kernel, length),
        grid=(seqs, pairs),
        out_shape=(
            jax.ShapeDtypeStruct((rows, pairs * 128), BF16),
            jax.ShapeDtypeStruct((rows, pairs * 128), BF16),
            jax.ShapeDtypeStruct((rows, 128), BF16),
            jax.ShapeDtypeStruct((rows, pairs * 128), F32),
        ),
        in_specs=[
            pl.BlockSpec(block, lambda s, h: (s, h)),
            pl.BlockSpec(block, lambda s, h: (s, pairs)),
            pl.BlockSpec(block, lambda s, h: (0, 0)),
            pl.BlockSpec(block, lambda s, h: (0, 0)),
        ],
        out_specs=(
            pl.BlockSpec(block, lambda s, h: (s, h)),
            pl.BlockSpec(block, lambda s, h: (s, h)),
            pl.BlockSpec(block, lambda s, h: (s, 0)),
            pl.BlockSpec(block, lambda s, h: (s, h)),
        ),
        compiler_params=pltpu.CompilerParams(vmem_limit_bytes=48 * 1024 * 1024),
        cost_estimate=pl.CostEstimate(
            flops=8 * rows * length * 128 * pairs,
            bytes_accessed=rows * pairs * 128 * 12,
            transcendentals=rows * length * 2 * pairs,
        ),
        name="attend",
    )(pre, pre, cosine, signed)


def attend_back_kernel(
    seqs,
    rows,
    q_ref,
    kv_ref,
    up_ref,
    log_ref,
    cos_ref,
    sin_ref,
    left_ref,
    right_ref,
    hidden_ref,
    in_ref,
    back_ref,
    out_ref,
    laid_ref,
    sum_ref,
    ffn_ref,
    swapped,
    *scratch,
):
    def late():
        size = swapped.shape[2]
        for part in range(4):
            turned = jnp.transpose(swapped[part].astype(F32))
            laid_ref[part * size : (part + 1) * size, :] = turned.astype(BF16)

    across, along, forward, own, finish = scatter_steps(
        rows,
        lambda chip, start: left_ref[pl.ds(start, 2 * rows), :],
        lambda at: right_ref[at, :],
        ffn_ref,
        scratch[:-3],
        swap=(in_ref, swapped, *scratch[-3:]),
        late=late,
    )
    scale = HEAD_DIM ** (-0.5)
    length = q_ref.shape[0] // seqs
    pairs = q_ref.shape[1] // 128
    across()
    along()

    def one_pair(index, carry):
        seq = index // pairs
        pair = index % pairs
        lanes_at = pl.ds(pl.multiple_of(pair * 128, 128), 128)
        base = pl.multiple_of(seq * length, length)

        @pl.when(index == 1)
        def _():
            forward()

        @pl.when(index == 2)
        def _():
            own()

        @pl.when(pair == 0)
        def _():
            sum_ref[...] = jnp.zeros_like(sum_ref)

        for block in range(length // QB):
            here = pl.ds(base + block * QB, QB)
            turned = []
            q_pair = q_ref[here, lanes_at]
            up_pair = up_ref[here, lanes_at]
            log_pair = log_ref[here, lanes_at]
            for head in range(2):
                lanes = slice(head * HEAD_DIM, (head + 1) * HEAD_DIM)
                query = q_pair[:, lanes] * jnp.asarray(scale, BF16)
                upstream = up_pair[:, lanes]
                logs = log_pair[:, head * HEAD_DIM : head * HEAD_DIM + 1]
                saved = []
                inner = None
                for start, size, diagonal in pieces_of(block):
                    keys = kv_ref[pl.ds(base + start, size), :HEAD_DIM]
                    values = kv_ref[pl.ds(base + start, size), HEAD_DIM:]
                    probability = jnp.exp(masked_scores(query, keys, diagonal) - logs)
                    prob_grad = matmul_nt(upstream, values)
                    term = jnp.sum(probability * prob_grad, axis=1, keepdims=True)
                    inner = term if inner is None else inner + term
                    saved.append((start, size, probability, prob_grad))
                out = None
                for start, size, probability, prob_grad in saved:
                    keys = kv_ref[pl.ds(base + start, size), :HEAD_DIM]
                    score_grad = (probability * (prob_grad - inner)).astype(BF16)
                    rounded = probability.astype(BF16)
                    term = jnp.dot(score_grad, keys, preferred_element_type=F32)
                    out = term if out is None else out + term
                    sum_ref[pl.ds(start, size), :] += jnp.concatenate(
                        [matmul_t(score_grad, query), matmul_t(rounded, upstream)], axis=1
                    )
                turned.append(out * scale)
            grad = jnp.concatenate(turned, axis=1)
            angle = pl.ds(block * QB, QB)
            back_ref[here, lanes_at] = (
                grad * cos_ref[angle, :] - swap_halves(grad) * sin_ref[angle, :]
            ).astype(BF16)

        @pl.when(pair == pairs - 1)
        def _():
            grad = sum_ref[...]
            lane = lax.broadcasted_iota(jnp.int32, grad.shape, 1)
            back = grad * cos_ref[...] - swap_halves(grad) * sin_ref[...]
            back_ref[pl.ds(base, length), pairs * 128 :] = jnp.where(
                lane < HEAD_DIM, back, grad
            ).astype(BF16)

        return carry

    lax.fori_loop(0, seqs * pairs, one_pair, 0)
    finish()

    def add(index, carry):
        at = pl.ds(pl.multiple_of(index * 32, 32), 32)
        out_ref[at, :] = (hidden_ref[at, :] + ffn_ref[at, :]).astype(BF16)
        return carry

    lax.fori_loop(0, rows // 32, add, 0)


def attend_back(
    number, queries, keyvals, upstream, logs, cosine, signed, seqs, left, right, hidden, swap
):
    total, width = queries.shape
    length = total // seqs
    rows = total // 8
    deep = swap.shape[0] // 4
    vmem = pl.BlockSpec(memory_space=pltpu.VMEM)
    return pl.pallas_call(
        functools.partial(attend_back_kernel, seqs, rows),
        out_shape=(
            jax.ShapeDtypeStruct((total, width + 128), BF16),
            jax.ShapeDtypeStruct(hidden.shape, BF16),
            jax.ShapeDtypeStruct((4 * swap.shape[1], deep), BF16),
        ),
        in_specs=[vmem] * 9 + [pl.BlockSpec(memory_space=pl.ANY)],
        out_specs=(vmem, vmem, vmem),
        scratch_shapes=[
            pltpu.VMEM((length, 128), F32),
            pltpu.VMEM(hidden.shape, F32),
            pltpu.VMEM((4, deep, swap.shape[1]), BF16),
        ]
        + scatter_scratch(rows, right.shape[0])
        + swap_scratch(),
        compiler_params=pltpu.CompilerParams(
            collective_id=number, has_side_effects=True, vmem_limit_bytes=56 * 1024 * 1024
        ),
        cost_estimate=pl.CostEstimate(flops=0, bytes_accessed=1024, transcendentals=0),
        name="attend_back",
    )(queries, keyvals, upstream, logs, cosine, signed, left, right, hidden, swap)


def gain_kernel(
    planes,
    parts,
    cols,
    terms_ref,
    up_ref,
    gain_ref,
    laid_ref,
    total,
    seen,
    far,
    mine,
    across,
    swapped,
    send_sems,
    recv_sems,
    *swap_sems,
):
    side, row, core, near_core, near_side, near_row = place()
    plane = lax.axis_index("dp")
    ctx = row * 2 + core
    others = [{"dp": (plane + step) % planes} for step in range(1, planes)]
    corner = {"ctx": (1 - row) * 2 + 1 - core}
    greet((near_core, near_side, near_row, corner) + tuple(others))
    total[...] = terms_ref[...]
    copies = []
    up_copies, up_local = swap_copies(up_ref, swapped, *swap_sems)
    for number, target in enumerate((near_core, near_row)):
        copy = remote(
            total, seen.at[number], send_sems.at[number], recv_sems.at[number], target
        )
        copy.start()
        copy.wait()
        total[...] += seen[number]
    for copy in up_copies + [up_local]:
        copy.start()
    for step, target in enumerate(others, 1):
        start = (((plane + step) % planes) * parts + ctx) * cols
        copy = remote(
            total.at[:, pl.ds(pl.multiple_of(start, cols), cols)],
            far.at[step - 1],
            send_sems.at[2 + step],
            recv_sems.at[2 + step],
            target,
        )
        copy.start()
        copies.append(copy)
    start = (plane * parts + ctx) * cols
    value = total[:, pl.ds(pl.multiple_of(start, cols), cols)]
    for number, copy in enumerate(copies):
        copy.wait_recv()
        value += far[number]
    mine[...] = value
    last = remote(mine, across, send_sems.at[2], recv_sems.at[2], near_side)
    last.start()
    copies.append(last)
    for copy in up_copies:
        copy.wait()
    up_local.wait()
    size = swapped.shape[2]
    for part in range(4):
        laid_ref[:, part * size : (part + 1) * size] = swapped[part]
    last.wait_recv()
    gain_ref[...] = value + across[...]
    for copy in copies:
        copy.wait_send()


def gain_sum(number, terms, up_sum):
    planes = lax.axis_size("dp")
    parts = lax.axis_size("ctx")
    rows, width = terms.shape
    cols = width // (planes * parts)
    deep = up_sum.shape[0] // parts
    vmem = pl.BlockSpec(memory_space=pltpu.VMEM)
    anywhere = pl.BlockSpec(memory_space=pl.ANY)
    return pl.pallas_call(
        functools.partial(gain_kernel, planes, parts, cols),
        out_shape=(
            jax.ShapeDtypeStruct((rows, cols), F32),
            jax.ShapeDtypeStruct((deep, parts * up_sum.shape[1]), BF16),
        ),
        in_specs=[vmem, anywhere],
        out_specs=(vmem,) * 2,
        scratch_shapes=[
            pltpu.VMEM((rows, width), F32),
            pltpu.VMEM((2, rows, width), F32),
            pltpu.VMEM((planes - 1, rows, cols), F32),
            pltpu.VMEM((rows, cols), F32),
            pltpu.VMEM((rows, cols), F32),
            pltpu.VMEM((parts, deep, up_sum.shape[1]), BF16),
            pltpu.SemaphoreType.DMA((planes + 2,)),
            pltpu.SemaphoreType.DMA((planes + 2,)),
        ]
        + swap_scratch(),
        compiler_params=pltpu.CompilerParams(collective_id=number, has_side_effects=True),
        cost_estimate=pl.CostEstimate(flops=0, bytes_accessed=1024, transcendentals=0),
        name="gain_sum",
    )(terms, up_sum)


def last_kernel(
    q_cols, attn_ref, query_ref, key_ref, value_ref, wide_ref, swapped, *swap_sems
):
    _, row, core, near_core, _, near_row = place()
    greet((near_core, near_row, {"ctx": (1 - row) * 2 + 1 - core}))
    copies, local = swap_copies(attn_ref, swapped, *swap_sems)
    for copy in copies + [local]:
        copy.start()
    for copy in copies:
        copy.wait()
    local.wait()
    kv = key_ref.shape[1] // 4
    for part in range(4):
        query_ref[:, part * q_cols : (part + 1) * q_cols] = swapped[part, :, :q_cols]
        turned = jnp.transpose(swapped[part, :, q_cols + 2 * kv :].astype(F32))
        wide_ref[part * q_cols : (part + 1) * q_cols, :] = turned.astype(BF16)
    for at, target in ((q_cols, key_ref), (q_cols + kv, value_ref)):
        target[...] = jnp.concatenate(
            [swapped[part, :, at : at + kv] for part in range(4)], axis=1
        )


def last_swap(number, attn_sum, q_cols, kv_cols):
    parts = lax.axis_size("ctx")
    deep = attn_sum.shape[0] // parts
    vmem = pl.BlockSpec(memory_space=pltpu.VMEM)
    return pl.pallas_call(
        functools.partial(last_kernel, q_cols),
        out_shape=(
            jax.ShapeDtypeStruct((deep, parts * q_cols), BF16),
            jax.ShapeDtypeStruct((deep, parts * kv_cols), BF16),
            jax.ShapeDtypeStruct((deep, parts * kv_cols), BF16),
            jax.ShapeDtypeStruct((parts * q_cols, deep), BF16),
        ),
        in_specs=[pl.BlockSpec(memory_space=pl.ANY)],
        out_specs=(vmem,) * 4,
        scratch_shapes=[pltpu.VMEM((parts, deep, attn_sum.shape[1]), BF16)] + swap_scratch(),
        compiler_params=pltpu.CompilerParams(collective_id=number, has_side_effects=True),
        cost_estimate=pl.CostEstimate(flops=0, bytes_accessed=1024, transcendentals=0),
        name="last_swap",
    )(attn_sum)


def lay_kernel(own_ref, far_ref, twin_ref, twin_far_ref, all_ref, sems):
    ctx = lax.axis_index("ctx")
    row, core = ctx // 2, ctx % 2
    span = own_ref.shape[1]
    copies = []
    for number, (part, a, b) in enumerate(
        (
            (own_ref, row, core),
            (twin_ref, row, 1 - core),
            (far_ref, 1 - row, core),
            (twin_far_ref, 1 - row, 1 - core),
        )
    ):
        start = pl.multiple_of((a * 2 + b) * span, span)
        copies.append(
            pltpu.make_async_copy(part, all_ref.at[:, pl.ds(start, span)], sems.at[number])
        )
        copies[-1].start()
    for copy in copies:
        copy.wait()


def along_ctx(block, earlier, later):
    seqs, span, width = block.shape
    cores = [(0, 1), (1, 0), (2, 3), (3, 2)]
    far = lax.ppermute(after(block, earlier), "ctx", [(0, 2), (1, 3), (2, 0), (3, 1)])
    far = after(far, later)
    twin, twin_far = lax.ppermute(block, "ctx", cores), lax.ppermute(far, "ctx", cores)
    whole = pl.pallas_call(
        lay_kernel,
        out_shape=jax.ShapeDtypeStruct((seqs, 4 * span, width), block.dtype),
        in_specs=[pl.BlockSpec(memory_space=pl.ANY)] * 4,
        out_specs=pl.BlockSpec(memory_space=pltpu.VMEM),
        scratch_shapes=[pltpu.SemaphoreType.DMA((4,))],
        compiler_params=pltpu.CompilerParams(vmem_limit_bytes=24 * 1024 * 1024),
        name="lay",
    )(block, far, twin, twin_far)
    return whole.reshape(seqs * 4 * span, width), (block, far, twin, twin_far)


def deal_kernel(q_ref, kv_ref, out_ref, all_ref, send_sems, recv_sems, local_sems):
    _, row, core, *_ = place()
    here = row * 2 + core
    peers = (row * 2 + 1 - core, (1 - row) * 2 + core, (1 - row) * 2 + 1 - core)
    greet([{"ctx": peer} for peer in peers])
    copies = []
    start = 0
    for which, source in enumerate((q_ref, kv_ref, out_ref)):
        cols = source.shape[1] // 4
        target = all_ref.at[here, :, pl.ds(start, cols)]
        start += cols
        for at, peer in enumerate(peers):
            copies.append(
                remote(
                    source.at[:, pl.ds(pl.multiple_of(peer * cols, cols), cols)],
                    target,
                    send_sems.at[which, at],
                    recv_sems.at[which, at],
                    {"ctx": peer},
                )
            )
        own = source.at[:, pl.ds(pl.multiple_of(here * cols, cols), cols)]
        copies.append(pltpu.make_async_copy(own, target, local_sems.at[which]))
    for copy in copies:
        copy.start()
    for copy in copies:
        copy.wait()


def deal(query, keyval, out):
    rows = query.shape[0]
    cols = (query.shape[1] + keyval.shape[1] + out.shape[1]) // 4
    return pl.pallas_call(
        deal_kernel,
        out_shape=jax.ShapeDtypeStruct((4, rows, cols), BF16),
        in_specs=[pl.BlockSpec(memory_space=pl.ANY)] * 3,
        out_specs=pl.BlockSpec(memory_space=pltpu.VMEM),
        scratch_shapes=[
            pltpu.SemaphoreType.DMA((3, 3)),
            pltpu.SemaphoreType.DMA((3, 3)),
            pltpu.SemaphoreType.DMA((3,)),
        ],
        compiler_params=pltpu.CompilerParams(collective_id=6, has_side_effects=True),
        cost_estimate=pl.CostEstimate(flops=0, bytes_accessed=1024, transcendentals=0),
        name="deal",
    )(query, keyval, out)


def share_kernel(gate_ref, up_ref, all_ref, send_sems, recv_sems, local_sems):
    _, row, core, *_ = place()
    here = row * 2 + core
    rows, units = gate_ref.shape[0], all_ref.shape[1] // 2
    peers = (row * 2 + 1 - core, (1 - row) * 2 + core, (1 - row) * 2 + 1 - core)
    greet([{"ctx": peer} for peer in peers])
    copies = []
    for which, source in enumerate((gate_ref, up_ref)):
        target = all_ref.at[
            pl.ds(pl.multiple_of(here * rows, rows), rows), pl.ds(which * units, units)
        ]
        for at, peer in enumerate(peers):
            copies.append(
                remote(
                    source.at[:, pl.ds(pl.multiple_of(peer * units, units), units)],
                    target,
                    send_sems.at[which, at],
                    recv_sems.at[which, at],
                    {"ctx": peer},
                )
            )
        own = source.at[:, pl.ds(pl.multiple_of(here * units, units), units)]
        copies.append(pltpu.make_async_copy(own, target, local_sems.at[which]))
    for copy in copies:
        copy.start()
    for copy in copies:
        copy.wait()


def share(gate, up):
    parts = lax.axis_size("ctx")
    anywhere = pl.BlockSpec(memory_space=pl.ANY)
    return pl.pallas_call(
        share_kernel,
        out_shape=jax.ShapeDtypeStruct((parts * gate.shape[0], 2 * gate.shape[1] // parts), BF16),
        in_specs=[anywhere, anywhere],
        out_specs=anywhere,
        scratch_shapes=[
            pltpu.SemaphoreType.DMA((2, 3)),
            pltpu.SemaphoreType.DMA((2, 3)),
            pltpu.SemaphoreType.DMA((2,)),
        ],
        compiler_params=pltpu.CompilerParams(
            collective_id=8, has_side_effects=True, vmem_limit_bytes=60 * 1024 * 1024
        ),
        cost_estimate=pl.CostEstimate(flops=0, bytes_accessed=1024, transcendentals=0),
        name="share",
    )(gate, up)


def after(value, *earlier):
    return lax.optimization_barrier((value,) + earlier)[0]


def to_units(weight):
    return lax.all_to_all(weight, "ctx", split_axis=1, concat_axis=0, tiled=True)


def swap_sides(block):
    return lax.ppermute(block, "tensor", [(0, 1), (1, 0)])


def on_plane(
    layer_input,
    attn_gain,
    w_query,
    w_key,
    w_value,
    w_out,
    ffn_gain,
    w_gate,
    w_up,
    w_down,
    cotangent,
):
    seqs, span, width = layer_input.shape
    planes = lax.axis_size("dp")
    parts = lax.axis_size("ctx")
    side = lax.axis_index("tensor")
    length = span * parts
    rows_w = w_query.shape[0]
    q_cols = w_query.shape[1] // parts
    kv_cols = w_key.shape[1] // parts

    theta = angles(jnp.arange(length), HEAD_DIM)
    cosine = jnp.tile(jnp.cos(theta), (1, 4))
    sine = jnp.sin(theta)
    signed = jnp.tile(jnp.concatenate([-sine, sine], axis=1), (1, 2))

    keyval = jnp.concatenate(
        [w_key.reshape(rows_w, parts, kv_cols), w_value.reshape(rows_w, parts, kv_cols)], axis=2
    ).reshape(rows_w, -1)
    mixed = deal(w_query, keyval, w_out.T)
    ready_w = mixed
    attn_w = lax.all_gather(mixed.reshape(parts * rows_w, -1), "dp", axis=0, tiled=True)
    qkv_cols = q_cols + 2 * kv_cols
    w_qkv = attn_w[:, :qkv_cols]
    w_out_t = attn_w[:, qkv_cols:]

    gate_up = share(after(w_gate, ready_w), w_up)
    own_in = lax.dynamic_index_in_dim(layer_input, side, 0, keepdims=False)
    own_cot = lax.dynamic_index_in_dim(cotangent, side, 0, keepdims=False)
    gains = jnp.concatenate(
        [attn_gain[None], ffn_gain[None], jnp.zeros((6, rows_w), BF16)]
    ).astype(F32)
    all_in, gains = plane_gather(after(own_in, ready_w), 10, gains=gains)
    gain_one = gains[:, 0].reshape(width)
    gain_two = gains[:, 1].reshape(width)
    gate_up = lax.all_gather(gate_up, "dp", axis=0, tiled=True)
    down_own = to_units(after(w_down, all_in).T)
    down_w = lax.all_gather(down_own, "dp", axis=0, tiled=True)

    all_f = all_in.astype(F32)
    normed_one = (all_f * rms_factor(all_f) * gain_one).astype(BF16)
    pre = after(jnp.dot(normed_one, w_qkv, preferred_element_type=F32), down_own)
    attended, queries, keyvals, logs = attend(pre, cosine, signed, seqs)
    inputs_f = own_in.astype(F32)
    factor_one = rms_factor(inputs_f)
    hidden = inputs_f + product_scatter(1, attended, attn_w, qkv_cols, q_cols)[0]
    factor_two = rms_factor(hidden)
    normed_own = (hidden * factor_two * gain_two).astype(BF16)
    normed_two = plane_gather(normed_own)[0]
    all_cot, cots = along_ctx(cotangent, down_own, attended)

    product, gate_slope, up_slope = ffn(normed_two, gate_up)
    down_grad = matmul_t(all_cot, product).astype(BF16)
    down_sum = lax.psum_scatter(down_grad, "dp", scatter_dimension=0, tiled=True)
    normed_two_grad, gate_grad, up_grad = ffn_back(
        3, cots, after(gate_slope, down_grad), up_slope, down_w, gate_up
    )
    gate_w_grad = matmul_t(normed_two, gate_grad).astype(BF16)
    gate_sum = lax.psum_scatter(gate_w_grad, "dp", scatter_dimension=0, tiled=True)
    hidden_back, ffn_gain_term = rms_back(normed_two_grad, hidden, factor_two, gain_two)
    hidden_grad = own_cot.astype(F32) + hidden_back
    hidden_low, up_w_grad = plane_gather(
        after(hidden_grad.astype(BF16), gate_w_grad), 7, [normed_two, up_grad]
    )
    up_sum = lax.psum_scatter(up_w_grad, "dp", scatter_dimension=0, tiled=True)
    attended_grad = jnp.dot(after(hidden_low, up_w_grad), w_out_t, preferred_element_type=F32).astype(BF16)
    out_w_grad = matmul_t(hidden_low, attended).astype(BF16)
    back, out_own, down_out = attend_back(
        5,
        queries,
        keyvals,
        attended_grad,
        logs,
        cosine,
        signed,
        seqs,
        product,
        down_w,
        hidden,
        down_sum,
    )
    out_other = swap_sides(out_own)
    qkv_grad = matmul_t(normed_one, back).astype(BF16)
    attn_grad = jnp.concatenate([qkv_grad, out_w_grad], axis=1)
    attn_sum = lax.psum_scatter(attn_grad, "dp", scatter_dimension=0, tiled=True)
    normed_one_grad, gate_out = product_scatter(
        4, after(back, attn_grad), attn_w, 0, qkv_cols, gate_sum
    )
    input_back, attn_gain_term = rms_back(normed_one_grad, inputs_f, factor_one, gain_one)
    input_own = (hidden_grad + input_back).astype(BF16)
    input_other = swap_sides(input_own)
    terms = jnp.stack([attn_gain_term, ffn_gain_term])
    gain_own, up_out = gain_sum(2, after(terms, input_own, out_other), up_sum)
    query_out, key_out, value_out, wide_out = last_swap(
        9, after(attn_sum, gain_own), q_cols, kv_cols
    )

    def both_sides(own, other):
        return jnp.where(side == 0, jnp.stack([own, other]), jnp.stack([other, own]))

    layer_output = both_sides(out_own, out_other)
    input_grad = both_sides(input_own, after(input_other, gain_own)).astype(F32)
    return (
        layer_output,
        input_grad,
        gain_own[0],
        query_out.astype(F32),
        key_out.astype(F32),
        value_out.astype(F32),
        wide_out.astype(F32),
        gain_own[1],
        gate_out.astype(F32),
        up_out.astype(F32),
        down_out.astype(F32),
    )


def fits_plane(mesh, shapes):
    sizes = mesh.shape
    seqs, length, width = shapes[0].shape
    kv_heads = shapes[3].shape[1] // HEAD_DIM
    return (
        sizes["tensor"] == 2
        and sizes["ctx"] == 4
        and seqs == 2 * sizes["dp"]
        and kv_heads == 8
        and shapes[2].shape[1] == 4 * shapes[3].shape[1]
        and length % (4 * QB) == 0
        and width % (128 * 4 * sizes["dp"]) == 0
    )


def placed(mesh, function):
    return jax.shard_map(
        function,
        mesh=mesh,
        in_specs=(
            P("dp", "ctx", None),
            P(("dp", "ctx")),
            P(("dp", "ctx"), "tensor"),
            P(("dp", "ctx"), "tensor"),
            P(("dp", "ctx"), "tensor"),
            P("tensor", ("dp", "ctx")),
            P(("dp", "ctx")),
            P(("dp", "ctx"), "tensor"),
            P(("dp", "ctx"), "tensor"),
            P("tensor", ("dp", "ctx")),
            P("dp", "ctx", None),
        ),
        out_specs=(
            P("dp", "ctx", None),
            P("dp", "ctx", None),
            P(("dp", "ctx")),
            P(("dp", "ctx"), "tensor"),
            P(("dp", "ctx"), "tensor"),
            P(("dp", "ctx"), "tensor"),
            P("tensor", ("dp", "ctx")),
            P(("dp", "ctx")),
            P(("dp", "ctx"), "tensor"),
            P(("dp", "ctx"), "tensor"),
            P("tensor", ("dp", "ctx")),
        ),
        check_vma=False,
    )


def solution(mesh):
    def whole(*arrays):
        return placed(mesh, on_plane if fits_plane(mesh, arrays) else on_device)(*arrays)

    return whole
```

```python
import functools
import math

import jax
import jax.numpy as jnp
from jax import lax
from jax.experimental import pallas as pl
from jax.experimental.pallas import tpu as pltpu
from jax.sharding import PartitionSpec as P

HEAD_DIM = 64


EPSILON = 1e-05
ROPE_BASE = 500000.0


def rotate(values, cosine, sine_val):
    middle = values.shape[-1] // 2
    leading = values[..., :middle]
    trailing = values[..., middle:]
    return jnp.concatenate(
        [leading * cosine - trailing * sine_val, trailing * cosine + leading * sine_val], axis=-1
    )


def unrotate(gradient, cosine, sine_val):
    middle = gradient.shape[-1] // 2
    leading = gradient[..., :middle]
    trailing = gradient[..., middle:]
    return jnp.concatenate(
        [leading * cosine + trailing * sine_val, trailing * cosine - leading * sine_val], axis=-1
    )


def angles(positions, head_dim):
    exponent = jnp.arange(head_dim // 2).astype(jnp.float32) * (
        -2.0 * math.log(ROPE_BASE) / head_dim
    )
    return positions.astype(jnp.float32)[:, None] * jnp.exp(exponent)[None, :]


def rms_factor(row_values):
    return lax.rsqrt(jnp.mean(row_values * row_values, axis=-1, keepdims=True) + EPSILON)


def rms_back(upstream, row_values, factor, gain_row):
    scaled = upstream * gain_row
    gain_term = jnp.sum(upstream * row_values * factor, axis=0)
    inner_mean = jnp.mean(scaled * row_values, axis=-1, keepdims=True)
    return (factor * scaled - row_values * (factor * factor * factor) * inner_mean, gain_term)


def matmul_t(left_op, right_op):
    return lax.dot_general(
        left_op, right_op, (((0,), (0,)), ((), ())), preferred_element_type=jnp.float32
    )


def matmul_nt(left_op, right_op):
    return lax.dot_general(
        left_op, right_op, (((1,), (1,)), ((), ())), preferred_element_type=jnp.float32
    )


def on_device(
    layer_input,
    attn_gain,
    w_query,
    w_key,
    w_value,
    w_out,
    ffn_gain,
    w_gate,
    w_up,
    w_down,
    cotangent,
):
    seq_dev, span_len, model_width = layer_input.shape
    row_count = seq_dev * span_len
    length_all = span_len * lax.axis_size("ctx")
    full_q, full_k, full_v, full_o, full_gate, full_up, full_down, gain_attn, gain_ffn = (
        lax.all_gather(w_query, ("dp", "ctx"), axis=0, tiled=True),
        lax.all_gather(w_key, ("dp", "ctx"), axis=0, tiled=True),
        lax.all_gather(w_value, ("dp", "ctx"), axis=0, tiled=True),
        lax.all_gather(w_out, ("dp", "ctx"), axis=1, tiled=True),
        lax.all_gather(w_gate, ("dp", "ctx"), axis=0, tiled=True),
        lax.all_gather(w_up, ("dp", "ctx"), axis=0, tiled=True),
        lax.all_gather(w_down, ("dp", "ctx"), axis=1, tiled=True),
        lax.all_gather(attn_gain, ("dp", "ctx"), axis=0, tiled=True),
        lax.all_gather(ffn_gain, ("dp", "ctx"), axis=0, tiled=True),
    )
    kv_local = full_k.shape[1] // HEAD_DIM
    group_size = full_q.shape[1] // HEAD_DIM // kv_local
    block_count = seq_dev * kv_local
    scale = HEAD_DIM ** (-0.5)
    query_pos = lax.axis_index("ctx") * span_len + jnp.arange(span_len)
    theta = angles(query_pos, HEAD_DIM)
    cosine = jnp.cos(theta)
    sine_val = jnp.sin(theta)
    causal = query_pos[:, None] >= jnp.arange(length_all)[None, :]
    inputs_f = layer_input.reshape(row_count, model_width).astype(jnp.float32)
    gain_one = gain_attn.astype(jnp.float32)
    gain_two = gain_ffn.astype(jnp.float32)
    factor_one = rms_factor(inputs_f)
    normed_one = (inputs_f * factor_one * gain_one).astype(jnp.bfloat16)
    query_pre = jnp.dot(normed_one, full_q, preferred_element_type=jnp.float32).reshape(
        seq_dev, span_len, kv_local, group_size, HEAD_DIM
    )
    queries = rotate(
        query_pre, cosine[None, :, None, None, :], sine_val[None, :, None, None, :]
    ).astype(jnp.bfloat16)
    key_pre = jnp.dot(normed_one, full_k, preferred_element_type=jnp.float32).reshape(
        seq_dev, span_len, kv_local, HEAD_DIM
    )
    keys_own = (
        rotate(key_pre, cosine[None, :, None, :], sine_val[None, :, None, :])
        .astype(jnp.bfloat16)
        .reshape(seq_dev, span_len, kv_local * HEAD_DIM)
    )
    values_own = (
        jnp.dot(normed_one, full_v, preferred_element_type=jnp.float32)
        .astype(jnp.bfloat16)
        .reshape(seq_dev, span_len, kv_local * HEAD_DIM)
    )
    keys_all, values_all = (
        lax.all_gather(keys_own, "ctx", axis=1, tiled=True),
        lax.all_gather(values_own, "ctx", axis=1, tiled=True),
    )
    query_blocks = jnp.transpose(queries, (0, 2, 1, 3, 4)).reshape(
        block_count, span_len, group_size, HEAD_DIM
    )
    key_blocks = jnp.transpose(
        keys_all.reshape(seq_dev, length_all, kv_local, HEAD_DIM), (0, 2, 1, 3)
    ).reshape(block_count, length_all, HEAD_DIM)
    value_blocks = jnp.transpose(
        values_all.reshape(seq_dev, length_all, kv_local, HEAD_DIM), (0, 2, 1, 3)
    ).reshape(block_count, length_all, HEAD_DIM)

    def scores_of(query_b, key_b):
        raw_scores = jnp.einsum("qgd,kd->gqk", query_b, key_b, preferred_element_type=jnp.float32)
        return jnp.where(causal[None], raw_scores * scale, -1e30)

    def attend(block_in):
        query_b, key_b, value_b = block_in
        scores = scores_of(query_b, key_b)
        peak_row = jnp.max(scores, axis=-1, keepdims=True)
        powers = jnp.exp(scores - peak_row)
        total_sum = jnp.sum(powers, axis=-1, keepdims=True)
        probability = (powers / total_sum).astype(jnp.bfloat16)
        mixed = jnp.einsum("gqk,kd->qgd", probability, value_b, preferred_element_type=jnp.float32)
        return (mixed.astype(jnp.bfloat16), peak_row + jnp.log(total_sum))

    mixed_blocks, logsum = lax.map(attend, (query_blocks, key_blocks, value_blocks))
    attended = jnp.transpose(
        mixed_blocks.reshape(seq_dev, kv_local, span_len, group_size, HEAD_DIM), (0, 2, 1, 3, 4)
    ).reshape(row_count, kv_local * group_size * HEAD_DIM)
    attn_part = jnp.dot(attended, full_o, preferred_element_type=jnp.float32)
    hidden = inputs_f + lax.psum(attn_part, "tensor")
    factor_two = rms_factor(hidden)
    normed_two = (hidden * factor_two * gain_two).astype(jnp.bfloat16)
    gate_pre = jnp.dot(normed_two, full_gate, preferred_element_type=jnp.float32)
    up_pre = jnp.dot(normed_two, full_up, preferred_element_type=jnp.float32)
    sigma = jax.nn.sigmoid(gate_pre)
    product = (gate_pre * sigma * up_pre).astype(jnp.bfloat16)
    ffn_part = jnp.dot(product, full_down, preferred_element_type=jnp.float32)
    out_f = hidden + lax.psum(ffn_part.astype(jnp.bfloat16), "tensor").astype(jnp.float32)
    layer_output = out_f.astype(jnp.bfloat16).reshape(seq_dev, span_len, model_width)
    grad_out = cotangent.reshape(row_count, model_width).astype(jnp.float32)
    grad_low = cotangent.reshape(row_count, model_width)
    down_grad = matmul_t(product, grad_low)
    prod_grad = matmul_nt(grad_low, full_down)
    gate_grad = (prod_grad * up_pre * sigma * (1.0 + gate_pre * (1.0 - sigma))).astype(jnp.bfloat16)
    up_grad = (prod_grad * gate_pre * sigma).astype(jnp.bfloat16)
    gate_w_grad = matmul_t(normed_two, gate_grad)
    up_w_grad = matmul_t(normed_two, up_grad)
    normed_two_part = matmul_nt(gate_grad, full_gate) + matmul_nt(up_grad, full_up)
    normed_two_grad = lax.psum(normed_two_part, "tensor")
    hidden_back, ffn_gain_term = rms_back(normed_two_grad, hidden, factor_two, gain_two)
    hidden_grad = grad_out + hidden_back
    hidden_low = hidden_grad.astype(jnp.bfloat16)
    out_w_grad = matmul_t(attended, hidden_low)
    attended_grad = matmul_nt(hidden_low, full_o).astype(jnp.bfloat16)
    upstream_blocks = jnp.transpose(
        attended_grad.reshape(seq_dev, span_len, kv_local, group_size, HEAD_DIM), (0, 2, 1, 3, 4)
    ).reshape(block_count, span_len, group_size, HEAD_DIM)

    def attend_back(block_in):
        query_b, key_b, value_b, logsum_b, upstream_b = block_in
        scores = scores_of(query_b, key_b)
        probability = jnp.exp(scores - logsum_b)
        rounded = probability.astype(jnp.bfloat16)
        value_grad = jnp.einsum(
            "gqk,qgd->kd", rounded, upstream_b, preferred_element_type=jnp.float32
        )
        prob_grad = jnp.einsum(
            "qgd,kd->gqk", upstream_b, value_b, preferred_element_type=jnp.float32
        )
        inner_sum = jnp.sum(probability * prob_grad, axis=-1, keepdims=True)
        score_grad = (probability * (prob_grad - inner_sum)).astype(jnp.bfloat16)
        query_grad = (
            jnp.einsum("gqk,kd->qgd", score_grad, key_b, preferred_element_type=jnp.float32) * scale
        )
        key_grad = (
            jnp.einsum("gqk,qgd->kd", score_grad, query_b, preferred_element_type=jnp.float32)
            * scale
        )
        return (query_grad, key_grad, value_grad)

    query_grads, key_grads, value_grads = lax.map(
        attend_back, (query_blocks, key_blocks, value_blocks, logsum, upstream_blocks)
    )
    key_rows = jnp.transpose(
        key_grads.reshape(seq_dev, kv_local, length_all, HEAD_DIM), (0, 2, 1, 3)
    ).reshape(seq_dev, length_all, kv_local * HEAD_DIM)
    value_rows = jnp.transpose(
        value_grads.reshape(seq_dev, kv_local, length_all, HEAD_DIM), (0, 2, 1, 3)
    ).reshape(seq_dev, length_all, kv_local * HEAD_DIM)
    key_mine, value_mine = (
        lax.psum_scatter(key_rows, "ctx", scatter_dimension=1, tiled=True),
        lax.psum_scatter(value_rows, "ctx", scatter_dimension=1, tiled=True),
    )
    key_low = (
        unrotate(
            key_mine.reshape(seq_dev, span_len, kv_local, HEAD_DIM),
            cosine[None, :, None, :],
            sine_val[None, :, None, :],
        )
        .astype(jnp.bfloat16)
        .reshape(row_count, kv_local * HEAD_DIM)
    )
    value_low = value_mine.astype(jnp.bfloat16).reshape(row_count, kv_local * HEAD_DIM)
    query_rot = jnp.transpose(
        query_grads.reshape(seq_dev, kv_local, span_len, group_size, HEAD_DIM), (0, 2, 1, 3, 4)
    )
    query_low = (
        unrotate(query_rot, cosine[None, :, None, None, :], sine_val[None, :, None, None, :])
        .astype(jnp.bfloat16)
        .reshape(row_count, kv_local * group_size * HEAD_DIM)
    )
    query_w_grad = matmul_t(normed_one, query_low)
    key_w_grad = matmul_t(normed_one, key_low)
    value_w_grad = matmul_t(normed_one, value_low)
    normed_one_part = (
        matmul_nt(query_low, full_q) + matmul_nt(key_low, full_k) + matmul_nt(value_low, full_v)
    )
    normed_one_grad = lax.psum(normed_one_part.astype(jnp.bfloat16), "tensor").astype(jnp.float32)
    input_back, attn_gain_term = rms_back(normed_one_grad, inputs_f, factor_one, gain_one)
    input_grad = (hidden_grad + input_back).reshape(seq_dev, span_len, model_width)
    (
        query_sum,
        key_sum,
        value_sum,
        out_sum,
        gate_sum,
        up_sum,
        down_sum,
        attn_gain_sum,
        ffn_gain_sum,
    ) = (
        lax.psum_scatter(query_w_grad, ("dp", "ctx"), scatter_dimension=0, tiled=True),
        lax.psum_scatter(key_w_grad, ("dp", "ctx"), scatter_dimension=0, tiled=True),
        lax.psum_scatter(value_w_grad, ("dp", "ctx"), scatter_dimension=0, tiled=True),
        lax.psum_scatter(out_w_grad, ("dp", "ctx"), scatter_dimension=1, tiled=True),
        lax.psum_scatter(gate_w_grad, ("dp", "ctx"), scatter_dimension=0, tiled=True),
        lax.psum_scatter(up_w_grad, ("dp", "ctx"), scatter_dimension=0, tiled=True),
        lax.psum_scatter(down_grad, ("dp", "ctx"), scatter_dimension=1, tiled=True),
        lax.psum_scatter(attn_gain_term, ("dp", "ctx"), scatter_dimension=0, tiled=True),
        lax.psum_scatter(ffn_gain_term, ("dp", "ctx"), scatter_dimension=0, tiled=True),
    )
    return (
        layer_output,
        input_grad,
        attn_gain_sum,
        query_sum,
        key_sum,
        value_sum,
        out_sum,
        ffn_gain_sum,
        gate_sum,
        up_sum,
        down_sum,
    )


MESH_ID = pl.DeviceIdType.MESH
BF16 = jnp.bfloat16
F32 = jnp.float32
QB = 256


def place():
    side = lax.axis_index("tensor")
    ctx = lax.axis_index("ctx")
    row = ctx // 2
    core = ctx % 2
    near_core = {"ctx": row * 2 + (1 - core)}
    near_side = {"tensor": 1 - side}
    near_row = {"ctx": (1 - row) * 2 + core}
    return side, row, core, near_core, near_side, near_row


def greet(neighbours):
    barrier = pltpu.get_barrier_semaphore()
    for target in neighbours:
        pl.semaphore_signal(barrier, inc=1, device_id=target, device_id_type=MESH_ID)
    pl.semaphore_wait(barrier, len(neighbours))


def remote(source, target, send_sem, recv_sem, device):
    return pltpu.make_async_remote_copy(
        src_ref=source,
        dst_ref=target,
        send_sem=send_sem,
        recv_sem=recv_sem,
        device_id=device,
        device_id_type=MESH_ID,
    )


def gather_kernel(rows, works, planes, block_ref, *refs):
    if works:
        left_ref, right_ref, all_ref, grad_ref, send_sems, recv_sems, local_sem = refs
    elif planes:
        gains_ref, all_ref, all_gains_ref, send_sems, recv_sems, local_sem, *gain_sems = refs
    else:
        all_ref, send_sems, recv_sems, local_sem = refs
    side, row, core, near_core, near_side, near_row = place()
    half = rows // 2

    def work(first, last):
        if not works:
            return
        size = left_ref.shape[1] // works

        def step(index, carry):
            at = pl.ds(pl.multiple_of(index * size, size), size)
            grad_ref[at, :] = matmul_t(left_ref[:, at], right_ref[...]).astype(BF16)
            return carry

        lax.fori_loop(first * works // 8, last * works // 8, step, 0)

    def spot(a, b, c, part=None):
        start = (a * 4 + b * 2 + c) * rows
        if part is None:
            return all_ref.at[pl.ds(pl.multiple_of(start, rows), rows)]
        return all_ref.at[pl.ds(pl.multiple_of(start + part * half, half), half)]

    targets = []
    if planes:
        plane = lax.axis_index("dp")
        here = row * 2 + core
        targets = [
            {"dp": (plane + step) % planes, "ctx": (here + turn) % 4}
            for step in range(planes)
            for turn in range(4)
            if step or turn
        ]
    greet([near_side] + (targets if planes else [near_core, near_row]))
    copies = []

    def send(number, source, target, device):
        copy = remote(source, target, send_sems.at[number], recv_sems.at[number], device)
        copy.start()
        copies.append(copy)
        return copy

    gain_copies = []
    if planes:
        mine = all_gains_ref.at[plane * 4 + here]
        gain_copies = [
            remote(gains_ref, mine, gain_sems[0].at[at], gain_sems[1].at[at], target)
            for at, target in enumerate(targets)
        ] + [pltpu.make_async_copy(gains_ref, mine, gain_sems[2])]
        for copy in gain_copies:
            copy.start()
    first = block_ref.at[pl.ds(0, half)]
    second = block_ref.at[pl.ds(half, half)]
    side_b = send(0, second, spot(side, row, core, 1), near_side)
    row_a = send(1, first, spot(side, row, core, 0), near_row)
    side_a = send(2, first, spot(side, row, core, 0), near_side)
    row_b = send(3, second, spot(side, row, core, 1), near_row)
    core_own = send(4, block_ref, spot(side, row, core), near_core)
    local = pltpu.make_async_copy(block_ref, spot(side, row, core), local_sem)
    local.start()
    work(0, 6)
    side_b.wait_recv()
    away_b = send(5, spot(1 - side, row, core, 1), spot(1 - side, row, core, 1), near_row)
    row_a.wait_recv()
    away_a = send(6, spot(side, 1 - row, core, 0), spot(side, 1 - row, core, 0), near_side)
    work(6, 8)
    side_a.wait_recv()
    core_side = send(7, spot(1 - side, row, core), spot(1 - side, row, core), near_core)
    row_b.wait_recv()
    core_row = send(8, spot(side, 1 - row, core), spot(side, 1 - row, core), near_core)
    away_a.wait_recv()
    core_away_a = send(
        9, spot(1 - side, 1 - row, core, 0), spot(1 - side, 1 - row, core, 0), near_core
    )
    away_b.wait_recv()
    core_away_b = send(
        10, spot(1 - side, 1 - row, core, 1), spot(1 - side, 1 - row, core, 1), near_core
    )
    for copy in (core_own, core_side, core_row, core_away_a, core_away_b):
        copy.wait_recv()
    for copy in copies:
        copy.wait_send()
    for copy in gain_copies:
        copy.wait()
    local.wait()


def plane_gather(block, number=0, pair=None, gains=None):
    rows, width = block.shape
    anywhere, vmem = pl.BlockSpec(memory_space=pl.ANY), pl.BlockSpec(memory_space=pltpu.VMEM)
    shapes, ins, outs = [jax.ShapeDtypeStruct((8 * rows, width), block.dtype)], [anywhere], [anywhere]
    operands = [block]
    if pair is not None:
        shapes.append(jax.ShapeDtypeStruct((pair[0].shape[1], pair[1].shape[1]), BF16))
        ins += [vmem, vmem]
        outs += [vmem]
        operands += pair
    planes, scratch = 0, []
    if gains is not None:
        planes = lax.axis_size("dp")
        shapes.append(jax.ShapeDtypeStruct((4 * planes,) + gains.shape, gains.dtype))
        ins += [vmem]
        outs += [vmem]
        operands += [gains]
        scratch = [pltpu.SemaphoreType.DMA((4 * planes - 1,))] * 2 + [pltpu.SemaphoreType.DMA]
    return pl.pallas_call(
        functools.partial(gather_kernel, rows, 8 if pair is not None else 0, planes),
        out_shape=tuple(shapes),
        in_specs=ins,
        out_specs=tuple(outs),
        scratch_shapes=[
            pltpu.SemaphoreType.DMA((11,)),
            pltpu.SemaphoreType.DMA((11,)),
            pltpu.SemaphoreType.DMA,
        ]
        + scratch,
        compiler_params=pltpu.CompilerParams(
            collective_id=number, has_side_effects=True, vmem_limit_bytes=60 * 1024 * 1024
        ),
        cost_estimate=pl.CostEstimate(flops=0, bytes_accessed=1024, transcendentals=0),
        name="plane_gather",
    )(*operands)


def swap_scratch():
    return [pltpu.SemaphoreType.DMA((3,))] * 2 + [pltpu.SemaphoreType.DMA]


def swap_copies(in_ref, out_ref, send_sems, recv_sems, local_sem):
    _, row, core, *_ = place()
    rows = out_ref.shape[1]
    here = row * 2 + core

    def block(index):
        return in_ref.at[pl.ds(pl.multiple_of(index * rows, rows), rows)]

    peers = (row * 2 + 1 - core, (1 - row) * 2 + core, (1 - row) * 2 + 1 - core)
    away = [
        remote(block(peer), out_ref.at[here], send_sems.at[at], recv_sems.at[at], {"ctx": peer})
        for at, peer in enumerate(peers)
    ]
    return away, pltpu.make_async_copy(block(here), out_ref.at[here], local_sem)


def norm_back(rows, grad_ref, value_ref, factor_ref, gain_ref, base_ref, out_ref, low_ref, term_ref):
    tile = 32
    gain = gain_ref[...]

    def step(index, total):
        here = pl.ds(pl.multiple_of(index * tile, tile), tile)
        grad, value, factor = grad_ref[here, :], value_ref[here, :], factor_ref[here, :]
        scaled = grad * gain
        inner = jnp.mean(scaled * value, axis=1, keepdims=True)
        back = factor * scaled - value * (factor * factor * factor) * inner
        result = base_ref[here, :].astype(F32) + back
        if out_ref is not None:
            out_ref[here, :] = result
        low_ref[here, :] = result.astype(BF16)
        return total + jnp.sum(grad * value * factor, axis=0, keepdims=True)

    total = lax.fori_loop(0, rows // tile, step, jnp.zeros((1, gain.shape[1]), F32))
    term_ref[...] = jnp.broadcast_to(total, term_ref.shape)


def scatter_steps(rows, left_of, right_of, out_ref, scratch, swap=None, late=None):
    made, other, to_side, to_row, from_side, from_row = scratch[:6]
    on_side, on_row, got_side, got_row, send_sems, recv_sems = scratch[6:]
    side, row, core, near_core, near_side, near_row = place()
    tile = 32
    wide = out_ref.shape[1] // 2

    chips = ((side, row), (1 - side, row), (side, 1 - row), (1 - side, 1 - row))
    routes = [
        (made.at[chip, part, 1 - core], other.at[chip, part], near_core)
        for chip in range(4)
        for part in range(2)
    ] + [
        (to_side.at[0], from_side.at[0], near_side),
        (to_row.at[0], from_row.at[0], near_row),
        (to_side.at[1], from_side.at[1], near_side),
        (to_row.at[1], from_row.at[1], near_row),
        (on_row, got_row, near_row),
        (on_side, got_side, near_side),
    ]
    copies = [
        remote(source, target, send_sems.at[at], recv_sems.at[at], device)
        for at, (source, target, device) in enumerate(routes)
    ]
    side_0, row_0, side_1, row_1, last_row, last_side = copies[8:]
    swapped = None if swap is None else swap_copies(*swap)

    def make(chip, part, first=False):
        a, b = chips[chip]
        start = pl.multiple_of((a * 4 + b * 2) * rows, 2 * rows)
        value = matmul_nt(left_of(chip, start), right_of(pl.ds(part * wide, wide)))
        made[chip, part, 0] = value[:rows].astype(BF16)
        made[chip, part, 1] = value[rows:].astype(BF16)
        if first:
            partners = (near_core, near_side, near_row)
            if swap is not None:
                partners += ({"ctx": (1 - row) * 2 + 1 - core},)
            greet(partners)
        copies[2 * chip + part].start()

    def both(chip, part, at):
        here = made[chip, part, core, pl.ds(at, tile), :].astype(F32)
        return here + other[chip, part, pl.ds(at, tile), :].astype(F32)

    def each(body):
        def step(index, carry):
            body(pl.multiple_of(index * tile, tile))
            return carry

        lax.fori_loop(0, rows // tile, step, 0)

    def put(target, chip, part, copy, extra=None):
        copies[2 * chip + part].wait_recv()

        def body(at):
            value = both(chip, part, at)
            if extra is not None:
                value = value + extra[pl.ds(at, tile), :].astype(F32)
            target[pl.ds(at, tile), :] = value.astype(BF16)

        each(body)
        copy.start()

    def across():
        make(3, 0, True)
        make(3, 1)
        put(to_side.at[0], 3, 0, side_0)
        put(to_row.at[0], 3, 1, row_0)
        if swap is not None:
            for copy in swapped[0] + [swapped[1]]:
                copy.start()

    def along():
        make(1, 0)
        make(2, 1)
        put(to_side.at[1], 1, 0, side_1)
        put(to_row.at[1], 2, 1, row_1)

    def forward():
        make(1, 1)
        make(2, 0)
        row_0.wait_recv()
        put(on_side, 1, 1, last_side, from_row.at[0])
        side_0.wait_recv()
        put(on_row, 2, 0, last_row, from_side.at[0])

    def own():
        make(0, 0)
        make(0, 1)

    def finish():
        copies[0].wait_recv()
        copies[1].wait_recv()
        side_1.wait_recv()
        row_1.wait_recv()

        def first_sum(at):
            here = pl.ds(at, tile)
            out_ref[here, :wide] = both(0, 0, at) + from_side[1, here, :].astype(F32)
            out_ref[here, wide:] = both(0, 1, at) + from_row[1, here, :].astype(F32)

        each(first_sum)
        if swap is not None:
            for copy in swapped[0]:
                copy.wait()
            swapped[1].wait()
            late()
        last_side.wait_recv()
        last_row.wait_recv()

        def last_sum(at):
            here = pl.ds(at, tile)
            out_ref[here, :wide] += got_row[here, :].astype(F32)
            out_ref[here, wide:] += got_side[here, :].astype(F32)

        each(last_sum)
        for copy in copies:
            copy.wait_send()

    return across, along, forward, own, finish


def scatter_scratch(rows, width):
    half = width // 2
    return (
        [pltpu.VMEM((4, 2, 2, rows, half), BF16), pltpu.VMEM((4, 2, rows, half), BF16)]
        + [pltpu.VMEM((2, rows, half), BF16)] * 4
        + [pltpu.VMEM((rows, half), BF16)] * 4
        + [pltpu.SemaphoreType.DMA((14,))] * 2
    )


def scatter_kernel(rows, swaps, columns, left, right, *refs):
    swap, late = None, None
    if swaps:
        in_ref, value_ref, factor_ref, gain_ref, base_ref, low_ref, term_ref, laid_ref = refs[:8]
        out_ref, *scratch = refs[8:]
        swapped = scratch[-4]
        swap = (in_ref, swapped, *scratch[-3:])
        scratch = scratch[:-4]

        def late():
            size = swapped.shape[2]
            for part in range(4):
                laid_ref[:, part * size : (part + 1) * size] = swapped[part]

    else:
        out_ref, *scratch = refs

    def left_of(chip, start):
        return left[pl.ds(start, 2 * rows), :]

    def right_of(at):
        return right[at, columns]

    for step in scatter_steps(rows, left_of, right_of, out_ref, scratch, swap=swap, late=late):
        step()
    if swaps:
        norm_back(
            rows, out_ref, value_ref, factor_ref, gain_ref, base_ref, None, low_ref, term_ref
        )


def product_scatter(number, left, right, start, size, swap=None, norm=()):
    total = left.shape[0]
    width = right.shape[0]
    rows = total // 8
    vmem = pl.BlockSpec(memory_space=pltpu.VMEM)
    if swap is None:
        shapes, ins, scratch = [jax.ShapeDtypeStruct((rows, width), F32)], [vmem, vmem], []
        operands = [left, right]
    else:
        deep = swap.shape[0] // 4
        shapes = [
            jax.ShapeDtypeStruct((rows, width), BF16),
            jax.ShapeDtypeStruct((8, width), F32),
            jax.ShapeDtypeStruct((deep, 4 * swap.shape[1]), swap.dtype),
        ]
        ins = [vmem, vmem, pl.BlockSpec(memory_space=pl.ANY)] + [vmem] * 4
        operands = [left, right, swap, *norm]
        scratch = [pltpu.VMEM((4, deep, swap.shape[1]), swap.dtype)] + swap_scratch()
    return pl.pallas_call(
        functools.partial(scatter_kernel, rows, swap is not None, slice(start, start + size)),
        out_shape=tuple(shapes),
        in_specs=ins,
        out_specs=tuple([vmem] * len(shapes)),
        scratch_shapes=([pltpu.VMEM((rows, width), F32)] if swap is not None else [])
        + scatter_scratch(rows, width)
        + scratch,
        compiler_params=pltpu.CompilerParams(
            collective_id=number, has_side_effects=True, vmem_limit_bytes=56 * 1024 * 1024
        ),
        cost_estimate=pl.CostEstimate(flops=0, bytes_accessed=1024, transcendentals=0),
        name="product_scatter",
    )(*operands)


def ffn_back_kernel(
    rows,
    own_ref,
    far_ref,
    twin_ref,
    twin_far_ref,
    gate_slope_ref,
    up_slope_ref,
    down_ref,
    right_ref,
    value_ref,
    factor_ref,
    gain_ref,
    base_ref,
    result_ref,
    low_ref,
    term_ref,
    gate_ref,
    up_ref,
    out_ref,
    cots,
    gate_slopes,
    up_slopes,
    lefts,
    sems,
    out_sems,
    *scratch,
):
    side, row, core, *_ = place()
    units = down_ref.shape[1]
    turns = (3, 1, 2, 0)
    chips = ((side, row), (1 - side, row), (side, 1 - row), (1 - side, 1 - row))
    starts = [pl.multiple_of((a * 4 + b * 2) * rows, 2 * rows) for a, b in chips]
    stored = []

    def fetch(turn):
        chip = turns[turn]
        near, away = (own_ref, twin_ref) if chip < 2 else (far_ref, twin_far_ref)
        there = pl.ds(starts[chip], 2 * rows)
        slot = turn % 2
        return [
            pltpu.make_async_copy(source, target, sems.at[which, slot])
            for which, (source, target) in enumerate(
                (
                    (near.at[chips[chip][0]], cots.at[slot, core]),
                    (away.at[chips[chip][0]], cots.at[slot, 1 - core]),
                    (gate_slope_ref.at[there], gate_slopes.at[slot]),
                    (up_slope_ref.at[there], up_slopes.at[slot]),
                )
            )
        ]

    def store(turn):
        there = pl.ds(starts[turns[turn]], 2 * rows)
        slot = turn % 2
        return [
            pltpu.make_async_copy(
                lefts.at[slot, :, pl.ds(which * units, units)],
                target.at[there],
                out_sems.at[which, slot],
            )
            for which, target in enumerate((gate_ref, up_ref))
        ]

    def start(copies):
        for copy in copies:
            copy.start()

    def wait(copies):
        for copy in copies:
            copy.wait()

    def left_of(chip, _):
        turn = turns.index(chip)
        slot = turn % 2
        if chip in stored:
            return lefts[slot]
        stored.append(chip)
        if turn == 0:
            start(fetch(0))
        if turn == 1:
            start(fetch(2))
        if turn == 2:
            start(fetch(3))
        if turn == 0:
            start(fetch(1))
        wait(fetch(turn))
        if turn > 1:
            wait(store(turn - 2))
        cot = cots[slot].reshape(2 * rows, cots.shape[3])
        grad = jnp.dot(cot, down_ref[...], preferred_element_type=F32)
        lefts[slot, :, :units] = (grad * gate_slopes[slot].astype(F32)).astype(BF16)
        lefts[slot, :, units:] = (grad * up_slopes[slot].astype(F32)).astype(BF16)
        start(store(turn))
        return lefts[slot]

    def right_of(at):
        return right_ref[at, :]

    for step in scatter_steps(rows, left_of, right_of, out_ref, scratch):
        step()
    norm_back(
        rows, out_ref, value_ref, factor_ref, gain_ref, base_ref, result_ref, low_ref, term_ref
    )
    wait(store(2))
    wait(store(3))


def ffn_back(number, cots, gate_slope, up_slope, down_w, gate_up, norm):
    total, units = gate_slope.shape
    width = down_w.shape[0]
    rows = total // 8
    vmem = pl.BlockSpec(memory_space=pltpu.VMEM)
    anywhere = pl.BlockSpec(memory_space=pl.ANY)
    return pl.pallas_call(
        functools.partial(ffn_back_kernel, rows),
        out_shape=(
            jax.ShapeDtypeStruct((rows, width), F32),
            jax.ShapeDtypeStruct((rows, width), BF16),
            jax.ShapeDtypeStruct((8, width), F32),
            jax.ShapeDtypeStruct((total, units), BF16),
            jax.ShapeDtypeStruct((total, units), BF16),
        ),
        in_specs=[anywhere] * 6 + [vmem] * 6,
        out_specs=(vmem, vmem, vmem, anywhere, anywhere),
        scratch_shapes=[
            pltpu.VMEM((rows, width), F32),
            pltpu.VMEM((2, 2, rows, width), BF16),
            pltpu.VMEM((2, 2 * rows, units), BF16),
            pltpu.VMEM((2, 2 * rows, units), BF16),
            pltpu.VMEM((2, 2 * rows, 2 * units), BF16),
            pltpu.SemaphoreType.DMA((4, 2)),
            pltpu.SemaphoreType.DMA((2, 2)),
        ]
        + scatter_scratch(rows, width),
        compiler_params=pltpu.CompilerParams(
            collective_id=number, has_side_effects=True, vmem_limit_bytes=60 * 1024 * 1024
        ),
        cost_estimate=pl.CostEstimate(flops=0, bytes_accessed=1024, transcendentals=0),
        name="ffn_back",
    )(*cots, gate_slope, up_slope, down_w, gate_up, *norm)


def ffn_kernel(in_ref, w_ref, product_ref, gate_slope_ref, up_slope_ref):
    units = product_ref.shape[1]
    wide = 512
    rows_in = in_ref[...]
    for start in range(0, units, wide):
        at = pl.ds(start, wide)
        gate = jnp.dot(rows_in, w_ref[:, at], preferred_element_type=F32)
        up = jnp.dot(rows_in, w_ref[:, pl.ds(units + start, wide)], preferred_element_type=F32)
        sigma = jax.nn.sigmoid(gate)
        active = gate * sigma
        product_ref[:, at] = (active * up).astype(BF16)
        gate_slope_ref[:, at] = (up * sigma * (1.0 + gate * (1.0 - sigma))).astype(BF16)
        up_slope_ref[:, at] = active.astype(BF16)


def ffn(rows_in, gate_up):
    total, width = rows_in.shape
    units = gate_up.shape[1] // 2
    rows = 512
    out = pl.BlockSpec((rows, units), lambda i: (i, 0))
    return pl.pallas_call(
        ffn_kernel,
        grid=(total // rows,),
        out_shape=(jax.ShapeDtypeStruct((total, units), BF16),) * 3,
        in_specs=[
            pl.BlockSpec((rows, width), lambda i: (i, 0)),
            pl.BlockSpec(
                (width, 2 * units), lambda i: (0, 0), pipeline_mode=pl.Buffered(1)
            ),
        ],
        out_specs=(out, out, out),
        compiler_params=pltpu.CompilerParams(vmem_limit_bytes=60 * 1024 * 1024),
        cost_estimate=pl.CostEstimate(flops=0, bytes_accessed=1024, transcendentals=0),
        name="ffn",
    )(rows_in, gate_up)


def swap_halves(values):
    width = values.shape[-1]
    lane = lax.broadcasted_iota(jnp.int32, values.shape, 1)
    ahead = pltpu.roll(values, width - HEAD_DIM // 2, 1)
    behind = pltpu.roll(values, HEAD_DIM // 2, 1)
    return jnp.where(lane % HEAD_DIM < HEAD_DIM // 2, ahead, behind)


def pieces_of(block):
    return ((0, block * QB, False), (block * QB, QB, True)) if block else ((0, QB, True),)


def masked_scores(query, keys, diagonal):
    scores = matmul_nt(query, keys)
    if diagonal:
        here = lax.broadcasted_iota(jnp.int32, scores.shape, 0)
        there = lax.broadcasted_iota(jnp.int32, scores.shape, 1)
        scores = jnp.where(here >= there, scores, -1e30)
    return scores


def attend_kernel(length, q_ref, kv_ref, cos_ref, sin_ref, att_ref, qrot_ref, kvrot_ref, log_ref):
    cosine = cos_ref[...]
    signed = sin_ref[...]
    scale = HEAD_DIM ** (-0.5)
    pre = q_ref[...]
    qrot_ref[...] = (pre * cosine + swap_halves(pre) * signed).astype(BF16)
    pre = kv_ref[...]
    lane = lax.broadcasted_iota(jnp.int32, pre.shape, 1)
    turned = jnp.where(lane < HEAD_DIM, pre * cosine + swap_halves(pre) * signed, pre)
    kvrot_ref[...] = turned.astype(BF16)
    for block in range(length // QB):
        here = pl.ds(block * QB, QB)
        logs = []
        mixed = []
        for head in range(2):
            query = qrot_ref[here, head * HEAD_DIM : (head + 1) * HEAD_DIM] * jnp.asarray(
                scale, BF16
            )
            scores = []
            for start, size, diagonal in pieces_of(block):
                keys = kvrot_ref[pl.ds(start, size), :HEAD_DIM]
                scores.append(masked_scores(query, keys, diagonal))
            peak = functools.reduce(
                jnp.maximum, [jnp.max(s, axis=1, keepdims=True) for s in scores]
            )
            powers = [jnp.exp(s - peak) for s in scores]
            total = sum(jnp.sum(p, axis=1, keepdims=True) for p in powers)
            inverse = 1.0 / total
            out = None
            for (start, size, _), power in zip(pieces_of(block), powers):
                values = kvrot_ref[pl.ds(start, size), HEAD_DIM:]
                term = jnp.dot(
                    (power * inverse).astype(BF16), values, preferred_element_type=F32
                )
                out = term if out is None else out + term
            mixed.append(out)
            logs.append(peak + jnp.log(total))
        att_ref[here, :] = jnp.concatenate(mixed, axis=1).astype(BF16)
        lane = lax.broadcasted_iota(jnp.int32, (QB, 128), 1)
        log_ref[here, :] = jnp.where(lane < HEAD_DIM, logs[0], logs[1])


def attend(pre, cosine, signed, seqs):
    rows = pre.shape[0]
    length = rows // seqs
    pairs = pre.shape[1] // 128 - 1
    block = (length, 128)
    return pl.pallas_call(
        functools.partial(attend_kernel, length),
        grid=(seqs, pairs),
        out_shape=(
            jax.ShapeDtypeStruct((rows, pairs * 128), BF16),
            jax.ShapeDtypeStruct((rows, pairs * 128), BF16),
            jax.ShapeDtypeStruct((rows, 128), BF16),
            jax.ShapeDtypeStruct((rows, pairs * 128), F32),
        ),
        in_specs=[
            pl.BlockSpec(block, lambda s, h: (s, h)),
            pl.BlockSpec(block, lambda s, h: (s, pairs)),
            pl.BlockSpec(block, lambda s, h: (0, 0)),
            pl.BlockSpec(block, lambda s, h: (0, 0)),
        ],
        out_specs=(
            pl.BlockSpec(block, lambda s, h: (s, h)),
            pl.BlockSpec(block, lambda s, h: (s, h)),
            pl.BlockSpec(block, lambda s, h: (s, 0)),
            pl.BlockSpec(block, lambda s, h: (s, h)),
        ),
        compiler_params=pltpu.CompilerParams(vmem_limit_bytes=48 * 1024 * 1024),
        cost_estimate=pl.CostEstimate(
            flops=8 * rows * length * 128 * pairs,
            bytes_accessed=rows * pairs * 128 * 12,
            transcendentals=rows * length * 2 * pairs,
        ),
        name="attend",
    )(pre, pre, cosine, signed)


def attend_back_kernel(
    seqs,
    rows,
    q_ref,
    kv_ref,
    up_ref,
    log_ref,
    cos_ref,
    sin_ref,
    left_ref,
    right_ref,
    hidden_ref,
    in_ref,
    back_ref,
    out_ref,
    laid_ref,
    sum_ref,
    ffn_ref,
    swapped,
    *scratch,
):
    def late():
        size = swapped.shape[2]
        for part in range(4):
            turned = jnp.transpose(swapped[part].astype(F32))
            laid_ref[part * size : (part + 1) * size, :] = turned.astype(BF16)

    across, along, forward, own, finish = scatter_steps(
        rows,
        lambda chip, start: left_ref[pl.ds(start, 2 * rows), :],
        lambda at: right_ref[at, :],
        ffn_ref,
        scratch[:-3],
        swap=(in_ref, swapped, *scratch[-3:]),
        late=late,
    )
    scale = HEAD_DIM ** (-0.5)
    length = q_ref.shape[0] // seqs
    pairs = q_ref.shape[1] // 128
    across()
    along()

    def one_pair(index, carry):
        seq = index // pairs
        pair = index % pairs
        lanes_at = pl.ds(pl.multiple_of(pair * 128, 128), 128)
        base = pl.multiple_of(seq * length, length)

        @pl.when(index == 1)
        def _():
            forward()

        @pl.when(index == 2)
        def _():
            own()

        @pl.when(pair == 0)
        def _():
            sum_ref[...] = jnp.zeros_like(sum_ref)

        for block in range(length // QB):
            here = pl.ds(base + block * QB, QB)
            turned = []
            q_pair = q_ref[here, lanes_at]
            up_pair = up_ref[here, lanes_at]
            log_pair = log_ref[here, lanes_at]
            for head in range(2):
                lanes = slice(head * HEAD_DIM, (head + 1) * HEAD_DIM)
                query = q_pair[:, lanes] * jnp.asarray(scale, BF16)
                upstream = up_pair[:, lanes]
                logs = log_pair[:, head * HEAD_DIM : head * HEAD_DIM + 1]
                saved = []
                inner = None
                for start, size, diagonal in pieces_of(block):
                    keys = kv_ref[pl.ds(base + start, size), :HEAD_DIM]
                    values = kv_ref[pl.ds(base + start, size), HEAD_DIM:]
                    probability = jnp.exp(masked_scores(query, keys, diagonal) - logs)
                    prob_grad = matmul_nt(upstream, values)
                    term = jnp.sum(probability * prob_grad, axis=1, keepdims=True)
                    inner = term if inner is None else inner + term
                    saved.append((start, size, probability, prob_grad))
                out = None
                for start, size, probability, prob_grad in saved:
                    keys = kv_ref[pl.ds(base + start, size), :HEAD_DIM]
                    score_grad = (probability * (prob_grad - inner)).astype(BF16)
                    rounded = probability.astype(BF16)
                    term = jnp.dot(score_grad, keys, preferred_element_type=F32)
                    out = term if out is None else out + term
                    sum_ref[pl.ds(start, size), :] += jnp.concatenate(
                        [matmul_t(score_grad, query), matmul_t(rounded, upstream)], axis=1
                    )
                turned.append(out * scale)
            grad = jnp.concatenate(turned, axis=1)
            angle = pl.ds(block * QB, QB)
            back_ref[here, lanes_at] = (
                grad * cos_ref[angle, :] - swap_halves(grad) * sin_ref[angle, :]
            ).astype(BF16)

        @pl.when(pair == pairs - 1)
        def _():
            grad = sum_ref[...]
            lane = lax.broadcasted_iota(jnp.int32, grad.shape, 1)
            back = grad * cos_ref[...] - swap_halves(grad) * sin_ref[...]
            back_ref[pl.ds(base, length), pairs * 128 :] = jnp.where(
                lane < HEAD_DIM, back, grad
            ).astype(BF16)

        return carry

    lax.fori_loop(0, seqs * pairs, one_pair, 0)
    finish()

    def add(index, carry):
        at = pl.ds(pl.multiple_of(index * 32, 32), 32)
        out_ref[at, :] = (hidden_ref[at, :] + ffn_ref[at, :]).astype(BF16)
        return carry

    lax.fori_loop(0, rows // 32, add, 0)


def attend_back(
    number, queries, keyvals, upstream, logs, cosine, signed, seqs, left, right, hidden, swap
):
    total, width = queries.shape
    length = total // seqs
    rows = total // 8
    deep = swap.shape[0] // 4
    vmem = pl.BlockSpec(memory_space=pltpu.VMEM)
    return pl.pallas_call(
        functools.partial(attend_back_kernel, seqs, rows),
        out_shape=(
            jax.ShapeDtypeStruct((total, width + 128), BF16),
            jax.ShapeDtypeStruct(hidden.shape, BF16),
            jax.ShapeDtypeStruct((4 * swap.shape[1], deep), BF16),
        ),
        in_specs=[vmem] * 9 + [pl.BlockSpec(memory_space=pl.ANY)],
        out_specs=(vmem, vmem, vmem),
        scratch_shapes=[
            pltpu.VMEM((length, 128), F32),
            pltpu.VMEM(hidden.shape, F32),
            pltpu.VMEM((4, deep, swap.shape[1]), BF16),
        ]
        + scatter_scratch(rows, right.shape[0])
        + swap_scratch(),
        compiler_params=pltpu.CompilerParams(
            collective_id=number, has_side_effects=True, vmem_limit_bytes=56 * 1024 * 1024
        ),
        cost_estimate=pl.CostEstimate(flops=0, bytes_accessed=1024, transcendentals=0),
        name="attend_back",
    )(queries, keyvals, upstream, logs, cosine, signed, left, right, hidden, swap)


def gain_kernel(
    planes,
    parts,
    cols,
    terms_ref,
    up_ref,
    gain_ref,
    laid_ref,
    total,
    seen,
    far,
    mine,
    across,
    swapped,
    send_sems,
    recv_sems,
    *swap_sems,
):
    side, row, core, near_core, near_side, near_row = place()
    plane = lax.axis_index("dp")
    ctx = row * 2 + core
    others = [{"dp": (plane + step) % planes} for step in range(1, planes)]
    corner = {"ctx": (1 - row) * 2 + 1 - core}
    greet((near_core, near_side, near_row, corner) + tuple(others))
    total[...] = terms_ref[...]
    copies = []
    up_copies, up_local = swap_copies(up_ref, swapped, *swap_sems)
    for number, target in enumerate((near_core, near_row)):
        copy = remote(
            total, seen.at[number], send_sems.at[number], recv_sems.at[number], target
        )
        copy.start()
        copy.wait()
        total[...] += seen[number]
    for copy in up_copies + [up_local]:
        copy.start()
    for step, target in enumerate(others, 1):
        start = (((plane + step) % planes) * parts + ctx) * cols
        copy = remote(
            total.at[:, pl.ds(pl.multiple_of(start, cols), cols)],
            far.at[step - 1],
            send_sems.at[2 + step],
            recv_sems.at[2 + step],
            target,
        )
        copy.start()
        copies.append(copy)
    start = (plane * parts + ctx) * cols
    value = total[:, pl.ds(pl.multiple_of(start, cols), cols)]
    for number, copy in enumerate(copies):
        copy.wait_recv()
        value += far[number]
    mine[...] = value
    last = remote(mine, across, send_sems.at[2], recv_sems.at[2], near_side)
    last.start()
    copies.append(last)
    for copy in up_copies:
        copy.wait()
    up_local.wait()
    size = swapped.shape[2]
    for part in range(4):
        laid_ref[:, part * size : (part + 1) * size] = swapped[part]
    last.wait_recv()
    gain_ref[...] = value + across[...]
    for copy in copies:
        copy.wait_send()


def gain_sum(number, terms, up_sum):
    planes = lax.axis_size("dp")
    parts = lax.axis_size("ctx")
    rows, width = terms.shape
    cols = width // (planes * parts)
    deep = up_sum.shape[0] // parts
    vmem = pl.BlockSpec(memory_space=pltpu.VMEM)
    anywhere = pl.BlockSpec(memory_space=pl.ANY)
    return pl.pallas_call(
        functools.partial(gain_kernel, planes, parts, cols),
        out_shape=(
            jax.ShapeDtypeStruct((rows, cols), F32),
            jax.ShapeDtypeStruct((deep, parts * up_sum.shape[1]), BF16),
        ),
        in_specs=[vmem, anywhere],
        out_specs=(vmem,) * 2,
        scratch_shapes=[
            pltpu.VMEM((rows, width), F32),
            pltpu.VMEM((2, rows, width), F32),
            pltpu.VMEM((planes - 1, rows, cols), F32),
            pltpu.VMEM((rows, cols), F32),
            pltpu.VMEM((rows, cols), F32),
            pltpu.VMEM((parts, deep, up_sum.shape[1]), BF16),
            pltpu.SemaphoreType.DMA((planes + 2,)),
            pltpu.SemaphoreType.DMA((planes + 2,)),
        ]
        + swap_scratch(),
        compiler_params=pltpu.CompilerParams(collective_id=number, has_side_effects=True),
        cost_estimate=pl.CostEstimate(flops=0, bytes_accessed=1024, transcendentals=0),
        name="gain_sum",
    )(terms, up_sum)


def last_kernel(
    q_cols, attn_ref, query_ref, key_ref, value_ref, wide_ref, swapped, *swap_sems
):
    _, row, core, near_core, _, near_row = place()
    greet((near_core, near_row, {"ctx": (1 - row) * 2 + 1 - core}))
    copies, local = swap_copies(attn_ref, swapped, *swap_sems)
    for copy in copies + [local]:
        copy.start()
    for copy in copies:
        copy.wait()
    local.wait()
    kv = key_ref.shape[1] // 4
    for part in range(4):
        query_ref[:, part * q_cols : (part + 1) * q_cols] = swapped[part, :, :q_cols]
        turned = jnp.transpose(swapped[part, :, q_cols + 2 * kv :].astype(F32))
        wide_ref[part * q_cols : (part + 1) * q_cols, :] = turned.astype(BF16)
    for at, target in ((q_cols, key_ref), (q_cols + kv, value_ref)):
        target[...] = jnp.concatenate(
            [swapped[part, :, at : at + kv] for part in range(4)], axis=1
        )


def last_swap(number, attn_sum, q_cols, kv_cols):
    parts = lax.axis_size("ctx")
    deep = attn_sum.shape[0] // parts
    vmem = pl.BlockSpec(memory_space=pltpu.VMEM)
    return pl.pallas_call(
        functools.partial(last_kernel, q_cols),
        out_shape=(
            jax.ShapeDtypeStruct((deep, parts * q_cols), BF16),
            jax.ShapeDtypeStruct((deep, parts * kv_cols), BF16),
            jax.ShapeDtypeStruct((deep, parts * kv_cols), BF16),
            jax.ShapeDtypeStruct((parts * q_cols, deep), BF16),
        ),
        in_specs=[pl.BlockSpec(memory_space=pl.ANY)],
        out_specs=(vmem,) * 4,
        scratch_shapes=[pltpu.VMEM((parts, deep, attn_sum.shape[1]), BF16)] + swap_scratch(),
        compiler_params=pltpu.CompilerParams(collective_id=number, has_side_effects=True),
        cost_estimate=pl.CostEstimate(flops=0, bytes_accessed=1024, transcendentals=0),
        name="last_swap",
    )(attn_sum)


def final_kernel(own_ref, other_ref, in_ref, in_other_ref, *refs):
    first = lax.axis_index("tensor") == 0
    sources, (out_ref, in_out_ref, *targets) = refs[:7], refs[7:]
    own, other = own_ref[...], other_ref[...]
    out_ref[0], out_ref[1] = jnp.where(first, own, other), jnp.where(first, other, own)
    own, other = in_ref[...].astype(F32), in_other_ref[...].astype(F32)
    in_out_ref[0], in_out_ref[1] = jnp.where(first, own, other), jnp.where(first, other, own)
    for source, target in zip(sources, targets):
        target[...] = source[...].astype(F32)


def final_forms(out_own, out_other, in_own, in_other, *grads):
    steps = 8
    rows, width = out_own.shape
    halves = pl.BlockSpec((rows // steps, width), lambda i: (i, 0))
    whole = pl.BlockSpec((2, rows // steps, width), lambda i: (0, i, 0))

    def block_of(grad):
        deep, wide = grad.shape
        if wide // steps % 128 == 0:
            return pl.BlockSpec((deep, wide // steps), lambda i: (0, i))
        return pl.BlockSpec((deep // steps, wide), lambda i: (i, 0))

    blocks = [block_of(grad) for grad in grads]
    return pl.pallas_call(
        final_kernel,
        grid=(steps,),
        out_shape=(
            jax.ShapeDtypeStruct((2, rows, width), BF16),
            jax.ShapeDtypeStruct((2, rows, width), F32),
        )
        + tuple(jax.ShapeDtypeStruct(grad.shape, F32) for grad in grads),
        in_specs=[halves] * 4 + blocks,
        out_specs=(whole, whole, *blocks),
        compiler_params=pltpu.CompilerParams(vmem_limit_bytes=60 * 1024 * 1024),
        cost_estimate=pl.CostEstimate(flops=0, bytes_accessed=1024, transcendentals=0),
        name="final_forms",
    )(out_own, out_other, in_own, in_other, *grads)


def lay_kernel(own_ref, far_ref, twin_ref, twin_far_ref, all_ref, sems):
    ctx = lax.axis_index("ctx")
    row, core = ctx // 2, ctx % 2
    span = own_ref.shape[1]
    copies = []
    for number, (part, a, b) in enumerate(
        (
            (own_ref, row, core),
            (twin_ref, row, 1 - core),
            (far_ref, 1 - row, core),
            (twin_far_ref, 1 - row, 1 - core),
        )
    ):
        start = pl.multiple_of((a * 2 + b) * span, span)
        copies.append(
            pltpu.make_async_copy(part, all_ref.at[:, pl.ds(start, span)], sems.at[number])
        )
        copies[-1].start()
    for copy in copies:
        copy.wait()


def along_ctx(block, earlier, later):
    seqs, span, width = block.shape
    cores = [(0, 1), (1, 0), (2, 3), (3, 2)]
    far = lax.ppermute(after(block, earlier), "ctx", [(0, 2), (1, 3), (2, 0), (3, 1)])
    far = after(far, later)
    twin, twin_far = lax.ppermute(block, "ctx", cores), lax.ppermute(far, "ctx", cores)
    whole = pl.pallas_call(
        lay_kernel,
        out_shape=jax.ShapeDtypeStruct((seqs, 4 * span, width), block.dtype),
        in_specs=[pl.BlockSpec(memory_space=pl.ANY)] * 4,
        out_specs=pl.BlockSpec(memory_space=pltpu.VMEM),
        scratch_shapes=[pltpu.SemaphoreType.DMA((4,))],
        compiler_params=pltpu.CompilerParams(vmem_limit_bytes=24 * 1024 * 1024),
        name="lay",
    )(block, far, twin, twin_far)
    return whole.reshape(seqs * 4 * span, width), (block, far, twin, twin_far)


def open_kernel(
    planes,
    q_ref,
    kv_ref,
    wide_ref,
    gate_ref,
    up_ref,
    down_ref,
    attn_ref,
    gate_up_ref,
    down_own_ref,
    send_sems,
    recv_sems,
    local_sems,
    line_send,
    line_recv,
):
    _, row, core, *_ = place()
    plane = lax.axis_index("dp")
    here = row * 2 + core
    rows, units = q_ref.shape[0], gate_ref.shape[1] // 4
    peers = (row * 2 + 1 - core, (1 - row) * 2 + core, (1 - row) * 2 + 1 - core)
    ahead, behind = {"dp": (plane + 1) % planes}, {"dp": (plane + planes - 1) % planes}
    barrier = pltpu.get_barrier_semaphore()
    more, fewer = plane + 1 < planes, plane > 0
    for peer in peers:
        pl.semaphore_signal(barrier, inc=1, device_id={"ctx": peer}, device_id_type=MESH_ID)

    @pl.when(more)
    def _():
        pl.semaphore_signal(barrier, inc=1, device_id=ahead, device_id_type=MESH_ID)

    @pl.when(fewer)
    def _():
        pl.semaphore_signal(barrier, inc=1, device_id=behind, device_id_type=MESH_ID)

    pl.semaphore_wait(barrier, 3 + more.astype(jnp.int32) + fewer.astype(jnp.int32))

    mine = pl.multiple_of(here * rows, rows)
    base = pl.multiple_of(plane * 4 * rows, 4 * rows)
    moves = []
    start = 0
    for source in (q_ref, kv_ref, wide_ref):
        cols = source.shape[1] // 4
        moves.append((source, cols, attn_ref.at[pl.ds(base + mine, rows), pl.ds(start, cols)]))
        start += cols
    for which, source in enumerate((gate_ref, up_ref)):
        lanes = pl.ds(which * units, units)
        moves.append((source, units, gate_up_ref.at[pl.ds(mine, rows), lanes]))
    moves.append((down_ref, units, down_own_ref.at[pl.ds(mine, rows)]))
    away, local = [], []
    for which, (source, cols, target) in enumerate(moves):

        def columns(index, source=source, cols=cols):
            return source.at[:, pl.ds(pl.multiple_of(index * cols, cols), cols)]

        away.append(
            [
                remote(
                    columns(peer),
                    target,
                    send_sems.at[which, at],
                    recv_sems.at[which, at],
                    {"ctx": peer},
                )
                for at, peer in enumerate(peers)
            ]
        )
        local.append(pltpu.make_async_copy(columns(here), target, local_sems.at[which]))
    for which in range(3):
        away[which][0].start()
        local[which].start()
    for at in (1, 2):
        for which in range(3):
            away[which][at].start()
    for which in range(3, 6):
        for copy in away[which]:
            copy.start()
        local[which].start()

    def hop(way, far, part):
        whose = plane - far if way == 0 else plane + far
        half = row if part == 0 else 1 - row
        spot = attn_ref.at[
            pl.ds(pl.multiple_of((whose * 4 + half * 2) * rows, 2 * rows), 2 * rows)
        ]
        return remote(
            spot,
            spot,
            line_send.at[way, far, part],
            line_recv.at[way, far, part],
            ahead if way == 0 else behind,
        )

    def sends(way, far):
        if way == 0:
            return (plane - far >= 0) & more
        return (plane + far < planes) & fewer

    def gets(way, far):
        return plane - 1 - far >= 0 if way == 0 else plane + 1 + far < planes

    def hop_start(way, far, part):
        @pl.when(sends(way, far))
        def _():
            hop(way, far, part).start()

    for which in range(3):
        local[which].wait()
        away[which][0].wait_recv()
    for way in range(2):
        hop_start(way, 0, 0)
    for which in range(3):
        away[which][1].wait_recv()
        away[which][2].wait_recv()
    for way in range(2):
        hop_start(way, 0, 1)
    for far in range(planes - 1):
        for part in range(2):
            for way in range(2):

                @pl.when(gets(way, far))
                def _(way=way, far=far, part=part):
                    hop(way, far, part).wait_recv()

                if far + 1 < planes - 1:
                    hop_start(way, far + 1, part)
    for far in range(planes - 1):
        for part in range(2):
            for way in range(2):

                @pl.when(sends(way, far))
                def _(way=way, far=far, part=part):
                    hop(way, far, part).wait_send()

    for which in range(6):
        if which > 2:
            local[which].wait()
            for copy in away[which]:
                copy.wait_recv()
        for copy in away[which]:
            copy.wait_send()


def open_weights(query, keyval, wide, gate, up, down):
    planes = lax.axis_size("dp")
    rows = query.shape[0]
    cols = (query.shape[1] + keyval.shape[1] + wide.shape[1]) // 4
    units = gate.shape[1] // 4
    anywhere, vmem = pl.BlockSpec(memory_space=pl.ANY), pl.BlockSpec(memory_space=pltpu.VMEM)
    return pl.pallas_call(
        functools.partial(open_kernel, planes),
        out_shape=(
            jax.ShapeDtypeStruct((planes * 4 * rows, cols), BF16),
            jax.ShapeDtypeStruct((4 * rows, 2 * units), BF16),
            jax.ShapeDtypeStruct((4 * rows, units), BF16),
        ),
        in_specs=[anywhere] * 6,
        out_specs=(vmem, anywhere, anywhere),
        scratch_shapes=[
            pltpu.SemaphoreType.DMA((6, 3)),
            pltpu.SemaphoreType.DMA((6, 3)),
            pltpu.SemaphoreType.DMA((6,)),
            pltpu.SemaphoreType.DMA((2, planes - 1, 2)),
            pltpu.SemaphoreType.DMA((2, planes - 1, 2)),
        ],
        compiler_params=pltpu.CompilerParams(
            collective_id=6, has_side_effects=True, vmem_limit_bytes=60 * 1024 * 1024
        ),
        cost_estimate=pl.CostEstimate(flops=0, bytes_accessed=1024, transcendentals=0),
        name="open_weights",
    )(query, keyval, wide, gate, up, down)


def after(value, *earlier):
    return lax.optimization_barrier((value,) + earlier)[0]


def to_units(weight):
    return lax.all_to_all(weight, "ctx", split_axis=1, concat_axis=0, tiled=True)


def swap_sides(block):
    return lax.ppermute(block, "tensor", [(0, 1), (1, 0)])


def on_plane(
    layer_input,
    attn_gain,
    w_query,
    w_key,
    w_value,
    w_out,
    ffn_gain,
    w_gate,
    w_up,
    w_down,
    cotangent,
):
    seqs, span, width = layer_input.shape
    planes = lax.axis_size("dp")
    parts = lax.axis_size("ctx")
    side = lax.axis_index("tensor")
    length = span * parts
    rows_w = w_query.shape[0]
    q_cols = w_query.shape[1] // parts
    kv_cols = w_key.shape[1] // parts

    theta = angles(jnp.arange(length), HEAD_DIM)
    cosine = jnp.tile(jnp.cos(theta), (1, 4))
    sine = jnp.sin(theta)
    signed = jnp.tile(jnp.concatenate([-sine, sine], axis=1), (1, 2))

    keyval = jnp.concatenate(
        [w_key.reshape(rows_w, parts, kv_cols), w_value.reshape(rows_w, parts, kv_cols)], axis=2
    ).reshape(rows_w, -1)
    attn_w, gate_up, down_own = open_weights(
        w_query, keyval, w_out.T, w_gate, w_up, w_down.T
    )
    qkv_cols = q_cols + 2 * kv_cols
    w_qkv = attn_w[:, :qkv_cols]
    w_out_t = attn_w[:, qkv_cols:]
    own_in = lax.dynamic_index_in_dim(layer_input, side, 0, keepdims=False)
    own_cot = lax.dynamic_index_in_dim(cotangent, side, 0, keepdims=False)
    gains = jnp.concatenate(
        [attn_gain[None], ffn_gain[None], jnp.zeros((6, rows_w), BF16)]
    ).astype(F32)
    all_in, gains = plane_gather(after(own_in, gate_up), 10, gains=gains)
    gain_one = gains[:, 0].reshape(width)
    gain_two = gains[:, 1].reshape(width)
    gate_up = lax.all_gather(gate_up, "dp", axis=0, tiled=True)
    down_w = lax.all_gather(down_own, "dp", axis=0, tiled=True)

    all_f = all_in.astype(F32)
    normed_one = (all_f * rms_factor(all_f) * gain_one).astype(BF16)
    pre = jnp.dot(normed_one, w_qkv, preferred_element_type=F32)
    attended, queries, keyvals, logs = attend(pre, cosine, signed, seqs)
    inputs_f = own_in.astype(F32)
    factor_one = rms_factor(inputs_f)
    hidden = inputs_f + product_scatter(1, attended, attn_w, qkv_cols, q_cols)[0]
    factor_two = rms_factor(hidden)
    normed_own = (hidden * factor_two * gain_two).astype(BF16)
    normed_two = plane_gather(normed_own)[0]
    all_cot, cots = along_ctx(cotangent, all_in, hidden)

    product, gate_slope, up_slope = ffn(normed_two, gate_up)
    down_grad = matmul_t(all_cot, product).astype(BF16)
    down_sum = lax.psum_scatter(down_grad, "dp", scatter_dimension=0, tiled=True)
    hidden_grad, hidden_own, ffn_term, gate_grad, up_grad = ffn_back(
        3,
        cots,
        after(gate_slope, down_grad),
        up_slope,
        down_w,
        gate_up,
        (hidden, factor_two, gain_two[None], own_cot),
    )
    gate_w_grad = matmul_t(normed_two, gate_grad).astype(BF16)
    gate_sum = lax.psum_scatter(gate_w_grad, "dp", scatter_dimension=0, tiled=True)
    hidden_low, up_w_grad = plane_gather(after(hidden_own, gate_w_grad), 7, [normed_two, up_grad])
    up_sum = lax.psum_scatter(up_w_grad, "dp", scatter_dimension=0, tiled=True)
    attended_grad = jnp.dot(after(hidden_low, up_w_grad), w_out_t, preferred_element_type=F32).astype(BF16)
    out_w_grad = matmul_t(hidden_low, attended).astype(BF16)
    back, out_own, down_out = attend_back(
        5,
        queries,
        keyvals,
        attended_grad,
        logs,
        cosine,
        signed,
        seqs,
        product,
        down_w,
        hidden,
        down_sum,
    )
    out_other = swap_sides(out_own)
    qkv_grad = matmul_t(normed_one, back).astype(BF16)
    attn_grad = jnp.concatenate([qkv_grad, out_w_grad], axis=1)
    attn_sum = lax.psum_scatter(attn_grad, "dp", scatter_dimension=0, tiled=True)
    input_own, attn_term, gate_out = product_scatter(
        4,
        after(back, attn_grad),
        attn_w,
        0,
        qkv_cols,
        gate_sum,
        (inputs_f, factor_one, gain_one[None], hidden_grad),
    )
    input_other = swap_sides(input_own)
    terms = jnp.concatenate([attn_term[:1], ffn_term[:1]])
    gain_own, up_out = gain_sum(2, after(terms, input_own, out_other), up_sum)
    query_out, key_out, value_out, wide_out = last_swap(
        9, after(attn_sum, gain_own), q_cols, kv_cols
    )

    layer_output, input_grad, query_out, key_out, value_out, wide_out, gate_out, up_out, down_out = (
        final_forms(
            out_own,
            out_other,
            input_own,
            after(input_other, gain_own),
            query_out,
            key_out,
            value_out,
            wide_out,
            gate_out,
            up_out,
            down_out,
        )
    )
    return (
        layer_output,
        input_grad,
        gain_own[0],
        query_out,
        key_out,
        value_out,
        wide_out,
        gain_own[1],
        gate_out,
        up_out,
        down_out,
    )


def fits_plane(mesh, shapes):
    sizes = mesh.shape
    seqs, length, width = shapes[0].shape
    kv_heads = shapes[3].shape[1] // HEAD_DIM
    return (
        sizes["tensor"] == 2
        and sizes["ctx"] == 4
        and seqs == 2 * sizes["dp"]
        and kv_heads == 8
        and shapes[2].shape[1] == 4 * shapes[3].shape[1]
        and length % (4 * QB) == 0
        and width % (128 * 4 * sizes["dp"]) == 0
    )


def placed(mesh, function):
    return jax.shard_map(
        function,
        mesh=mesh,
        in_specs=(
            P("dp", "ctx", None),
            P(("dp", "ctx")),
            P(("dp", "ctx"), "tensor"),
            P(("dp", "ctx"), "tensor"),
            P(("dp", "ctx"), "tensor"),
            P("tensor", ("dp", "ctx")),
            P(("dp", "ctx")),
            P(("dp", "ctx"), "tensor"),
            P(("dp", "ctx"), "tensor"),
            P("tensor", ("dp", "ctx")),
            P("dp", "ctx", None),
        ),
        out_specs=(
            P("dp", "ctx", None),
            P("dp", "ctx", None),
            P(("dp", "ctx")),
            P(("dp", "ctx"), "tensor"),
            P(("dp", "ctx"), "tensor"),
            P(("dp", "ctx"), "tensor"),
            P("tensor", ("dp", "ctx")),
            P(("dp", "ctx")),
            P(("dp", "ctx"), "tensor"),
            P(("dp", "ctx"), "tensor"),
            P("tensor", ("dp", "ctx")),
        ),
        check_vma=False,
    )


def solution(mesh):
    def whole(*arrays):
        return placed(mesh, on_plane if fits_plane(mesh, arrays) else on_device)(*arrays)

    return whole
```

```python
import functools
import math

import jax
import jax.numpy as jnp
from jax import lax
from jax.experimental import pallas as pl
from jax.experimental.pallas import tpu as pltpu
from jax.sharding import PartitionSpec as P

HEAD_DIM = 64


EPSILON = 1e-05
ROPE_BASE = 500000.0


def rotate(values, cosine, sine_val):
    middle = values.shape[-1] // 2
    leading = values[..., :middle]
    trailing = values[..., middle:]
    return jnp.concatenate(
        [leading * cosine - trailing * sine_val, trailing * cosine + leading * sine_val], axis=-1
    )


def unrotate(gradient, cosine, sine_val):
    middle = gradient.shape[-1] // 2
    leading = gradient[..., :middle]
    trailing = gradient[..., middle:]
    return jnp.concatenate(
        [leading * cosine + trailing * sine_val, trailing * cosine - leading * sine_val], axis=-1
    )


def angles(positions, head_dim):
    exponent = jnp.arange(head_dim // 2).astype(jnp.float32) * (
        -2.0 * math.log(ROPE_BASE) / head_dim
    )
    return positions.astype(jnp.float32)[:, None] * jnp.exp(exponent)[None, :]


def rms_factor(row_values):
    return lax.rsqrt(jnp.mean(row_values * row_values, axis=-1, keepdims=True) + EPSILON)


def rms_back(upstream, row_values, factor, gain_row):
    scaled = upstream * gain_row
    gain_term = jnp.sum(upstream * row_values * factor, axis=0)
    inner_mean = jnp.mean(scaled * row_values, axis=-1, keepdims=True)
    return (factor * scaled - row_values * (factor * factor * factor) * inner_mean, gain_term)


def matmul_t(left_op, right_op):
    return lax.dot_general(
        left_op, right_op, (((0,), (0,)), ((), ())), preferred_element_type=jnp.float32
    )


def matmul_nt(left_op, right_op):
    return lax.dot_general(
        left_op, right_op, (((1,), (1,)), ((), ())), preferred_element_type=jnp.float32
    )


def on_device(
    layer_input,
    attn_gain,
    w_query,
    w_key,
    w_value,
    w_out,
    ffn_gain,
    w_gate,
    w_up,
    w_down,
    cotangent,
):
    seq_dev, span_len, model_width = layer_input.shape
    row_count = seq_dev * span_len
    length_all = span_len * lax.axis_size("ctx")
    full_q, full_k, full_v, full_o, full_gate, full_up, full_down, gain_attn, gain_ffn = (
        lax.all_gather(w_query, ("dp", "ctx"), axis=0, tiled=True),
        lax.all_gather(w_key, ("dp", "ctx"), axis=0, tiled=True),
        lax.all_gather(w_value, ("dp", "ctx"), axis=0, tiled=True),
        lax.all_gather(w_out, ("dp", "ctx"), axis=1, tiled=True),
        lax.all_gather(w_gate, ("dp", "ctx"), axis=0, tiled=True),
        lax.all_gather(w_up, ("dp", "ctx"), axis=0, tiled=True),
        lax.all_gather(w_down, ("dp", "ctx"), axis=1, tiled=True),
        lax.all_gather(attn_gain, ("dp", "ctx"), axis=0, tiled=True),
        lax.all_gather(ffn_gain, ("dp", "ctx"), axis=0, tiled=True),
    )
    kv_local = full_k.shape[1] // HEAD_DIM
    group_size = full_q.shape[1] // HEAD_DIM // kv_local
    block_count = seq_dev * kv_local
    scale = HEAD_DIM ** (-0.5)
    query_pos = lax.axis_index("ctx") * span_len + jnp.arange(span_len)
    theta = angles(query_pos, HEAD_DIM)
    cosine = jnp.cos(theta)
    sine_val = jnp.sin(theta)
    causal = query_pos[:, None] >= jnp.arange(length_all)[None, :]
    inputs_f = layer_input.reshape(row_count, model_width).astype(jnp.float32)
    gain_one = gain_attn.astype(jnp.float32)
    gain_two = gain_ffn.astype(jnp.float32)
    factor_one = rms_factor(inputs_f)
    normed_one = (inputs_f * factor_one * gain_one).astype(jnp.bfloat16)
    query_pre = jnp.dot(normed_one, full_q, preferred_element_type=jnp.float32).reshape(
        seq_dev, span_len, kv_local, group_size, HEAD_DIM
    )
    queries = rotate(
        query_pre, cosine[None, :, None, None, :], sine_val[None, :, None, None, :]
    ).astype(jnp.bfloat16)
    key_pre = jnp.dot(normed_one, full_k, preferred_element_type=jnp.float32).reshape(
        seq_dev, span_len, kv_local, HEAD_DIM
    )
    keys_own = (
        rotate(key_pre, cosine[None, :, None, :], sine_val[None, :, None, :])
        .astype(jnp.bfloat16)
        .reshape(seq_dev, span_len, kv_local * HEAD_DIM)
    )
    values_own = (
        jnp.dot(normed_one, full_v, preferred_element_type=jnp.float32)
        .astype(jnp.bfloat16)
        .reshape(seq_dev, span_len, kv_local * HEAD_DIM)
    )
    keys_all, values_all = (
        lax.all_gather(keys_own, "ctx", axis=1, tiled=True),
        lax.all_gather(values_own, "ctx", axis=1, tiled=True),
    )
    query_blocks = jnp.transpose(queries, (0, 2, 1, 3, 4)).reshape(
        block_count, span_len, group_size, HEAD_DIM
    )
    key_blocks = jnp.transpose(
        keys_all.reshape(seq_dev, length_all, kv_local, HEAD_DIM), (0, 2, 1, 3)
    ).reshape(block_count, length_all, HEAD_DIM)
    value_blocks = jnp.transpose(
        values_all.reshape(seq_dev, length_all, kv_local, HEAD_DIM), (0, 2, 1, 3)
    ).reshape(block_count, length_all, HEAD_DIM)

    def scores_of(query_b, key_b):
        raw_scores = jnp.einsum("qgd,kd->gqk", query_b, key_b, preferred_element_type=jnp.float32)
        return jnp.where(causal[None], raw_scores * scale, -1e30)

    def attend(block_in):
        query_b, key_b, value_b = block_in
        scores = scores_of(query_b, key_b)
        peak_row = jnp.max(scores, axis=-1, keepdims=True)
        powers = jnp.exp(scores - peak_row)
        total_sum = jnp.sum(powers, axis=-1, keepdims=True)
        probability = (powers / total_sum).astype(jnp.bfloat16)
        mixed = jnp.einsum("gqk,kd->qgd", probability, value_b, preferred_element_type=jnp.float32)
        return (mixed.astype(jnp.bfloat16), peak_row + jnp.log(total_sum))

    mixed_blocks, logsum = lax.map(attend, (query_blocks, key_blocks, value_blocks))
    attended = jnp.transpose(
        mixed_blocks.reshape(seq_dev, kv_local, span_len, group_size, HEAD_DIM), (0, 2, 1, 3, 4)
    ).reshape(row_count, kv_local * group_size * HEAD_DIM)
    attn_part = jnp.dot(attended, full_o, preferred_element_type=jnp.float32)
    hidden = inputs_f + lax.psum(attn_part, "tensor")
    factor_two = rms_factor(hidden)
    normed_two = (hidden * factor_two * gain_two).astype(jnp.bfloat16)
    gate_pre = jnp.dot(normed_two, full_gate, preferred_element_type=jnp.float32)
    up_pre = jnp.dot(normed_two, full_up, preferred_element_type=jnp.float32)
    sigma = jax.nn.sigmoid(gate_pre)
    product = (gate_pre * sigma * up_pre).astype(jnp.bfloat16)
    ffn_part = jnp.dot(product, full_down, preferred_element_type=jnp.float32)
    out_f = hidden + lax.psum(ffn_part.astype(jnp.bfloat16), "tensor").astype(jnp.float32)
    layer_output = out_f.astype(jnp.bfloat16).reshape(seq_dev, span_len, model_width)
    grad_out = cotangent.reshape(row_count, model_width).astype(jnp.float32)
    grad_low = cotangent.reshape(row_count, model_width)
    down_grad = matmul_t(product, grad_low)
    prod_grad = matmul_nt(grad_low, full_down)
    gate_grad = (prod_grad * up_pre * sigma * (1.0 + gate_pre * (1.0 - sigma))).astype(jnp.bfloat16)
    up_grad = (prod_grad * gate_pre * sigma).astype(jnp.bfloat16)
    gate_w_grad = matmul_t(normed_two, gate_grad)
    up_w_grad = matmul_t(normed_two, up_grad)
    normed_two_part = matmul_nt(gate_grad, full_gate) + matmul_nt(up_grad, full_up)
    normed_two_grad = lax.psum(normed_two_part, "tensor")
    hidden_back, ffn_gain_term = rms_back(normed_two_grad, hidden, factor_two, gain_two)
    hidden_grad = grad_out + hidden_back
    hidden_low = hidden_grad.astype(jnp.bfloat16)
    out_w_grad = matmul_t(attended, hidden_low)
    attended_grad = matmul_nt(hidden_low, full_o).astype(jnp.bfloat16)
    upstream_blocks = jnp.transpose(
        attended_grad.reshape(seq_dev, span_len, kv_local, group_size, HEAD_DIM), (0, 2, 1, 3, 4)
    ).reshape(block_count, span_len, group_size, HEAD_DIM)

    def attend_back(block_in):
        query_b, key_b, value_b, logsum_b, upstream_b = block_in
        scores = scores_of(query_b, key_b)
        probability = jnp.exp(scores - logsum_b)
        rounded = probability.astype(jnp.bfloat16)
        value_grad = jnp.einsum(
            "gqk,qgd->kd", rounded, upstream_b, preferred_element_type=jnp.float32
        )
        prob_grad = jnp.einsum(
            "qgd,kd->gqk", upstream_b, value_b, preferred_element_type=jnp.float32
        )
        inner_sum = jnp.sum(probability * prob_grad, axis=-1, keepdims=True)
        score_grad = (probability * (prob_grad - inner_sum)).astype(jnp.bfloat16)
        query_grad = (
            jnp.einsum("gqk,kd->qgd", score_grad, key_b, preferred_element_type=jnp.float32) * scale
        )
        key_grad = (
            jnp.einsum("gqk,qgd->kd", score_grad, query_b, preferred_element_type=jnp.float32)
            * scale
        )
        return (query_grad, key_grad, value_grad)

    query_grads, key_grads, value_grads = lax.map(
        attend_back, (query_blocks, key_blocks, value_blocks, logsum, upstream_blocks)
    )
    key_rows = jnp.transpose(
        key_grads.reshape(seq_dev, kv_local, length_all, HEAD_DIM), (0, 2, 1, 3)
    ).reshape(seq_dev, length_all, kv_local * HEAD_DIM)
    value_rows = jnp.transpose(
        value_grads.reshape(seq_dev, kv_local, length_all, HEAD_DIM), (0, 2, 1, 3)
    ).reshape(seq_dev, length_all, kv_local * HEAD_DIM)
    key_mine, value_mine = (
        lax.psum_scatter(key_rows, "ctx", scatter_dimension=1, tiled=True),
        lax.psum_scatter(value_rows, "ctx", scatter_dimension=1, tiled=True),
    )
    key_low = (
        unrotate(
            key_mine.reshape(seq_dev, span_len, kv_local, HEAD_DIM),
            cosine[None, :, None, :],
            sine_val[None, :, None, :],
        )
        .astype(jnp.bfloat16)
        .reshape(row_count, kv_local * HEAD_DIM)
    )
    value_low = value_mine.astype(jnp.bfloat16).reshape(row_count, kv_local * HEAD_DIM)
    query_rot = jnp.transpose(
        query_grads.reshape(seq_dev, kv_local, span_len, group_size, HEAD_DIM), (0, 2, 1, 3, 4)
    )
    query_low = (
        unrotate(query_rot, cosine[None, :, None, None, :], sine_val[None, :, None, None, :])
        .astype(jnp.bfloat16)
        .reshape(row_count, kv_local * group_size * HEAD_DIM)
    )
    query_w_grad = matmul_t(normed_one, query_low)
    key_w_grad = matmul_t(normed_one, key_low)
    value_w_grad = matmul_t(normed_one, value_low)
    normed_one_part = (
        matmul_nt(query_low, full_q) + matmul_nt(key_low, full_k) + matmul_nt(value_low, full_v)
    )
    normed_one_grad = lax.psum(normed_one_part.astype(jnp.bfloat16), "tensor").astype(jnp.float32)
    input_back, attn_gain_term = rms_back(normed_one_grad, inputs_f, factor_one, gain_one)
    input_grad = (hidden_grad + input_back).reshape(seq_dev, span_len, model_width)
    (
        query_sum,
        key_sum,
        value_sum,
        out_sum,
        gate_sum,
        up_sum,
        down_sum,
        attn_gain_sum,
        ffn_gain_sum,
    ) = (
        lax.psum_scatter(query_w_grad, ("dp", "ctx"), scatter_dimension=0, tiled=True),
        lax.psum_scatter(key_w_grad, ("dp", "ctx"), scatter_dimension=0, tiled=True),
        lax.psum_scatter(value_w_grad, ("dp", "ctx"), scatter_dimension=0, tiled=True),
        lax.psum_scatter(out_w_grad, ("dp", "ctx"), scatter_dimension=1, tiled=True),
        lax.psum_scatter(gate_w_grad, ("dp", "ctx"), scatter_dimension=0, tiled=True),
        lax.psum_scatter(up_w_grad, ("dp", "ctx"), scatter_dimension=0, tiled=True),
        lax.psum_scatter(down_grad, ("dp", "ctx"), scatter_dimension=1, tiled=True),
        lax.psum_scatter(attn_gain_term, ("dp", "ctx"), scatter_dimension=0, tiled=True),
        lax.psum_scatter(ffn_gain_term, ("dp", "ctx"), scatter_dimension=0, tiled=True),
    )
    return (
        layer_output,
        input_grad,
        attn_gain_sum,
        query_sum,
        key_sum,
        value_sum,
        out_sum,
        ffn_gain_sum,
        gate_sum,
        up_sum,
        down_sum,
    )


MESH_ID = pl.DeviceIdType.MESH
BF16 = jnp.bfloat16
F32 = jnp.float32
QB = 256


def place():
    side = lax.axis_index("tensor")
    ctx = lax.axis_index("ctx")
    row = ctx // 2
    core = ctx % 2
    near_core = {"ctx": row * 2 + (1 - core)}
    near_side = {"tensor": 1 - side}
    near_row = {"ctx": (1 - row) * 2 + core}
    return side, row, core, near_core, near_side, near_row


def greet(neighbours):
    barrier = pltpu.get_barrier_semaphore()
    for target in neighbours:
        pl.semaphore_signal(barrier, inc=1, device_id=target, device_id_type=MESH_ID)
    pl.semaphore_wait(barrier, len(neighbours))


def remote(source, target, send_sem, recv_sem, device):
    return pltpu.make_async_remote_copy(
        src_ref=source,
        dst_ref=target,
        send_sem=send_sem,
        recv_sem=recv_sem,
        device_id=device,
        device_id_type=MESH_ID,
    )


def gather_kernel(rows, works, planes, block_ref, *refs):
    if works:
        left_ref, right_ref, all_ref, grad_ref, send_sems, recv_sems, local_sem = refs
    elif planes:
        gains_ref, all_ref, all_gains_ref, send_sems, recv_sems, local_sem, *gain_sems = refs
    else:
        all_ref, send_sems, recv_sems, local_sem = refs
    side, row, core, near_core, near_side, near_row = place()
    half = rows // 2

    def work(first, last):
        if not works:
            return
        size = left_ref.shape[1] // works

        def step(index, carry):
            at = pl.ds(pl.multiple_of(index * size, size), size)
            grad_ref[at, :] = matmul_t(left_ref[:, at], right_ref[...]).astype(BF16)
            return carry

        lax.fori_loop(first * works // 8, last * works // 8, step, 0)

    def spot(a, b, c, part=None):
        start = (a * 4 + b * 2 + c) * rows
        if part is None:
            return all_ref.at[pl.ds(pl.multiple_of(start, rows), rows)]
        return all_ref.at[pl.ds(pl.multiple_of(start + part * half, half), half)]

    targets = []
    if planes:
        plane = lax.axis_index("dp")
        here = row * 2 + core
        targets = [
            {"dp": (plane + step) % planes, "ctx": (here + turn) % 4}
            for step in range(planes)
            for turn in range(4)
            if step or turn
        ]
    greet([near_side] + (targets if planes else [near_core, near_row]))
    copies = []

    def send(number, source, target, device):
        copy = remote(source, target, send_sems.at[number], recv_sems.at[number], device)
        copy.start()
        copies.append(copy)
        return copy

    gain_copies = []
    if planes:
        mine = all_gains_ref.at[plane * 4 + here]
        gain_copies = [
            remote(gains_ref, mine, gain_sems[0].at[at], gain_sems[1].at[at], target)
            for at, target in enumerate(targets)
        ] + [pltpu.make_async_copy(gains_ref, mine, gain_sems[2])]
        for copy in gain_copies:
            copy.start()
    first = block_ref.at[pl.ds(0, half)]
    second = block_ref.at[pl.ds(half, half)]
    side_b = send(0, second, spot(side, row, core, 1), near_side)
    row_a = send(1, first, spot(side, row, core, 0), near_row)
    side_a = send(2, first, spot(side, row, core, 0), near_side)
    row_b = send(3, second, spot(side, row, core, 1), near_row)
    core_own = send(4, block_ref, spot(side, row, core), near_core)
    local = pltpu.make_async_copy(block_ref, spot(side, row, core), local_sem)
    local.start()
    work(0, 6)
    side_b.wait_recv()
    away_b = send(5, spot(1 - side, row, core, 1), spot(1 - side, row, core, 1), near_row)
    row_a.wait_recv()
    away_a = send(6, spot(side, 1 - row, core, 0), spot(side, 1 - row, core, 0), near_side)
    work(6, 8)
    side_a.wait_recv()
    core_side = send(7, spot(1 - side, row, core), spot(1 - side, row, core), near_core)
    row_b.wait_recv()
    core_row = send(8, spot(side, 1 - row, core), spot(side, 1 - row, core), near_core)
    away_a.wait_recv()
    core_away_a = send(
        9, spot(1 - side, 1 - row, core, 0), spot(1 - side, 1 - row, core, 0), near_core
    )
    away_b.wait_recv()
    core_away_b = send(
        10, spot(1 - side, 1 - row, core, 1), spot(1 - side, 1 - row, core, 1), near_core
    )
    for copy in (core_own, core_side, core_row, core_away_a, core_away_b):
        copy.wait_recv()
    for copy in copies:
        copy.wait_send()
    for copy in gain_copies:
        copy.wait()
    local.wait()


def plane_gather(block, number=0, pair=None, gains=None):
    rows, width = block.shape
    anywhere, vmem = pl.BlockSpec(memory_space=pl.ANY), pl.BlockSpec(memory_space=pltpu.VMEM)
    shapes, ins, outs = [jax.ShapeDtypeStruct((8 * rows, width), block.dtype)], [anywhere], [anywhere]
    operands = [block]
    if pair is not None:
        shapes.append(jax.ShapeDtypeStruct((pair[0].shape[1], pair[1].shape[1]), BF16))
        ins += [vmem, vmem]
        outs += [vmem]
        operands += pair
    planes, scratch = 0, []
    if gains is not None:
        planes = lax.axis_size("dp")
        shapes.append(jax.ShapeDtypeStruct((4 * planes,) + gains.shape, gains.dtype))
        ins += [vmem]
        outs += [vmem]
        operands += [gains]
        scratch = [pltpu.SemaphoreType.DMA((4 * planes - 1,))] * 2 + [pltpu.SemaphoreType.DMA]
    return pl.pallas_call(
        functools.partial(gather_kernel, rows, 8 if pair is not None else 0, planes),
        out_shape=tuple(shapes),
        in_specs=ins,
        out_specs=tuple(outs),
        scratch_shapes=[
            pltpu.SemaphoreType.DMA((11,)),
            pltpu.SemaphoreType.DMA((11,)),
            pltpu.SemaphoreType.DMA,
        ]
        + scratch,
        compiler_params=pltpu.CompilerParams(
            collective_id=number, has_side_effects=True, vmem_limit_bytes=60 * 1024 * 1024
        ),
        cost_estimate=pl.CostEstimate(flops=0, bytes_accessed=1024, transcendentals=0),
        name="plane_gather",
    )(*operands)


def swap_scratch():
    return [pltpu.SemaphoreType.DMA((3,))] * 2 + [pltpu.SemaphoreType.DMA]


def swap_copies(in_ref, out_ref, send_sems, recv_sems, local_sem):
    _, row, core, *_ = place()
    rows = out_ref.shape[1]
    here = row * 2 + core

    def block(index):
        return in_ref.at[pl.ds(pl.multiple_of(index * rows, rows), rows)]

    peers = (row * 2 + 1 - core, (1 - row) * 2 + core, (1 - row) * 2 + 1 - core)
    away = [
        remote(block(peer), out_ref.at[here], send_sems.at[at], recv_sems.at[at], {"ctx": peer})
        for at, peer in enumerate(peers)
    ]
    return away, pltpu.make_async_copy(block(here), out_ref.at[here], local_sem)


def norm_back(rows, grad_ref, value_ref, factor_ref, gain_ref, base_ref, out_ref, low_ref, term_ref):
    tile = 32
    gain = gain_ref[...]

    def step(index, total):
        here = pl.ds(pl.multiple_of(index * tile, tile), tile)
        grad, value, factor = grad_ref[here, :], value_ref[here, :], factor_ref[here, :]
        scaled = grad * gain
        inner = jnp.mean(scaled * value, axis=1, keepdims=True)
        back = factor * scaled - value * (factor * factor * factor) * inner
        result = base_ref[here, :].astype(F32) + back
        if out_ref is not None:
            out_ref[here, :] = result
        low_ref[here, :] = result.astype(BF16)
        return total + jnp.sum(grad * value * factor, axis=0, keepdims=True)

    total = lax.fori_loop(0, rows // tile, step, jnp.zeros((1, gain.shape[1]), F32))
    term_ref[...] = jnp.broadcast_to(total, term_ref.shape)


def scatter_steps(rows, left_of, right_of, out_ref, scratch, swap=None, late=None):
    made, other, to_side, to_row, from_side, from_row = scratch[:6]
    on_side, on_row, got_side, got_row, send_sems, recv_sems = scratch[6:]
    side, row, core, near_core, near_side, near_row = place()
    tile = 32
    wide = out_ref.shape[1] // 2

    chips = ((side, row), (1 - side, row), (side, 1 - row), (1 - side, 1 - row))
    routes = [
        (made.at[chip, part, 1 - core], other.at[chip, part], near_core)
        for chip in range(4)
        for part in range(2)
    ] + [
        (to_side.at[0], from_side.at[0], near_side),
        (to_row.at[0], from_row.at[0], near_row),
        (to_side.at[1], from_side.at[1], near_side),
        (to_row.at[1], from_row.at[1], near_row),
        (on_row, got_row, near_row),
        (on_side, got_side, near_side),
    ]
    copies = [
        remote(source, target, send_sems.at[at], recv_sems.at[at], device)
        for at, (source, target, device) in enumerate(routes)
    ]
    side_0, row_0, side_1, row_1, last_row, last_side = copies[8:]
    swapped = None if swap is None else swap_copies(*swap)

    def make(chip, part, first=False):
        a, b = chips[chip]
        start = pl.multiple_of((a * 4 + b * 2) * rows, 2 * rows)
        value = matmul_nt(left_of(chip, start), right_of(pl.ds(part * wide, wide)))
        made[chip, part, 0] = value[:rows].astype(BF16)
        made[chip, part, 1] = value[rows:].astype(BF16)
        if first:
            partners = (near_core, near_side, near_row)
            if swap is not None:
                partners += ({"ctx": (1 - row) * 2 + 1 - core},)
            greet(partners)
        copies[2 * chip + part].start()

    def both(chip, part, at):
        here = made[chip, part, core, pl.ds(at, tile), :].astype(F32)
        return here + other[chip, part, pl.ds(at, tile), :].astype(F32)

    def each(body):
        def step(index, carry):
            body(pl.multiple_of(index * tile, tile))
            return carry

        lax.fori_loop(0, rows // tile, step, 0)

    def put(target, chip, part, copy, extra=None):
        copies[2 * chip + part].wait_recv()

        def body(at):
            value = both(chip, part, at)
            if extra is not None:
                value = value + extra[pl.ds(at, tile), :].astype(F32)
            target[pl.ds(at, tile), :] = value.astype(BF16)

        each(body)
        copy.start()

    def across():
        make(3, 0, True)
        make(3, 1)
        put(to_side.at[0], 3, 0, side_0)
        put(to_row.at[0], 3, 1, row_0)
        if swap is not None:
            for copy in swapped[0] + [swapped[1]]:
                copy.start()

    def along():
        make(1, 0)
        make(2, 1)
        put(to_side.at[1], 1, 0, side_1)
        put(to_row.at[1], 2, 1, row_1)

    def forward():
        make(1, 1)
        make(2, 0)
        row_0.wait_recv()
        put(on_side, 1, 1, last_side, from_row.at[0])
        side_0.wait_recv()
        put(on_row, 2, 0, last_row, from_side.at[0])

    def own():
        make(0, 0)
        make(0, 1)

    def finish():
        copies[0].wait_recv()
        copies[1].wait_recv()
        side_1.wait_recv()
        row_1.wait_recv()

        def first_sum(at):
            here = pl.ds(at, tile)
            out_ref[here, :wide] = both(0, 0, at) + from_side[1, here, :].astype(F32)
            out_ref[here, wide:] = both(0, 1, at) + from_row[1, here, :].astype(F32)

        each(first_sum)
        if swap is not None:
            for copy in swapped[0]:
                copy.wait()
            swapped[1].wait()
            late()
        last_side.wait_recv()
        last_row.wait_recv()

        def last_sum(at):
            here = pl.ds(at, tile)
            out_ref[here, :wide] += got_row[here, :].astype(F32)
            out_ref[here, wide:] += got_side[here, :].astype(F32)

        each(last_sum)
        for copy in copies:
            copy.wait_send()

    return across, along, forward, own, finish


def scatter_scratch(rows, width):
    half = width // 2
    return (
        [pltpu.VMEM((4, 2, 2, rows, half), BF16), pltpu.VMEM((4, 2, rows, half), BF16)]
        + [pltpu.VMEM((2, rows, half), BF16)] * 4
        + [pltpu.VMEM((rows, half), BF16)] * 4
        + [pltpu.SemaphoreType.DMA((14,))] * 2
    )


def scatter_kernel(rows, swaps, columns, left, right, *refs):
    swap, late = None, None
    if swaps:
        in_ref, value_ref, factor_ref, gain_ref, base_ref, low_ref, term_ref, laid_ref = refs[:8]
        out_ref, *scratch = refs[8:]
        swapped = scratch[-4]
        swap = (in_ref, swapped, *scratch[-3:])
        scratch = scratch[:-4]

        def late():
            size = swapped.shape[2]
            for part in range(4):
                laid_ref[:, part * size : (part + 1) * size] = swapped[part]

    else:
        out_ref, *scratch = refs

    def left_of(chip, start):
        return left[pl.ds(start, 2 * rows), :]

    def right_of(at):
        return right[at, columns]

    for step in scatter_steps(rows, left_of, right_of, out_ref, scratch, swap=swap, late=late):
        step()
    if swaps:
        norm_back(
            rows, out_ref, value_ref, factor_ref, gain_ref, base_ref, None, low_ref, term_ref
        )


def product_scatter(number, left, right, start, size, swap=None, norm=()):
    total = left.shape[0]
    width = right.shape[0]
    rows = total // 8
    vmem = pl.BlockSpec(memory_space=pltpu.VMEM)
    if swap is None:
        shapes, ins, scratch = [jax.ShapeDtypeStruct((rows, width), F32)], [vmem, vmem], []
        operands = [left, right]
    else:
        deep = swap.shape[0] // 4
        shapes = [
            jax.ShapeDtypeStruct((rows, width), BF16),
            jax.ShapeDtypeStruct((8, width), F32),
            jax.ShapeDtypeStruct((deep, 4 * swap.shape[1]), swap.dtype),
        ]
        ins = [vmem, vmem, pl.BlockSpec(memory_space=pl.ANY)] + [vmem] * 4
        operands = [left, right, swap, *norm]
        scratch = [pltpu.VMEM((4, deep, swap.shape[1]), swap.dtype)] + swap_scratch()
    return pl.pallas_call(
        functools.partial(scatter_kernel, rows, swap is not None, slice(start, start + size)),
        out_shape=tuple(shapes),
        in_specs=ins,
        out_specs=tuple([vmem] * len(shapes)),
        scratch_shapes=([pltpu.VMEM((rows, width), F32)] if swap is not None else [])
        + scatter_scratch(rows, width)
        + scratch,
        compiler_params=pltpu.CompilerParams(
            collective_id=number, has_side_effects=True, vmem_limit_bytes=56 * 1024 * 1024
        ),
        cost_estimate=pl.CostEstimate(flops=0, bytes_accessed=1024, transcendentals=0),
        name="product_scatter",
    )(*operands)


def ffn_back_kernel(
    rows,
    own_ref,
    far_ref,
    twin_ref,
    twin_far_ref,
    gate_slope_ref,
    up_slope_ref,
    down_ref,
    right_ref,
    value_ref,
    factor_ref,
    gain_ref,
    base_ref,
    result_ref,
    low_ref,
    term_ref,
    gate_ref,
    up_ref,
    out_ref,
    cots,
    gate_slopes,
    up_slopes,
    lefts,
    sems,
    out_sems,
    *scratch,
):
    side, row, core, *_ = place()
    units = down_ref.shape[1]
    turns = (3, 1, 2, 0)
    chips = ((side, row), (1 - side, row), (side, 1 - row), (1 - side, 1 - row))
    starts = [pl.multiple_of((a * 4 + b * 2) * rows, 2 * rows) for a, b in chips]
    stored = []

    def fetch(turn):
        chip = turns[turn]
        near, away = (own_ref, twin_ref) if chip < 2 else (far_ref, twin_far_ref)
        there = pl.ds(starts[chip], 2 * rows)
        slot = turn % 2
        return [
            pltpu.make_async_copy(source, target, sems.at[which, slot])
            for which, (source, target) in enumerate(
                (
                    (near.at[chips[chip][0]], cots.at[slot, core]),
                    (away.at[chips[chip][0]], cots.at[slot, 1 - core]),
                    (gate_slope_ref.at[there], gate_slopes.at[slot]),
                    (up_slope_ref.at[there], up_slopes.at[slot]),
                )
            )
        ]

    def store(turn):
        there = pl.ds(starts[turns[turn]], 2 * rows)
        slot = turn % 2
        return [
            pltpu.make_async_copy(
                lefts.at[slot, :, pl.ds(which * units, units)],
                target.at[there],
                out_sems.at[which, slot],
            )
            for which, target in enumerate((gate_ref, up_ref))
        ]

    def start(copies):
        for copy in copies:
            copy.start()

    def wait(copies):
        for copy in copies:
            copy.wait()

    def left_of(chip, _):
        turn = turns.index(chip)
        slot = turn % 2
        if chip in stored:
            return lefts[slot]
        stored.append(chip)
        if turn == 0:
            start(fetch(0))
        if turn == 1:
            start(fetch(2))
        if turn == 2:
            start(fetch(3))
        if turn == 0:
            start(fetch(1))
        wait(fetch(turn))
        if turn > 1:
            wait(store(turn - 2))
        cot = cots[slot].reshape(2 * rows, cots.shape[3])
        grad = jnp.dot(cot, down_ref[...], preferred_element_type=F32)
        lefts[slot, :, :units] = (grad * gate_slopes[slot].astype(F32)).astype(BF16)
        lefts[slot, :, units:] = (grad * up_slopes[slot].astype(F32)).astype(BF16)
        start(store(turn))
        return lefts[slot]

    def right_of(at):
        return right_ref[at, :]

    for step in scatter_steps(rows, left_of, right_of, out_ref, scratch):
        step()
    norm_back(
        rows, out_ref, value_ref, factor_ref, gain_ref, base_ref, result_ref, low_ref, term_ref
    )
    wait(store(2))
    wait(store(3))


def ffn_back(number, cots, gate_slope, up_slope, down_w, gate_up, norm):
    total, units = gate_slope.shape
    width = down_w.shape[0]
    rows = total // 8
    vmem = pl.BlockSpec(memory_space=pltpu.VMEM)
    anywhere = pl.BlockSpec(memory_space=pl.ANY)
    return pl.pallas_call(
        functools.partial(ffn_back_kernel, rows),
        out_shape=(
            jax.ShapeDtypeStruct((rows, width), F32),
            jax.ShapeDtypeStruct((rows, width), BF16),
            jax.ShapeDtypeStruct((8, width), F32),
            jax.ShapeDtypeStruct((total, units), BF16),
            jax.ShapeDtypeStruct((total, units), BF16),
        ),
        in_specs=[anywhere] * 6 + [vmem] * 6,
        out_specs=(vmem, vmem, vmem, anywhere, anywhere),
        scratch_shapes=[
            pltpu.VMEM((rows, width), F32),
            pltpu.VMEM((2, 2, rows, width), BF16),
            pltpu.VMEM((2, 2 * rows, units), BF16),
            pltpu.VMEM((2, 2 * rows, units), BF16),
            pltpu.VMEM((2, 2 * rows, 2 * units), BF16),
            pltpu.SemaphoreType.DMA((4, 2)),
            pltpu.SemaphoreType.DMA((2, 2)),
        ]
        + scatter_scratch(rows, width),
        compiler_params=pltpu.CompilerParams(
            collective_id=number, has_side_effects=True, vmem_limit_bytes=60 * 1024 * 1024
        ),
        cost_estimate=pl.CostEstimate(flops=0, bytes_accessed=1024, transcendentals=0),
        name="ffn_back",
    )(*cots, gate_slope, up_slope, down_w, gate_up, *norm)


def ffn_kernel(in_ref, w_ref, product_ref, gate_slope_ref, up_slope_ref):
    units = product_ref.shape[1]
    wide = 512
    rows_in = in_ref[...]
    for start in range(0, units, wide):
        at = pl.ds(start, wide)
        gate = jnp.dot(rows_in, w_ref[:, at], preferred_element_type=F32)
        up = jnp.dot(rows_in, w_ref[:, pl.ds(units + start, wide)], preferred_element_type=F32)
        sigma = jax.nn.sigmoid(gate)
        active = gate * sigma
        product_ref[:, at] = (active * up).astype(BF16)
        gate_slope_ref[:, at] = (up * sigma * (1.0 + gate * (1.0 - sigma))).astype(BF16)
        up_slope_ref[:, at] = active.astype(BF16)


def ffn(rows_in, gate_up):
    total, width = rows_in.shape
    units = gate_up.shape[1] // 2
    rows = 512
    out = pl.BlockSpec((rows, units), lambda i: (i, 0))
    return pl.pallas_call(
        ffn_kernel,
        grid=(total // rows,),
        out_shape=(jax.ShapeDtypeStruct((total, units), BF16),) * 3,
        in_specs=[
            pl.BlockSpec((rows, width), lambda i: (i, 0)),
            pl.BlockSpec(
                (width, 2 * units), lambda i: (0, 0), pipeline_mode=pl.Buffered(1)
            ),
        ],
        out_specs=(out, out, out),
        compiler_params=pltpu.CompilerParams(vmem_limit_bytes=60 * 1024 * 1024),
        cost_estimate=pl.CostEstimate(flops=0, bytes_accessed=1024, transcendentals=0),
        name="ffn",
    )(rows_in, gate_up)


def swap_halves(values):
    width = values.shape[-1]
    lane = lax.broadcasted_iota(jnp.int32, values.shape, 1)
    ahead = pltpu.roll(values, width - HEAD_DIM // 2, 1)
    behind = pltpu.roll(values, HEAD_DIM // 2, 1)
    return jnp.where(lane % HEAD_DIM < HEAD_DIM // 2, ahead, behind)


def pieces_of(block):
    return ((0, block * QB, False), (block * QB, QB, True)) if block else ((0, QB, True),)


def masked_scores(query, keys, diagonal):
    scores = matmul_nt(query, keys)
    if diagonal:
        here = lax.broadcasted_iota(jnp.int32, scores.shape, 0)
        there = lax.broadcasted_iota(jnp.int32, scores.shape, 1)
        scores = jnp.where(here >= there, scores, -1e30)
    return scores


def attend_kernel(length, q_ref, kv_ref, cos_ref, sin_ref, att_ref, qrot_ref, kvrot_ref, log_ref):
    cosine = cos_ref[...]
    signed = sin_ref[...]
    scale = HEAD_DIM ** (-0.5)
    pre = q_ref[...]
    qrot_ref[...] = (pre * cosine + swap_halves(pre) * signed).astype(BF16)
    pre = kv_ref[...]
    lane = lax.broadcasted_iota(jnp.int32, pre.shape, 1)
    turned = jnp.where(lane < HEAD_DIM, pre * cosine + swap_halves(pre) * signed, pre)
    kvrot_ref[...] = turned.astype(BF16)
    for block in range(length // QB):
        here = pl.ds(block * QB, QB)
        logs = []
        mixed = []
        for head in range(2):
            query = qrot_ref[here, head * HEAD_DIM : (head + 1) * HEAD_DIM] * jnp.asarray(
                scale, BF16
            )
            scores = []
            for start, size, diagonal in pieces_of(block):
                keys = kvrot_ref[pl.ds(start, size), :HEAD_DIM]
                scores.append(masked_scores(query, keys, diagonal))
            peak = functools.reduce(
                jnp.maximum, [jnp.max(s, axis=1, keepdims=True) for s in scores]
            )
            powers = [jnp.exp(s - peak) for s in scores]
            total = sum(jnp.sum(p, axis=1, keepdims=True) for p in powers)
            inverse = 1.0 / total
            out = None
            for (start, size, _), power in zip(pieces_of(block), powers):
                values = kvrot_ref[pl.ds(start, size), HEAD_DIM:]
                term = jnp.dot(
                    (power * inverse).astype(BF16), values, preferred_element_type=F32
                )
                out = term if out is None else out + term
            mixed.append(out)
            logs.append(peak + jnp.log(total))
        att_ref[here, :] = jnp.concatenate(mixed, axis=1).astype(BF16)
        lane = lax.broadcasted_iota(jnp.int32, (QB, 128), 1)
        log_ref[here, :] = jnp.where(lane < HEAD_DIM, logs[0], logs[1])


def attend(pre, cosine, signed, seqs):
    rows = pre.shape[0]
    length = rows // seqs
    pairs = pre.shape[1] // 128 - 1
    block = (length, 128)
    return pl.pallas_call(
        functools.partial(attend_kernel, length),
        grid=(seqs, pairs),
        out_shape=(
            jax.ShapeDtypeStruct((rows, pairs * 128), BF16),
            jax.ShapeDtypeStruct((rows, pairs * 128), BF16),
            jax.ShapeDtypeStruct((rows, 128), BF16),
            jax.ShapeDtypeStruct((rows, pairs * 128), F32),
        ),
        in_specs=[
            pl.BlockSpec(block, lambda s, h: (s, h)),
            pl.BlockSpec(block, lambda s, h: (s, pairs)),
            pl.BlockSpec(block, lambda s, h: (0, 0)),
            pl.BlockSpec(block, lambda s, h: (0, 0)),
        ],
        out_specs=(
            pl.BlockSpec(block, lambda s, h: (s, h)),
            pl.BlockSpec(block, lambda s, h: (s, h)),
            pl.BlockSpec(block, lambda s, h: (s, 0)),
            pl.BlockSpec(block, lambda s, h: (s, h)),
        ),
        compiler_params=pltpu.CompilerParams(vmem_limit_bytes=48 * 1024 * 1024),
        cost_estimate=pl.CostEstimate(
            flops=8 * rows * length * 128 * pairs,
            bytes_accessed=rows * pairs * 128 * 12,
            transcendentals=rows * length * 2 * pairs,
        ),
        name="attend",
    )(pre, pre, cosine, signed)


def attend_back_kernel(
    seqs,
    rows,
    q_ref,
    kv_ref,
    up_ref,
    log_ref,
    cos_ref,
    sin_ref,
    left_ref,
    right_ref,
    hidden_ref,
    in_ref,
    back_ref,
    out_ref,
    laid_ref,
    sum_ref,
    ffn_ref,
    swapped,
    *scratch,
):
    def late():
        size = swapped.shape[2]
        for part in range(4):
            turned = jnp.transpose(swapped[part].astype(F32))
            laid_ref[part * size : (part + 1) * size, :] = turned.astype(BF16)

    across, along, forward, own, finish = scatter_steps(
        rows,
        lambda chip, start: left_ref[pl.ds(start, 2 * rows), :],
        lambda at: right_ref[at, :],
        ffn_ref,
        scratch[:-3],
        swap=(in_ref, swapped, *scratch[-3:]),
        late=late,
    )
    scale = HEAD_DIM ** (-0.5)
    length = q_ref.shape[0] // seqs
    pairs = q_ref.shape[1] // 128
    across()
    along()

    def one_pair(index, carry):
        seq = index // pairs
        pair = index % pairs
        lanes_at = pl.ds(pl.multiple_of(pair * 128, 128), 128)
        base = pl.multiple_of(seq * length, length)

        @pl.when(index == 1)
        def _():
            forward()

        @pl.when(index == 2)
        def _():
            own()

        @pl.when(pair == 0)
        def _():
            sum_ref[...] = jnp.zeros_like(sum_ref)

        for block in range(length // QB):
            here = pl.ds(base + block * QB, QB)
            turned = []
            q_pair = q_ref[here, lanes_at]
            up_pair = up_ref[here, lanes_at]
            log_pair = log_ref[here, lanes_at]
            for head in range(2):
                lanes = slice(head * HEAD_DIM, (head + 1) * HEAD_DIM)
                query = q_pair[:, lanes] * jnp.asarray(scale, BF16)
                upstream = up_pair[:, lanes]
                logs = log_pair[:, head * HEAD_DIM : head * HEAD_DIM + 1]
                saved = []
                inner = None
                for start, size, diagonal in pieces_of(block):
                    keys = kv_ref[pl.ds(base + start, size), :HEAD_DIM]
                    values = kv_ref[pl.ds(base + start, size), HEAD_DIM:]
                    probability = jnp.exp(masked_scores(query, keys, diagonal) - logs)
                    prob_grad = matmul_nt(upstream, values)
                    term = jnp.sum(probability * prob_grad, axis=1, keepdims=True)
                    inner = term if inner is None else inner + term
                    saved.append((start, size, probability, prob_grad))
                out = None
                for start, size, probability, prob_grad in saved:
                    keys = kv_ref[pl.ds(base + start, size), :HEAD_DIM]
                    score_grad = (probability * (prob_grad - inner)).astype(BF16)
                    rounded = probability.astype(BF16)
                    term = jnp.dot(score_grad, keys, preferred_element_type=F32)
                    out = term if out is None else out + term
                    sum_ref[pl.ds(start, size), :] += jnp.concatenate(
                        [matmul_t(score_grad, query), matmul_t(rounded, upstream)], axis=1
                    )
                turned.append(out * scale)
            grad = jnp.concatenate(turned, axis=1)
            angle = pl.ds(block * QB, QB)
            back_ref[here, lanes_at] = (
                grad * cos_ref[angle, :] - swap_halves(grad) * sin_ref[angle, :]
            ).astype(BF16)

        @pl.when(pair == pairs - 1)
        def _():
            grad = sum_ref[...]
            lane = lax.broadcasted_iota(jnp.int32, grad.shape, 1)
            back = grad * cos_ref[...] - swap_halves(grad) * sin_ref[...]
            back_ref[pl.ds(base, length), pairs * 128 :] = jnp.where(
                lane < HEAD_DIM, back, grad
            ).astype(BF16)

        return carry

    lax.fori_loop(0, seqs * pairs, one_pair, 0)
    finish()

    def add(index, carry):
        at = pl.ds(pl.multiple_of(index * 32, 32), 32)
        out_ref[at, :] = (hidden_ref[at, :] + ffn_ref[at, :]).astype(BF16)
        return carry

    lax.fori_loop(0, rows // 32, add, 0)


def attend_back(
    number, queries, keyvals, upstream, logs, cosine, signed, seqs, left, right, hidden, swap
):
    total, width = queries.shape
    length = total // seqs
    rows = total // 8
    deep = swap.shape[0] // 4
    vmem = pl.BlockSpec(memory_space=pltpu.VMEM)
    return pl.pallas_call(
        functools.partial(attend_back_kernel, seqs, rows),
        out_shape=(
            jax.ShapeDtypeStruct((total, width + 128), BF16),
            jax.ShapeDtypeStruct(hidden.shape, BF16),
            jax.ShapeDtypeStruct((4 * swap.shape[1], deep), BF16),
        ),
        in_specs=[vmem] * 9 + [pl.BlockSpec(memory_space=pl.ANY)],
        out_specs=(vmem, vmem, vmem),
        scratch_shapes=[
            pltpu.VMEM((length, 128), F32),
            pltpu.VMEM(hidden.shape, F32),
            pltpu.VMEM((4, deep, swap.shape[1]), BF16),
        ]
        + scatter_scratch(rows, right.shape[0])
        + swap_scratch(),
        compiler_params=pltpu.CompilerParams(
            collective_id=number, has_side_effects=True, vmem_limit_bytes=56 * 1024 * 1024
        ),
        cost_estimate=pl.CostEstimate(flops=0, bytes_accessed=1024, transcendentals=0),
        name="attend_back",
    )(queries, keyvals, upstream, logs, cosine, signed, left, right, hidden, swap)


def gain_kernel(
    planes,
    parts,
    cols,
    attn_term_ref,
    ffn_term_ref,
    up_ref,
    gain_ref,
    laid_ref,
    total,
    seen,
    far,
    mine,
    across,
    swapped,
    send_sems,
    recv_sems,
    *swap_sems,
):
    side, row, core, near_core, near_side, near_row = place()
    plane = lax.axis_index("dp")
    ctx = row * 2 + core
    others = [{"dp": (plane + step) % planes} for step in range(1, planes)]
    corner = {"ctx": (1 - row) * 2 + 1 - core}
    greet((near_core, near_side, near_row, corner) + tuple(others))
    first = lax.broadcasted_iota(jnp.int32, total.shape, 0) == 0
    total[...] = jnp.where(first, attn_term_ref[...], ffn_term_ref[...])
    copies = []
    up_copies, up_local = swap_copies(up_ref, swapped, *swap_sems)
    for number, target in enumerate((near_core, near_row)):
        copy = remote(
            total, seen.at[number], send_sems.at[number], recv_sems.at[number], target
        )
        copy.start()
        copy.wait()
        total[...] += seen[number]
    for copy in up_copies + [up_local]:
        copy.start()
    for step, target in enumerate(others, 1):
        start = (((plane + step) % planes) * parts + ctx) * cols
        copy = remote(
            total.at[:, pl.ds(pl.multiple_of(start, cols), cols)],
            far.at[step - 1],
            send_sems.at[2 + step],
            recv_sems.at[2 + step],
            target,
        )
        copy.start()
        copies.append(copy)
    start = (plane * parts + ctx) * cols
    value = total[:, pl.ds(pl.multiple_of(start, cols), cols)]
    for number, copy in enumerate(copies):
        copy.wait_recv()
        value += far[number]
    mine[...] = value
    last = remote(mine, across, send_sems.at[2], recv_sems.at[2], near_side)
    last.start()
    copies.append(last)
    for copy in up_copies:
        copy.wait()
    up_local.wait()
    size = swapped.shape[2]
    for part in range(4):
        laid_ref[:, part * size : (part + 1) * size] = swapped[part]
    last.wait_recv()
    gain_ref[...] = value + across[...]
    for copy in copies:
        copy.wait_send()


def gain_sum(number, attn_term, ffn_term, up_sum):
    planes = lax.axis_size("dp")
    parts = lax.axis_size("ctx")
    rows, width = attn_term.shape
    cols = width // (planes * parts)
    deep = up_sum.shape[0] // parts
    vmem = pl.BlockSpec(memory_space=pltpu.VMEM)
    anywhere = pl.BlockSpec(memory_space=pl.ANY)
    return pl.pallas_call(
        functools.partial(gain_kernel, planes, parts, cols),
        out_shape=(
            jax.ShapeDtypeStruct((rows, cols), F32),
            jax.ShapeDtypeStruct((deep, parts * up_sum.shape[1]), BF16),
        ),
        in_specs=[vmem, vmem, anywhere],
        out_specs=(vmem,) * 2,
        scratch_shapes=[
            pltpu.VMEM((rows, width), F32),
            pltpu.VMEM((2, rows, width), F32),
            pltpu.VMEM((planes - 1, rows, cols), F32),
            pltpu.VMEM((rows, cols), F32),
            pltpu.VMEM((rows, cols), F32),
            pltpu.VMEM((parts, deep, up_sum.shape[1]), BF16),
            pltpu.SemaphoreType.DMA((planes + 2,)),
            pltpu.SemaphoreType.DMA((planes + 2,)),
        ]
        + swap_scratch(),
        compiler_params=pltpu.CompilerParams(collective_id=number, has_side_effects=True),
        cost_estimate=pl.CostEstimate(flops=0, bytes_accessed=1024, transcendentals=0),
        name="gain_sum",
    )(attn_term, ffn_term, up_sum)


def last_kernel(
    q_cols, attn_ref, query_ref, key_ref, value_ref, wide_ref, swapped, *swap_sems
):
    _, row, core, near_core, _, near_row = place()
    greet((near_core, near_row, {"ctx": (1 - row) * 2 + 1 - core}))
    copies, local = swap_copies(attn_ref, swapped, *swap_sems)
    for copy in copies + [local]:
        copy.start()
    for copy in copies:
        copy.wait()
    local.wait()
    kv = key_ref.shape[1] // 4
    for part in range(4):
        query_ref[:, part * q_cols : (part + 1) * q_cols] = swapped[part, :, :q_cols]
        turned = jnp.transpose(swapped[part, :, q_cols + 2 * kv :].astype(F32))
        wide_ref[part * q_cols : (part + 1) * q_cols, :] = turned.astype(BF16)
    for at, target in ((q_cols, key_ref), (q_cols + kv, value_ref)):
        target[...] = jnp.concatenate(
            [swapped[part, :, at : at + kv] for part in range(4)], axis=1
        )


def last_swap(number, attn_sum, q_cols, kv_cols):
    parts = lax.axis_size("ctx")
    deep = attn_sum.shape[0] // parts
    vmem = pl.BlockSpec(memory_space=pltpu.VMEM)
    return pl.pallas_call(
        functools.partial(last_kernel, q_cols),
        out_shape=(
            jax.ShapeDtypeStruct((deep, parts * q_cols), BF16),
            jax.ShapeDtypeStruct((deep, parts * kv_cols), BF16),
            jax.ShapeDtypeStruct((deep, parts * kv_cols), BF16),
            jax.ShapeDtypeStruct((parts * q_cols, deep), BF16),
        ),
        in_specs=[pl.BlockSpec(memory_space=pl.ANY)],
        out_specs=(vmem,) * 4,
        scratch_shapes=[pltpu.VMEM((parts, deep, attn_sum.shape[1]), BF16)] + swap_scratch(),
        compiler_params=pltpu.CompilerParams(collective_id=number, has_side_effects=True),
        cost_estimate=pl.CostEstimate(flops=0, bytes_accessed=1024, transcendentals=0),
        name="last_swap",
    )(attn_sum)


def final_kernel(own_ref, other_ref, *refs):
    first = lax.axis_index("tensor") == 0
    half = len(refs) // 2
    sources, (out_ref, *targets) = refs[:half], refs[half:]
    own, other = own_ref[...].astype(out_ref.dtype), other_ref[...].astype(out_ref.dtype)
    out_ref[0], out_ref[1] = jnp.where(first, own, other), jnp.where(first, other, own)
    for source, target in zip(sources, targets):
        target[...] = source[...].astype(F32)


def final_forms(own, other, dtype, *grads):
    steps = 4
    rows, width = own.shape
    halves = pl.BlockSpec((rows // steps, width), lambda i: (i, 0))
    whole = pl.BlockSpec((2, rows // steps, width), lambda i: (0, i, 0))

    def block_of(grad):
        deep, wide = grad.shape
        if wide // steps % 128 == 0:
            return pl.BlockSpec((deep, wide // steps), lambda i: (0, i))
        return pl.BlockSpec((deep // steps, wide), lambda i: (i, 0))

    blocks = [block_of(grad) for grad in grads]
    return pl.pallas_call(
        final_kernel,
        grid=(steps,),
        out_shape=(jax.ShapeDtypeStruct((2, rows, width), dtype),)
        + tuple(jax.ShapeDtypeStruct(grad.shape, F32) for grad in grads),
        in_specs=[halves] * 2 + blocks,
        out_specs=(whole, *blocks),
        compiler_params=pltpu.CompilerParams(vmem_limit_bytes=60 * 1024 * 1024),
        cost_estimate=pl.CostEstimate(flops=0, bytes_accessed=1024, transcendentals=0),
        name="final_forms",
    )(own, other, *grads)


def lay_kernel(own_ref, far_ref, twin_ref, twin_far_ref, all_ref, sems):
    ctx = lax.axis_index("ctx")
    row, core = ctx // 2, ctx % 2
    span = own_ref.shape[1]
    copies = []
    for number, (part, a, b) in enumerate(
        (
            (own_ref, row, core),
            (twin_ref, row, 1 - core),
            (far_ref, 1 - row, core),
            (twin_far_ref, 1 - row, 1 - core),
        )
    ):
        start = pl.multiple_of((a * 2 + b) * span, span)
        copies.append(
            pltpu.make_async_copy(part, all_ref.at[:, pl.ds(start, span)], sems.at[number])
        )
        copies[-1].start()
    for copy in copies:
        copy.wait()


def along_ctx(block, earlier, later):
    seqs, span, width = block.shape
    cores = [(0, 1), (1, 0), (2, 3), (3, 2)]
    far = lax.ppermute(after(block, earlier), "ctx", [(0, 2), (1, 3), (2, 0), (3, 1)])
    far = after(far, later)
    twin, twin_far = lax.ppermute(block, "ctx", cores), lax.ppermute(far, "ctx", cores)
    whole = pl.pallas_call(
        lay_kernel,
        out_shape=jax.ShapeDtypeStruct((seqs, 4 * span, width), block.dtype),
        in_specs=[pl.BlockSpec(memory_space=pl.ANY)] * 4,
        out_specs=pl.BlockSpec(memory_space=pltpu.VMEM),
        scratch_shapes=[pltpu.SemaphoreType.DMA((4,))],
        compiler_params=pltpu.CompilerParams(vmem_limit_bytes=24 * 1024 * 1024),
        name="lay",
    )(block, far, twin, twin_far)
    return whole.reshape(seqs * 4 * span, width), (block, far, twin, twin_far)


def open_kernel(
    planes,
    q_ref,
    key_ref,
    value_ref,
    out_ref,
    gate_ref,
    up_ref,
    down_in_ref,
    attn_ref,
    gate_up_ref,
    down_own_ref,
    key_in,
    value_in,
    out_in,
    down_in,
    kv_ref,
    wide_ref,
    down_ref,
    load_sems,
    send_sems,
    recv_sems,
    local_sems,
    line_send,
    line_recv,
):
    _, row, core, *_ = place()
    plane = lax.axis_index("dp")
    here = row * 2 + core
    rows, units = q_ref.shape[0], gate_ref.shape[1] // 4
    peers = (row * 2 + 1 - core, (1 - row) * 2 + core, (1 - row) * 2 + 1 - core)
    ahead, behind = {"dp": (plane + 1) % planes}, {"dp": (plane + planes - 1) % planes}
    barrier = pltpu.get_barrier_semaphore()
    more, fewer = plane + 1 < planes, plane > 0
    for peer in peers:
        pl.semaphore_signal(barrier, inc=1, device_id={"ctx": peer}, device_id_type=MESH_ID)

    @pl.when(more)
    def _():
        pl.semaphore_signal(barrier, inc=1, device_id=ahead, device_id_type=MESH_ID)

    @pl.when(fewer)
    def _():
        pl.semaphore_signal(barrier, inc=1, device_id=behind, device_id_type=MESH_ID)

    loads = [
        pltpu.make_async_copy(source, target, load_sems.at[at])
        for at, (source, target) in enumerate(
            ((key_ref, key_in), (value_ref, value_in), (out_ref, out_in), (down_in_ref, down_in))
        )
    ]
    for load in loads:
        load.start()
    for load in loads[:3]:
        load.wait()
    size = key_in.shape[1] // 4
    for part in range(4):
        lanes = slice(part * size, (part + 1) * size)
        kv_ref[:, part * 2 * size : (part + 1) * 2 * size] = jnp.concatenate(
            [key_in[:, lanes], value_in[:, lanes]], axis=1
        )
    wide_ref[...] = jnp.transpose(out_in[...].astype(F32)).astype(BF16)
    pl.semaphore_wait(barrier, 3 + more.astype(jnp.int32) + fewer.astype(jnp.int32))

    mine = pl.multiple_of(here * rows, rows)
    base = pl.multiple_of(plane * 4 * rows, 4 * rows)
    moves = []
    start = 0
    for source in (q_ref, kv_ref, wide_ref):
        cols = source.shape[1] // 4
        moves.append((source, cols, attn_ref.at[pl.ds(base + mine, rows), pl.ds(start, cols)]))
        start += cols
    for which, source in enumerate((gate_ref, up_ref)):
        lanes = pl.ds(which * units, units)
        moves.append((source, units, gate_up_ref.at[pl.ds(mine, rows), lanes]))
    moves.append((down_ref, units, down_own_ref.at[pl.ds(mine, rows)]))
    away, local = [], []
    for which, (source, cols, target) in enumerate(moves):

        def columns(index, source=source, cols=cols):
            return source.at[:, pl.ds(pl.multiple_of(index * cols, cols), cols)]

        away.append(
            [
                remote(
                    columns(peer),
                    target,
                    send_sems.at[which, at],
                    recv_sems.at[which, at],
                    {"ctx": peer},
                )
                for at, peer in enumerate(peers)
            ]
        )
        local.append(pltpu.make_async_copy(columns(here), target, local_sems.at[which]))
    for which in range(3):
        away[which][0].start()
        local[which].start()
    for at in (1, 2):
        for which in range(3):
            away[which][at].start()
    for which in range(3, 5):
        for copy in away[which]:
            copy.start()
        local[which].start()

    def hop(way, far, part):
        whose = plane - far if way == 0 else plane + far
        half = row if part == 0 else 1 - row
        spot = attn_ref.at[
            pl.ds(pl.multiple_of((whose * 4 + half * 2) * rows, 2 * rows), 2 * rows)
        ]
        return remote(
            spot,
            spot,
            line_send.at[way, far, part],
            line_recv.at[way, far, part],
            ahead if way == 0 else behind,
        )

    def sends(way, far):
        if way == 0:
            return (plane - far >= 0) & more
        return (plane + far < planes) & fewer

    def gets(way, far):
        return plane - 1 - far >= 0 if way == 0 else plane + 1 + far < planes

    def hop_start(way, far, part):
        @pl.when(sends(way, far))
        def _():
            hop(way, far, part).start()

    for which in range(3):
        local[which].wait()
        away[which][0].wait_recv()
    for way in range(2):
        hop_start(way, 0, 0)
    for which in range(3):
        away[which][1].wait_recv()
        away[which][2].wait_recv()
    for way in range(2):
        hop_start(way, 0, 1)
    loads[3].wait()
    for part in range(4):
        there = slice(part * units, (part + 1) * units)
        down_ref[:, there] = jnp.transpose(down_in[there, :].astype(F32)).astype(BF16)
    for copy in away[5] + [local[5]]:
        copy.start()
    for far in range(planes - 1):
        for part in range(2):
            for way in range(2):

                @pl.when(gets(way, far))
                def _(way=way, far=far, part=part):
                    hop(way, far, part).wait_recv()

                if far + 1 < planes - 1:
                    hop_start(way, far + 1, part)
    for far in range(planes - 1):
        for part in range(2):
            for way in range(2):

                @pl.when(sends(way, far))
                def _(way=way, far=far, part=part):
                    hop(way, far, part).wait_send()

    for which in range(6):
        if which > 2:
            local[which].wait()
            for copy in away[which]:
                copy.wait_recv()
        for copy in away[which]:
            copy.wait_send()


def open_weights(query, key, value, out, gate, up, down):
    planes = lax.axis_size("dp")
    rows = query.shape[0]
    cols = (query.shape[1] + 2 * key.shape[1] + out.shape[0]) // 4
    units = gate.shape[1] // 4
    anywhere, vmem = pl.BlockSpec(memory_space=pl.ANY), pl.BlockSpec(memory_space=pltpu.VMEM)
    return pl.pallas_call(
        functools.partial(open_kernel, planes),
        out_shape=(
            jax.ShapeDtypeStruct((planes * 4 * rows, cols), BF16),
            jax.ShapeDtypeStruct((4 * rows, 2 * units), BF16),
            jax.ShapeDtypeStruct((4 * rows, units), BF16),
        ),
        in_specs=[anywhere] * 7,
        out_specs=(vmem, anywhere, anywhere),
        scratch_shapes=[
            pltpu.VMEM(key.shape, BF16),
            pltpu.VMEM(value.shape, BF16),
            pltpu.VMEM(out.shape, BF16),
            pltpu.VMEM(down.shape, BF16),
            pltpu.VMEM((rows, 2 * key.shape[1]), BF16),
            pltpu.VMEM((rows, out.shape[0]), BF16),
            pltpu.VMEM((rows, down.shape[0]), BF16),
            pltpu.SemaphoreType.DMA((4,)),
            pltpu.SemaphoreType.DMA((6, 3)),
            pltpu.SemaphoreType.DMA((6, 3)),
            pltpu.SemaphoreType.DMA((6,)),
            pltpu.SemaphoreType.DMA((2, planes - 1, 2)),
            pltpu.SemaphoreType.DMA((2, planes - 1, 2)),
        ],
        compiler_params=pltpu.CompilerParams(
            collective_id=6, has_side_effects=True, vmem_limit_bytes=60 * 1024 * 1024
        ),
        cost_estimate=pl.CostEstimate(flops=0, bytes_accessed=1024, transcendentals=0),
        name="open_weights",
    )(query, key, value, out, gate, up, down)


def after(value, *earlier):
    return lax.optimization_barrier((value,) + earlier)[0]


def to_units(weight):
    return lax.all_to_all(weight, "ctx", split_axis=1, concat_axis=0, tiled=True)


def swap_sides(block):
    return lax.ppermute(block, "tensor", [(0, 1), (1, 0)])


def on_plane(
    layer_input,
    attn_gain,
    w_query,
    w_key,
    w_value,
    w_out,
    ffn_gain,
    w_gate,
    w_up,
    w_down,
    cotangent,
):
    seqs, span, width = layer_input.shape
    planes = lax.axis_size("dp")
    parts = lax.axis_size("ctx")
    side = lax.axis_index("tensor")
    length = span * parts
    rows_w = w_query.shape[0]
    q_cols = w_query.shape[1] // parts
    kv_cols = w_key.shape[1] // parts

    theta = angles(jnp.arange(length), HEAD_DIM)
    cosine = jnp.tile(jnp.cos(theta), (1, 4))
    sine = jnp.sin(theta)
    signed = jnp.tile(jnp.concatenate([-sine, sine], axis=1), (1, 2))

    attn_w, gate_up, down_own = open_weights(w_query, w_key, w_value, w_out, w_gate, w_up, w_down)
    qkv_cols = q_cols + 2 * kv_cols
    w_qkv = attn_w[:, :qkv_cols]
    w_out_t = attn_w[:, qkv_cols:]
    own_in = lax.dynamic_index_in_dim(layer_input, side, 0, keepdims=False)
    own_cot = lax.dynamic_index_in_dim(cotangent, side, 0, keepdims=False)
    gains = jnp.concatenate(
        [attn_gain[None], ffn_gain[None], jnp.zeros((6, rows_w), BF16)]
    ).astype(F32)
    all_in, gains = plane_gather(after(own_in, gate_up), 10, gains=gains)
    gain_one = gains[:, 0].reshape(width)
    gain_two = gains[:, 1].reshape(width)
    gate_up = lax.all_gather(gate_up, "dp", axis=0, tiled=True)
    down_w = lax.all_gather(down_own, "dp", axis=0, tiled=True)

    all_f = all_in.astype(F32)
    normed_one = (all_f * rms_factor(all_f) * gain_one).astype(BF16)
    pre = jnp.dot(normed_one, w_qkv, preferred_element_type=F32)
    attended, queries, keyvals, logs = attend(pre, cosine, signed, seqs)
    inputs_f = own_in.astype(F32)
    factor_one = rms_factor(inputs_f)
    hidden = inputs_f + product_scatter(1, attended, attn_w, qkv_cols, q_cols)[0]
    factor_two = rms_factor(hidden)
    normed_own = (hidden * factor_two * gain_two).astype(BF16)
    normed_two = plane_gather(normed_own)[0]
    all_cot, cots = along_ctx(cotangent, all_in, hidden)

    product, gate_slope, up_slope = ffn(normed_two, gate_up)
    down_grad = matmul_t(all_cot, product).astype(BF16)
    down_sum = lax.psum_scatter(down_grad, "dp", scatter_dimension=0, tiled=True)
    hidden_grad, hidden_own, ffn_term, gate_grad, up_grad = ffn_back(
        3,
        cots,
        after(gate_slope, down_grad),
        up_slope,
        down_w,
        gate_up,
        (hidden, factor_two, gain_two[None], own_cot),
    )
    gate_w_grad = matmul_t(normed_two, gate_grad).astype(BF16)
    gate_sum = lax.psum_scatter(gate_w_grad, "dp", scatter_dimension=0, tiled=True)
    hidden_low, up_w_grad = plane_gather(after(hidden_own, gate_w_grad), 7, [normed_two, up_grad])
    up_sum = lax.psum_scatter(up_w_grad, "dp", scatter_dimension=0, tiled=True)
    attended_grad = jnp.dot(after(hidden_low, up_w_grad), w_out_t, preferred_element_type=F32).astype(BF16)
    out_w_grad = matmul_t(hidden_low, attended).astype(BF16)
    back, out_own, down_out = attend_back(
        5,
        queries,
        keyvals,
        attended_grad,
        logs,
        cosine,
        signed,
        seqs,
        product,
        down_w,
        hidden,
        down_sum,
    )
    out_other = swap_sides(out_own)
    qkv_grad = matmul_t(normed_one, back).astype(BF16)
    attn_grad = jnp.concatenate([qkv_grad, out_w_grad], axis=1)
    attn_sum = lax.psum_scatter(attn_grad, "dp", scatter_dimension=0, tiled=True)
    input_own, attn_term, gate_out = product_scatter(
        4,
        after(back, attn_grad),
        attn_w,
        0,
        qkv_cols,
        gate_sum,
        (inputs_f, factor_one, gain_one[None], hidden_grad),
    )
    input_other = swap_sides(input_own)
    layer_output, gate_out, down_out = final_forms(
        out_own, after(out_other, input_own), BF16, gate_out, down_out
    )
    gain_own, up_out = gain_sum(2, after(attn_term, layer_output), ffn_term, up_sum)
    query_out, key_out, value_out, wide_out = last_swap(
        9, after(attn_sum, gain_own), q_cols, kv_cols
    )
    input_grad, query_out, key_out, value_out, wide_out, up_out = final_forms(
        input_own,
        after(input_other, gain_own),
        F32,
        query_out,
        key_out,
        value_out,
        wide_out,
        up_out,
    )
    return (
        layer_output,
        input_grad,
        gain_own[0],
        query_out,
        key_out,
        value_out,
        wide_out,
        gain_own[1],
        gate_out,
        up_out,
        down_out,
    )


def fits_plane(mesh, shapes):
    sizes = mesh.shape
    seqs, length, width = shapes[0].shape
    kv_heads = shapes[3].shape[1] // HEAD_DIM
    return (
        sizes["tensor"] == 2
        and sizes["ctx"] == 4
        and seqs == 2 * sizes["dp"]
        and kv_heads == 8
        and shapes[2].shape[1] == 4 * shapes[3].shape[1]
        and length % (4 * QB) == 0
        and width % (128 * 4 * sizes["dp"]) == 0
    )


def placed(mesh, function):
    return jax.shard_map(
        function,
        mesh=mesh,
        in_specs=(
            P("dp", "ctx", None),
            P(("dp", "ctx")),
            P(("dp", "ctx"), "tensor"),
            P(("dp", "ctx"), "tensor"),
            P(("dp", "ctx"), "tensor"),
            P("tensor", ("dp", "ctx")),
            P(("dp", "ctx")),
            P(("dp", "ctx"), "tensor"),
            P(("dp", "ctx"), "tensor"),
            P("tensor", ("dp", "ctx")),
            P("dp", "ctx", None),
        ),
        out_specs=(
            P("dp", "ctx", None),
            P("dp", "ctx", None),
            P(("dp", "ctx")),
            P(("dp", "ctx"), "tensor"),
            P(("dp", "ctx"), "tensor"),
            P(("dp", "ctx"), "tensor"),
            P("tensor", ("dp", "ctx")),
            P(("dp", "ctx")),
            P(("dp", "ctx"), "tensor"),
            P(("dp", "ctx"), "tensor"),
            P("tensor", ("dp", "ctx")),
        ),
        check_vma=False,
    )


def solution(mesh):
    def whole(*arrays):
        return placed(mesh, on_plane if fits_plane(mesh, arrays) else on_device)(*arrays)

    return whole
```

```python
import functools
import math

import jax
import jax.numpy as jnp
from jax import lax
from jax.experimental import pallas as pl
from jax.experimental.pallas import tpu as pltpu
from jax.sharding import PartitionSpec as P

HEAD_DIM = 64


EPSILON = 1e-05
ROPE_BASE = 500000.0


def rotate(values, cosine, sine_val):
    middle = values.shape[-1] // 2
    leading = values[..., :middle]
    trailing = values[..., middle:]
    return jnp.concatenate(
        [leading * cosine - trailing * sine_val, trailing * cosine + leading * sine_val], axis=-1
    )


def unrotate(gradient, cosine, sine_val):
    middle = gradient.shape[-1] // 2
    leading = gradient[..., :middle]
    trailing = gradient[..., middle:]
    return jnp.concatenate(
        [leading * cosine + trailing * sine_val, trailing * cosine - leading * sine_val], axis=-1
    )


def angles(positions, head_dim):
    exponent = jnp.arange(head_dim // 2).astype(jnp.float32) * (
        -2.0 * math.log(ROPE_BASE) / head_dim
    )
    return positions.astype(jnp.float32)[:, None] * jnp.exp(exponent)[None, :]


def rms_factor(row_values):
    return lax.rsqrt(jnp.mean(row_values * row_values, axis=-1, keepdims=True) + EPSILON)


def rms_back(upstream, row_values, factor, gain_row):
    scaled = upstream * gain_row
    gain_term = jnp.sum(upstream * row_values * factor, axis=0)
    inner_mean = jnp.mean(scaled * row_values, axis=-1, keepdims=True)
    return (factor * scaled - row_values * (factor * factor * factor) * inner_mean, gain_term)


def matmul_t(left_op, right_op):
    return lax.dot_general(
        left_op, right_op, (((0,), (0,)), ((), ())), preferred_element_type=jnp.float32
    )


def matmul_nt(left_op, right_op):
    return lax.dot_general(
        left_op, right_op, (((1,), (1,)), ((), ())), preferred_element_type=jnp.float32
    )


def on_device(
    layer_input,
    attn_gain,
    w_query,
    w_key,
    w_value,
    w_out,
    ffn_gain,
    w_gate,
    w_up,
    w_down,
    cotangent,
):
    seq_dev, span_len, model_width = layer_input.shape
    row_count = seq_dev * span_len
    length_all = span_len * lax.axis_size("ctx")
    full_q, full_k, full_v, full_o, full_gate, full_up, full_down, gain_attn, gain_ffn = (
        lax.all_gather(w_query, ("dp", "ctx"), axis=0, tiled=True),
        lax.all_gather(w_key, ("dp", "ctx"), axis=0, tiled=True),
        lax.all_gather(w_value, ("dp", "ctx"), axis=0, tiled=True),
        lax.all_gather(w_out, ("dp", "ctx"), axis=1, tiled=True),
        lax.all_gather(w_gate, ("dp", "ctx"), axis=0, tiled=True),
        lax.all_gather(w_up, ("dp", "ctx"), axis=0, tiled=True),
        lax.all_gather(w_down, ("dp", "ctx"), axis=1, tiled=True),
        lax.all_gather(attn_gain, ("dp", "ctx"), axis=0, tiled=True),
        lax.all_gather(ffn_gain, ("dp", "ctx"), axis=0, tiled=True),
    )
    kv_local = full_k.shape[1] // HEAD_DIM
    group_size = full_q.shape[1] // HEAD_DIM // kv_local
    block_count = seq_dev * kv_local
    scale = HEAD_DIM ** (-0.5)
    query_pos = lax.axis_index("ctx") * span_len + jnp.arange(span_len)
    theta = angles(query_pos, HEAD_DIM)
    cosine = jnp.cos(theta)
    sine_val = jnp.sin(theta)
    causal = query_pos[:, None] >= jnp.arange(length_all)[None, :]
    inputs_f = layer_input.reshape(row_count, model_width).astype(jnp.float32)
    gain_one = gain_attn.astype(jnp.float32)
    gain_two = gain_ffn.astype(jnp.float32)
    factor_one = rms_factor(inputs_f)
    normed_one = (inputs_f * factor_one * gain_one).astype(jnp.bfloat16)
    query_pre = jnp.dot(normed_one, full_q, preferred_element_type=jnp.float32).reshape(
        seq_dev, span_len, kv_local, group_size, HEAD_DIM
    )
    queries = rotate(
        query_pre, cosine[None, :, None, None, :], sine_val[None, :, None, None, :]
    ).astype(jnp.bfloat16)
    key_pre = jnp.dot(normed_one, full_k, preferred_element_type=jnp.float32).reshape(
        seq_dev, span_len, kv_local, HEAD_DIM
    )
    keys_own = (
        rotate(key_pre, cosine[None, :, None, :], sine_val[None, :, None, :])
        .astype(jnp.bfloat16)
        .reshape(seq_dev, span_len, kv_local * HEAD_DIM)
    )
    values_own = (
        jnp.dot(normed_one, full_v, preferred_element_type=jnp.float32)
        .astype(jnp.bfloat16)
        .reshape(seq_dev, span_len, kv_local * HEAD_DIM)
    )
    keys_all, values_all = (
        lax.all_gather(keys_own, "ctx", axis=1, tiled=True),
        lax.all_gather(values_own, "ctx", axis=1, tiled=True),
    )
    query_blocks = jnp.transpose(queries, (0, 2, 1, 3, 4)).reshape(
        block_count, span_len, group_size, HEAD_DIM
    )
    key_blocks = jnp.transpose(
        keys_all.reshape(seq_dev, length_all, kv_local, HEAD_DIM), (0, 2, 1, 3)
    ).reshape(block_count, length_all, HEAD_DIM)
    value_blocks = jnp.transpose(
        values_all.reshape(seq_dev, length_all, kv_local, HEAD_DIM), (0, 2, 1, 3)
    ).reshape(block_count, length_all, HEAD_DIM)

    def scores_of(query_b, key_b):
        raw_scores = jnp.einsum("qgd,kd->gqk", query_b, key_b, preferred_element_type=jnp.float32)
        return jnp.where(causal[None], raw_scores * scale, -1e30)

    def attend(block_in):
        query_b, key_b, value_b = block_in
        scores = scores_of(query_b, key_b)
        peak_row = jnp.max(scores, axis=-1, keepdims=True)
        powers = jnp.exp(scores - peak_row)
        total_sum = jnp.sum(powers, axis=-1, keepdims=True)
        probability = (powers / total_sum).astype(jnp.bfloat16)
        mixed = jnp.einsum("gqk,kd->qgd", probability, value_b, preferred_element_type=jnp.float32)
        return (mixed.astype(jnp.bfloat16), peak_row + jnp.log(total_sum))

    mixed_blocks, logsum = lax.map(attend, (query_blocks, key_blocks, value_blocks))
    attended = jnp.transpose(
        mixed_blocks.reshape(seq_dev, kv_local, span_len, group_size, HEAD_DIM), (0, 2, 1, 3, 4)
    ).reshape(row_count, kv_local * group_size * HEAD_DIM)
    attn_part = jnp.dot(attended, full_o, preferred_element_type=jnp.float32)
    hidden = inputs_f + lax.psum(attn_part, "tensor")
    factor_two = rms_factor(hidden)
    normed_two = (hidden * factor_two * gain_two).astype(jnp.bfloat16)
    gate_pre = jnp.dot(normed_two, full_gate, preferred_element_type=jnp.float32)
    up_pre = jnp.dot(normed_two, full_up, preferred_element_type=jnp.float32)
    sigma = jax.nn.sigmoid(gate_pre)
    product = (gate_pre * sigma * up_pre).astype(jnp.bfloat16)
    ffn_part = jnp.dot(product, full_down, preferred_element_type=jnp.float32)
    out_f = hidden + lax.psum(ffn_part.astype(jnp.bfloat16), "tensor").astype(jnp.float32)
    layer_output = out_f.astype(jnp.bfloat16).reshape(seq_dev, span_len, model_width)
    grad_out = cotangent.reshape(row_count, model_width).astype(jnp.float32)
    grad_low = cotangent.reshape(row_count, model_width)
    down_grad = matmul_t(product, grad_low)
    prod_grad = matmul_nt(grad_low, full_down)
    gate_grad = (prod_grad * up_pre * sigma * (1.0 + gate_pre * (1.0 - sigma))).astype(jnp.bfloat16)
    up_grad = (prod_grad * gate_pre * sigma).astype(jnp.bfloat16)
    gate_w_grad = matmul_t(normed_two, gate_grad)
    up_w_grad = matmul_t(normed_two, up_grad)
    normed_two_part = matmul_nt(gate_grad, full_gate) + matmul_nt(up_grad, full_up)
    normed_two_grad = lax.psum(normed_two_part, "tensor")
    hidden_back, ffn_gain_term = rms_back(normed_two_grad, hidden, factor_two, gain_two)
    hidden_grad = grad_out + hidden_back
    hidden_low = hidden_grad.astype(jnp.bfloat16)
    out_w_grad = matmul_t(attended, hidden_low)
    attended_grad = matmul_nt(hidden_low, full_o).astype(jnp.bfloat16)
    upstream_blocks = jnp.transpose(
        attended_grad.reshape(seq_dev, span_len, kv_local, group_size, HEAD_DIM), (0, 2, 1, 3, 4)
    ).reshape(block_count, span_len, group_size, HEAD_DIM)

    def attend_back(block_in):
        query_b, key_b, value_b, logsum_b, upstream_b = block_in
        scores = scores_of(query_b, key_b)
        probability = jnp.exp(scores - logsum_b)
        rounded = probability.astype(jnp.bfloat16)
        value_grad = jnp.einsum(
            "gqk,qgd->kd", rounded, upstream_b, preferred_element_type=jnp.float32
        )
        prob_grad = jnp.einsum(
            "qgd,kd->gqk", upstream_b, value_b, preferred_element_type=jnp.float32
        )
        inner_sum = jnp.sum(probability * prob_grad, axis=-1, keepdims=True)
        score_grad = (probability * (prob_grad - inner_sum)).astype(jnp.bfloat16)
        query_grad = (
            jnp.einsum("gqk,kd->qgd", score_grad, key_b, preferred_element_type=jnp.float32) * scale
        )
        key_grad = (
            jnp.einsum("gqk,qgd->kd", score_grad, query_b, preferred_element_type=jnp.float32)
            * scale
        )
        return (query_grad, key_grad, value_grad)

    query_grads, key_grads, value_grads = lax.map(
        attend_back, (query_blocks, key_blocks, value_blocks, logsum, upstream_blocks)
    )
    key_rows = jnp.transpose(
        key_grads.reshape(seq_dev, kv_local, length_all, HEAD_DIM), (0, 2, 1, 3)
    ).reshape(seq_dev, length_all, kv_local * HEAD_DIM)
    value_rows = jnp.transpose(
        value_grads.reshape(seq_dev, kv_local, length_all, HEAD_DIM), (0, 2, 1, 3)
    ).reshape(seq_dev, length_all, kv_local * HEAD_DIM)
    key_mine, value_mine = (
        lax.psum_scatter(key_rows, "ctx", scatter_dimension=1, tiled=True),
        lax.psum_scatter(value_rows, "ctx", scatter_dimension=1, tiled=True),
    )
    key_low = (
        unrotate(
            key_mine.reshape(seq_dev, span_len, kv_local, HEAD_DIM),
            cosine[None, :, None, :],
            sine_val[None, :, None, :],
        )
        .astype(jnp.bfloat16)
        .reshape(row_count, kv_local * HEAD_DIM)
    )
    value_low = value_mine.astype(jnp.bfloat16).reshape(row_count, kv_local * HEAD_DIM)
    query_rot = jnp.transpose(
        query_grads.reshape(seq_dev, kv_local, span_len, group_size, HEAD_DIM), (0, 2, 1, 3, 4)
    )
    query_low = (
        unrotate(query_rot, cosine[None, :, None, None, :], sine_val[None, :, None, None, :])
        .astype(jnp.bfloat16)
        .reshape(row_count, kv_local * group_size * HEAD_DIM)
    )
    query_w_grad = matmul_t(normed_one, query_low)
    key_w_grad = matmul_t(normed_one, key_low)
    value_w_grad = matmul_t(normed_one, value_low)
    normed_one_part = (
        matmul_nt(query_low, full_q) + matmul_nt(key_low, full_k) + matmul_nt(value_low, full_v)
    )
    normed_one_grad = lax.psum(normed_one_part.astype(jnp.bfloat16), "tensor").astype(jnp.float32)
    input_back, attn_gain_term = rms_back(normed_one_grad, inputs_f, factor_one, gain_one)
    input_grad = (hidden_grad + input_back).reshape(seq_dev, span_len, model_width)
    (
        query_sum,
        key_sum,
        value_sum,
        out_sum,
        gate_sum,
        up_sum,
        down_sum,
        attn_gain_sum,
        ffn_gain_sum,
    ) = (
        lax.psum_scatter(query_w_grad, ("dp", "ctx"), scatter_dimension=0, tiled=True),
        lax.psum_scatter(key_w_grad, ("dp", "ctx"), scatter_dimension=0, tiled=True),
        lax.psum_scatter(value_w_grad, ("dp", "ctx"), scatter_dimension=0, tiled=True),
        lax.psum_scatter(out_w_grad, ("dp", "ctx"), scatter_dimension=1, tiled=True),
        lax.psum_scatter(gate_w_grad, ("dp", "ctx"), scatter_dimension=0, tiled=True),
        lax.psum_scatter(up_w_grad, ("dp", "ctx"), scatter_dimension=0, tiled=True),
        lax.psum_scatter(down_grad, ("dp", "ctx"), scatter_dimension=1, tiled=True),
        lax.psum_scatter(attn_gain_term, ("dp", "ctx"), scatter_dimension=0, tiled=True),
        lax.psum_scatter(ffn_gain_term, ("dp", "ctx"), scatter_dimension=0, tiled=True),
    )
    return (
        layer_output,
        input_grad,
        attn_gain_sum,
        query_sum,
        key_sum,
        value_sum,
        out_sum,
        ffn_gain_sum,
        gate_sum,
        up_sum,
        down_sum,
    )


MESH_ID = pl.DeviceIdType.MESH
BF16 = jnp.bfloat16
F32 = jnp.float32
QB = 256


def place():
    side = lax.axis_index("tensor")
    ctx = lax.axis_index("ctx")
    row = ctx // 2
    core = ctx % 2
    near_core = {"ctx": row * 2 + (1 - core)}
    near_side = {"tensor": 1 - side}
    near_row = {"ctx": (1 - row) * 2 + core}
    return side, row, core, near_core, near_side, near_row


def greet(neighbours):
    barrier = pltpu.get_barrier_semaphore()
    for target in neighbours:
        pl.semaphore_signal(barrier, inc=1, device_id=target, device_id_type=MESH_ID)
    pl.semaphore_wait(barrier, len(neighbours))


def remote(source, target, send_sem, recv_sem, device):
    return pltpu.make_async_remote_copy(
        src_ref=source,
        dst_ref=target,
        send_sem=send_sem,
        recv_sem=recv_sem,
        device_id=device,
        device_id_type=MESH_ID,
    )


class Line:
    def __init__(self, planes, all_ref, send_sems, recv_sems):
        self.planes, self.all_ref = planes, all_ref
        self.send_sems, self.recv_sems = send_sems, recv_sems
        self.plane = lax.axis_index("dp")
        self.rows = all_ref.shape[0] // planes
        self.more, self.fewer = self.plane + 1 < planes, self.plane > 0
        self.ahead = {"dp": (self.plane + 1) % planes}
        self.behind = {"dp": (self.plane + planes - 1) % planes}

    def shard(self, whose):
        return self.all_ref.at[pl.ds(pl.multiple_of(whose * self.rows, self.rows), self.rows)]

    def greet(self, neighbours):
        barrier = pltpu.get_barrier_semaphore()
        for target in neighbours:
            pl.semaphore_signal(barrier, inc=1, device_id=target, device_id_type=MESH_ID)
        for there, target in ((self.more, self.ahead), (self.fewer, self.behind)):

            @pl.when(there)
            def _(target=target):
                pl.semaphore_signal(barrier, inc=1, device_id=target, device_id_type=MESH_ID)

        count = len(neighbours) + self.more.astype(jnp.int32) + self.fewer.astype(jnp.int32)
        pl.semaphore_wait(barrier, count)

    def hop(self, way, far):
        spot = self.shard(self.plane - far if way == 0 else self.plane + far)
        return remote(
            spot,
            spot,
            self.send_sems.at[way, far],
            self.recv_sems.at[way, far],
            self.ahead if way == 0 else self.behind,
        )

    def sends(self, way, far):
        if way == 0:
            return (self.plane - far >= 0) & self.more
        return (self.plane + far < self.planes) & self.fewer

    def gets(self, way, far):
        if way == 0:
            return self.plane - 1 - far >= 0
        return self.plane + 1 + far < self.planes

    def send(self, far):
        for way in range(2):

            @pl.when(self.sends(way, far))
            def _(way=way):
                self.hop(way, far).start()

    def take(self, far):
        for way in range(2):

            @pl.when(self.gets(way, far))
            def _(way=way):
                self.hop(way, far).wait_recv()

        if far + 1 < self.planes - 1:
            self.send(far + 1)

    def settle(self):
        for far in range(self.planes - 1):
            for way in range(2):

                @pl.when(self.sends(way, far))
                def _(way=way, far=far):
                    self.hop(way, far).wait_send()


def gather_kernel(rows, works, planes, lines, block_ref, *refs):
    if works:
        left_ref, right_ref, all_ref, grad_ref, send_sems, recv_sems, local_sem = refs
    elif planes:
        gains_ref, all_ref, all_gains_ref, send_sems, recv_sems, local_sem, *gain_sems = refs
    elif lines:
        shard_ref, all_ref, line_ref, send_sems, recv_sems, local_sem, *line_sems = refs
        line = Line(lines, line_ref, *line_sems[:2])
    else:
        all_ref, send_sems, recv_sems, local_sem = refs
    side, row, core, near_core, near_side, near_row = place()
    half = rows // 2

    def work(first, last):
        if not works:
            return
        size = left_ref.shape[1] // works

        def step(index, carry):
            at = pl.ds(pl.multiple_of(index * size, size), size)
            grad_ref[at, :] = matmul_t(left_ref[:, at], right_ref[...]).astype(BF16)
            return carry

        lax.fori_loop(first * works // 8, last * works // 8, step, 0)

    def spot(a, b, c, part=None):
        start = (a * 4 + b * 2 + c) * rows
        if part is None:
            return all_ref.at[pl.ds(pl.multiple_of(start, rows), rows)]
        return all_ref.at[pl.ds(pl.multiple_of(start + part * half, half), half)]

    targets = []
    if planes:
        plane = lax.axis_index("dp")
        here = row * 2 + core
        targets = [
            {"dp": (plane + step) % planes, "ctx": (here + turn) % 4}
            for step in range(planes)
            for turn in range(4)
            if step or turn
        ]
    if lines:
        line.greet([near_side, near_core, near_row])
    else:
        greet([near_side] + (targets if planes else [near_core, near_row]))
    copies = []

    def send(number, source, target, device):
        copy = remote(source, target, send_sems.at[number], recv_sems.at[number], device)
        copy.start()
        copies.append(copy)
        return copy

    gain_copies = []
    if planes:
        mine = all_gains_ref.at[plane * 4 + here]
        gain_copies = [
            remote(gains_ref, mine, gain_sems[0].at[at], gain_sems[1].at[at], target)
            for at, target in enumerate(targets)
        ] + [pltpu.make_async_copy(gains_ref, mine, gain_sems[2])]
        for copy in gain_copies:
            copy.start()
    first = block_ref.at[pl.ds(0, half)]
    second = block_ref.at[pl.ds(half, half)]
    side_b = send(0, second, spot(side, row, core, 1), near_side)
    row_a = send(1, first, spot(side, row, core, 0), near_row)
    side_a = send(2, first, spot(side, row, core, 0), near_side)
    row_b = send(3, second, spot(side, row, core, 1), near_row)
    core_own = send(4, block_ref, spot(side, row, core), near_core)
    local = pltpu.make_async_copy(block_ref, spot(side, row, core), local_sem)
    local.start()
    if lines:
        own = pltpu.make_async_copy(shard_ref, line.shard(line.plane), line_sems[2])
        own.start()
        own.wait()
        line.send(0)
    work(0, 6)
    side_b.wait_recv()
    away_b = send(5, spot(1 - side, row, core, 1), spot(1 - side, row, core, 1), near_row)
    row_a.wait_recv()
    away_a = send(6, spot(side, 1 - row, core, 0), spot(side, 1 - row, core, 0), near_side)
    work(6, 8)
    if lines:
        line.take(0)
    side_a.wait_recv()
    core_side = send(7, spot(1 - side, row, core), spot(1 - side, row, core), near_core)
    row_b.wait_recv()
    core_row = send(8, spot(side, 1 - row, core), spot(side, 1 - row, core), near_core)
    for far in range(1, lines - 1):
        line.take(far)
    away_a.wait_recv()
    core_away_a = send(
        9, spot(1 - side, 1 - row, core, 0), spot(1 - side, 1 - row, core, 0), near_core
    )
    away_b.wait_recv()
    core_away_b = send(
        10, spot(1 - side, 1 - row, core, 1), spot(1 - side, 1 - row, core, 1), near_core
    )
    for copy in (core_own, core_side, core_row, core_away_a, core_away_b):
        copy.wait_recv()
    for copy in copies:
        copy.wait_send()
    for copy in gain_copies:
        copy.wait()
    if lines:
        line.settle()
    local.wait()


def plane_gather(block, number=0, pair=None, gains=None, shard=None):
    rows, width = block.shape
    anywhere, vmem = pl.BlockSpec(memory_space=pl.ANY), pl.BlockSpec(memory_space=pltpu.VMEM)
    shapes, ins, outs = [jax.ShapeDtypeStruct((8 * rows, width), block.dtype)], [anywhere], [anywhere]
    operands = [block]
    if pair is not None:
        shapes.append(jax.ShapeDtypeStruct((pair[0].shape[1], pair[1].shape[1]), BF16))
        ins += [vmem, vmem]
        outs += [vmem]
        operands += pair
    planes, lines, scratch = 0, 0, []
    if shard is not None:
        lines = lax.axis_size("dp")
        shapes.append(jax.ShapeDtypeStruct((lines * shard.shape[0], shard.shape[1]), shard.dtype))
        ins += [anywhere]
        outs += [vmem]
        operands += [shard]
        scratch = [pltpu.SemaphoreType.DMA((2, lines - 1))] * 2 + [pltpu.SemaphoreType.DMA]
    if gains is not None:
        planes = lax.axis_size("dp")
        shapes.append(jax.ShapeDtypeStruct((4 * planes,) + gains.shape, gains.dtype))
        ins += [vmem]
        outs += [vmem]
        operands += [gains]
        scratch = [pltpu.SemaphoreType.DMA((4 * planes - 1,))] * 2 + [pltpu.SemaphoreType.DMA]
    return pl.pallas_call(
        functools.partial(gather_kernel, rows, 8 if pair is not None else 0, planes, lines),
        out_shape=tuple(shapes),
        in_specs=ins,
        out_specs=tuple(outs),
        scratch_shapes=[
            pltpu.SemaphoreType.DMA((11,)),
            pltpu.SemaphoreType.DMA((11,)),
            pltpu.SemaphoreType.DMA,
        ]
        + scratch,
        compiler_params=pltpu.CompilerParams(
            collective_id=number, has_side_effects=True, vmem_limit_bytes=60 * 1024 * 1024
        ),
        cost_estimate=pl.CostEstimate(flops=0, bytes_accessed=1024, transcendentals=0),
        name="plane_gather",
    )(*operands)


def swap_scratch():
    return [pltpu.SemaphoreType.DMA((3,))] * 2 + [pltpu.SemaphoreType.DMA]


def swap_copies(in_ref, out_ref, send_sems, recv_sems, local_sem):
    _, row, core, *_ = place()
    rows = out_ref.shape[1]
    here = row * 2 + core

    def block(index):
        return in_ref.at[pl.ds(pl.multiple_of(index * rows, rows), rows)]

    peers = (row * 2 + 1 - core, (1 - row) * 2 + core, (1 - row) * 2 + 1 - core)
    away = [
        remote(block(peer), out_ref.at[here], send_sems.at[at], recv_sems.at[at], {"ctx": peer})
        for at, peer in enumerate(peers)
    ]
    return away, pltpu.make_async_copy(block(here), out_ref.at[here], local_sem)


def norm_back(rows, grad_ref, value_ref, factor_ref, gain_ref, base_ref, out_ref, low_ref, term_ref):
    tile = 32
    gain = gain_ref[...]

    def step(index, total):
        here = pl.ds(pl.multiple_of(index * tile, tile), tile)
        grad, value, factor = grad_ref[here, :], value_ref[here, :], factor_ref[here, :]
        scaled = grad * gain
        inner = jnp.mean(scaled * value, axis=1, keepdims=True)
        back = factor * scaled - value * (factor * factor * factor) * inner
        result = base_ref[here, :].astype(F32) + back
        if out_ref is not None:
            out_ref[here, :] = result
        low_ref[here, :] = result.astype(BF16)
        return total + jnp.sum(grad * value * factor, axis=0, keepdims=True)

    total = lax.fori_loop(0, rows // tile, step, jnp.zeros((1, gain.shape[1]), F32))
    term_ref[...] = jnp.broadcast_to(total, term_ref.shape)


def scatter_steps(rows, left_of, right_of, out_ref, scratch, swap=None, late=None):
    made, other, to_side, to_row, from_side, from_row = scratch[:6]
    on_side, on_row, got_side, got_row, send_sems, recv_sems = scratch[6:]
    side, row, core, near_core, near_side, near_row = place()
    tile = 32
    wide = out_ref.shape[1] // 2

    chips = ((side, row), (1 - side, row), (side, 1 - row), (1 - side, 1 - row))
    routes = [
        (made.at[chip, part, 1 - core], other.at[chip, part], near_core)
        for chip in range(4)
        for part in range(2)
    ] + [
        (to_side.at[0], from_side.at[0], near_side),
        (to_row.at[0], from_row.at[0], near_row),
        (to_side.at[1], from_side.at[1], near_side),
        (to_row.at[1], from_row.at[1], near_row),
        (on_row, got_row, near_row),
        (on_side, got_side, near_side),
    ]
    copies = [
        remote(source, target, send_sems.at[at], recv_sems.at[at], device)
        for at, (source, target, device) in enumerate(routes)
    ]
    side_0, row_0, side_1, row_1, last_row, last_side = copies[8:]
    swapped = None if swap is None else swap_copies(*swap)

    def make(chip, part, first=False):
        a, b = chips[chip]
        start = pl.multiple_of((a * 4 + b * 2) * rows, 2 * rows)
        left, value, first_col = left_of(chip, start), None, 0
        for right in right_of(pl.ds(part * wide, wide)):
            last_col = first_col + right.shape[1]
            term = matmul_nt(left[:, first_col:last_col], right)
            value = term if value is None else value + term
            first_col = last_col
        made[chip, part, 0] = value[:rows].astype(BF16)
        made[chip, part, 1] = value[rows:].astype(BF16)
        if first:
            partners = (near_core, near_side, near_row)
            if swap is not None:
                partners += ({"ctx": (1 - row) * 2 + 1 - core},)
            greet(partners)
        copies[2 * chip + part].start()

    def both(chip, part, at):
        here = made[chip, part, core, pl.ds(at, tile), :].astype(F32)
        return here + other[chip, part, pl.ds(at, tile), :].astype(F32)

    def each(body):
        def step(index, carry):
            body(pl.multiple_of(index * tile, tile))
            return carry

        lax.fori_loop(0, rows // tile, step, 0)

    def put(target, chip, part, copy, extra=None):
        copies[2 * chip + part].wait_recv()

        def body(at):
            value = both(chip, part, at)
            if extra is not None:
                value = value + extra[pl.ds(at, tile), :].astype(F32)
            target[pl.ds(at, tile), :] = value.astype(BF16)

        each(body)
        copy.start()

    def across():
        make(3, 0, True)
        make(3, 1)
        put(to_side.at[0], 3, 0, side_0)
        put(to_row.at[0], 3, 1, row_0)
        if swap is not None:
            for copy in swapped[0] + [swapped[1]]:
                copy.start()

    def along():
        make(1, 0)
        make(2, 1)
        put(to_side.at[1], 1, 0, side_1)
        put(to_row.at[1], 2, 1, row_1)

    def forward():
        make(1, 1)
        make(2, 0)
        row_0.wait_recv()
        put(on_side, 1, 1, last_side, from_row.at[0])
        side_0.wait_recv()
        put(on_row, 2, 0, last_row, from_side.at[0])

    def own():
        make(0, 0)
        make(0, 1)

    def finish():
        copies[0].wait_recv()
        copies[1].wait_recv()
        side_1.wait_recv()
        row_1.wait_recv()

        def first_sum(at):
            here = pl.ds(at, tile)
            out_ref[here, :wide] = both(0, 0, at) + from_side[1, here, :].astype(F32)
            out_ref[here, wide:] = both(0, 1, at) + from_row[1, here, :].astype(F32)

        each(first_sum)
        if swap is not None:
            for copy in swapped[0]:
                copy.wait()
            swapped[1].wait()
            late()
        last_side.wait_recv()
        last_row.wait_recv()

        def last_sum(at):
            here = pl.ds(at, tile)
            out_ref[here, :wide] += got_row[here, :].astype(F32)
            out_ref[here, wide:] += got_side[here, :].astype(F32)

        each(last_sum)
        for copy in copies:
            copy.wait_send()

    return across, along, forward, own, finish


def scatter_scratch(rows, width):
    half = width // 2
    return (
        [pltpu.VMEM((4, 2, 2, rows, half), BF16), pltpu.VMEM((4, 2, rows, half), BF16)]
        + [pltpu.VMEM((2, rows, half), BF16)] * 4
        + [pltpu.VMEM((rows, half), BF16)] * 4
        + [pltpu.SemaphoreType.DMA((14,))] * 2
    )


def scatter_kernel(rows, swaps, columns, left, right, *refs):
    swap, late = None, None
    if swaps:
        in_ref, value_ref, factor_ref, gain_ref, base_ref, low_ref, term_ref, laid_ref = refs[:8]
        out_ref, *scratch = refs[8:]
        swapped = scratch[-4]
        swap = (in_ref, swapped, *scratch[-3:])
        scratch = scratch[:-4]

        def late():
            size = swapped.shape[2]
            for part in range(4):
                laid_ref[:, part * size : (part + 1) * size] = swapped[part]

    else:
        out_ref, *scratch = refs

    def left_of(chip, start):
        return left[pl.ds(start, 2 * rows), :]

    def right_of(at):
        return [right[at, columns]]

    for step in scatter_steps(rows, left_of, right_of, out_ref, scratch, swap=swap, late=late):
        step()
    if swaps:
        norm_back(
            rows, out_ref, value_ref, factor_ref, gain_ref, base_ref, None, low_ref, term_ref
        )


def product_scatter(number, left, right, start, size, swap=None, norm=()):
    total = left.shape[0]
    width = right.shape[0]
    rows = total // 8
    vmem = pl.BlockSpec(memory_space=pltpu.VMEM)
    if swap is None:
        shapes, ins, scratch = [jax.ShapeDtypeStruct((rows, width), F32)], [vmem, vmem], []
        operands = [left, right]
    else:
        deep = swap.shape[0] // 4
        shapes = [
            jax.ShapeDtypeStruct((rows, width), BF16),
            jax.ShapeDtypeStruct((8, width), F32),
            jax.ShapeDtypeStruct((deep, 4 * swap.shape[1]), swap.dtype),
        ]
        ins = [vmem, vmem, pl.BlockSpec(memory_space=pl.ANY)] + [vmem] * 4
        operands = [left, right, swap, *norm]
        scratch = [pltpu.VMEM((4, deep, swap.shape[1]), swap.dtype)] + swap_scratch()
    return pl.pallas_call(
        functools.partial(scatter_kernel, rows, swap is not None, slice(start, start + size)),
        out_shape=tuple(shapes),
        in_specs=ins,
        out_specs=tuple([vmem] * len(shapes)),
        scratch_shapes=([pltpu.VMEM((rows, width), F32)] if swap is not None else [])
        + scatter_scratch(rows, width)
        + scratch,
        compiler_params=pltpu.CompilerParams(
            collective_id=number, has_side_effects=True, vmem_limit_bytes=56 * 1024 * 1024
        ),
        cost_estimate=pl.CostEstimate(flops=0, bytes_accessed=1024, transcendentals=0),
        name="product_scatter",
    )(*operands)


def ffn_back_kernel(
    rows,
    own_ref,
    far_ref,
    twin_ref,
    twin_far_ref,
    gate_slope_ref,
    up_slope_ref,
    down_lead_ref,
    down_ref,
    right_ref,
    value_ref,
    factor_ref,
    gain_ref,
    base_ref,
    result_ref,
    low_ref,
    term_ref,
    gate_ref,
    up_ref,
    out_ref,
    weight,
    weight_sems,
    cots,
    gate_slopes,
    up_slopes,
    lefts,
    sems,
    out_sems,
    *scratch,
):
    side, row, core, *_ = place()
    lead = down_lead_ref.shape[1]
    units = lead + down_ref.shape[1]
    turns = (3, 1, 2, 0)
    chips = ((side, row), (1 - side, row), (side, 1 - row), (1 - side, 1 - row))
    starts = [pl.multiple_of((a * 4 + b * 2) * rows, 2 * rows) for a, b in chips]
    stored = []

    def fetch(turn):
        chip = turns[turn]
        near, away = (own_ref, twin_ref) if chip < 2 else (far_ref, twin_far_ref)
        there = pl.ds(starts[chip], 2 * rows)
        slot = turn % 2
        return [
            pltpu.make_async_copy(source, target, sems.at[which, slot])
            for which, (source, target) in enumerate(
                (
                    (near.at[chips[chip][0]], cots.at[slot, core]),
                    (away.at[chips[chip][0]], cots.at[slot, 1 - core]),
                    (gate_slope_ref.at[there], gate_slopes.at[slot]),
                    (up_slope_ref.at[there], up_slopes.at[slot]),
                )
            )
        ]

    def store(turn):
        there = pl.ds(starts[turns[turn]], 2 * rows)
        slot = turn % 2
        return [
            pltpu.make_async_copy(
                lefts.at[slot, :, pl.ds(which * units, units)],
                target.at[there],
                out_sems.at[which, slot],
            )
            for which, target in enumerate((gate_ref, up_ref))
        ]

    joins = [
        pltpu.make_async_copy(source, weight.at[:, pl.ds(first, source.shape[1])], weight_sems.at[at])
        for at, (source, first) in enumerate(((down_lead_ref, 0), (down_ref, lead)))
    ]

    def start(copies):
        for copy in copies:
            copy.start()

    def wait(copies):
        for copy in copies:
            copy.wait()

    def left_of(chip, _):
        turn = turns.index(chip)
        slot = turn % 2
        if chip in stored:
            return lefts[slot]
        stored.append(chip)
        if turn == 0:
            start(joins)
            start(fetch(0))
        if turn == 1:
            start(fetch(2))
        if turn == 2:
            start(fetch(3))
        if turn == 0:
            start(fetch(1))
        if turn == 0:
            wait(joins)
        wait(fetch(turn))
        if turn > 1:
            wait(store(turn - 2))
        cot = cots[slot].reshape(2 * rows, cots.shape[3])
        grad = jnp.dot(cot, weight[...], preferred_element_type=F32)
        lefts[slot, :, :units] = (grad * gate_slopes[slot].astype(F32)).astype(BF16)
        lefts[slot, :, units:] = (grad * up_slopes[slot].astype(F32)).astype(BF16)
        start(store(turn))
        return lefts[slot]

    def right_of(at):
        return [right_ref[at, :]]

    for step in scatter_steps(rows, left_of, right_of, out_ref, scratch):
        step()
    norm_back(
        rows, out_ref, value_ref, factor_ref, gain_ref, base_ref, result_ref, low_ref, term_ref
    )
    wait(store(2))
    wait(store(3))


def ffn_back(number, cots, gate_slope, up_slope, down_lead, down_w, gate_up, norm):
    total, units = gate_slope.shape
    width = down_w.shape[0]
    rows = total // 8
    vmem = pl.BlockSpec(memory_space=pltpu.VMEM)
    anywhere = pl.BlockSpec(memory_space=pl.ANY)
    return pl.pallas_call(
        functools.partial(ffn_back_kernel, rows),
        out_shape=(
            jax.ShapeDtypeStruct((rows, width), F32),
            jax.ShapeDtypeStruct((rows, width), BF16),
            jax.ShapeDtypeStruct((8, width), F32),
            jax.ShapeDtypeStruct((total, units), BF16),
            jax.ShapeDtypeStruct((total, units), BF16),
        ),
        in_specs=[anywhere] * 8 + [vmem] * 5,
        out_specs=(vmem, vmem, vmem, anywhere, anywhere),
        scratch_shapes=[
            pltpu.VMEM((rows, width), F32),
            pltpu.VMEM((width, units), BF16),
            pltpu.SemaphoreType.DMA((2,)),
            pltpu.VMEM((2, 2, rows, width), BF16),
            pltpu.VMEM((2, 2 * rows, units), BF16),
            pltpu.VMEM((2, 2 * rows, units), BF16),
            pltpu.VMEM((2, 2 * rows, 2 * units), BF16),
            pltpu.SemaphoreType.DMA((4, 2)),
            pltpu.SemaphoreType.DMA((2, 2)),
        ]
        + scatter_scratch(rows, width),
        compiler_params=pltpu.CompilerParams(
            collective_id=number, has_side_effects=True, vmem_limit_bytes=60 * 1024 * 1024
        ),
        cost_estimate=pl.CostEstimate(flops=0, bytes_accessed=1024, transcendentals=0),
        name="ffn_back",
    )(*cots, gate_slope, up_slope, down_lead, down_w, gate_up, *norm)


def ffn_kernel(in_ref, w_ref, product_ref, gate_slope_ref, up_slope_ref):
    units = product_ref.shape[1]
    wide = 512
    rows_in = in_ref[...]
    for start in range(0, units, wide):
        at = pl.ds(start, wide)
        gate = jnp.dot(rows_in, w_ref[:, at], preferred_element_type=F32)
        up = jnp.dot(rows_in, w_ref[:, pl.ds(units + start, wide)], preferred_element_type=F32)
        sigma = jax.nn.sigmoid(gate)
        active = gate * sigma
        product_ref[:, at] = (active * up).astype(BF16)
        gate_slope_ref[:, at] = (up * sigma * (1.0 + gate * (1.0 - sigma))).astype(BF16)
        up_slope_ref[:, at] = active.astype(BF16)


def ffn(rows_in, gate_up):
    total, width = rows_in.shape
    units = gate_up.shape[1] // 2
    rows = 512
    out = pl.BlockSpec((rows, units), lambda i: (i, 0))
    return pl.pallas_call(
        ffn_kernel,
        grid=(total // rows,),
        out_shape=(jax.ShapeDtypeStruct((total, units), BF16),) * 3,
        in_specs=[
            pl.BlockSpec((rows, width), lambda i: (i, 0)),
            pl.BlockSpec(
                (width, 2 * units), lambda i: (0, 0), pipeline_mode=pl.Buffered(1)
            ),
        ],
        out_specs=(out, out, out),
        compiler_params=pltpu.CompilerParams(vmem_limit_bytes=60 * 1024 * 1024),
        cost_estimate=pl.CostEstimate(flops=0, bytes_accessed=1024, transcendentals=0),
        name="ffn",
    )(rows_in, gate_up)


def swap_halves(values):
    width = values.shape[-1]
    lane = lax.broadcasted_iota(jnp.int32, values.shape, 1)
    ahead = pltpu.roll(values, width - HEAD_DIM // 2, 1)
    behind = pltpu.roll(values, HEAD_DIM // 2, 1)
    return jnp.where(lane % HEAD_DIM < HEAD_DIM // 2, ahead, behind)


def pieces_of(block):
    return ((0, block * QB, False), (block * QB, QB, True)) if block else ((0, QB, True),)


def masked_scores(query, keys, diagonal):
    scores = matmul_nt(query, keys)
    if diagonal:
        here = lax.broadcasted_iota(jnp.int32, scores.shape, 0)
        there = lax.broadcasted_iota(jnp.int32, scores.shape, 1)
        scores = jnp.where(here >= there, scores, -1e30)
    return scores


def attend_kernel(length, q_ref, kv_ref, cos_ref, sin_ref, att_ref, qrot_ref, kvrot_ref, log_ref):
    cosine = cos_ref[...]
    signed = sin_ref[...]
    scale = HEAD_DIM ** (-0.5)
    pre = q_ref[...]
    qrot_ref[...] = (pre * cosine + swap_halves(pre) * signed).astype(BF16)
    pre = kv_ref[...]
    lane = lax.broadcasted_iota(jnp.int32, pre.shape, 1)
    turned = jnp.where(lane < HEAD_DIM, pre * cosine + swap_halves(pre) * signed, pre)
    kvrot_ref[...] = turned.astype(BF16)
    for block in range(length // QB):
        here = pl.ds(block * QB, QB)
        logs = []
        mixed = []
        for head in range(2):
            query = qrot_ref[here, head * HEAD_DIM : (head + 1) * HEAD_DIM] * jnp.asarray(
                scale, BF16
            )
            scores = []
            for start, size, diagonal in pieces_of(block):
                keys = kvrot_ref[pl.ds(start, size), :HEAD_DIM]
                scores.append(masked_scores(query, keys, diagonal))
            peak = functools.reduce(
                jnp.maximum, [jnp.max(s, axis=1, keepdims=True) for s in scores]
            )
            powers = [jnp.exp(s - peak) for s in scores]
            total = sum(jnp.sum(p, axis=1, keepdims=True) for p in powers)
            inverse = 1.0 / total
            out = None
            for (start, size, _), power in zip(pieces_of(block), powers):
                values = kvrot_ref[pl.ds(start, size), HEAD_DIM:]
                term = jnp.dot(
                    (power * inverse).astype(BF16), values, preferred_element_type=F32
                )
                out = term if out is None else out + term
            mixed.append(out)
            logs.append(peak + jnp.log(total))
        att_ref[here, :] = jnp.concatenate(mixed, axis=1).astype(BF16)
        lane = lax.broadcasted_iota(jnp.int32, (QB, 128), 1)
        log_ref[here, :] = jnp.where(lane < HEAD_DIM, logs[0], logs[1])


def attend(pre, cosine, signed, seqs):
    rows = pre.shape[0]
    length = rows // seqs
    pairs = pre.shape[1] // 128 - 1
    block = (length, 128)
    return pl.pallas_call(
        functools.partial(attend_kernel, length),
        grid=(seqs, pairs),
        out_shape=(
            jax.ShapeDtypeStruct((rows, pairs * 128), BF16),
            jax.ShapeDtypeStruct((rows, pairs * 128), BF16),
            jax.ShapeDtypeStruct((rows, 128), BF16),
            jax.ShapeDtypeStruct((rows, pairs * 128), F32),
        ),
        in_specs=[
            pl.BlockSpec(block, lambda s, h: (s, h)),
            pl.BlockSpec(block, lambda s, h: (s, pairs)),
            pl.BlockSpec(block, lambda s, h: (0, 0)),
            pl.BlockSpec(block, lambda s, h: (0, 0)),
        ],
        out_specs=(
            pl.BlockSpec(block, lambda s, h: (s, h)),
            pl.BlockSpec(block, lambda s, h: (s, h)),
            pl.BlockSpec(block, lambda s, h: (s, 0)),
            pl.BlockSpec(block, lambda s, h: (s, h)),
        ),
        compiler_params=pltpu.CompilerParams(vmem_limit_bytes=60 * 1024 * 1024),
        cost_estimate=pl.CostEstimate(
            flops=8 * rows * length * 128 * pairs,
            bytes_accessed=rows * pairs * 128 * 12,
            transcendentals=rows * length * 2 * pairs,
        ),
        name="attend",
    )(pre, pre, cosine, signed)


def attend_back_kernel(
    seqs,
    rows,
    q_ref,
    kv_ref,
    up_ref,
    log_ref,
    cos_ref,
    sin_ref,
    left_ref,
    right_lead_ref,
    right_ref,
    hidden_ref,
    in_ref,
    back_ref,
    out_ref,
    laid_ref,
    sum_ref,
    ffn_ref,
    swapped,
    *scratch,
):
    def late():
        size = swapped.shape[2]
        for part in range(4):
            turned = jnp.transpose(swapped[part].astype(F32))
            laid_ref[part * size : (part + 1) * size, :] = turned.astype(BF16)

    across, along, forward, own, finish = scatter_steps(
        rows,
        lambda chip, start: left_ref[pl.ds(start, 2 * rows), :],
        lambda at: [right_lead_ref[at, :], right_ref[at, :]],
        ffn_ref,
        scratch[:-3],
        swap=(in_ref, swapped, *scratch[-3:]),
        late=late,
    )
    scale = HEAD_DIM ** (-0.5)
    length = q_ref.shape[0] // seqs
    pairs = q_ref.shape[1] // 128
    across()
    along()

    def one_pair(index, carry):
        seq = index // pairs
        pair = index % pairs
        lanes_at = pl.ds(pl.multiple_of(pair * 128, 128), 128)
        base = pl.multiple_of(seq * length, length)

        @pl.when(index == 1)
        def _():
            forward()

        @pl.when(index == 2)
        def _():
            own()

        @pl.when(pair == 0)
        def _():
            sum_ref[...] = jnp.zeros_like(sum_ref)

        for block in range(length // QB):
            here = pl.ds(base + block * QB, QB)
            turned = []
            q_pair = q_ref[here, lanes_at]
            up_pair = up_ref[here, lanes_at]
            log_pair = log_ref[here, lanes_at]
            for head in range(2):
                lanes = slice(head * HEAD_DIM, (head + 1) * HEAD_DIM)
                query = q_pair[:, lanes] * jnp.asarray(scale, BF16)
                upstream = up_pair[:, lanes]
                logs = log_pair[:, head * HEAD_DIM : head * HEAD_DIM + 1]
                saved = []
                inner = None
                for start, size, diagonal in pieces_of(block):
                    keys = kv_ref[pl.ds(base + start, size), :HEAD_DIM]
                    values = kv_ref[pl.ds(base + start, size), HEAD_DIM:]
                    probability = jnp.exp(masked_scores(query, keys, diagonal) - logs)
                    prob_grad = matmul_nt(upstream, values)
                    term = jnp.sum(probability * prob_grad, axis=1, keepdims=True)
                    inner = term if inner is None else inner + term
                    saved.append((start, size, probability, prob_grad))
                out = None
                for start, size, probability, prob_grad in saved:
                    keys = kv_ref[pl.ds(base + start, size), :HEAD_DIM]
                    score_grad = (probability * (prob_grad - inner)).astype(BF16)
                    rounded = probability.astype(BF16)
                    term = jnp.dot(score_grad, keys, preferred_element_type=F32)
                    out = term if out is None else out + term
                    sum_ref[pl.ds(start, size), :] += jnp.concatenate(
                        [matmul_t(score_grad, query), matmul_t(rounded, upstream)], axis=1
                    )
                turned.append(out * scale)
            grad = jnp.concatenate(turned, axis=1)
            angle = pl.ds(block * QB, QB)
            back_ref[here, lanes_at] = (
                grad * cos_ref[angle, :] - swap_halves(grad) * sin_ref[angle, :]
            ).astype(BF16)

        @pl.when(pair == pairs - 1)
        def _():
            grad = sum_ref[...]
            lane = lax.broadcasted_iota(jnp.int32, grad.shape, 1)
            back = grad * cos_ref[...] - swap_halves(grad) * sin_ref[...]
            back_ref[pl.ds(base, length), pairs * 128 :] = jnp.where(
                lane < HEAD_DIM, back, grad
            ).astype(BF16)

        return carry

    lax.fori_loop(0, seqs * pairs, one_pair, 0)
    finish()

    def add(index, carry):
        at = pl.ds(pl.multiple_of(index * 32, 32), 32)
        out_ref[at, :] = (hidden_ref[at, :] + ffn_ref[at, :]).astype(BF16)
        return carry

    lax.fori_loop(0, rows // 32, add, 0)


def attend_back(
    number, queries, keyvals, upstream, logs, cosine, signed, seqs, left, lead, right, hidden, swap
):
    total, width = queries.shape
    length = total // seqs
    rows = total // 8
    deep = swap.shape[0] // 4
    vmem = pl.BlockSpec(memory_space=pltpu.VMEM)
    return pl.pallas_call(
        functools.partial(attend_back_kernel, seqs, rows),
        out_shape=(
            jax.ShapeDtypeStruct((total, width + 128), BF16),
            jax.ShapeDtypeStruct(hidden.shape, BF16),
            jax.ShapeDtypeStruct((4 * swap.shape[1], deep), BF16),
        ),
        in_specs=[vmem] * 10 + [pl.BlockSpec(memory_space=pl.ANY)],
        out_specs=(vmem, vmem, vmem),
        scratch_shapes=[
            pltpu.VMEM((length, 128), F32),
            pltpu.VMEM(hidden.shape, F32),
            pltpu.VMEM((4, deep, swap.shape[1]), BF16),
        ]
        + scatter_scratch(rows, right.shape[0])
        + swap_scratch(),
        compiler_params=pltpu.CompilerParams(
            collective_id=number, has_side_effects=True, vmem_limit_bytes=56 * 1024 * 1024
        ),
        cost_estimate=pl.CostEstimate(flops=0, bytes_accessed=1024, transcendentals=0),
        name="attend_back",
    )(queries, keyvals, upstream, logs, cosine, signed, left, lead, right, hidden, swap)


def gain_kernel(
    planes,
    parts,
    cols,
    attn_term_ref,
    ffn_term_ref,
    up_ref,
    gain_ref,
    laid_ref,
    total,
    seen,
    far,
    mine,
    across,
    swapped,
    send_sems,
    recv_sems,
    *swap_sems,
):
    side, row, core, near_core, near_side, near_row = place()
    plane = lax.axis_index("dp")
    ctx = row * 2 + core
    others = [{"dp": (plane + step) % planes} for step in range(1, planes)]
    corner = {"ctx": (1 - row) * 2 + 1 - core}
    greet((near_core, near_side, near_row, corner) + tuple(others))
    first = lax.broadcasted_iota(jnp.int32, total.shape, 0) == 0
    total[...] = jnp.where(first, attn_term_ref[...], ffn_term_ref[...])
    copies = []
    up_copies, up_local = swap_copies(up_ref, swapped, *swap_sems)
    for number, target in enumerate((near_core, near_row)):
        copy = remote(
            total, seen.at[number], send_sems.at[number], recv_sems.at[number], target
        )
        copy.start()
        copy.wait()
        total[...] += seen[number]
    for copy in up_copies + [up_local]:
        copy.start()
    for step, target in enumerate(others, 1):
        start = (((plane + step) % planes) * parts + ctx) * cols
        copy = remote(
            total.at[:, pl.ds(pl.multiple_of(start, cols), cols)],
            far.at[step - 1],
            send_sems.at[2 + step],
            recv_sems.at[2 + step],
            target,
        )
        copy.start()
        copies.append(copy)
    start = (plane * parts + ctx) * cols
    value = total[:, pl.ds(pl.multiple_of(start, cols), cols)]
    for number, copy in enumerate(copies):
        copy.wait_recv()
        value += far[number]
    mine[...] = value
    last = remote(mine, across, send_sems.at[2], recv_sems.at[2], near_side)
    last.start()
    copies.append(last)
    for copy in up_copies:
        copy.wait()
    up_local.wait()
    size = swapped.shape[2]
    for part in range(4):
        laid_ref[:, part * size : (part + 1) * size] = swapped[part]
    last.wait_recv()
    gain_ref[...] = value + across[...]
    for copy in copies:
        copy.wait_send()


def gain_sum(number, attn_term, ffn_term, up_sum):
    planes = lax.axis_size("dp")
    parts = lax.axis_size("ctx")
    rows, width = attn_term.shape
    cols = width // (planes * parts)
    deep = up_sum.shape[0] // parts
    vmem = pl.BlockSpec(memory_space=pltpu.VMEM)
    anywhere = pl.BlockSpec(memory_space=pl.ANY)
    return pl.pallas_call(
        functools.partial(gain_kernel, planes, parts, cols),
        out_shape=(
            jax.ShapeDtypeStruct((rows, cols), F32),
            jax.ShapeDtypeStruct((deep, parts * up_sum.shape[1]), BF16),
        ),
        in_specs=[vmem, vmem, anywhere],
        out_specs=(vmem,) * 2,
        scratch_shapes=[
            pltpu.VMEM((rows, width), F32),
            pltpu.VMEM((2, rows, width), F32),
            pltpu.VMEM((planes - 1, rows, cols), F32),
            pltpu.VMEM((rows, cols), F32),
            pltpu.VMEM((rows, cols), F32),
            pltpu.VMEM((parts, deep, up_sum.shape[1]), BF16),
            pltpu.SemaphoreType.DMA((planes + 2,)),
            pltpu.SemaphoreType.DMA((planes + 2,)),
        ]
        + swap_scratch(),
        compiler_params=pltpu.CompilerParams(collective_id=number, has_side_effects=True),
        cost_estimate=pl.CostEstimate(flops=0, bytes_accessed=1024, transcendentals=0),
        name="gain_sum",
    )(attn_term, ffn_term, up_sum)


def last_kernel(
    q_cols, attn_ref, query_ref, key_ref, value_ref, wide_ref, swapped, *swap_sems
):
    _, row, core, near_core, _, near_row = place()
    greet((near_core, near_row, {"ctx": (1 - row) * 2 + 1 - core}))
    copies, local = swap_copies(attn_ref, swapped, *swap_sems)
    for copy in copies + [local]:
        copy.start()
    for copy in copies:
        copy.wait()
    local.wait()
    kv = key_ref.shape[1] // 4
    for part in range(4):
        query_ref[:, part * q_cols : (part + 1) * q_cols] = swapped[part, :, :q_cols]
        turned = jnp.transpose(swapped[part, :, q_cols + 2 * kv :].astype(F32))
        wide_ref[part * q_cols : (part + 1) * q_cols, :] = turned.astype(BF16)
    for at, target in ((q_cols, key_ref), (q_cols + kv, value_ref)):
        target[...] = jnp.concatenate(
            [swapped[part, :, at : at + kv] for part in range(4)], axis=1
        )


def last_swap(number, attn_sum, q_cols, kv_cols):
    parts = lax.axis_size("ctx")
    deep = attn_sum.shape[0] // parts
    vmem = pl.BlockSpec(memory_space=pltpu.VMEM)
    return pl.pallas_call(
        functools.partial(last_kernel, q_cols),
        out_shape=(
            jax.ShapeDtypeStruct((deep, parts * q_cols), BF16),
            jax.ShapeDtypeStruct((deep, parts * kv_cols), BF16),
            jax.ShapeDtypeStruct((deep, parts * kv_cols), BF16),
            jax.ShapeDtypeStruct((parts * q_cols, deep), BF16),
        ),
        in_specs=[pl.BlockSpec(memory_space=pl.ANY)],
        out_specs=(vmem,) * 4,
        scratch_shapes=[pltpu.VMEM((parts, deep, attn_sum.shape[1]), BF16)] + swap_scratch(),
        compiler_params=pltpu.CompilerParams(collective_id=number, has_side_effects=True),
        cost_estimate=pl.CostEstimate(flops=0, bytes_accessed=1024, transcendentals=0),
        name="last_swap",
    )(attn_sum)


def final_kernel(own_ref, other_ref, *refs):
    first = lax.axis_index("tensor") == 0
    half = len(refs) // 2
    sources, (out_ref, *targets) = refs[:half], refs[half:]
    own, other = own_ref[...].astype(out_ref.dtype), other_ref[...].astype(out_ref.dtype)
    out_ref[0], out_ref[1] = jnp.where(first, own, other), jnp.where(first, other, own)
    for source, target in zip(sources, targets):
        target[...] = source[...].astype(F32)


def final_forms(own, other, dtype, *grads):
    steps = 4
    rows, width = own.shape
    halves = pl.BlockSpec((rows // steps, width), lambda i: (i, 0))
    whole = pl.BlockSpec((2, rows // steps, width), lambda i: (0, i, 0))

    def block_of(grad):
        deep, wide = grad.shape
        if wide // steps % 128 == 0:
            return pl.BlockSpec((deep, wide // steps), lambda i: (0, i))
        return pl.BlockSpec((deep // steps, wide), lambda i: (i, 0))

    blocks = [block_of(grad) for grad in grads]
    return pl.pallas_call(
        final_kernel,
        grid=(steps,),
        out_shape=(jax.ShapeDtypeStruct((2, rows, width), dtype),)
        + tuple(jax.ShapeDtypeStruct(grad.shape, F32) for grad in grads),
        in_specs=[halves] * 2 + blocks,
        out_specs=(whole, *blocks),
        compiler_params=pltpu.CompilerParams(vmem_limit_bytes=60 * 1024 * 1024),
        cost_estimate=pl.CostEstimate(flops=0, bytes_accessed=1024, transcendentals=0),
        name="final_forms",
    )(own, other, *grads)


def lay_kernel(own_ref, far_ref, twin_ref, twin_far_ref, all_ref, sems):
    ctx = lax.axis_index("ctx")
    row, core = ctx // 2, ctx % 2
    span = own_ref.shape[1]
    copies = []
    for number, (part, a, b) in enumerate(
        (
            (own_ref, row, core),
            (twin_ref, row, 1 - core),
            (far_ref, 1 - row, core),
            (twin_far_ref, 1 - row, 1 - core),
        )
    ):
        start = pl.multiple_of((a * 2 + b) * span, span)
        copies.append(
            pltpu.make_async_copy(part, all_ref.at[:, pl.ds(start, span)], sems.at[number])
        )
        copies[-1].start()
    for copy in copies:
        copy.wait()


def along_ctx(block, earlier, later):
    seqs, span, width = block.shape
    cores = [(0, 1), (1, 0), (2, 3), (3, 2)]
    far = lax.ppermute(after(block, earlier), "ctx", [(0, 2), (1, 3), (2, 0), (3, 1)])
    far = after(far, later)
    twin, twin_far = lax.ppermute(block, "ctx", cores), lax.ppermute(far, "ctx", cores)
    return block, far, twin, twin_far


def lay_along(parts):
    seqs, span, width = parts[0].shape
    whole = pl.pallas_call(
        lay_kernel,
        out_shape=jax.ShapeDtypeStruct((seqs, 4 * span, width), parts[0].dtype),
        in_specs=[pl.BlockSpec(memory_space=pl.ANY)] * 4,
        out_specs=pl.BlockSpec(memory_space=pltpu.VMEM),
        scratch_shapes=[pltpu.SemaphoreType.DMA((4,))],
        compiler_params=pltpu.CompilerParams(vmem_limit_bytes=24 * 1024 * 1024),
        name="lay",
    )(*parts)
    return whole.reshape(seqs * 4 * span, width)


def open_kernel(
    planes,
    q_ref,
    key_ref,
    value_ref,
    out_ref,
    gate_ref,
    up_ref,
    down_in_ref,
    attn_ref,
    gate_up_ref,
    down_lead_ref,
    down_own_ref,
    key_in,
    value_in,
    out_in,
    down_in,
    kv_ref,
    wide_ref,
    down_ref,
    load_sems,
    send_sems,
    recv_sems,
    local_sems,
    line_send,
    line_recv,
):
    _, row, core, *_ = place()
    plane = lax.axis_index("dp")
    here = row * 2 + core
    rows, units = q_ref.shape[0], gate_ref.shape[1] // 4
    peers = (row * 2 + 1 - core, (1 - row) * 2 + core, (1 - row) * 2 + 1 - core)
    ahead, behind = {"dp": (plane + 1) % planes}, {"dp": (plane + planes - 1) % planes}
    barrier = pltpu.get_barrier_semaphore()
    more, fewer = plane + 1 < planes, plane > 0
    for peer in peers:
        pl.semaphore_signal(barrier, inc=1, device_id={"ctx": peer}, device_id_type=MESH_ID)

    @pl.when(more)
    def _():
        pl.semaphore_signal(barrier, inc=1, device_id=ahead, device_id_type=MESH_ID)

    @pl.when(fewer)
    def _():
        pl.semaphore_signal(barrier, inc=1, device_id=behind, device_id_type=MESH_ID)

    loads = [
        pltpu.make_async_copy(source, target, load_sems.at[at])
        for at, (source, target) in enumerate(
            ((key_ref, key_in), (value_ref, value_in), (out_ref, out_in), (down_in_ref, down_in))
        )
    ]
    for load in loads:
        load.start()
    for load in loads[:3]:
        load.wait()
    size = key_in.shape[1] // 4
    for part in range(4):
        lanes = slice(part * size, (part + 1) * size)
        kv_ref[:, part * 2 * size : (part + 1) * 2 * size] = jnp.concatenate(
            [key_in[:, lanes], value_in[:, lanes]], axis=1
        )
    wide_ref[...] = jnp.transpose(out_in[...].astype(F32)).astype(BF16)
    pl.semaphore_wait(barrier, 3 + more.astype(jnp.int32) + fewer.astype(jnp.int32))

    mine = pl.multiple_of(here * rows, rows)
    base = pl.multiple_of(plane * 4 * rows, 4 * rows)
    moves = []
    start = 0
    for source in (q_ref, kv_ref, wide_ref):
        cols = source.shape[1] // 4
        target = attn_ref.at[pl.ds(base + mine, rows), pl.ds(start, cols)]
        moves.append((source, cols, 0, cols, target))
        start += cols
    for which, source in enumerate((gate_ref, up_ref)):
        target = gate_up_ref.at[pl.ds(mine, rows), pl.ds(which * units, units)]
        moves.append((source, units, 0, units, target))
    lead = down_lead_ref.shape[1]
    moves.append((down_ref, units, 0, lead, down_lead_ref.at[pl.ds(mine, rows)]))
    moves.append((down_ref, units, lead, units - lead, down_own_ref.at[pl.ds(mine, rows)]))
    away, local = [], []
    for which, (source, stride, shift, cols, target) in enumerate(moves):

        def columns(index, source=source, stride=stride, shift=shift, cols=cols):
            return source.at[:, pl.ds(pl.multiple_of(index * stride + shift, 128), cols)]

        away.append(
            [
                remote(
                    columns(peer),
                    target,
                    send_sems.at[which, at],
                    recv_sems.at[which, at],
                    {"ctx": peer},
                )
                for at, peer in enumerate(peers)
            ]
        )
        local.append(pltpu.make_async_copy(columns(here), target, local_sems.at[which]))
    for which in range(3):
        away[which][0].start()
        local[which].start()
    for at in (1, 2):
        for which in range(3):
            away[which][at].start()
    for which in range(3, 5):
        for copy in away[which]:
            copy.start()
        local[which].start()

    def hop(way, far, part):
        whose = plane - far if way == 0 else plane + far
        half = row if part == 0 else 1 - row
        spot = attn_ref.at[
            pl.ds(pl.multiple_of((whose * 4 + half * 2) * rows, 2 * rows), 2 * rows)
        ]
        return remote(
            spot,
            spot,
            line_send.at[way, far, part],
            line_recv.at[way, far, part],
            ahead if way == 0 else behind,
        )

    def sends(way, far):
        if way == 0:
            return (plane - far >= 0) & more
        return (plane + far < planes) & fewer

    def gets(way, far):
        return plane - 1 - far >= 0 if way == 0 else plane + 1 + far < planes

    def hop_start(way, far, part):
        @pl.when(sends(way, far))
        def _():
            hop(way, far, part).start()

    for which in range(3):
        local[which].wait()
        away[which][0].wait_recv()
    for way in range(2):
        hop_start(way, 0, 0)
    for which in range(3):
        away[which][1].wait_recv()
        away[which][2].wait_recv()
    for way in range(2):
        hop_start(way, 0, 1)
    loads[3].wait()
    for part in range(4):
        there = slice(part * units, (part + 1) * units)
        down_ref[:, there] = jnp.transpose(down_in[there, :].astype(F32)).astype(BF16)
    for copy in away[5] + away[6] + [local[5], local[6]]:
        copy.start()
    for far in range(planes - 1):
        for part in range(2):
            for way in range(2):

                @pl.when(gets(way, far))
                def _(way=way, far=far, part=part):
                    hop(way, far, part).wait_recv()

                if far + 1 < planes - 1:
                    hop_start(way, far + 1, part)
    for far in range(planes - 1):
        for part in range(2):
            for way in range(2):

                @pl.when(sends(way, far))
                def _(way=way, far=far, part=part):
                    hop(way, far, part).wait_send()

    for which in range(7):
        if which > 2:
            local[which].wait()
            for copy in away[which]:
                copy.wait_recv()
        for copy in away[which]:
            copy.wait_send()


def open_weights(query, key, value, out, gate, up, down, lead):
    planes = lax.axis_size("dp")
    rows = query.shape[0]
    cols = (query.shape[1] + 2 * key.shape[1] + out.shape[0]) // 4
    units = gate.shape[1] // 4
    anywhere, vmem = pl.BlockSpec(memory_space=pl.ANY), pl.BlockSpec(memory_space=pltpu.VMEM)
    return pl.pallas_call(
        functools.partial(open_kernel, planes),
        out_shape=(
            jax.ShapeDtypeStruct((planes * 4 * rows, cols), BF16),
            jax.ShapeDtypeStruct((4 * rows, 2 * units), BF16),
            jax.ShapeDtypeStruct((4 * rows, lead), BF16),
            jax.ShapeDtypeStruct((4 * rows, units - lead), BF16),
        ),
        in_specs=[anywhere] * 7,
        out_specs=(vmem, anywhere, anywhere, anywhere),
        scratch_shapes=[
            pltpu.VMEM(key.shape, BF16),
            pltpu.VMEM(value.shape, BF16),
            pltpu.VMEM(out.shape, BF16),
            pltpu.VMEM(down.shape, BF16),
            pltpu.VMEM((rows, 2 * key.shape[1]), BF16),
            pltpu.VMEM((rows, out.shape[0]), BF16),
            pltpu.VMEM((rows, down.shape[0]), BF16),
            pltpu.SemaphoreType.DMA((4,)),
            pltpu.SemaphoreType.DMA((7, 3)),
            pltpu.SemaphoreType.DMA((7, 3)),
            pltpu.SemaphoreType.DMA((7,)),
            pltpu.SemaphoreType.DMA((2, planes - 1, 2)),
            pltpu.SemaphoreType.DMA((2, planes - 1, 2)),
        ],
        compiler_params=pltpu.CompilerParams(
            collective_id=6, has_side_effects=True, vmem_limit_bytes=60 * 1024 * 1024
        ),
        cost_estimate=pl.CostEstimate(flops=0, bytes_accessed=1024, transcendentals=0),
        name="open_weights",
    )(query, key, value, out, gate, up, down)


def after(value, *earlier):
    return lax.optimization_barrier((value,) + earlier)[0]


def to_units(weight):
    return lax.all_to_all(weight, "ctx", split_axis=1, concat_axis=0, tiled=True)


def swap_sides(block):
    return lax.ppermute(block, "tensor", [(0, 1), (1, 0)])


def on_plane(
    layer_input,
    attn_gain,
    w_query,
    w_key,
    w_value,
    w_out,
    ffn_gain,
    w_gate,
    w_up,
    w_down,
    cotangent,
):
    seqs, span, width = layer_input.shape
    planes = lax.axis_size("dp")
    parts = lax.axis_size("ctx")
    side = lax.axis_index("tensor")
    length = span * parts
    rows_w = w_query.shape[0]
    q_cols = w_query.shape[1] // parts
    kv_cols = w_key.shape[1] // parts

    theta = angles(jnp.arange(length), HEAD_DIM)
    cosine = jnp.tile(jnp.cos(theta), (1, 4))
    sine = jnp.sin(theta)
    signed = jnp.tile(jnp.concatenate([-sine, sine], axis=1), (1, 2))

    attn_w, gate_up, lead_own, down_own = open_weights(
        w_query, w_key, w_value, w_out, w_gate, w_up, w_down, w_down.shape[0] // parts // 8
    )
    qkv_cols = q_cols + 2 * kv_cols
    w_qkv = attn_w[:, :qkv_cols]
    w_out_t = attn_w[:, qkv_cols:]
    own_in = lax.dynamic_index_in_dim(layer_input, side, 0, keepdims=False)
    own_cot = lax.dynamic_index_in_dim(cotangent, side, 0, keepdims=False)
    gains = jnp.concatenate(
        [attn_gain[None], ffn_gain[None], jnp.zeros((6, rows_w), BF16)]
    ).astype(F32)
    all_in, gains = plane_gather(after(own_in, gate_up), 10, gains=gains)
    gain_one = gains[:, 0].reshape(width)
    gain_two = gains[:, 1].reshape(width)
    gate_up = lax.all_gather(gate_up, "dp", axis=0, tiled=True)
    down_w = lax.all_gather(down_own, "dp", axis=0, tiled=True)

    all_f = all_in.astype(F32)
    normed_one = (all_f * rms_factor(all_f) * gain_one).astype(BF16)
    pre = jnp.dot(normed_one, w_qkv, preferred_element_type=F32)
    attended, queries, keyvals, logs = attend(pre, cosine, signed, seqs)
    inputs_f = own_in.astype(F32)
    factor_one = rms_factor(inputs_f)
    hidden = inputs_f + product_scatter(1, attended, attn_w, qkv_cols, q_cols)[0]
    factor_two = rms_factor(hidden)
    normed_own = (hidden * factor_two * gain_two).astype(BF16)
    normed_two, down_lead = plane_gather(normed_own, shard=lead_own)
    cots = along_ctx(cotangent, all_in, hidden)

    product, gate_slope, up_slope = ffn(normed_two, gate_up)
    all_cot = lay_along((after(cots[0], product),) + cots[1:])
    down_grad = matmul_t(all_cot, product).astype(BF16)
    down_sum = lax.psum_scatter(down_grad, "dp", scatter_dimension=0, tiled=True)
    hidden_grad, hidden_own, ffn_term, gate_grad, up_grad = ffn_back(
        3,
        cots,
        after(gate_slope, down_grad),
        up_slope,
        down_lead,
        down_w,
        gate_up,
        (hidden, factor_two, gain_two[None], own_cot),
    )
    gate_w_grad = matmul_t(normed_two, gate_grad).astype(BF16)
    gate_sum = lax.psum_scatter(gate_w_grad, "dp", scatter_dimension=0, tiled=True)
    hidden_low, up_w_grad = plane_gather(after(hidden_own, gate_w_grad), 7, [normed_two, up_grad])
    up_sum = lax.psum_scatter(up_w_grad, "dp", scatter_dimension=0, tiled=True)
    attended_grad = jnp.dot(after(hidden_low, up_w_grad), w_out_t, preferred_element_type=F32).astype(BF16)
    out_w_grad = matmul_t(hidden_low, attended).astype(BF16)
    back, out_own, down_out = attend_back(
        5,
        queries,
        keyvals,
        attended_grad,
        logs,
        cosine,
        signed,
        seqs,
        product,
        down_lead,
        down_w,
        hidden,
        down_sum,
    )
    out_other = swap_sides(out_own)
    qkv_grad = matmul_t(normed_one, back).astype(BF16)
    attn_grad = jnp.concatenate([qkv_grad, out_w_grad], axis=1)
    attn_sum = lax.psum_scatter(attn_grad, "dp", scatter_dimension=0, tiled=True)
    input_own, attn_term, gate_out = product_scatter(
        4,
        after(back, attn_grad),
        attn_w,
        0,
        qkv_cols,
        gate_sum,
        (inputs_f, factor_one, gain_one[None], hidden_grad),
    )
    input_other = swap_sides(input_own)
    layer_output, gate_out, down_out = final_forms(
        out_own, after(out_other, input_own), BF16, gate_out, down_out
    )
    gain_own, up_out = gain_sum(2, after(attn_term, layer_output), ffn_term, up_sum)
    query_out, key_out, value_out, wide_out = last_swap(
        9, after(attn_sum, gain_own), q_cols, kv_cols
    )
    input_grad, query_out, key_out, value_out, wide_out, up_out = final_forms(
        input_own,
        after(input_other, gain_own),
        F32,
        query_out,
        key_out,
        value_out,
        wide_out,
        up_out,
    )
    return (
        layer_output,
        input_grad,
        gain_own[0],
        query_out,
        key_out,
        value_out,
        wide_out,
        gain_own[1],
        gate_out,
        up_out,
        down_out,
    )


def fits_plane(mesh, shapes):
    sizes = mesh.shape
    seqs, length, width = shapes[0].shape
    kv_heads = shapes[3].shape[1] // HEAD_DIM
    return (
        sizes["tensor"] == 2
        and sizes["ctx"] == 4
        and seqs == 2 * sizes["dp"]
        and kv_heads == 8
        and shapes[2].shape[1] == 4 * shapes[3].shape[1]
        and length % (4 * QB) == 0
        and width % (128 * 4 * sizes["dp"]) == 0
    )


def placed(mesh, function):
    return jax.shard_map(
        function,
        mesh=mesh,
        in_specs=(
            P("dp", "ctx", None),
            P(("dp", "ctx")),
            P(("dp", "ctx"), "tensor"),
            P(("dp", "ctx"), "tensor"),
            P(("dp", "ctx"), "tensor"),
            P("tensor", ("dp", "ctx")),
            P(("dp", "ctx")),
            P(("dp", "ctx"), "tensor"),
            P(("dp", "ctx"), "tensor"),
            P("tensor", ("dp", "ctx")),
            P("dp", "ctx", None),
        ),
        out_specs=(
            P("dp", "ctx", None),
            P("dp", "ctx", None),
            P(("dp", "ctx")),
            P(("dp", "ctx"), "tensor"),
            P(("dp", "ctx"), "tensor"),
            P(("dp", "ctx"), "tensor"),
            P("tensor", ("dp", "ctx")),
            P(("dp", "ctx")),
            P(("dp", "ctx"), "tensor"),
            P(("dp", "ctx"), "tensor"),
            P("tensor", ("dp", "ctx")),
        ),
        check_vma=False,
    )


def solution(mesh):
    def whole(*arrays):
        return placed(mesh, on_plane if fits_plane(mesh, arrays) else on_device)(*arrays)

    return whole
```

```python
import functools
import math

import jax
import jax.numpy as jnp
from jax import lax
from jax.experimental import pallas as pl
from jax.experimental.pallas import tpu as pltpu
from jax.sharding import PartitionSpec as P

HEAD_DIM = 64


EPSILON = 1e-05
ROPE_BASE = 500000.0


def rotate(values, cosine, sine_val):
    middle = values.shape[-1] // 2
    leading = values[..., :middle]
    trailing = values[..., middle:]
    return jnp.concatenate(
        [leading * cosine - trailing * sine_val, trailing * cosine + leading * sine_val], axis=-1
    )


def unrotate(gradient, cosine, sine_val):
    middle = gradient.shape[-1] // 2
    leading = gradient[..., :middle]
    trailing = gradient[..., middle:]
    return jnp.concatenate(
        [leading * cosine + trailing * sine_val, trailing * cosine - leading * sine_val], axis=-1
    )


def angles(positions, head_dim):
    exponent = jnp.arange(head_dim // 2).astype(jnp.float32) * (
        -2.0 * math.log(ROPE_BASE) / head_dim
    )
    return positions.astype(jnp.float32)[:, None] * jnp.exp(exponent)[None, :]


def rms_factor(row_values):
    return lax.rsqrt(jnp.mean(row_values * row_values, axis=-1, keepdims=True) + EPSILON)


def rms_back(upstream, row_values, factor, gain_row):
    scaled = upstream * gain_row
    gain_term = jnp.sum(upstream * row_values * factor, axis=0)
    inner_mean = jnp.mean(scaled * row_values, axis=-1, keepdims=True)
    return (factor * scaled - row_values * (factor * factor * factor) * inner_mean, gain_term)


def matmul_t(left_op, right_op):
    return lax.dot_general(
        left_op, right_op, (((0,), (0,)), ((), ())), preferred_element_type=jnp.float32
    )


def matmul_nt(left_op, right_op):
    return lax.dot_general(
        left_op, right_op, (((1,), (1,)), ((), ())), preferred_element_type=jnp.float32
    )


def on_device(
    layer_input,
    attn_gain,
    w_query,
    w_key,
    w_value,
    w_out,
    ffn_gain,
    w_gate,
    w_up,
    w_down,
    cotangent,
):
    seq_dev, span_len, model_width = layer_input.shape
    row_count = seq_dev * span_len
    length_all = span_len * lax.axis_size("ctx")
    full_q, full_k, full_v, full_o, full_gate, full_up, full_down, gain_attn, gain_ffn = (
        lax.all_gather(w_query, ("dp", "ctx"), axis=0, tiled=True),
        lax.all_gather(w_key, ("dp", "ctx"), axis=0, tiled=True),
        lax.all_gather(w_value, ("dp", "ctx"), axis=0, tiled=True),
        lax.all_gather(w_out, ("dp", "ctx"), axis=1, tiled=True),
        lax.all_gather(w_gate, ("dp", "ctx"), axis=0, tiled=True),
        lax.all_gather(w_up, ("dp", "ctx"), axis=0, tiled=True),
        lax.all_gather(w_down, ("dp", "ctx"), axis=1, tiled=True),
        lax.all_gather(attn_gain, ("dp", "ctx"), axis=0, tiled=True),
        lax.all_gather(ffn_gain, ("dp", "ctx"), axis=0, tiled=True),
    )
    kv_local = full_k.shape[1] // HEAD_DIM
    group_size = full_q.shape[1] // HEAD_DIM // kv_local
    block_count = seq_dev * kv_local
    scale = HEAD_DIM ** (-0.5)
    query_pos = lax.axis_index("ctx") * span_len + jnp.arange(span_len)
    theta = angles(query_pos, HEAD_DIM)
    cosine = jnp.cos(theta)
    sine_val = jnp.sin(theta)
    causal = query_pos[:, None] >= jnp.arange(length_all)[None, :]
    inputs_f = layer_input.reshape(row_count, model_width).astype(jnp.float32)
    gain_one = gain_attn.astype(jnp.float32)
    gain_two = gain_ffn.astype(jnp.float32)
    factor_one = rms_factor(inputs_f)
    normed_one = (inputs_f * factor_one * gain_one).astype(jnp.bfloat16)
    query_pre = jnp.dot(normed_one, full_q, preferred_element_type=jnp.float32).reshape(
        seq_dev, span_len, kv_local, group_size, HEAD_DIM
    )
    queries = rotate(
        query_pre, cosine[None, :, None, None, :], sine_val[None, :, None, None, :]
    ).astype(jnp.bfloat16)
    key_pre = jnp.dot(normed_one, full_k, preferred_element_type=jnp.float32).reshape(
        seq_dev, span_len, kv_local, HEAD_DIM
    )
    keys_own = (
        rotate(key_pre, cosine[None, :, None, :], sine_val[None, :, None, :])
        .astype(jnp.bfloat16)
        .reshape(seq_dev, span_len, kv_local * HEAD_DIM)
    )
    values_own = (
        jnp.dot(normed_one, full_v, preferred_element_type=jnp.float32)
        .astype(jnp.bfloat16)
        .reshape(seq_dev, span_len, kv_local * HEAD_DIM)
    )
    keys_all, values_all = (
        lax.all_gather(keys_own, "ctx", axis=1, tiled=True),
        lax.all_gather(values_own, "ctx", axis=1, tiled=True),
    )
    query_blocks = jnp.transpose(queries, (0, 2, 1, 3, 4)).reshape(
        block_count, span_len, group_size, HEAD_DIM
    )
    key_blocks = jnp.transpose(
        keys_all.reshape(seq_dev, length_all, kv_local, HEAD_DIM), (0, 2, 1, 3)
    ).reshape(block_count, length_all, HEAD_DIM)
    value_blocks = jnp.transpose(
        values_all.reshape(seq_dev, length_all, kv_local, HEAD_DIM), (0, 2, 1, 3)
    ).reshape(block_count, length_all, HEAD_DIM)

    def scores_of(query_b, key_b):
        raw_scores = jnp.einsum("qgd,kd->gqk", query_b, key_b, preferred_element_type=jnp.float32)
        return jnp.where(causal[None], raw_scores * scale, -1e30)

    def attend(block_in):
        query_b, key_b, value_b = block_in
        scores = scores_of(query_b, key_b)
        peak_row = jnp.max(scores, axis=-1, keepdims=True)
        powers = jnp.exp(scores - peak_row)
        total_sum = jnp.sum(powers, axis=-1, keepdims=True)
        probability = (powers / total_sum).astype(jnp.bfloat16)
        mixed = jnp.einsum("gqk,kd->qgd", probability, value_b, preferred_element_type=jnp.float32)
        return (mixed.astype(jnp.bfloat16), peak_row + jnp.log(total_sum))

    mixed_blocks, logsum = lax.map(attend, (query_blocks, key_blocks, value_blocks))
    attended = jnp.transpose(
        mixed_blocks.reshape(seq_dev, kv_local, span_len, group_size, HEAD_DIM), (0, 2, 1, 3, 4)
    ).reshape(row_count, kv_local * group_size * HEAD_DIM)
    attn_part = jnp.dot(attended, full_o, preferred_element_type=jnp.float32)
    hidden = inputs_f + lax.psum(attn_part, "tensor")
    factor_two = rms_factor(hidden)
    normed_two = (hidden * factor_two * gain_two).astype(jnp.bfloat16)
    gate_pre = jnp.dot(normed_two, full_gate, preferred_element_type=jnp.float32)
    up_pre = jnp.dot(normed_two, full_up, preferred_element_type=jnp.float32)
    sigma = jax.nn.sigmoid(gate_pre)
    product = (gate_pre * sigma * up_pre).astype(jnp.bfloat16)
    ffn_part = jnp.dot(product, full_down, preferred_element_type=jnp.float32)
    out_f = hidden + lax.psum(ffn_part.astype(jnp.bfloat16), "tensor").astype(jnp.float32)
    layer_output = out_f.astype(jnp.bfloat16).reshape(seq_dev, span_len, model_width)
    grad_out = cotangent.reshape(row_count, model_width).astype(jnp.float32)
    grad_low = cotangent.reshape(row_count, model_width)
    down_grad = matmul_t(product, grad_low)
    prod_grad = matmul_nt(grad_low, full_down)
    gate_grad = (prod_grad * up_pre * sigma * (1.0 + gate_pre * (1.0 - sigma))).astype(jnp.bfloat16)
    up_grad = (prod_grad * gate_pre * sigma).astype(jnp.bfloat16)
    gate_w_grad = matmul_t(normed_two, gate_grad)
    up_w_grad = matmul_t(normed_two, up_grad)
    normed_two_part = matmul_nt(gate_grad, full_gate) + matmul_nt(up_grad, full_up)
    normed_two_grad = lax.psum(normed_two_part, "tensor")
    hidden_back, ffn_gain_term = rms_back(normed_two_grad, hidden, factor_two, gain_two)
    hidden_grad = grad_out + hidden_back
    hidden_low = hidden_grad.astype(jnp.bfloat16)
    out_w_grad = matmul_t(attended, hidden_low)
    attended_grad = matmul_nt(hidden_low, full_o).astype(jnp.bfloat16)
    upstream_blocks = jnp.transpose(
        attended_grad.reshape(seq_dev, span_len, kv_local, group_size, HEAD_DIM), (0, 2, 1, 3, 4)
    ).reshape(block_count, span_len, group_size, HEAD_DIM)

    def attend_back(block_in):
        query_b, key_b, value_b, logsum_b, upstream_b = block_in
        scores = scores_of(query_b, key_b)
        probability = jnp.exp(scores - logsum_b)
        rounded = probability.astype(jnp.bfloat16)
        value_grad = jnp.einsum(
            "gqk,qgd->kd", rounded, upstream_b, preferred_element_type=jnp.float32
        )
        prob_grad = jnp.einsum(
            "qgd,kd->gqk", upstream_b, value_b, preferred_element_type=jnp.float32
        )
        inner_sum = jnp.sum(probability * prob_grad, axis=-1, keepdims=True)
        score_grad = (probability * (prob_grad - inner_sum)).astype(jnp.bfloat16)
        query_grad = (
            jnp.einsum("gqk,kd->qgd", score_grad, key_b, preferred_element_type=jnp.float32) * scale
        )
        key_grad = (
            jnp.einsum("gqk,qgd->kd", score_grad, query_b, preferred_element_type=jnp.float32)
            * scale
        )
        return (query_grad, key_grad, value_grad)

    query_grads, key_grads, value_grads = lax.map(
        attend_back, (query_blocks, key_blocks, value_blocks, logsum, upstream_blocks)
    )
    key_rows = jnp.transpose(
        key_grads.reshape(seq_dev, kv_local, length_all, HEAD_DIM), (0, 2, 1, 3)
    ).reshape(seq_dev, length_all, kv_local * HEAD_DIM)
    value_rows = jnp.transpose(
        value_grads.reshape(seq_dev, kv_local, length_all, HEAD_DIM), (0, 2, 1, 3)
    ).reshape(seq_dev, length_all, kv_local * HEAD_DIM)
    key_mine, value_mine = (
        lax.psum_scatter(key_rows, "ctx", scatter_dimension=1, tiled=True),
        lax.psum_scatter(value_rows, "ctx", scatter_dimension=1, tiled=True),
    )
    key_low = (
        unrotate(
            key_mine.reshape(seq_dev, span_len, kv_local, HEAD_DIM),
            cosine[None, :, None, :],
            sine_val[None, :, None, :],
        )
        .astype(jnp.bfloat16)
        .reshape(row_count, kv_local * HEAD_DIM)
    )
    value_low = value_mine.astype(jnp.bfloat16).reshape(row_count, kv_local * HEAD_DIM)
    query_rot = jnp.transpose(
        query_grads.reshape(seq_dev, kv_local, span_len, group_size, HEAD_DIM), (0, 2, 1, 3, 4)
    )
    query_low = (
        unrotate(query_rot, cosine[None, :, None, None, :], sine_val[None, :, None, None, :])
        .astype(jnp.bfloat16)
        .reshape(row_count, kv_local * group_size * HEAD_DIM)
    )
    query_w_grad = matmul_t(normed_one, query_low)
    key_w_grad = matmul_t(normed_one, key_low)
    value_w_grad = matmul_t(normed_one, value_low)
    normed_one_part = (
        matmul_nt(query_low, full_q) + matmul_nt(key_low, full_k) + matmul_nt(value_low, full_v)
    )
    normed_one_grad = lax.psum(normed_one_part.astype(jnp.bfloat16), "tensor").astype(jnp.float32)
    input_back, attn_gain_term = rms_back(normed_one_grad, inputs_f, factor_one, gain_one)
    input_grad = (hidden_grad + input_back).reshape(seq_dev, span_len, model_width)
    (
        query_sum,
        key_sum,
        value_sum,
        out_sum,
        gate_sum,
        up_sum,
        down_sum,
        attn_gain_sum,
        ffn_gain_sum,
    ) = (
        lax.psum_scatter(query_w_grad, ("dp", "ctx"), scatter_dimension=0, tiled=True),
        lax.psum_scatter(key_w_grad, ("dp", "ctx"), scatter_dimension=0, tiled=True),
        lax.psum_scatter(value_w_grad, ("dp", "ctx"), scatter_dimension=0, tiled=True),
        lax.psum_scatter(out_w_grad, ("dp", "ctx"), scatter_dimension=1, tiled=True),
        lax.psum_scatter(gate_w_grad, ("dp", "ctx"), scatter_dimension=0, tiled=True),
        lax.psum_scatter(up_w_grad, ("dp", "ctx"), scatter_dimension=0, tiled=True),
        lax.psum_scatter(down_grad, ("dp", "ctx"), scatter_dimension=1, tiled=True),
        lax.psum_scatter(attn_gain_term, ("dp", "ctx"), scatter_dimension=0, tiled=True),
        lax.psum_scatter(ffn_gain_term, ("dp", "ctx"), scatter_dimension=0, tiled=True),
    )
    return (
        layer_output,
        input_grad,
        attn_gain_sum,
        query_sum,
        key_sum,
        value_sum,
        out_sum,
        ffn_gain_sum,
        gate_sum,
        up_sum,
        down_sum,
    )


MESH_ID = pl.DeviceIdType.MESH
BF16 = jnp.bfloat16
F32 = jnp.float32
QB = 256


def place():
    side = lax.axis_index("tensor")
    ctx = lax.axis_index("ctx")
    row = ctx // 2
    core = ctx % 2
    near_core = {"ctx": row * 2 + (1 - core)}
    near_side = {"tensor": 1 - side}
    near_row = {"ctx": (1 - row) * 2 + core}
    return side, row, core, near_core, near_side, near_row


def greet(neighbours):
    barrier = pltpu.get_barrier_semaphore()
    for target in neighbours:
        pl.semaphore_signal(barrier, inc=1, device_id=target, device_id_type=MESH_ID)
    pl.semaphore_wait(barrier, len(neighbours))


def remote(source, target, send_sem, recv_sem, device):
    return pltpu.make_async_remote_copy(
        src_ref=source,
        dst_ref=target,
        send_sem=send_sem,
        recv_sem=recv_sem,
        device_id=device,
        device_id_type=MESH_ID,
    )


class Line:
    def __init__(self, planes, all_ref, send_sems, recv_sems):
        self.planes, self.all_ref = planes, all_ref
        self.send_sems, self.recv_sems = send_sems, recv_sems
        self.plane = lax.axis_index("dp")
        self.rows = all_ref.shape[0] // planes
        self.more, self.fewer = self.plane + 1 < planes, self.plane > 0
        self.ahead = {"dp": (self.plane + 1) % planes}
        self.behind = {"dp": (self.plane + planes - 1) % planes}

    def shard(self, whose):
        return self.all_ref.at[pl.ds(pl.multiple_of(whose * self.rows, self.rows), self.rows)]

    def greet(self, neighbours):
        barrier = pltpu.get_barrier_semaphore()
        for target in neighbours:
            pl.semaphore_signal(barrier, inc=1, device_id=target, device_id_type=MESH_ID)
        for there, target in ((self.more, self.ahead), (self.fewer, self.behind)):

            @pl.when(there)
            def _(target=target):
                pl.semaphore_signal(barrier, inc=1, device_id=target, device_id_type=MESH_ID)

        count = len(neighbours) + self.more.astype(jnp.int32) + self.fewer.astype(jnp.int32)
        pl.semaphore_wait(barrier, count)

    def hop(self, way, far):
        spot = self.shard(self.plane - far if way == 0 else self.plane + far)
        return remote(
            spot,
            spot,
            self.send_sems.at[way, far],
            self.recv_sems.at[way, far],
            self.ahead if way == 0 else self.behind,
        )

    def sends(self, way, far):
        if way == 0:
            return (self.plane - far >= 0) & self.more
        return (self.plane + far < self.planes) & self.fewer

    def gets(self, way, far):
        if way == 0:
            return self.plane - 1 - far >= 0
        return self.plane + 1 + far < self.planes

    def send(self, far):
        for way in range(2):

            @pl.when(self.sends(way, far))
            def _(way=way):
                self.hop(way, far).start()

    def take(self, far):
        for way in range(2):

            @pl.when(self.gets(way, far))
            def _(way=way):
                self.hop(way, far).wait_recv()

        if far + 1 < self.planes - 1:
            self.send(far + 1)

    def settle(self):
        for far in range(self.planes - 1):
            for way in range(2):

                @pl.when(self.sends(way, far))
                def _(way=way, far=far):
                    self.hop(way, far).wait_send()


def gather_kernel(rows, works, planes, lines, block_ref, *refs):
    if works:
        left_ref, right_ref, all_ref, grad_ref, send_sems, recv_sems, local_sem = refs
    elif planes:
        gains_ref, all_ref, all_gains_ref, send_sems, recv_sems, local_sem, *gain_sems = refs
    elif lines:
        shard_ref, all_ref, line_ref, send_sems, recv_sems, local_sem, *line_sems = refs
        line = Line(lines, line_ref, *line_sems[:2])
    else:
        all_ref, send_sems, recv_sems, local_sem = refs
    side, row, core, near_core, near_side, near_row = place()
    half = rows // 2

    def work(first, last):
        if not works:
            return
        size = left_ref.shape[1] // works

        def step(index, carry):
            at = pl.ds(pl.multiple_of(index * size, size), size)
            grad_ref[at, :] = matmul_t(left_ref[:, at], right_ref[...]).astype(BF16)
            return carry

        lax.fori_loop(first * works // 8, last * works // 8, step, 0)

    def spot(a, b, c, part=None):
        start = (a * 4 + b * 2 + c) * rows
        if part is None:
            return all_ref.at[pl.ds(pl.multiple_of(start, rows), rows)]
        return all_ref.at[pl.ds(pl.multiple_of(start + part * half, half), half)]

    targets = []
    if planes:
        plane = lax.axis_index("dp")
        here = row * 2 + core
        targets = [
            {"dp": (plane + step) % planes, "ctx": (here + turn) % 4}
            for step in range(planes)
            for turn in range(4)
            if step or turn
        ]
    if lines:
        line.greet([near_side, near_core, near_row])
    else:
        greet([near_side] + (targets if planes else [near_core, near_row]))
    copies = []

    def send(number, source, target, device):
        copy = remote(source, target, send_sems.at[number], recv_sems.at[number], device)
        copy.start()
        copies.append(copy)
        return copy

    gain_copies = []
    if planes:
        mine = all_gains_ref.at[plane * 4 + here]
        gain_copies = [
            remote(gains_ref, mine, gain_sems[0].at[at], gain_sems[1].at[at], target)
            for at, target in enumerate(targets)
        ] + [pltpu.make_async_copy(gains_ref, mine, gain_sems[2])]
        for copy in gain_copies:
            copy.start()
    first = block_ref.at[pl.ds(0, half)]
    second = block_ref.at[pl.ds(half, half)]
    side_b = send(0, second, spot(side, row, core, 1), near_side)
    row_a = send(1, first, spot(side, row, core, 0), near_row)
    side_a = send(2, first, spot(side, row, core, 0), near_side)
    row_b = send(3, second, spot(side, row, core, 1), near_row)
    core_own = send(4, block_ref, spot(side, row, core), near_core)
    local = pltpu.make_async_copy(block_ref, spot(side, row, core), local_sem)
    local.start()
    if lines:
        own = pltpu.make_async_copy(shard_ref, line.shard(line.plane), line_sems[2])
        own.start()
        own.wait()
        line.send(0)
    work(0, 6)
    side_b.wait_recv()
    away_b = send(5, spot(1 - side, row, core, 1), spot(1 - side, row, core, 1), near_row)
    row_a.wait_recv()
    away_a = send(6, spot(side, 1 - row, core, 0), spot(side, 1 - row, core, 0), near_side)
    work(6, 8)
    if lines:
        line.take(0)
    side_a.wait_recv()
    core_side = send(7, spot(1 - side, row, core), spot(1 - side, row, core), near_core)
    row_b.wait_recv()
    core_row = send(8, spot(side, 1 - row, core), spot(side, 1 - row, core), near_core)
    for far in range(1, lines - 2):
        line.take(far)
    away_a.wait_recv()
    core_away_a = send(
        9, spot(1 - side, 1 - row, core, 0), spot(1 - side, 1 - row, core, 0), near_core
    )
    away_b.wait_recv()
    core_away_b = send(
        10, spot(1 - side, 1 - row, core, 1), spot(1 - side, 1 - row, core, 1), near_core
    )
    if lines > 2:
        line.take(lines - 2)
    for copy in (core_own, core_side, core_row, core_away_a, core_away_b):
        copy.wait_recv()
    for copy in copies:
        copy.wait_send()
    for copy in gain_copies:
        copy.wait()
    if lines:
        line.settle()
    local.wait()


def plane_gather(block, number=0, pair=None, gains=None, shard=None):
    rows, width = block.shape
    anywhere, vmem = pl.BlockSpec(memory_space=pl.ANY), pl.BlockSpec(memory_space=pltpu.VMEM)
    shapes, ins, outs = [jax.ShapeDtypeStruct((8 * rows, width), block.dtype)], [anywhere], [anywhere]
    operands = [block]
    if pair is not None:
        shapes.append(jax.ShapeDtypeStruct((pair[0].shape[1], pair[1].shape[1]), BF16))
        ins += [vmem, vmem]
        outs += [vmem]
        operands += pair
    planes, lines, scratch = 0, 0, []
    if shard is not None:
        lines = lax.axis_size("dp")
        shapes.append(jax.ShapeDtypeStruct((lines * shard.shape[0], shard.shape[1]), shard.dtype))
        ins += [anywhere]
        outs += [vmem]
        operands += [shard]
        scratch = [pltpu.SemaphoreType.DMA((2, lines - 1))] * 2 + [pltpu.SemaphoreType.DMA]
    if gains is not None:
        planes = lax.axis_size("dp")
        shapes.append(jax.ShapeDtypeStruct((4 * planes,) + gains.shape, gains.dtype))
        ins += [vmem]
        outs += [vmem]
        operands += [gains]
        scratch = [pltpu.SemaphoreType.DMA((4 * planes - 1,))] * 2 + [pltpu.SemaphoreType.DMA]
    return pl.pallas_call(
        functools.partial(gather_kernel, rows, 8 if pair is not None else 0, planes, lines),
        out_shape=tuple(shapes),
        in_specs=ins,
        out_specs=tuple(outs),
        scratch_shapes=[
            pltpu.SemaphoreType.DMA((11,)),
            pltpu.SemaphoreType.DMA((11,)),
            pltpu.SemaphoreType.DMA,
        ]
        + scratch,
        compiler_params=pltpu.CompilerParams(
            collective_id=number, has_side_effects=True, vmem_limit_bytes=60 * 1024 * 1024
        ),
        cost_estimate=pl.CostEstimate(flops=0, bytes_accessed=1024, transcendentals=0),
        name="plane_gather",
    )(*operands)


def swap_scratch():
    return [pltpu.SemaphoreType.DMA((3,))] * 2 + [pltpu.SemaphoreType.DMA]


def swap_copies(in_ref, out_ref, send_sems, recv_sems, local_sem):
    _, row, core, *_ = place()
    rows = out_ref.shape[1]
    here = row * 2 + core

    def block(index):
        return in_ref.at[pl.ds(pl.multiple_of(index * rows, rows), rows)]

    peers = (row * 2 + 1 - core, (1 - row) * 2 + core, (1 - row) * 2 + 1 - core)
    away = [
        remote(block(peer), out_ref.at[here], send_sems.at[at], recv_sems.at[at], {"ctx": peer})
        for at, peer in enumerate(peers)
    ]
    return away, pltpu.make_async_copy(block(here), out_ref.at[here], local_sem)


def norm_back(rows, grad_ref, value_ref, factor_ref, gain_ref, base_ref, out_ref, low_ref, term_ref):
    tile = 32
    gain = gain_ref[...]

    def step(index, total):
        here = pl.ds(pl.multiple_of(index * tile, tile), tile)
        grad, value, factor = grad_ref[here, :], value_ref[here, :], factor_ref[here, :]
        scaled = grad * gain
        inner = jnp.mean(scaled * value, axis=1, keepdims=True)
        back = factor * scaled - value * (factor * factor * factor) * inner
        result = base_ref[here, :].astype(F32) + back
        if out_ref is not None:
            out_ref[here, :] = result
        low_ref[here, :] = result.astype(BF16)
        return total + jnp.sum(grad * value * factor, axis=0, keepdims=True)

    total = lax.fori_loop(0, rows // tile, step, jnp.zeros((1, gain.shape[1]), F32))
    term_ref[...] = jnp.broadcast_to(total, term_ref.shape)


def scatter_steps(rows, left_of, right_of, out_ref, scratch, swap=None, late=None):
    made, other, to_side, to_row, from_side, from_row = scratch[:6]
    on_side, on_row, got_side, got_row, send_sems, recv_sems = scratch[6:]
    side, row, core, near_core, near_side, near_row = place()
    tile = 32
    wide = out_ref.shape[1] // 2

    chips = ((side, row), (1 - side, row), (side, 1 - row), (1 - side, 1 - row))
    routes = [
        (made.at[chip, part, 1 - core], other.at[chip, part], near_core)
        for chip in range(4)
        for part in range(2)
    ] + [
        (to_side.at[0], from_side.at[0], near_side),
        (to_row.at[0], from_row.at[0], near_row),
        (to_side.at[1], from_side.at[1], near_side),
        (to_row.at[1], from_row.at[1], near_row),
        (on_row, got_row, near_row),
        (on_side, got_side, near_side),
    ]
    copies = [
        remote(source, target, send_sems.at[at], recv_sems.at[at], device)
        for at, (source, target, device) in enumerate(routes)
    ]
    side_0, row_0, side_1, row_1, last_row, last_side = copies[8:]
    swapped = None if swap is None else swap_copies(*swap)

    def make(chip, part, first=False):
        a, b = chips[chip]
        start = pl.multiple_of((a * 4 + b * 2) * rows, 2 * rows)
        left, value, first_col = left_of(chip, start), None, 0
        for right in right_of(pl.ds(part * wide, wide)):
            last_col = first_col + right.shape[1]
            term = matmul_nt(left[:, first_col:last_col], right)
            value = term if value is None else value + term
            first_col = last_col
        made[chip, part, 0] = value[:rows].astype(BF16)
        made[chip, part, 1] = value[rows:].astype(BF16)
        if first:
            partners = (near_core, near_side, near_row)
            if swap is not None:
                partners += ({"ctx": (1 - row) * 2 + 1 - core},)
            greet(partners)
        copies[2 * chip + part].start()

    def both(chip, part, at):
        here = made[chip, part, core, pl.ds(at, tile), :].astype(F32)
        return here + other[chip, part, pl.ds(at, tile), :].astype(F32)

    def each(body):
        def step(index, carry):
            body(pl.multiple_of(index * tile, tile))
            return carry

        lax.fori_loop(0, rows // tile, step, 0)

    def put(target, chip, part, copy, extra=None):
        copies[2 * chip + part].wait_recv()

        def body(at):
            value = both(chip, part, at)
            if extra is not None:
                value = value + extra[pl.ds(at, tile), :].astype(F32)
            target[pl.ds(at, tile), :] = value.astype(BF16)

        each(body)
        copy.start()

    def across():
        make(3, 0, True)
        make(3, 1)
        put(to_side.at[0], 3, 0, side_0)
        put(to_row.at[0], 3, 1, row_0)
        if swap is not None:
            for copy in swapped[0] + [swapped[1]]:
                copy.start()

    def along():
        make(1, 0)
        make(2, 1)
        put(to_side.at[1], 1, 0, side_1)
        put(to_row.at[1], 2, 1, row_1)

    def forward():
        make(1, 1)
        make(2, 0)
        row_0.wait_recv()
        put(on_side, 1, 1, last_side, from_row.at[0])
        side_0.wait_recv()
        put(on_row, 2, 0, last_row, from_side.at[0])

    def own():
        make(0, 0)
        make(0, 1)

    def finish():
        copies[0].wait_recv()
        copies[1].wait_recv()
        side_1.wait_recv()
        row_1.wait_recv()

        def first_sum(at):
            here = pl.ds(at, tile)
            out_ref[here, :wide] = both(0, 0, at) + from_side[1, here, :].astype(F32)
            out_ref[here, wide:] = both(0, 1, at) + from_row[1, here, :].astype(F32)

        each(first_sum)
        if swap is not None:
            for copy in swapped[0]:
                copy.wait()
            swapped[1].wait()
            late()
        last_side.wait_recv()
        last_row.wait_recv()

        def last_sum(at):
            here = pl.ds(at, tile)
            out_ref[here, :wide] += got_row[here, :].astype(F32)
            out_ref[here, wide:] += got_side[here, :].astype(F32)

        each(last_sum)
        for copy in copies:
            copy.wait_send()

    return across, along, forward, own, finish


def scatter_scratch(rows, width):
    half = width // 2
    return (
        [pltpu.VMEM((4, 2, 2, rows, half), BF16), pltpu.VMEM((4, 2, rows, half), BF16)]
        + [pltpu.VMEM((2, rows, half), BF16)] * 4
        + [pltpu.VMEM((rows, half), BF16)] * 4
        + [pltpu.SemaphoreType.DMA((14,))] * 2
    )


def scatter_kernel(rows, swaps, columns, left, right, *refs):
    swap, late = None, None
    if swaps:
        in_ref, value_ref, factor_ref, gain_ref, base_ref, low_ref, term_ref, laid_ref = refs[:8]
        out_ref, *scratch = refs[8:]
        swapped = scratch[-4]
        swap = (in_ref, swapped, *scratch[-3:])
        scratch = scratch[:-4]

        def late():
            size = swapped.shape[2]
            for part in range(4):
                laid_ref[:, part * size : (part + 1) * size] = swapped[part]

    else:
        out_ref, *scratch = refs

    def left_of(chip, start):
        return left[pl.ds(start, 2 * rows), :]

    def right_of(at):
        return [right[at, columns]]

    for step in scatter_steps(rows, left_of, right_of, out_ref, scratch, swap=swap, late=late):
        step()
    if swaps:
        norm_back(
            rows, out_ref, value_ref, factor_ref, gain_ref, base_ref, None, low_ref, term_ref
        )


def product_scatter(number, left, right, start, size, swap=None, norm=()):
    total = left.shape[0]
    width = right.shape[0]
    rows = total // 8
    vmem = pl.BlockSpec(memory_space=pltpu.VMEM)
    if swap is None:
        shapes, ins, scratch = [jax.ShapeDtypeStruct((rows, width), F32)], [vmem, vmem], []
        operands = [left, right]
    else:
        deep = swap.shape[0] // 4
        shapes = [
            jax.ShapeDtypeStruct((rows, width), BF16),
            jax.ShapeDtypeStruct((8, width), F32),
            jax.ShapeDtypeStruct((deep, 4 * swap.shape[1]), swap.dtype),
        ]
        ins = [vmem, vmem, pl.BlockSpec(memory_space=pl.ANY)] + [vmem] * 4
        operands = [left, right, swap, *norm]
        scratch = [pltpu.VMEM((4, deep, swap.shape[1]), swap.dtype)] + swap_scratch()
    return pl.pallas_call(
        functools.partial(scatter_kernel, rows, swap is not None, slice(start, start + size)),
        out_shape=tuple(shapes),
        in_specs=ins,
        out_specs=tuple([vmem] * len(shapes)),
        scratch_shapes=([pltpu.VMEM((rows, width), F32)] if swap is not None else [])
        + scatter_scratch(rows, width)
        + scratch,
        compiler_params=pltpu.CompilerParams(
            collective_id=number, has_side_effects=True, vmem_limit_bytes=56 * 1024 * 1024
        ),
        cost_estimate=pl.CostEstimate(flops=0, bytes_accessed=1024, transcendentals=0),
        name="product_scatter",
    )(*operands)


def ffn_back_kernel(
    rows,
    own_ref,
    far_ref,
    twin_ref,
    twin_far_ref,
    gate_slope_ref,
    up_slope_ref,
    down_lead_ref,
    down_ref,
    right_ref,
    value_ref,
    factor_ref,
    gain_ref,
    base_ref,
    result_ref,
    low_ref,
    term_ref,
    gate_ref,
    up_ref,
    out_ref,
    weight,
    weight_sems,
    cots,
    gate_slopes,
    up_slopes,
    lefts,
    sems,
    out_sems,
    *scratch,
):
    side, row, core, *_ = place()
    lead = down_lead_ref.shape[1]
    units = lead + down_ref.shape[1]
    turns = (3, 1, 2, 0)
    chips = ((side, row), (1 - side, row), (side, 1 - row), (1 - side, 1 - row))
    starts = [pl.multiple_of((a * 4 + b * 2) * rows, 2 * rows) for a, b in chips]
    stored = []

    def fetch(turn):
        chip = turns[turn]
        near, away = (own_ref, twin_ref) if chip < 2 else (far_ref, twin_far_ref)
        there = pl.ds(starts[chip], 2 * rows)
        slot = turn % 2
        return [
            pltpu.make_async_copy(source, target, sems.at[which, slot])
            for which, (source, target) in enumerate(
                (
                    (near.at[chips[chip][0]], cots.at[slot, core]),
                    (away.at[chips[chip][0]], cots.at[slot, 1 - core]),
                    (gate_slope_ref.at[there], gate_slopes.at[slot]),
                    (up_slope_ref.at[there], up_slopes.at[slot]),
                )
            )
        ]

    def store(turn):
        there = pl.ds(starts[turns[turn]], 2 * rows)
        slot = turn % 2
        return [
            pltpu.make_async_copy(
                lefts.at[slot, :, pl.ds(which * units, units)],
                target.at[there],
                out_sems.at[which, slot],
            )
            for which, target in enumerate((gate_ref, up_ref))
        ]

    joins = [
        pltpu.make_async_copy(source, weight.at[:, pl.ds(first, source.shape[1])], weight_sems.at[at])
        for at, (source, first) in enumerate(((down_lead_ref, 0), (down_ref, lead)))
    ]

    def start(copies):
        for copy in copies:
            copy.start()

    def wait(copies):
        for copy in copies:
            copy.wait()

    def left_of(chip, _):
        turn = turns.index(chip)
        slot = turn % 2
        if chip in stored:
            return lefts[slot]
        stored.append(chip)
        if turn == 0:
            start(joins)
            start(fetch(0))
        if turn == 1:
            start(fetch(2))
        if turn == 2:
            start(fetch(3))
        if turn == 0:
            start(fetch(1))
        if turn == 0:
            wait(joins)
        wait(fetch(turn))
        if turn > 1:
            wait(store(turn - 2))
        cot = cots[slot].reshape(2 * rows, cots.shape[3])
        grad = jnp.dot(cot, weight[...], preferred_element_type=F32)
        lefts[slot, :, :units] = (grad * gate_slopes[slot].astype(F32)).astype(BF16)
        lefts[slot, :, units:] = (grad * up_slopes[slot].astype(F32)).astype(BF16)
        start(store(turn))
        return lefts[slot]

    def right_of(at):
        return [right_ref[at, :]]

    for step in scatter_steps(rows, left_of, right_of, out_ref, scratch):
        step()
    norm_back(
        rows, out_ref, value_ref, factor_ref, gain_ref, base_ref, result_ref, low_ref, term_ref
    )
    wait(store(2))
    wait(store(3))


def ffn_back(number, cots, gate_slope, up_slope, down_lead, down_w, gate_up, norm):
    total, units = gate_slope.shape
    width = down_w.shape[0]
    rows = total // 8
    vmem = pl.BlockSpec(memory_space=pltpu.VMEM)
    anywhere = pl.BlockSpec(memory_space=pl.ANY)
    return pl.pallas_call(
        functools.partial(ffn_back_kernel, rows),
        out_shape=(
            jax.ShapeDtypeStruct((rows, width), F32),
            jax.ShapeDtypeStruct((rows, width), BF16),
            jax.ShapeDtypeStruct((8, width), F32),
            jax.ShapeDtypeStruct((total, units), BF16),
            jax.ShapeDtypeStruct((total, units), BF16),
        ),
        in_specs=[anywhere] * 8 + [vmem] * 5,
        out_specs=(vmem, vmem, vmem, anywhere, anywhere),
        scratch_shapes=[
            pltpu.VMEM((rows, width), F32),
            pltpu.VMEM((width, units), BF16),
            pltpu.SemaphoreType.DMA((2,)),
            pltpu.VMEM((2, 2, rows, width), BF16),
            pltpu.VMEM((2, 2 * rows, units), BF16),
            pltpu.VMEM((2, 2 * rows, units), BF16),
            pltpu.VMEM((2, 2 * rows, 2 * units), BF16),
            pltpu.SemaphoreType.DMA((4, 2)),
            pltpu.SemaphoreType.DMA((2, 2)),
        ]
        + scatter_scratch(rows, width),
        compiler_params=pltpu.CompilerParams(
            collective_id=number, has_side_effects=True, vmem_limit_bytes=60 * 1024 * 1024
        ),
        cost_estimate=pl.CostEstimate(flops=0, bytes_accessed=1024, transcendentals=0),
        name="ffn_back",
    )(*cots, gate_slope, up_slope, down_lead, down_w, gate_up, *norm)


def ffn_kernel(in_ref, w_ref, product_ref, gate_slope_ref, up_slope_ref):
    units = product_ref.shape[1]
    wide = 512
    rows_in = in_ref[...]
    for start in range(0, units, wide):
        at = pl.ds(start, wide)
        gate = jnp.dot(rows_in, w_ref[:, at], preferred_element_type=F32)
        up = jnp.dot(rows_in, w_ref[:, pl.ds(units + start, wide)], preferred_element_type=F32)
        sigma = jax.nn.sigmoid(gate)
        active = gate * sigma
        product_ref[:, at] = (active * up).astype(BF16)
        gate_slope_ref[:, at] = (up * sigma * (1.0 + gate * (1.0 - sigma))).astype(BF16)
        up_slope_ref[:, at] = active.astype(BF16)


def ffn(rows_in, gate_up):
    total, width = rows_in.shape
    units = gate_up.shape[1] // 2
    rows = 512
    out = pl.BlockSpec((rows, units), lambda i: (i, 0))
    return pl.pallas_call(
        ffn_kernel,
        grid=(total // rows,),
        out_shape=(jax.ShapeDtypeStruct((total, units), BF16),) * 3,
        in_specs=[
            pl.BlockSpec((rows, width), lambda i: (i, 0)),
            pl.BlockSpec(
                (width, 2 * units), lambda i: (0, 0), pipeline_mode=pl.Buffered(1)
            ),
        ],
        out_specs=(out, out, out),
        compiler_params=pltpu.CompilerParams(vmem_limit_bytes=60 * 1024 * 1024),
        cost_estimate=pl.CostEstimate(flops=0, bytes_accessed=1024, transcendentals=0),
        name="ffn",
    )(rows_in, gate_up)


def swap_halves(values):
    width = values.shape[-1]
    lane = lax.broadcasted_iota(jnp.int32, values.shape, 1)
    ahead = pltpu.roll(values, width - HEAD_DIM // 2, 1)
    behind = pltpu.roll(values, HEAD_DIM // 2, 1)
    return jnp.where(lane % HEAD_DIM < HEAD_DIM // 2, ahead, behind)


def pieces_of(block):
    return ((0, block * QB, False), (block * QB, QB, True)) if block else ((0, QB, True),)


def masked_scores(query, keys, diagonal):
    scores = matmul_nt(query, keys)
    if diagonal:
        here = lax.broadcasted_iota(jnp.int32, scores.shape, 0)
        there = lax.broadcasted_iota(jnp.int32, scores.shape, 1)
        scores = jnp.where(here >= there, scores, -1e30)
    return scores


def attend_kernel(length, q_ref, kv_ref, cos_ref, sin_ref, att_ref, qrot_ref, kvrot_ref, log_ref):
    cosine = cos_ref[...]
    signed = sin_ref[...]
    scale = HEAD_DIM ** (-0.5)
    pre = q_ref[...]
    qrot_ref[...] = (pre * cosine + swap_halves(pre) * signed).astype(BF16)
    pre = kv_ref[...]
    lane = lax.broadcasted_iota(jnp.int32, pre.shape, 1)
    turned = jnp.where(lane < HEAD_DIM, pre * cosine + swap_halves(pre) * signed, pre)
    kvrot_ref[...] = turned.astype(BF16)
    for block in range(length // QB):
        here = pl.ds(block * QB, QB)
        logs = []
        mixed = []
        for head in range(2):
            query = qrot_ref[here, head * HEAD_DIM : (head + 1) * HEAD_DIM] * jnp.asarray(
                scale, BF16
            )
            scores = []
            for start, size, diagonal in pieces_of(block):
                keys = kvrot_ref[pl.ds(start, size), :HEAD_DIM]
                scores.append(masked_scores(query, keys, diagonal))
            peak = functools.reduce(
                jnp.maximum, [jnp.max(s, axis=1, keepdims=True) for s in scores]
            )
            powers = [jnp.exp(s - peak) for s in scores]
            total = sum(jnp.sum(p, axis=1, keepdims=True) for p in powers)
            inverse = 1.0 / total
            out = None
            for (start, size, _), power in zip(pieces_of(block), powers):
                values = kvrot_ref[pl.ds(start, size), HEAD_DIM:]
                term = jnp.dot(
                    (power * inverse).astype(BF16), values, preferred_element_type=F32
                )
                out = term if out is None else out + term
            mixed.append(out)
            logs.append(peak + jnp.log(total))
        att_ref[here, :] = jnp.concatenate(mixed, axis=1).astype(BF16)
        lane = lax.broadcasted_iota(jnp.int32, (QB, 128), 1)
        log_ref[here, :] = jnp.where(lane < HEAD_DIM, logs[0], logs[1])


def attend(pre, cosine, signed, seqs):
    rows = pre.shape[0]
    length = rows // seqs
    pairs = pre.shape[1] // 128 - 1
    block = (length, 128)
    return pl.pallas_call(
        functools.partial(attend_kernel, length),
        grid=(seqs, pairs),
        out_shape=(
            jax.ShapeDtypeStruct((rows, pairs * 128), BF16),
            jax.ShapeDtypeStruct((rows, pairs * 128), BF16),
            jax.ShapeDtypeStruct((rows, 128), BF16),
            jax.ShapeDtypeStruct((rows, pairs * 128), F32),
        ),
        in_specs=[
            pl.BlockSpec(block, lambda s, h: (s, h)),
            pl.BlockSpec(block, lambda s, h: (s, pairs)),
            pl.BlockSpec(block, lambda s, h: (0, 0)),
            pl.BlockSpec(block, lambda s, h: (0, 0)),
        ],
        out_specs=(
            pl.BlockSpec(block, lambda s, h: (s, h)),
            pl.BlockSpec(block, lambda s, h: (s, h)),
            pl.BlockSpec(block, lambda s, h: (s, 0)),
            pl.BlockSpec(block, lambda s, h: (s, h)),
        ),
        compiler_params=pltpu.CompilerParams(vmem_limit_bytes=60 * 1024 * 1024),
        cost_estimate=pl.CostEstimate(
            flops=8 * rows * length * 128 * pairs,
            bytes_accessed=rows * pairs * 128 * 12,
            transcendentals=rows * length * 2 * pairs,
        ),
        name="attend",
    )(pre, pre, cosine, signed)


def attend_back_kernel(
    seqs,
    rows,
    q_ref,
    kv_ref,
    up_ref,
    log_ref,
    cos_ref,
    sin_ref,
    left_ref,
    right_lead_ref,
    right_ref,
    hidden_ref,
    in_ref,
    back_ref,
    out_ref,
    laid_ref,
    sum_ref,
    ffn_ref,
    swapped,
    *scratch,
):
    def late():
        size = swapped.shape[2]
        for part in range(4):
            turned = jnp.transpose(swapped[part].astype(F32))
            laid_ref[part * size : (part + 1) * size, :] = turned.astype(BF16)

    across, along, forward, own, finish = scatter_steps(
        rows,
        lambda chip, start: left_ref[pl.ds(start, 2 * rows), :],
        lambda at: [right_lead_ref[at, :], right_ref[at, :]],
        ffn_ref,
        scratch[:-3],
        swap=(in_ref, swapped, *scratch[-3:]),
        late=late,
    )
    scale = HEAD_DIM ** (-0.5)
    length = q_ref.shape[0] // seqs
    pairs = q_ref.shape[1] // 128
    across()
    along()

    def one_pair(index, carry):
        seq = index // pairs
        pair = index % pairs
        lanes_at = pl.ds(pl.multiple_of(pair * 128, 128), 128)
        base = pl.multiple_of(seq * length, length)

        @pl.when(index == 1)
        def _():
            forward()

        @pl.when(index == 2)
        def _():
            own()

        @pl.when(pair == 0)
        def _():
            sum_ref[...] = jnp.zeros_like(sum_ref)

        for block in range(length // QB):
            here = pl.ds(base + block * QB, QB)
            turned = []
            q_pair = q_ref[here, lanes_at]
            up_pair = up_ref[here, lanes_at]
            log_pair = log_ref[here, lanes_at]
            for head in range(2):
                lanes = slice(head * HEAD_DIM, (head + 1) * HEAD_DIM)
                query = q_pair[:, lanes] * jnp.asarray(scale, BF16)
                upstream = up_pair[:, lanes]
                logs = log_pair[:, head * HEAD_DIM : head * HEAD_DIM + 1]
                saved = []
                inner = None
                for start, size, diagonal in pieces_of(block):
                    keys = kv_ref[pl.ds(base + start, size), :HEAD_DIM]
                    values = kv_ref[pl.ds(base + start, size), HEAD_DIM:]
                    probability = jnp.exp(masked_scores(query, keys, diagonal) - logs)
                    prob_grad = matmul_nt(upstream, values)
                    term = jnp.sum(probability * prob_grad, axis=1, keepdims=True)
                    inner = term if inner is None else inner + term
                    saved.append((start, size, probability, prob_grad))
                out = None
                for start, size, probability, prob_grad in saved:
                    keys = kv_ref[pl.ds(base + start, size), :HEAD_DIM]
                    score_grad = (probability * (prob_grad - inner)).astype(BF16)
                    rounded = probability.astype(BF16)
                    term = jnp.dot(score_grad, keys, preferred_element_type=F32)
                    out = term if out is None else out + term
                    sum_ref[pl.ds(start, size), :] += jnp.concatenate(
                        [matmul_t(score_grad, query), matmul_t(rounded, upstream)], axis=1
                    )
                turned.append(out * scale)
            grad = jnp.concatenate(turned, axis=1)
            angle = pl.ds(block * QB, QB)
            back_ref[here, lanes_at] = (
                grad * cos_ref[angle, :] - swap_halves(grad) * sin_ref[angle, :]
            ).astype(BF16)

        @pl.when(pair == pairs - 1)
        def _():
            grad = sum_ref[...]
            lane = lax.broadcasted_iota(jnp.int32, grad.shape, 1)
            back = grad * cos_ref[...] - swap_halves(grad) * sin_ref[...]
            back_ref[pl.ds(base, length), pairs * 128 :] = jnp.where(
                lane < HEAD_DIM, back, grad
            ).astype(BF16)

        return carry

    lax.fori_loop(0, seqs * pairs, one_pair, 0)
    finish()

    def add(index, carry):
        at = pl.ds(pl.multiple_of(index * 32, 32), 32)
        out_ref[at, :] = (hidden_ref[at, :] + ffn_ref[at, :]).astype(BF16)
        return carry

    lax.fori_loop(0, rows // 32, add, 0)


def attend_back(
    number, queries, keyvals, upstream, logs, cosine, signed, seqs, left, lead, right, hidden, swap
):
    total, width = queries.shape
    length = total // seqs
    rows = total // 8
    deep = swap.shape[0] // 4
    vmem = pl.BlockSpec(memory_space=pltpu.VMEM)
    return pl.pallas_call(
        functools.partial(attend_back_kernel, seqs, rows),
        out_shape=(
            jax.ShapeDtypeStruct((total, width + 128), BF16),
            jax.ShapeDtypeStruct(hidden.shape, BF16),
            jax.ShapeDtypeStruct((4 * swap.shape[1], deep), BF16),
        ),
        in_specs=[vmem] * 10 + [pl.BlockSpec(memory_space=pl.ANY)],
        out_specs=(vmem, vmem, vmem),
        scratch_shapes=[
            pltpu.VMEM((length, 128), F32),
            pltpu.VMEM(hidden.shape, F32),
            pltpu.VMEM((4, deep, swap.shape[1]), BF16),
        ]
        + scatter_scratch(rows, right.shape[0])
        + swap_scratch(),
        compiler_params=pltpu.CompilerParams(
            collective_id=number, has_side_effects=True, vmem_limit_bytes=56 * 1024 * 1024
        ),
        cost_estimate=pl.CostEstimate(flops=0, bytes_accessed=1024, transcendentals=0),
        name="attend_back",
    )(queries, keyvals, upstream, logs, cosine, signed, left, lead, right, hidden, swap)


def gain_kernel(
    planes,
    parts,
    cols,
    attn_term_ref,
    ffn_term_ref,
    up_ref,
    gain_ref,
    laid_ref,
    total,
    seen,
    far,
    mine,
    across,
    swapped,
    send_sems,
    recv_sems,
    *swap_sems,
):
    side, row, core, near_core, near_side, near_row = place()
    plane = lax.axis_index("dp")
    ctx = row * 2 + core
    others = [{"dp": (plane + step) % planes} for step in range(1, planes)]
    corner = {"ctx": (1 - row) * 2 + 1 - core}
    greet((near_core, near_side, near_row, corner) + tuple(others))
    first = lax.broadcasted_iota(jnp.int32, total.shape, 0) == 0
    total[...] = jnp.where(first, attn_term_ref[...], ffn_term_ref[...])
    copies = []
    up_copies, up_local = swap_copies(up_ref, swapped, *swap_sems)
    for number, target in enumerate((near_core, near_row)):
        copy = remote(
            total, seen.at[number], send_sems.at[number], recv_sems.at[number], target
        )
        copy.start()
        copy.wait()
        total[...] += seen[number]
    for copy in up_copies + [up_local]:
        copy.start()
    for step, target in enumerate(others, 1):
        start = (((plane + step) % planes) * parts + ctx) * cols
        copy = remote(
            total.at[:, pl.ds(pl.multiple_of(start, cols), cols)],
            far.at[step - 1],
            send_sems.at[2 + step],
            recv_sems.at[2 + step],
            target,
        )
        copy.start()
        copies.append(copy)
    start = (plane * parts + ctx) * cols
    value = total[:, pl.ds(pl.multiple_of(start, cols), cols)]
    for number, copy in enumerate(copies):
        copy.wait_recv()
        value += far[number]
    mine[...] = value
    last = remote(mine, across, send_sems.at[2], recv_sems.at[2], near_side)
    last.start()
    copies.append(last)
    for copy in up_copies:
        copy.wait()
    up_local.wait()
    size = swapped.shape[2]
    for part in range(4):
        laid_ref[:, part * size : (part + 1) * size] = swapped[part]
    last.wait_recv()
    gain_ref[...] = value + across[...]
    for copy in copies:
        copy.wait_send()


def gain_sum(number, attn_term, ffn_term, up_sum):
    planes = lax.axis_size("dp")
    parts = lax.axis_size("ctx")
    rows, width = attn_term.shape
    cols = width // (planes * parts)
    deep = up_sum.shape[0] // parts
    vmem = pl.BlockSpec(memory_space=pltpu.VMEM)
    anywhere = pl.BlockSpec(memory_space=pl.ANY)
    return pl.pallas_call(
        functools.partial(gain_kernel, planes, parts, cols),
        out_shape=(
            jax.ShapeDtypeStruct((rows, cols), F32),
            jax.ShapeDtypeStruct((deep, parts * up_sum.shape[1]), BF16),
        ),
        in_specs=[vmem, vmem, anywhere],
        out_specs=(vmem,) * 2,
        scratch_shapes=[
            pltpu.VMEM((rows, width), F32),
            pltpu.VMEM((2, rows, width), F32),
            pltpu.VMEM((planes - 1, rows, cols), F32),
            pltpu.VMEM((rows, cols), F32),
            pltpu.VMEM((rows, cols), F32),
            pltpu.VMEM((parts, deep, up_sum.shape[1]), BF16),
            pltpu.SemaphoreType.DMA((planes + 2,)),
            pltpu.SemaphoreType.DMA((planes + 2,)),
        ]
        + swap_scratch(),
        compiler_params=pltpu.CompilerParams(collective_id=number, has_side_effects=True),
        cost_estimate=pl.CostEstimate(flops=0, bytes_accessed=1024, transcendentals=0),
        name="gain_sum",
    )(attn_term, ffn_term, up_sum)


def last_kernel(
    q_cols, attn_ref, query_ref, key_ref, value_ref, wide_ref, swapped, *swap_sems
):
    _, row, core, near_core, _, near_row = place()
    greet((near_core, near_row, {"ctx": (1 - row) * 2 + 1 - core}))
    copies, local = swap_copies(attn_ref, swapped, *swap_sems)
    for copy in copies + [local]:
        copy.start()
    for copy in copies:
        copy.wait()
    local.wait()
    kv = key_ref.shape[1] // 4
    for part in range(4):
        query_ref[:, part * q_cols : (part + 1) * q_cols] = swapped[part, :, :q_cols]
        turned = jnp.transpose(swapped[part, :, q_cols + 2 * kv :].astype(F32))
        wide_ref[part * q_cols : (part + 1) * q_cols, :] = turned.astype(BF16)
    for at, target in ((q_cols, key_ref), (q_cols + kv, value_ref)):
        target[...] = jnp.concatenate(
            [swapped[part, :, at : at + kv] for part in range(4)], axis=1
        )


def last_swap(number, attn_sum, q_cols, kv_cols):
    parts = lax.axis_size("ctx")
    deep = attn_sum.shape[0] // parts
    vmem = pl.BlockSpec(memory_space=pltpu.VMEM)
    return pl.pallas_call(
        functools.partial(last_kernel, q_cols),
        out_shape=(
            jax.ShapeDtypeStruct((deep, parts * q_cols), BF16),
            jax.ShapeDtypeStruct((deep, parts * kv_cols), BF16),
            jax.ShapeDtypeStruct((deep, parts * kv_cols), BF16),
            jax.ShapeDtypeStruct((parts * q_cols, deep), BF16),
        ),
        in_specs=[pl.BlockSpec(memory_space=pl.ANY)],
        out_specs=(vmem,) * 4,
        scratch_shapes=[pltpu.VMEM((parts, deep, attn_sum.shape[1]), BF16)] + swap_scratch(),
        compiler_params=pltpu.CompilerParams(collective_id=number, has_side_effects=True),
        cost_estimate=pl.CostEstimate(flops=0, bytes_accessed=1024, transcendentals=0),
        name="last_swap",
    )(attn_sum)


def final_kernel(own_ref, other_ref, *refs):
    first = lax.axis_index("tensor") == 0
    half = len(refs) // 2
    sources, (out_ref, *targets) = refs[:half], refs[half:]
    own, other = own_ref[...].astype(out_ref.dtype), other_ref[...].astype(out_ref.dtype)
    out_ref[0], out_ref[1] = jnp.where(first, own, other), jnp.where(first, other, own)
    for source, target in zip(sources, targets):
        target[...] = source[...].astype(F32)


def final_forms(own, other, dtype, *grads):
    steps = 2
    rows, width = own.shape
    halves = pl.BlockSpec((rows // steps, width), lambda i: (i, 0))
    whole = pl.BlockSpec((2, rows // steps, width), lambda i: (0, i, 0))

    def block_of(grad):
        deep, wide = grad.shape
        if wide // steps % 128 == 0:
            return pl.BlockSpec((deep, wide // steps), lambda i: (0, i))
        return pl.BlockSpec((deep // steps, wide), lambda i: (i, 0))

    blocks = [block_of(grad) for grad in grads]
    return pl.pallas_call(
        final_kernel,
        grid=(steps,),
        out_shape=(jax.ShapeDtypeStruct((2, rows, width), dtype),)
        + tuple(jax.ShapeDtypeStruct(grad.shape, F32) for grad in grads),
        in_specs=[halves] * 2 + blocks,
        out_specs=(whole, *blocks),
        compiler_params=pltpu.CompilerParams(vmem_limit_bytes=60 * 1024 * 1024),
        cost_estimate=pl.CostEstimate(flops=0, bytes_accessed=1024, transcendentals=0),
        name="final_forms",
    )(own, other, *grads)


def lay_kernel(own_ref, far_ref, twin_ref, twin_far_ref, all_ref, sems):
    ctx = lax.axis_index("ctx")
    row, core = ctx // 2, ctx % 2
    span = own_ref.shape[1]
    copies = []
    for number, (part, a, b) in enumerate(
        (
            (own_ref, row, core),
            (twin_ref, row, 1 - core),
            (far_ref, 1 - row, core),
            (twin_far_ref, 1 - row, 1 - core),
        )
    ):
        start = pl.multiple_of((a * 2 + b) * span, span)
        copies.append(
            pltpu.make_async_copy(part, all_ref.at[:, pl.ds(start, span)], sems.at[number])
        )
        copies[-1].start()
    for copy in copies:
        copy.wait()


def along_ctx(block, earlier, later):
    seqs, span, width = block.shape
    cores = [(0, 1), (1, 0), (2, 3), (3, 2)]
    far = lax.ppermute(after(block, earlier), "ctx", [(0, 2), (1, 3), (2, 0), (3, 1)])
    far = after(far, later)
    twin, twin_far = lax.ppermute(block, "ctx", cores), lax.ppermute(far, "ctx", cores)
    return block, far, twin, twin_far


def lay_along(parts):
    seqs, span, width = parts[0].shape
    whole = pl.pallas_call(
        lay_kernel,
        out_shape=jax.ShapeDtypeStruct((seqs, 4 * span, width), parts[0].dtype),
        in_specs=[pl.BlockSpec(memory_space=pl.ANY)] * 4,
        out_specs=pl.BlockSpec(memory_space=pltpu.VMEM),
        scratch_shapes=[pltpu.SemaphoreType.DMA((4,))],
        compiler_params=pltpu.CompilerParams(vmem_limit_bytes=24 * 1024 * 1024),
        name="lay",
    )(*parts)
    return whole.reshape(seqs * 4 * span, width)


def open_kernel(
    planes,
    q_ref,
    key_ref,
    value_ref,
    out_ref,
    gate_ref,
    up_ref,
    down_in_ref,
    attn_ref,
    gate_up_ref,
    down_lead_ref,
    down_own_ref,
    key_in,
    value_in,
    out_in,
    down_in,
    kv_ref,
    wide_ref,
    down_ref,
    load_sems,
    send_sems,
    recv_sems,
    local_sems,
    line_send,
    line_recv,
):
    _, row, core, *_ = place()
    plane = lax.axis_index("dp")
    here = row * 2 + core
    rows, units = q_ref.shape[0], gate_ref.shape[1] // 4
    peers = (row * 2 + 1 - core, (1 - row) * 2 + core, (1 - row) * 2 + 1 - core)
    ahead, behind = {"dp": (plane + 1) % planes}, {"dp": (plane + planes - 1) % planes}
    barrier = pltpu.get_barrier_semaphore()
    more, fewer = plane + 1 < planes, plane > 0
    for peer in peers:
        pl.semaphore_signal(barrier, inc=1, device_id={"ctx": peer}, device_id_type=MESH_ID)

    @pl.when(more)
    def _():
        pl.semaphore_signal(barrier, inc=1, device_id=ahead, device_id_type=MESH_ID)

    @pl.when(fewer)
    def _():
        pl.semaphore_signal(barrier, inc=1, device_id=behind, device_id_type=MESH_ID)

    loads = [
        pltpu.make_async_copy(source, target, load_sems.at[at])
        for at, (source, target) in enumerate(
            ((key_ref, key_in), (value_ref, value_in), (out_ref, out_in), (down_in_ref, down_in))
        )
    ]
    for load in loads:
        load.start()
    for load in loads[:3]:
        load.wait()
    size = key_in.shape[1] // 4
    for part in range(4):
        lanes = slice(part * size, (part + 1) * size)
        kv_ref[:, part * 2 * size : (part + 1) * 2 * size] = jnp.concatenate(
            [key_in[:, lanes], value_in[:, lanes]], axis=1
        )
    wide_ref[...] = jnp.transpose(out_in[...].astype(F32)).astype(BF16)
    pl.semaphore_wait(barrier, 3 + more.astype(jnp.int32) + fewer.astype(jnp.int32))

    mine = pl.multiple_of(here * rows, rows)
    base = pl.multiple_of(plane * 4 * rows, 4 * rows)
    moves = []
    start = 0
    for source in (q_ref, kv_ref, wide_ref):
        cols = source.shape[1] // 4
        target = attn_ref.at[pl.ds(base + mine, rows), pl.ds(start, cols)]
        moves.append((source, cols, 0, cols, target))
        start += cols
    for which, source in enumerate((gate_ref, up_ref)):
        target = gate_up_ref.at[pl.ds(mine, rows), pl.ds(which * units, units)]
        moves.append((source, units, 0, units, target))
    lead = down_lead_ref.shape[1]
    moves.append((down_ref, units, 0, lead, down_lead_ref.at[pl.ds(mine, rows)]))
    moves.append((down_ref, units, lead, units - lead, down_own_ref.at[pl.ds(mine, rows)]))
    away, local = [], []
    for which, (source, stride, shift, cols, target) in enumerate(moves):

        def columns(index, source=source, stride=stride, shift=shift, cols=cols):
            return source.at[:, pl.ds(pl.multiple_of(index * stride + shift, 128), cols)]

        away.append(
            [
                remote(
                    columns(peer),
                    target,
                    send_sems.at[which, at],
                    recv_sems.at[which, at],
                    {"ctx": peer},
                )
                for at, peer in enumerate(peers)
            ]
        )
        local.append(pltpu.make_async_copy(columns(here), target, local_sems.at[which]))
    for which in range(3):
        away[which][0].start()
        local[which].start()
    for at in (1, 2):
        for which in range(3):
            away[which][at].start()
    for which in range(3, 5):
        for copy in away[which]:
            copy.start()
        local[which].start()

    def hop(way, far, part):
        whose = plane - far if way == 0 else plane + far
        half = row if part == 0 else 1 - row
        spot = attn_ref.at[
            pl.ds(pl.multiple_of((whose * 4 + half * 2) * rows, 2 * rows), 2 * rows)
        ]
        return remote(
            spot,
            spot,
            line_send.at[way, far, part],
            line_recv.at[way, far, part],
            ahead if way == 0 else behind,
        )

    def sends(way, far):
        if way == 0:
            return (plane - far >= 0) & more
        return (plane + far < planes) & fewer

    def gets(way, far):
        return plane - 1 - far >= 0 if way == 0 else plane + 1 + far < planes

    def hop_start(way, far, part):
        @pl.when(sends(way, far))
        def _():
            hop(way, far, part).start()

    for which in range(3):
        local[which].wait()
        away[which][0].wait_recv()
    for way in range(2):
        hop_start(way, 0, 0)
    for which in range(3):
        away[which][1].wait_recv()
        away[which][2].wait_recv()
    for way in range(2):
        hop_start(way, 0, 1)
    loads[3].wait()
    for part in range(4):
        there = slice(part * units, (part + 1) * units)
        down_ref[:, there] = jnp.transpose(down_in[there, :].astype(F32)).astype(BF16)
    for copy in away[5] + away[6] + [local[5], local[6]]:
        copy.start()
    for far in range(planes - 1):
        for part in range(2):
            for way in range(2):

                @pl.when(gets(way, far))
                def _(way=way, far=far, part=part):
                    hop(way, far, part).wait_recv()

                if far + 1 < planes - 1:
                    hop_start(way, far + 1, part)
    for far in range(planes - 1):
        for part in range(2):
            for way in range(2):

                @pl.when(sends(way, far))
                def _(way=way, far=far, part=part):
                    hop(way, far, part).wait_send()

    for which in range(7):
        if which > 2:
            local[which].wait()
            for copy in away[which]:
                copy.wait_recv()
        for copy in away[which]:
            copy.wait_send()


def open_weights(query, key, value, out, gate, up, down, lead):
    planes = lax.axis_size("dp")
    rows = query.shape[0]
    cols = (query.shape[1] + 2 * key.shape[1] + out.shape[0]) // 4
    units = gate.shape[1] // 4
    anywhere, vmem = pl.BlockSpec(memory_space=pl.ANY), pl.BlockSpec(memory_space=pltpu.VMEM)
    return pl.pallas_call(
        functools.partial(open_kernel, planes),
        out_shape=(
            jax.ShapeDtypeStruct((planes * 4 * rows, cols), BF16),
            jax.ShapeDtypeStruct((4 * rows, 2 * units), BF16),
            jax.ShapeDtypeStruct((4 * rows, lead), BF16),
            jax.ShapeDtypeStruct((4 * rows, units - lead), BF16),
        ),
        in_specs=[anywhere] * 7,
        out_specs=(vmem, anywhere, anywhere, anywhere),
        scratch_shapes=[
            pltpu.VMEM(key.shape, BF16),
            pltpu.VMEM(value.shape, BF16),
            pltpu.VMEM(out.shape, BF16),
            pltpu.VMEM(down.shape, BF16),
            pltpu.VMEM((rows, 2 * key.shape[1]), BF16),
            pltpu.VMEM((rows, out.shape[0]), BF16),
            pltpu.VMEM((rows, down.shape[0]), BF16),
            pltpu.SemaphoreType.DMA((4,)),
            pltpu.SemaphoreType.DMA((7, 3)),
            pltpu.SemaphoreType.DMA((7, 3)),
            pltpu.SemaphoreType.DMA((7,)),
            pltpu.SemaphoreType.DMA((2, planes - 1, 2)),
            pltpu.SemaphoreType.DMA((2, planes - 1, 2)),
        ],
        compiler_params=pltpu.CompilerParams(
            collective_id=6, has_side_effects=True, vmem_limit_bytes=60 * 1024 * 1024
        ),
        cost_estimate=pl.CostEstimate(flops=0, bytes_accessed=1024, transcendentals=0),
        name="open_weights",
    )(query, key, value, out, gate, up, down)


def after(value, *earlier):
    return lax.optimization_barrier((value,) + earlier)[0]


def to_units(weight):
    return lax.all_to_all(weight, "ctx", split_axis=1, concat_axis=0, tiled=True)


def swap_sides(block):
    return lax.ppermute(block, "tensor", [(0, 1), (1, 0)])


def on_plane(
    layer_input,
    attn_gain,
    w_query,
    w_key,
    w_value,
    w_out,
    ffn_gain,
    w_gate,
    w_up,
    w_down,
    cotangent,
):
    seqs, span, width = layer_input.shape
    planes = lax.axis_size("dp")
    parts = lax.axis_size("ctx")
    side = lax.axis_index("tensor")
    length = span * parts
    rows_w = w_query.shape[0]
    q_cols = w_query.shape[1] // parts
    kv_cols = w_key.shape[1] // parts

    theta = angles(jnp.arange(length), HEAD_DIM)
    cosine = jnp.tile(jnp.cos(theta), (1, 4))
    sine = jnp.sin(theta)
    signed = jnp.tile(jnp.concatenate([-sine, sine], axis=1), (1, 2))

    attn_w, gate_up, lead_own, down_own = open_weights(
        w_query, w_key, w_value, w_out, w_gate, w_up, w_down, w_down.shape[0] // parts // 8
    )
    qkv_cols = q_cols + 2 * kv_cols
    w_qkv = attn_w[:, :qkv_cols]
    w_out_t = attn_w[:, qkv_cols:]
    own_in = lax.dynamic_index_in_dim(layer_input, side, 0, keepdims=False)
    own_cot = lax.dynamic_index_in_dim(cotangent, side, 0, keepdims=False)
    gains = jnp.concatenate(
        [attn_gain[None], ffn_gain[None], jnp.zeros((6, rows_w), BF16)]
    ).astype(F32)
    all_in, gains = plane_gather(after(own_in, gate_up), 10, gains=gains)
    gain_one = gains[:, 0].reshape(width)
    gain_two = gains[:, 1].reshape(width)
    gate_up = lax.all_gather(gate_up, "dp", axis=0, tiled=True)
    down_w = lax.all_gather(down_own, "dp", axis=0, tiled=True)

    all_f = all_in.astype(F32)
    normed_one = (all_f * rms_factor(all_f) * gain_one).astype(BF16)
    pre = jnp.dot(normed_one, w_qkv, preferred_element_type=F32)
    attended, queries, keyvals, logs = attend(pre, cosine, signed, seqs)
    inputs_f = own_in.astype(F32)
    factor_one = rms_factor(inputs_f)
    hidden = inputs_f + product_scatter(1, attended, attn_w, qkv_cols, q_cols)[0]
    factor_two = rms_factor(hidden)
    normed_own = (hidden * factor_two * gain_two).astype(BF16)
    normed_two, down_lead = plane_gather(normed_own, shard=lead_own)
    cots = along_ctx(cotangent, all_in, hidden)

    product, gate_slope, up_slope = ffn(normed_two, gate_up)
    all_cot = lay_along((after(cots[0], product),) + cots[1:])
    down_grad = matmul_t(all_cot, product).astype(BF16)
    down_sum = lax.psum_scatter(down_grad, "dp", scatter_dimension=0, tiled=True)
    hidden_grad, hidden_own, ffn_term, gate_grad, up_grad = ffn_back(
        3,
        cots,
        after(gate_slope, down_grad),
        up_slope,
        down_lead,
        down_w,
        gate_up,
        (hidden, factor_two, gain_two[None], own_cot),
    )
    gate_w_grad = matmul_t(normed_two, gate_grad).astype(BF16)
    gate_sum = lax.psum_scatter(gate_w_grad, "dp", scatter_dimension=0, tiled=True)
    hidden_low, up_w_grad = plane_gather(after(hidden_own, gate_w_grad), 7, [normed_two, up_grad])
    up_sum = lax.psum_scatter(up_w_grad, "dp", scatter_dimension=0, tiled=True)
    attended_grad = jnp.dot(after(hidden_low, up_w_grad), w_out_t, preferred_element_type=F32).astype(BF16)
    out_w_grad = matmul_t(hidden_low, attended).astype(BF16)
    back, out_own, down_out = attend_back(
        5,
        queries,
        keyvals,
        attended_grad,
        logs,
        cosine,
        signed,
        seqs,
        product,
        down_lead,
        down_w,
        hidden,
        down_sum,
    )
    out_other = swap_sides(out_own)
    qkv_grad = matmul_t(normed_one, back).astype(BF16)
    attn_grad = jnp.concatenate([qkv_grad, out_w_grad], axis=1)
    attn_sum = lax.psum_scatter(attn_grad, "dp", scatter_dimension=0, tiled=True)
    input_own, attn_term, gate_out = product_scatter(
        4,
        after(back, attn_grad),
        attn_w,
        0,
        qkv_cols,
        gate_sum,
        (inputs_f, factor_one, gain_one[None], hidden_grad),
    )
    input_other = swap_sides(input_own)
    layer_output, gate_out, down_out = final_forms(
        out_own, after(out_other, input_own), BF16, gate_out, down_out
    )
    gain_own, up_out = gain_sum(2, after(attn_term, layer_output), ffn_term, up_sum)
    query_out, key_out, value_out, wide_out = last_swap(
        9, after(attn_sum, gain_own), q_cols, kv_cols
    )
    input_grad, query_out, key_out, value_out, wide_out, up_out = final_forms(
        input_own,
        after(input_other, gain_own),
        F32,
        query_out,
        key_out,
        value_out,
        wide_out,
        up_out,
    )
    return (
        layer_output,
        input_grad,
        gain_own[0],
        query_out,
        key_out,
        value_out,
        wide_out,
        gain_own[1],
        gate_out,
        up_out,
        down_out,
    )


def fits_plane(mesh, shapes):
    sizes = mesh.shape
    seqs, length, width = shapes[0].shape
    kv_heads = shapes[3].shape[1] // HEAD_DIM
    return (
        sizes["tensor"] == 2
        and sizes["ctx"] == 4
        and seqs == 2 * sizes["dp"]
        and kv_heads == 8
        and shapes[2].shape[1] == 4 * shapes[3].shape[1]
        and length % (4 * QB) == 0
        and width % (128 * 4 * sizes["dp"]) == 0
    )


def placed(mesh, function):
    return jax.shard_map(
        function,
        mesh=mesh,
        in_specs=(
            P("dp", "ctx", None),
            P(("dp", "ctx")),
            P(("dp", "ctx"), "tensor"),
            P(("dp", "ctx"), "tensor"),
            P(("dp", "ctx"), "tensor"),
            P("tensor", ("dp", "ctx")),
            P(("dp", "ctx")),
            P(("dp", "ctx"), "tensor"),
            P(("dp", "ctx"), "tensor"),
            P("tensor", ("dp", "ctx")),
            P("dp", "ctx", None),
        ),
        out_specs=(
            P("dp", "ctx", None),
            P("dp", "ctx", None),
            P(("dp", "ctx")),
            P(("dp", "ctx"), "tensor"),
            P(("dp", "ctx"), "tensor"),
            P(("dp", "ctx"), "tensor"),
            P("tensor", ("dp", "ctx")),
            P(("dp", "ctx")),
            P(("dp", "ctx"), "tensor"),
            P(("dp", "ctx"), "tensor"),
            P("tensor", ("dp", "ctx")),
        ),
        check_vma=False,
    )


def solution(mesh):
    def whole(*arrays):
        return placed(mesh, on_plane if fits_plane(mesh, arrays) else on_device)(*arrays)

    return whole
```
